32 devices in a mesh: blk: 16 (over z, y, core), uly: 2 (over x).
Axes of the slice: x: 2, y: 2, z: 4, core: 2. Of those that a mesh axis runs over, the one named last changes fastest.
Arguments:
- tokens: bfloat16 [4096, 5120], P(('blk', 'uly')), may hold values from -6 to 6
- query_base: bfloat16 [4096, 5120], P(('blk', 'uly')), may hold values from -9 to 9
- key_base: bfloat16 [4096, 5120], P(('blk', 'uly')), may hold values from -9 to 9
- value_base: bfloat16 [4096, 5120], P(('blk', 'uly')), may hold values from -6 to 6
- out_grad: bfloat16 [4096, 5120], P(('blk', 'uly')), may hold values from -0.059814453 to 0.059814453
- down_q: bfloat16 [5120, 64], replicated, may hold values from -0.078125 to 0.078125
- up_q: bfloat16 [64, 5120], replicated, may hold values from -0.75 to 0.75
- down_v: bfloat16 [5120, 64], replicated, may hold values from -0.078125 to 0.078125
- up_v: bfloat16 [64, 5120], replicated, may hold values from -0.75 to 0.75
Outputs:
- attended: bfloat16 [4096, 5120], P(('blk', 'uly'))
- grad_down_q: bfloat16 [5120, 64], replicated
- grad_up_q: bfloat16 [64, 5120], P(None, 'uly')
- grad_down_v: bfloat16 [5120, 64], replicated
- grad_up_v: bfloat16 [64, 5120], P(None, 'uly')
The draws below stay inside these ranges and needn't reach their ends.
All inputs are finite; a program needn't handle non-finite values.
Results may differ from the reference program's by a relative error of at most 0.025.
Values may be sent and summed in bfloat16 or wider, within the bound.
A program may use at most 128 MiB of HBM per device.

```python
import jax
import jax.numpy as jnp
from jax import lax

D = 5120
HEADS = 40
HEAD = 128
RANK = 64
BLOCK = 256
TOKENS = 4096


def shared_bases(key):
    base = jax.random.fold_in(key, 7)
    key_query, key_keys = jax.random.split(base, 2)
    query = jnp.clip(1.5 * jax.random.normal(key_query, (TOKENS, D), jnp.float32), -9.0, 9.0)
    keys = jnp.clip(1.5 * jax.random.normal(key_keys, (TOKENS, D), jnp.float32), -9.0, 9.0)
    return (query, keys)


def draw_query_base(key, part):
    return shared_bases(key)[0].astype(jnp.bfloat16)


def draw_key_base(key, part):
    return shared_bases(key)[1].astype(jnp.bfloat16)


def shard_levels(rng, dims, shards, low, top_value):
    gain = 1.0
    for axis_at, blocks in shards:
        steps = jax.random.uniform(jax.random.fold_in(jax.random.fold_in(rng, 6), axis_at), (blocks,), jnp.float32, low / len(shards), top_value / len(shards))
        gain = gain * jnp.repeat(jnp.exp(steps), dims[axis_at] // blocks).reshape((-1,) + (1,) * (len(dims) - 1 - axis_at))
    return gain


def scatter_about(own_key, dims, deviation, bound, cuts=(), held_as=jnp.bfloat16):
    result = jax.random.normal(own_key, dims, jnp.float32) * deviation
    if len(cuts) > 0:
        result = shard_levels(own_key, dims, cuts, -0.22, 0.18) * result
    return jnp.clip(result, min=-bound, max=bound).astype(held_as)


def setup_inputs(seed: int = 0) -> dict:
    key_of = jax.random.split(jax.random.key(seed), 10)
    tokens = scatter_about(key_of[0], (TOKENS, D), 1.0, 6.0, ((0, 32),))
    query_base = draw_query_base(jax.random.fold_in(key_of[9], 71), 0)
    key_base = draw_key_base(jax.random.fold_in(key_of[9], 71), 0)
    value_base = scatter_about(key_of[3], (TOKENS, D), 1.0, 6.0, ((0, 32),))
    out_grad = scatter_about(key_of[4], (TOKENS, D), 0.01, 0.059814453, ((0, 32),))
    down_q = scatter_about(key_of[5], (D, RANK), D ** -0.5, 0.078125)
    up_q = scatter_about(key_of[6], (RANK, D), RANK ** -0.5, 0.75)
    down_v = scatter_about(key_of[7], (D, RANK), D ** -0.5, 0.078125)
    up_v = scatter_about(key_of[8], (RANK, D), RANK ** -0.5, 0.75)
    return {"tokens": tokens, "query_base": query_base, "key_base": key_base, "value_base": value_base, "out_grad": out_grad, "down_q": down_q, "up_q": up_q, "down_v": down_v, "up_v": up_v}


def inner(left, right):
    return lax.dot_general(left, right, (((0,), (0,)), ((), ())), preferred_element_type=jnp.float32)


def head_pass(query, keys, values, upstream, usable, scale):
    scores = jnp.dot(query, keys.T, preferred_element_type=jnp.float32) * scale
    scores = jnp.where(usable[None, :], scores, -jnp.inf)
    top = jnp.max(scores, axis=1, keepdims=True)
    total = jnp.sum(jnp.exp(scores - top), axis=1, keepdims=True)
    probs = jnp.exp(scores - top - jnp.log(total)).astype(jnp.bfloat16)
    attended = jnp.dot(probs, values, preferred_element_type=jnp.float32).astype(jnp.bfloat16)
    delta = jnp.sum(upstream.astype(jnp.float32) * attended.astype(jnp.float32), axis=1, keepdims=True)
    prob_grad = jnp.dot(upstream, values.T, preferred_element_type=jnp.float32)
    score_grad = (probs.astype(jnp.float32) * (prob_grad - delta)).astype(jnp.bfloat16)
    query_grad = (jnp.dot(score_grad, keys, preferred_element_type=jnp.float32) * scale).astype(jnp.bfloat16)
    value_terms = jnp.dot(probs.T, upstream, preferred_element_type=jnp.float32)
    return attended, query_grad, value_terms


def reference(tokens, query_base, key_base, value_base, out_grad, down_q, up_q, down_v, up_v):
    low_q = jnp.dot(tokens, down_q, preferred_element_type=jnp.float32).astype(jnp.bfloat16)
    low_v = jnp.dot(tokens, down_v, preferred_element_type=jnp.float32).astype(jnp.bfloat16)
    query = (query_base.astype(jnp.float32) + jnp.dot(low_q, up_q, preferred_element_type=jnp.float32)).astype(jnp.bfloat16)
    value = (value_base.astype(jnp.float32) + jnp.dot(low_v, up_v, preferred_element_type=jnp.float32)).astype(jnp.bfloat16)
    nblocks = TOKENS // BLOCK

    def blocks(array):
        return array.reshape(nblocks, BLOCK, HEADS, HEAD).transpose(0, 2, 1, 3)

    query_b = blocks(query)
    keys_b = blocks(key_base)
    values_b = blocks(value)
    upstream_b = blocks(out_grad)
    keys_p = jnp.concatenate([jnp.zeros_like(keys_b[:1]), keys_b[:-1]], 0)
    values_p = jnp.concatenate([jnp.zeros_like(values_b[:1]), values_b[:-1]], 0)
    column = jnp.arange(2 * BLOCK)
    scale = HEAD ** -0.5
    first = jnp.arange(nblocks) == 0

    def per_block(items):
        q_blk, k_blk, kp_blk, v_blk, vp_blk, g_blk, leading = items
        usable = jnp.logical_or(column >= BLOCK, jnp.logical_not(leading))

        def per_head(parts):
            q_one, k_one, kp_one, v_one, vp_one, g_one = parts
            return head_pass(q_one, jnp.concatenate([kp_one, k_one], 0), jnp.concatenate([vp_one, v_one], 0), g_one, usable, scale)

        return lax.map(per_head, (q_blk, k_blk, kp_blk, v_blk, vp_blk, g_blk))

    attended_b, query_grad_b, value_terms = lax.map(per_block, (query_b, keys_b, keys_p, values_b, values_p, upstream_b, first))
    prior_part = value_terms[:, :, :BLOCK]
    own_part = value_terms[:, :, BLOCK:]
    incoming = jnp.concatenate([prior_part[1:], jnp.zeros_like(prior_part[:1])], 0)
    value_grad_b = (own_part + incoming).astype(jnp.bfloat16)

    def unblock(array):
        return array.transpose(0, 2, 1, 3).reshape(TOKENS, D)

    attended = unblock(attended_b)
    query_grad = unblock(query_grad_b)
    value_grad = unblock(value_grad_b)
    lowrank = jnp.concatenate([
        jnp.dot(query_grad, up_q.T, preferred_element_type=jnp.float32),
        jnp.dot(value_grad, up_v.T, preferred_element_type=jnp.float32)], 1).astype(jnp.bfloat16)
    down_total = inner(tokens, lowrank)
    grad_down_q = down_total[:, :RANK].astype(jnp.bfloat16)
    grad_down_v = down_total[:, RANK:].astype(jnp.bfloat16)
    grad_up_q = inner(low_q, query_grad).astype(jnp.bfloat16)
    grad_up_v = inner(low_v, value_grad).astype(jnp.bfloat16)
    return attended, grad_down_q, grad_up_q, grad_down_v, grad_up_v
```

```python
import functools

import jax
import jax.numpy as jnp
from jax import lax
from jax.experimental import pallas as pl
from jax.experimental.pallas import tpu as pltpu
from jax.sharding import PartitionSpec as P

HEAD = 128
CHUNK = 256
MESH = pl.DeviceIdType.MESH
F32 = jnp.float32
BF16 = jnp.bfloat16


def inner(left, right):
    return lax.dot_general(left, right, (((0,), (0,)), ((), ())), preferred_element_type=F32)


def outer(left, right):
    return lax.dot_general(left, right, (((1,), (1,)), ((), ())), preferred_element_type=F32)


def dot(left, right):
    return jnp.dot(left, right, preferred_element_type=F32)


def attention_kernel(
    nb, nu,
    tokens, query_base, key_base, value_base, out_grad, down_q, up_q, down_v, up_v,
    att_ref, gup_ref, low_out,
    kbuf, vbuf, lbuf, tok, qs, gs, downs, ups, lrq, lrv, lrin,
    local_sem, xsend, xrecv, fsend, frecv, lsend, lrecv, msend, mrecv, rsend, rrecv,
):
    blk = lax.axis_index("blk")
    u = lax.axis_index("uly")
    rows, width = tokens.shape
    rank = up_q.shape[0]
    span = nu * rows
    chunks = width // CHUNK
    has_prev = blk > 0
    has_next = blk < nb - 1
    mine = pl.ds(pl.multiple_of(span + u * rows, rows), rows)

    def peer(j):
        return lax.rem(u + j, nu)

    def source(j):
        return lax.rem(u - j + nu, nu)

    def cols(c):
        return pl.ds(pl.multiple_of(c * CHUNK, CHUNK), CHUNK)

    barrier = pltpu.get_barrier_semaphore()
    for j in range(1, nu):
        pl.semaphore_signal(barrier, inc=1, device_id=(blk, peer(j)), device_id_type=MESH)

    @pl.when(has_prev)
    def _():
        for j in range(nu):
            pl.semaphore_signal(barrier, inc=1, device_id=(blk - 1, peer(j)), device_id_type=MESH)

    @pl.when(has_next)
    def _():
        for j in range(nu):
            pl.semaphore_signal(barrier, inc=1, device_id=(blk + 1, peer(j)), device_id_type=MESH)

    local = [
        pltpu.make_async_copy(src, dst, local_sem.at[i])
        for i, (src, dst) in enumerate(
            (
                (tokens, tok), (down_q, downs.at[pl.ds(0, rank)]), (down_v, downs.at[pl.ds(rank, rank)]),
                (up_q, ups.at[pl.ds(0, rank)]), (up_v, ups.at[pl.ds(rank, rank)]),
                (value_base, vbuf.at[mine]), (key_base, kbuf.at[mine]),
                (query_base, qs), (out_grad, gs),
            )
        )
    ]
    for copy in local:
        copy.start()

    edge = jnp.logical_or(blk == 0, blk == nb - 1)

    @pl.when(edge)
    def _():
        pl.semaphore_wait(barrier, 2 * nu - 1)

    @pl.when(jnp.logical_not(edge))
    def _():
        pl.semaphore_wait(barrier, 3 * nu - 1)

    bufs = (kbuf, vbuf)

    def across(a, j, c):
        src = key_base.at[:, cols(c)] if a == 0 else vbuf.at[mine, cols(c)]
        return pltpu.make_async_remote_copy(
            src_ref=src, dst_ref=bufs[a].at[mine, cols(c)],
            send_sem=xsend.at[a, j, c], recv_sem=xrecv.at[a, j, c],
            device_id=(blk, peer(j)), device_id_type=MESH,
        )

    def crossed(a, j, c):
        here = bufs[a].at[pl.ds(pl.multiple_of(span + source(j) * rows, rows), rows), cols(c)]
        return pltpu.make_async_remote_copy(
            src_ref=here, dst_ref=here,
            send_sem=xsend.at[a, j, c], recv_sem=xrecv.at[a, j, c],
            device_id=(blk, peer(j)), device_id_type=MESH,
        )

    def onward(a, j, c):
        s = source(j)
        if a == 0 and j == 0:
            src = key_base.at[:, cols(c)]
        else:
            src = bufs[a].at[pl.ds(pl.multiple_of(span + s * rows, rows), rows), cols(c)]
        return pltpu.make_async_remote_copy(
            src_ref=src, dst_ref=bufs[a].at[pl.ds(pl.multiple_of(s * rows, rows), rows), cols(c)],
            send_sem=fsend.at[a, j, c], recv_sem=frecv.at[a, j, c],
            device_id=(blk + 1, u), device_id_type=MESH,
        )

    def arrived(a, j, c):
        here = bufs[a].at[pl.ds(pl.multiple_of(source(j) * rows, rows), rows), cols(c)]
        return pltpu.make_async_remote_copy(
            src_ref=here, dst_ref=here,
            send_sem=fsend.at[a, j, c], recv_sem=frecv.at[a, j, c],
            device_id=(blk, peer(1)), device_id_type=MESH,
        )

    def low_across(j):
        return pltpu.make_async_remote_copy(
            src_ref=lbuf.at[mine], dst_ref=lbuf.at[mine],
            send_sem=lsend.at[j], recv_sem=lrecv.at[j],
            device_id=(blk, peer(j)), device_id_type=MESH,
        )

    def low_crossed(j):
        here = lbuf.at[pl.ds(pl.multiple_of(span + source(j) * rows, rows), rows)]
        return pltpu.make_async_remote_copy(
            src_ref=here, dst_ref=here, send_sem=lsend.at[j], recv_sem=lrecv.at[j],
            device_id=(blk, peer(j)), device_id_type=MESH,
        )

    def low_onward(j):
        s = source(j)
        return pltpu.make_async_remote_copy(
            src_ref=lbuf.at[pl.ds(pl.multiple_of(span + s * rows, rows), rows)],
            dst_ref=lbuf.at[pl.ds(pl.multiple_of(s * rows, rows), rows)],
            send_sem=msend.at[j], recv_sem=mrecv.at[j],
            device_id=(blk + 1, u), device_id_type=MESH,
        )

    def low_arrived(j):
        here = lbuf.at[pl.ds(pl.multiple_of(source(j) * rows, rows), rows)]
        return pltpu.make_async_remote_copy(
            src_ref=here, dst_ref=here, send_sem=msend.at[j], recv_sem=mrecv.at[j],
            device_id=(blk, peer(1)), device_id_type=MESH,
        )

    early = min(3 * 512 // CHUNK, chunks)
    ahead = min(2048 // CHUNK, chunks)
    for c in range(early):
        for j in range(1, nu):
            across(0, j, c).start()

    @pl.when(has_next)
    def _():
        for c in range(ahead):
            onward(0, 0, c).start()

    lane = lax.broadcasted_iota(jnp.int32, (rows, 2 * rank), 1)
    for i in range(3):
        local[i].wait()
    low = outer(tok[...], downs[...])
    low_qm = jnp.where(lane < rank, low, 0.0).astype(BF16)
    low_vm = jnp.where(lane >= rank, low, 0.0).astype(BF16)
    lbuf[mine, :] = low_vm
    for i in range(3, 6):
        local[i].wait()

    @pl.loop(0, chunks)
    def _(c):
        part = dot(low_vm, ups[:, cols(c)])
        vbuf[mine, cols(c)] = (vbuf[mine, cols(c)].astype(F32) + part).astype(BF16)

    for j in range(1, nu):
        low_across(j).start()

    @pl.when(has_next)
    def _():
        low_onward(0).start()

    @pl.loop(0, chunks)
    def _(c):
        @pl.when(c >= early)
        def _():
            for j in range(1, nu):
                across(0, j, c).start()

        for j in range(1, nu):
            across(1, j, c).start()

    @pl.when(has_next)
    def _():
        for c in range(ahead):
            onward(1, 0, c).start()

    lrq[...] = jnp.zeros_like(lrq)
    lrv[...] = jnp.zeros_like(lrv)

    @pl.when(jnp.logical_not(has_prev))
    def _():
        kbuf[pl.ds(0, span), :] = jnp.zeros((span, width), BF16)
        vbuf[pl.ds(0, span), :] = jnp.zeros((span, width), BF16)
        lbuf[pl.ds(0, span), :] = jnp.zeros((span, 2 * rank), BF16)

    for i in range(6, 9):
        local[i].wait()

    scale = HEAD ** (-0.5)
    key_at = lax.broadcasted_iota(jnp.int32, (rows, 2 * span), 1)
    usable = jnp.logical_or(key_at >= span, has_prev)

    def head(h):
        at = pl.ds(pl.multiple_of(h * HEAD, HEAD), HEAD)
        up = ups[:, at]
        keys = kbuf[:, at]
        values = vbuf[:, at]
        grad = gs[:, at]
        query = (qs[:, at].astype(F32) + dot(low_qm, up)).astype(BF16)
        scores = jnp.where(usable, outer(query, keys) * scale, -jnp.inf)
        weights = jnp.exp(scores - jnp.max(scores, axis=1, keepdims=True))
        total = jnp.sum(weights, axis=1, keepdims=True)
        probs = (weights * (1.0 / total)).astype(BF16)
        attended = dot(probs, values).astype(BF16)
        delta = jnp.sum(grad.astype(F32) * attended.astype(F32), axis=1, keepdims=True)
        score_grad = (probs.astype(F32) * (outer(grad, values) - delta)).astype(BF16)
        query_grad = (dot(score_grad, keys) * scale).astype(BF16)
        seen = dot(probs, lbuf[...]).astype(BF16)
        gup = (inner(low_qm, query_grad) + inner(seen, grad)).astype(BF16)
        lifted = jnp.where(lane >= rank, outer(grad, up), 0.0).astype(BF16)
        return attended, gup, outer(query_grad, up), inner(probs, lifted)

    together = 2 if span <= 2 * HEAD else 1

    def head_group(first):
        results = [head(first + i) for i in range(together)]
        for i, (attended, gup, _, _) in enumerate(results):
            h = first + i
            att_ref[:, pl.ds(pl.multiple_of(h * HEAD, HEAD), HEAD)] = attended
            gup_ref[pl.ds(pl.multiple_of(h * 2 * rank, 2 * rank), 2 * rank), :] = gup
        lrq[...] += jnp.where(lane < rank, sum(r[2] for r in results), 0.0)
        lrv[...] += sum(r[3] for r in results)

    heads = CHUNK // HEAD

    @pl.loop(0, chunks + 1)
    def _(c):
        @pl.when(c == 0)
        def _():
            for j in range(1, nu):
                low_crossed(j).wait_recv()

                @pl.when(has_next)
                def _():
                    low_onward(j).start()

            @pl.when(has_prev)
            def _():
                for j in range(nu):
                    low_arrived(j).wait_recv()

        @pl.when(c < chunks)
        def _():
            for a in range(2):
                for j in range(1, nu):
                    crossed(a, j, c).wait_recv()

                    @pl.when(has_next)
                    def _():
                        onward(a, j, c).start()

            @pl.when(jnp.logical_and(has_next, c + ahead < chunks))
            def _():
                for a in range(2):
                    onward(a, 0, c + ahead).start()

        @pl.when(c > 0)
        def _():
            @pl.when(has_prev)
            def _():
                for a in range(2):
                    for j in range(nu):
                        arrived(a, j, c - 1).wait_recv()

            @pl.loop(0, heads // together)
            def _(i):
                head_group((c - 1) * heads + i * together)

    def terms(k, j, base):
        s = peer(j)
        return pltpu.make_async_remote_copy(
            src_ref=lrv.at[pl.ds(pl.multiple_of(base + s * rows, rows), rows)],
            dst_ref=lrin.at[k, j],
            send_sem=rsend.at[k, j], recv_sem=rrecv.at[k, j],
            device_id=(blk - k, s), device_id_type=MESH,
        )

    for j in range(1, nu):
        terms(0, j, span).start()

    @pl.when(has_prev)
    def _():
        for j in range(nu):
            terms(1, j, 0).start()

    @pl.loop(0, chunks)
    def _(c):
        for a in range(2):
            for j in range(1, nu):
                across(a, j, c).wait_send()

            @pl.when(has_next)
            def _():
                for j in range(nu):
                    onward(a, j, c).wait_send()

    for j in range(1, nu):
        low_across(j).wait_send()

    @pl.when(has_next)
    def _():
        for j in range(nu):
            low_onward(j).wait_send()

    lrq[...] += lrv[mine, :]
    for j in range(1, nu):
        terms(0, j, span).wait_recv()
        lrq[...] += lrin[0, j]

    @pl.when(has_next)
    def _():
        for j in range(nu):
            terms(1, j, 0).wait_recv()
            lrq[...] += lrin[1, j]

    low_out[...] = lrq[...].astype(BF16)
    for j in range(1, nu):
        terms(0, j, span).wait_send()

    @pl.when(has_prev)
    def _():
        for j in range(nu):
            terms(1, j, 0).wait_send()


def attention(nb, nu, *operands):
    rows, width = operands[0].shape
    rank = operands[6].shape[0]
    span = nu * rows
    chunks = width // CHUNK
    dma = pltpu.SemaphoreType.DMA
    anywhere = pl.BlockSpec(memory_space=pl.ANY)
    here = pl.BlockSpec(memory_space=pltpu.VMEM)
    return pl.pallas_call(
        functools.partial(attention_kernel, nb, nu),
        out_shape=(
            jax.ShapeDtypeStruct((rows, width), BF16),
            jax.ShapeDtypeStruct((width // HEAD * 2 * rank, HEAD), BF16),
            jax.ShapeDtypeStruct((rows, 2 * rank), BF16),
        ),
        in_specs=[anywhere] * 9,
        out_specs=(here, here, here),
        scratch_shapes=[
            pltpu.VMEM((2 * span, width), BF16),
            pltpu.VMEM((2 * span, width), BF16),
            pltpu.VMEM((2 * span, 2 * rank), BF16),
            pltpu.VMEM((rows, width), BF16),
            pltpu.VMEM((rows, width), BF16),
            pltpu.VMEM((rows, width), BF16),
            pltpu.VMEM((2 * rank, width), BF16),
            pltpu.VMEM((2 * rank, width), BF16),
            pltpu.VMEM((rows, 2 * rank), F32),
            pltpu.VMEM((2 * span, 2 * rank), F32),
            pltpu.VMEM((2, nu, rows, 2 * rank), F32),
            dma((9,)),
            dma((2, nu, chunks)), dma((2, nu, chunks)),
            dma((2, nu, chunks)), dma((2, nu, chunks)),
            dma((nu,)), dma((nu,)), dma((nu,)), dma((nu,)),
            dma((2, nu)), dma((2, nu)),
        ],
        compiler_params=pltpu.CompilerParams(
            collective_id=0, has_side_effects=True, vmem_limit_bytes=65_000_000
        ),
    )(*operands)


def reduction_kernel(
    nb, nu,
    tokens, lowrank, gup,
    downq_out, downv_out, upq_out, upv_out,
    tok, terms, pair, part, plane_in, line, line_in, down, ups, flat,
    local_sem, psend, precv, asend, arecv, bsend, brecv, csend, crecv, dsend, drecv, esend, erecv,
):
    blk = lax.axis_index("blk")
    u = lax.axis_index("uly")
    core = lax.rem(blk, 2)
    chip = blk // 2
    other = chip * 2 + 1 - core
    half = nb // 2
    inners = plane_in.shape[1] // nu
    outers = half // inners
    y = lax.rem(chip, inners)
    z = chip // inners
    group = nu * inners
    rows, width = tokens.shape
    rank = upq_out.shape[0]
    region = pair.shape[2]
    sub = plane_in.shape[2]
    piece = line_in.shape[2]

    def split(o, sign):
        pu = lax.rem(u + sign * (o // inners) + nu, nu)
        py = lax.rem(y + sign * lax.rem(o, inners) + inners, inners)
        return pu, py

    def plane_dev(o):
        pu, py = split(o, 1)
        return ((z * inners + py) * 2 + core, pu)

    def peer_z(o):
        return lax.rem(z + o, outers)

    def from_z(o):
        return lax.rem(z - o + outers, outers)

    def line_dev(o):
        return ((peer_z(o) * inners + y) * 2 + core, u)

    def subs(p):
        return pl.ds(pl.multiple_of(p * sub, sub), sub)

    barrier = pltpu.get_barrier_semaphore()
    pl.semaphore_signal(barrier, inc=1, device_id=(other, u), device_id_type=MESH)
    for o in range(1, group):
        pl.semaphore_signal(barrier, inc=1, device_id=plane_dev(o), device_id_type=MESH)
    for o in range(1, outers):
        pl.semaphore_signal(barrier, inc=1, device_id=line_dev(o), device_id_type=MESH)

    load = pltpu.make_async_copy(tokens, tok, local_sem.at[0])
    load.start()
    pl.semaphore_wait(barrier, group + outers - 1)

    def remote(src, dst, send, recv, device):
        return pltpu.make_async_remote_copy(
            src_ref=src, dst_ref=dst, send_sem=send, recv_sem=recv,
            device_id=device, device_id_type=MESH,
        )

    def swap(t, v):
        rows_at = pl.ds(pl.multiple_of((v * 2 + 1 - core) * region, region), region)
        return remote(
            (terms if t == 0 else gup).at[rows_at], pair.at[t, v],
            psend.at[t, v], precv.at[t, v], (other, u),
        )

    def scatter(t, o):
        pu, py = split(o, 1)
        return remote(
            part.at[t, pu, subs(py)], plane_in.at[t, o],
            asend.at[t, o], arecv.at[t, o], plane_dev(o),
        )

    def pass_on(t, o):
        at = pl.ds(pl.multiple_of(peer_z(o) * piece, piece), piece)
        return remote(
            line.at[t, at], line_in.at[t, o], bsend.at[t, o], brecv.at[t, o], line_dev(o)
        )

    def whole(t, v, k, p):
        return down.at[v, k, subs(p)] if t == 0 else ups.at[k, subs(p)]

    def piece_at(p, q):
        return pl.ds(pl.multiple_of(p * sub + q * piece, piece), piece)

    def small(t, q):
        return down.at[u, core, piece_at(y, q)] if t == 0 else ups.at[core, piece_at(y, q)]

    def along(t, o):
        return remote(small(t, z), small(t, z), csend.at[t, o], crecv.at[t, o], line_dev(o))

    def came(t, o):
        here = small(t, from_z(o))
        return remote(here, here, csend.at[t, o], crecv.at[t, o], line_dev(o))

    def spread(t, o):
        here = whole(t, u, core, y)
        return remote(here, here, dsend.at[t, o], drecv.at[t, o], plane_dev(o))

    def landed(t, o):
        pu, py = split(o, -1)
        here = whole(t, pu, core, py)
        return remote(here, here, dsend.at[t, o], drecv.at[t, o], (other, u))

    def share(t, o):
        pu, py = split(o, -1)
        here = whole(t, pu, core, py)
        return remote(here, here, esend.at[t, o], erecv.at[t, o], (other, u))

    def shared(t, o):
        pu, py = split(o, -1)
        here = whole(t, pu, 1 - core, py)
        return remote(here, here, esend.at[t, o], erecv.at[t, o], (other, u))

    if part.shape[2] > region:
        part[...] = jnp.zeros_like(part)
    for v in range(nu):
        swap(1, v).start()

    load.wait()
    lows = lowrank[...]

    @pl.loop(0, width // HEAD)
    def _(h):
        cols = pl.ds(pl.multiple_of(h * HEAD, HEAD), HEAD)
        here = pl.ds(pl.multiple_of(h * 2 * rank, 2 * rank), 2 * rank)
        terms[here, :] = inner(lows, tok[:, cols]).astype(BF16)

    for v in range(nu):
        swap(0, v).start()

    for t in (1, 0):
        for v in range(nu):
            rows_at = pl.ds(pl.multiple_of((v * 2 + core) * region, region), region)
            own = (terms if t == 0 else gup)[rows_at, :]
            swap(t, v).wait_recv()
            part[t, v, pl.ds(0, region), :] = (
                own.astype(F32) + pair[t, v].astype(F32)
            ).astype(BF16)
        for o in range(1, group):
            scatter(t, o).start()

    for t in (1, 0):
        total = part[t, u, subs(y), :].astype(F32)
        for o in range(1, group):
            scatter(t, o).wait_recv()
            total = total + plane_in[t, o].astype(F32)
        line[t, :, :] = total.astype(BF16)
        for o in range(1, outers):
            pass_on(t, o).start()

    for t in (1, 0):
        total = line[t, pl.ds(pl.multiple_of(z * piece, piece), piece), :].astype(F32)
        for o in range(1, outers):
            pass_on(t, o).wait_recv()
            total = total + line_in[t, o].astype(F32)
        small(t, z)[...] = total.astype(BF16)
        for o in range(1, outers):
            along(t, o).start()

    counts = (group, inners)
    for t in (1, 0):
        for o in range(1, outers):
            came(t, o).wait_recv()
        for o in range(1, counts[t]):
            spread(t, o).start()
        share(t, 0).start()

    for t in (1, 0):
        for o in range(1, counts[t]):
            landed(t, o).wait_recv()
            share(t, o).start()

    for t in (1, 0):
        for o in range(counts[t]):
            shared(t, o).wait_recv()
        places = [(v, k) for v in range(nu if t == 0 else 1) for k in range(2)]
        for n, (v, k) in enumerate(places):
            flat[pl.ds(n * region, region), :] = (
                down[v, k, pl.ds(0, region), :] if t == 0 else ups[k, pl.ds(0, region), :]
            )
        outs = (downq_out, downv_out) if t == 0 else (upq_out, upv_out)
        for h in range(len(places) * region // (2 * rank)):
            cols = pl.ds(h * HEAD, HEAD)
            outs[0][:, cols] = flat[pl.ds(h * 2 * rank, rank), :]
            outs[1][:, cols] = flat[pl.ds(h * 2 * rank + rank, rank), :]

    for t in (1, 0):
        for v in range(nu):
            swap(t, v).wait_send()
        for o in range(1, group):
            scatter(t, o).wait_send()
        for o in range(1, outers):
            pass_on(t, o).wait_send()
            along(t, o).wait_send()
        for o in range(1, counts[t]):
            spread(t, o).wait_send()
        for o in range(counts[t]):
            share(t, o).wait_send()


def reduction(nb, nu, tokens, lowrank, gup):
    rows, width = tokens.shape
    rank = lowrank.shape[1] // 2
    half = nb // 2
    inners = 2 if half % 2 == 0 else 1
    outers = half // inners
    group = nu * inners
    region = width // (2 * nu)
    piece = -(-region // (16 * half)) * 16
    sub = outers * piece
    held = half * piece
    dma = pltpu.SemaphoreType.DMA
    here = pl.BlockSpec(memory_space=pltpu.VMEM)
    lanes = lowrank.shape[1]
    return pl.pallas_call(
        functools.partial(reduction_kernel, nb, nu),
        out_shape=(
            jax.ShapeDtypeStruct((rank, width), BF16),
            jax.ShapeDtypeStruct((rank, width), BF16),
            jax.ShapeDtypeStruct((rank, width // nu), BF16),
            jax.ShapeDtypeStruct((rank, width // nu), BF16),
        ),
        in_specs=[pl.BlockSpec(memory_space=pl.ANY), here, here],
        out_specs=(here, here, here, here),
        scratch_shapes=[
            pltpu.VMEM((rows, width), BF16),
            pltpu.VMEM((width, lanes), BF16),
            pltpu.VMEM((2, nu, region, lanes), BF16),
            pltpu.VMEM((2, nu, held, lanes), BF16),
            pltpu.VMEM((2, group, sub, lanes), BF16),
            pltpu.VMEM((2, sub, lanes), BF16),
            pltpu.VMEM((2, outers, piece, lanes), BF16),
            pltpu.VMEM((nu, 2, held, lanes), BF16),
            pltpu.VMEM((2, held, lanes), BF16),
            pltpu.VMEM((2 * nu * region, lanes), BF16),
            dma((1,)),
            dma((2, nu)), dma((2, nu)),
            dma((2, group)), dma((2, group)),
            dma((2, outers)), dma((2, outers)),
            dma((2, outers)), dma((2, outers)),
            dma((2, group)), dma((2, group)),
            dma((2, group)), dma((2, group)),
        ],
        compiler_params=pltpu.CompilerParams(collective_id=1, has_side_effects=True),
    )(tokens, lowrank, gup)


def per_device(nb, nu, tokens, query_base, key_base, value_base, out_grad, down_q, up_q, down_v, up_v):
    attended, gup, lowrank = attention(
        nb, nu, tokens, query_base, key_base, value_base, out_grad, down_q.T, up_q, down_v.T, up_v
    )
    grad_down_q, grad_down_v, grad_up_q, grad_up_v = reduction(nb, nu, tokens, lowrank, gup)
    return attended, grad_down_q.T, grad_up_q, grad_down_v.T, grad_up_v


def solution(mesh):
    split = P(("blk", "uly"), None)
    return jax.shard_map(
        functools.partial(per_device, mesh.shape["blk"], mesh.shape["uly"]),
        mesh=mesh,
        in_specs=(split,) * 5 + (P(),) * 4,
        out_specs=(split, P(), P(None, "uly"), P(), P(None, "uly")),
        check_vma=False,
    )
```

```python
import functools

import jax
import jax.numpy as jnp
from jax import lax
from jax.experimental import pallas as pl
from jax.experimental.pallas import tpu as pltpu
from jax.sharding import PartitionSpec as P

HEAD = 128
CHUNK = 256
MESH = pl.DeviceIdType.MESH
F32 = jnp.float32
BF16 = jnp.bfloat16


def inner(left, right):
    return lax.dot_general(left, right, (((0,), (0,)), ((), ())), preferred_element_type=F32)


def outer(left, right):
    return lax.dot_general(left, right, (((1,), (1,)), ((), ())), preferred_element_type=F32)


def dot(left, right):
    return jnp.dot(left, right, preferred_element_type=F32)


def attention_kernel(
    nb, nu,
    tokens, query_base, key_base, value_base, out_grad, down_q, up_q, down_v, up_v,
    att_ref, gup_ref, low_out,
    kbuf, vbuf, lbuf, tok, qs, gs, downs, ups, lrq, lrv, lrin,
    local_sem, xsend, xrecv, fsend, frecv, lsend, lrecv, msend, mrecv, rsend, rrecv,
):
    blk = lax.axis_index("blk")
    u = lax.axis_index("uly")
    rows, width = tokens.shape
    rank = up_q.shape[0]
    span = nu * rows
    chunks = width // CHUNK
    has_prev = blk > 0
    has_next = blk < nb - 1
    mine = pl.ds(pl.multiple_of(span + u * rows, rows), rows)

    def peer(j):
        return lax.rem(u + j, nu)

    def source(j):
        return lax.rem(u - j + nu, nu)

    def cols(c):
        return pl.ds(pl.multiple_of(c * CHUNK, CHUNK), CHUNK)

    barrier = pltpu.get_barrier_semaphore()
    for j in range(1, nu):
        pl.semaphore_signal(barrier, inc=1, device_id=(blk, peer(j)), device_id_type=MESH)

    @pl.when(has_prev)
    def _():
        for j in range(nu):
            pl.semaphore_signal(barrier, inc=1, device_id=(blk - 1, peer(j)), device_id_type=MESH)

    @pl.when(has_next)
    def _():
        for j in range(nu):
            pl.semaphore_signal(barrier, inc=1, device_id=(blk + 1, peer(j)), device_id_type=MESH)

    local = [
        pltpu.make_async_copy(src, dst, local_sem.at[i])
        for i, (src, dst) in enumerate(
            (
                (tokens, tok), (down_q, downs.at[pl.ds(0, rank)]), (down_v, downs.at[pl.ds(rank, rank)]),
                (up_q, ups.at[pl.ds(0, rank)]), (up_v, ups.at[pl.ds(rank, rank)]),
                (value_base, vbuf.at[mine]), (key_base, kbuf.at[mine]),
                (query_base, qs), (out_grad, gs),
            )
        )
    ]
    for copy in local:
        copy.start()

    edge = jnp.logical_or(blk == 0, blk == nb - 1)

    @pl.when(edge)
    def _():
        pl.semaphore_wait(barrier, 2 * nu - 1)

    @pl.when(jnp.logical_not(edge))
    def _():
        pl.semaphore_wait(barrier, 3 * nu - 1)

    bufs = (kbuf, vbuf)

    def across(a, j, c):
        src = key_base.at[:, cols(c)] if a == 0 else vbuf.at[mine, cols(c)]
        return pltpu.make_async_remote_copy(
            src_ref=src, dst_ref=bufs[a].at[mine, cols(c)],
            send_sem=xsend.at[a, j, c], recv_sem=xrecv.at[a, j, c],
            device_id=(blk, peer(j)), device_id_type=MESH,
        )

    def crossed(a, j, c):
        here = bufs[a].at[pl.ds(pl.multiple_of(span + source(j) * rows, rows), rows), cols(c)]
        return pltpu.make_async_remote_copy(
            src_ref=here, dst_ref=here,
            send_sem=xsend.at[a, j, c], recv_sem=xrecv.at[a, j, c],
            device_id=(blk, peer(j)), device_id_type=MESH,
        )

    def onward(a, j, c):
        s = source(j)
        if a == 0 and j == 0:
            src = key_base.at[:, cols(c)]
        else:
            src = bufs[a].at[pl.ds(pl.multiple_of(span + s * rows, rows), rows), cols(c)]
        return pltpu.make_async_remote_copy(
            src_ref=src, dst_ref=bufs[a].at[pl.ds(pl.multiple_of(s * rows, rows), rows), cols(c)],
            send_sem=fsend.at[a, j, c], recv_sem=frecv.at[a, j, c],
            device_id=(blk + 1, u), device_id_type=MESH,
        )

    def arrived(a, j, c):
        here = bufs[a].at[pl.ds(pl.multiple_of(source(j) * rows, rows), rows), cols(c)]
        return pltpu.make_async_remote_copy(
            src_ref=here, dst_ref=here,
            send_sem=fsend.at[a, j, c], recv_sem=frecv.at[a, j, c],
            device_id=(blk, peer(1)), device_id_type=MESH,
        )

    def low_across(j):
        return pltpu.make_async_remote_copy(
            src_ref=lbuf.at[mine], dst_ref=lbuf.at[mine],
            send_sem=lsend.at[j], recv_sem=lrecv.at[j],
            device_id=(blk, peer(j)), device_id_type=MESH,
        )

    def low_crossed(j):
        here = lbuf.at[pl.ds(pl.multiple_of(span + source(j) * rows, rows), rows)]
        return pltpu.make_async_remote_copy(
            src_ref=here, dst_ref=here, send_sem=lsend.at[j], recv_sem=lrecv.at[j],
            device_id=(blk, peer(j)), device_id_type=MESH,
        )

    def low_onward(j):
        s = source(j)
        return pltpu.make_async_remote_copy(
            src_ref=lbuf.at[pl.ds(pl.multiple_of(span + s * rows, rows), rows)],
            dst_ref=lbuf.at[pl.ds(pl.multiple_of(s * rows, rows), rows)],
            send_sem=msend.at[j], recv_sem=mrecv.at[j],
            device_id=(blk + 1, u), device_id_type=MESH,
        )

    def low_arrived(j):
        here = lbuf.at[pl.ds(pl.multiple_of(source(j) * rows, rows), rows)]
        return pltpu.make_async_remote_copy(
            src_ref=here, dst_ref=here, send_sem=msend.at[j], recv_sem=mrecv.at[j],
            device_id=(blk, peer(1)), device_id_type=MESH,
        )

    early = min(3 * 512 // CHUNK, chunks)
    ahead = min(2048 // CHUNK, chunks)
    for c in range(early):
        for j in range(1, nu):
            across(0, j, c).start()

    @pl.when(has_next)
    def _():
        for c in range(ahead):
            onward(0, 0, c).start()

    lane = lax.broadcasted_iota(jnp.int32, (rows, 2 * rank), 1)
    for i in range(3):
        local[i].wait()
    low = outer(tok[...], downs[...])
    low_qm = jnp.where(lane < rank, low, 0.0).astype(BF16)
    low_vm = jnp.where(lane >= rank, low, 0.0).astype(BF16)
    lbuf[mine, :] = low_vm
    for i in range(3, 6):
        local[i].wait()

    @pl.loop(0, chunks)
    def _(c):
        part = dot(low_vm, ups[:, cols(c)])
        vbuf[mine, cols(c)] = (vbuf[mine, cols(c)].astype(F32) + part).astype(BF16)

    for j in range(1, nu):
        low_across(j).start()

    @pl.when(has_next)
    def _():
        low_onward(0).start()

    @pl.loop(0, chunks)
    def _(c):
        @pl.when(c >= early)
        def _():
            for j in range(1, nu):
                across(0, j, c).start()

        for j in range(1, nu):
            across(1, j, c).start()

    @pl.when(has_next)
    def _():
        for c in range(ahead):
            onward(1, 0, c).start()

    lrq[...] = jnp.zeros_like(lrq)
    lrv[...] = jnp.zeros_like(lrv)

    @pl.when(jnp.logical_not(has_prev))
    def _():
        kbuf[pl.ds(0, span), :] = jnp.zeros((span, width), BF16)
        vbuf[pl.ds(0, span), :] = jnp.zeros((span, width), BF16)
        lbuf[pl.ds(0, span), :] = jnp.zeros((span, 2 * rank), BF16)

    for i in range(6, 9):
        local[i].wait()

    scale = HEAD ** (-0.5)
    key_at = lax.broadcasted_iota(jnp.int32, (rows, 2 * span), 1)
    usable = jnp.logical_or(key_at >= span, has_prev)

    def head(h):
        at = pl.ds(pl.multiple_of(h * HEAD, HEAD), HEAD)
        up = ups[:, at]
        keys = kbuf[:, at]
        values = vbuf[:, at]
        grad = gs[:, at]
        query = (qs[:, at].astype(F32) + dot(low_qm, up)).astype(BF16)
        scores = jnp.where(usable, outer(query, keys) * scale, -jnp.inf)
        weights = jnp.exp(scores - jnp.max(scores, axis=1, keepdims=True))
        total = jnp.sum(weights, axis=1, keepdims=True)
        probs = (weights * (1.0 / total)).astype(BF16)
        attended = dot(probs, values).astype(BF16)
        delta = jnp.sum(grad.astype(F32) * attended.astype(F32), axis=1, keepdims=True)
        score_grad = (probs.astype(F32) * (outer(grad, values) - delta)).astype(BF16)
        query_grad = (dot(score_grad, keys) * scale).astype(BF16)
        seen = dot(probs, lbuf[...]).astype(BF16)
        gup = (inner(low_qm, query_grad) + inner(seen, grad)).astype(BF16)
        lifted = jnp.where(lane >= rank, outer(grad, up), 0.0).astype(BF16)
        return attended, gup, outer(query_grad, up), inner(probs, lifted)

    together = 2 if span <= 2 * HEAD else 1

    def head_group(first):
        results = [head(first + i) for i in range(together)]
        for i, (attended, gup, _, _) in enumerate(results):
            h = first + i
            att_ref[:, pl.ds(pl.multiple_of(h * HEAD, HEAD), HEAD)] = attended
            gup_ref[pl.ds(pl.multiple_of(h * 2 * rank, 2 * rank), 2 * rank), :] = gup
        lrq[...] += jnp.where(lane < rank, sum(r[2] for r in results), 0.0)
        lrv[...] += sum(r[3] for r in results)

    heads = CHUNK // HEAD

    @pl.loop(0, chunks + 1)
    def _(c):
        @pl.when(c == 0)
        def _():
            for j in range(1, nu):
                low_crossed(j).wait_recv()

                @pl.when(has_next)
                def _():
                    low_onward(j).start()

            @pl.when(has_prev)
            def _():
                for j in range(nu):
                    low_arrived(j).wait_recv()

        @pl.when(c < chunks)
        def _():
            for a in range(2):
                for j in range(1, nu):
                    crossed(a, j, c).wait_recv()

                    @pl.when(has_next)
                    def _():
                        onward(a, j, c).start()

            @pl.when(jnp.logical_and(has_next, c + ahead < chunks))
            def _():
                for a in range(2):
                    onward(a, 0, c + ahead).start()

        @pl.when(c > 0)
        def _():
            @pl.when(has_prev)
            def _():
                for a in range(2):
                    for j in range(nu):
                        arrived(a, j, c - 1).wait_recv()

            @pl.loop(0, heads // together)
            def _(i):
                head_group((c - 1) * heads + i * together)

    def terms(k, j, base):
        s = peer(j)
        return pltpu.make_async_remote_copy(
            src_ref=lrv.at[pl.ds(pl.multiple_of(base + s * rows, rows), rows)],
            dst_ref=lrin.at[k, j],
            send_sem=rsend.at[k, j], recv_sem=rrecv.at[k, j],
            device_id=(blk - k, s), device_id_type=MESH,
        )

    for j in range(1, nu):
        terms(0, j, span).start()

    @pl.when(has_prev)
    def _():
        for j in range(nu):
            terms(1, j, 0).start()

    @pl.loop(0, chunks)
    def _(c):
        for a in range(2):
            for j in range(1, nu):
                across(a, j, c).wait_send()

            @pl.when(has_next)
            def _():
                for j in range(nu):
                    onward(a, j, c).wait_send()

    for j in range(1, nu):
        low_across(j).wait_send()

    @pl.when(has_next)
    def _():
        for j in range(nu):
            low_onward(j).wait_send()

    lrq[...] += lrv[mine, :]
    for j in range(1, nu):
        terms(0, j, span).wait_recv()
        lrq[...] += lrin[0, j]

    @pl.when(has_next)
    def _():
        for j in range(nu):
            terms(1, j, 0).wait_recv()
            lrq[...] += lrin[1, j]

    low_out[...] = lrq[...].astype(BF16)
    for j in range(1, nu):
        terms(0, j, span).wait_send()

    @pl.when(has_prev)
    def _():
        for j in range(nu):
            terms(1, j, 0).wait_send()


def attention(nb, nu, *operands):
    rows, width = operands[0].shape
    rank = operands[6].shape[0]
    span = nu * rows
    chunks = width // CHUNK
    dma = pltpu.SemaphoreType.DMA
    anywhere = pl.BlockSpec(memory_space=pl.ANY)
    here = pl.BlockSpec(memory_space=pltpu.VMEM)
    return pl.pallas_call(
        functools.partial(attention_kernel, nb, nu),
        out_shape=(
            jax.ShapeDtypeStruct((rows, width), BF16),
            jax.ShapeDtypeStruct((width // HEAD * 2 * rank, HEAD), BF16),
            jax.ShapeDtypeStruct((rows, 2 * rank), BF16),
        ),
        in_specs=[anywhere] * 9,
        out_specs=(here, here, here),
        scratch_shapes=[
            pltpu.VMEM((2 * span, width), BF16),
            pltpu.VMEM((2 * span, width), BF16),
            pltpu.VMEM((2 * span, 2 * rank), BF16),
            pltpu.VMEM((rows, width), BF16),
            pltpu.VMEM((rows, width), BF16),
            pltpu.VMEM((rows, width), BF16),
            pltpu.VMEM((2 * rank, width), BF16),
            pltpu.VMEM((2 * rank, width), BF16),
            pltpu.VMEM((rows, 2 * rank), F32),
            pltpu.VMEM((2 * span, 2 * rank), F32),
            pltpu.VMEM((2, nu, rows, 2 * rank), F32),
            dma((9,)),
            dma((2, nu, chunks)), dma((2, nu, chunks)),
            dma((2, nu, chunks)), dma((2, nu, chunks)),
            dma((nu,)), dma((nu,)), dma((nu,)), dma((nu,)),
            dma((2, nu)), dma((2, nu)),
        ],
        compiler_params=pltpu.CompilerParams(
            collective_id=0, has_side_effects=True, vmem_limit_bytes=65_000_000
        ),
    )(*operands)


def reduction_kernel(
    nb, nu,
    tokens, lowrank, gup,
    downq_out, downv_out, upq_out, upv_out,
    tok, terms, pair, part, plane_in, line, line_in, down, ups, flat,
    local_sem, psend, precv, asend, arecv, bsend, brecv, csend, crecv, dsend, drecv, esend, erecv,
):
    blk = lax.axis_index("blk")
    u = lax.axis_index("uly")
    core = lax.rem(blk, 2)
    chip = blk // 2
    other = chip * 2 + 1 - core
    half = nb // 2
    inners = plane_in.shape[1] // nu
    outers = half // inners
    y = lax.rem(chip, inners)
    z = chip // inners
    group = nu * inners
    rows, width = tokens.shape
    rank = upq_out.shape[0]
    region = pair.shape[2]
    sub = plane_in.shape[2]
    piece = line_in.shape[2]

    def split(o, sign):
        pu = lax.rem(u + sign * (o // inners) + nu, nu)
        py = lax.rem(y + sign * lax.rem(o, inners) + inners, inners)
        return pu, py

    def plane_dev(o):
        pu, py = split(o, 1)
        return ((z * inners + py) * 2 + core, pu)

    def peer_z(o):
        return lax.rem(z + o, outers)

    def from_z(o):
        return lax.rem(z - o + outers, outers)

    def line_dev(o):
        return ((peer_z(o) * inners + y) * 2 + core, u)

    def subs(p):
        return pl.ds(pl.multiple_of(p * sub, sub), sub)

    barrier = pltpu.get_barrier_semaphore()
    pl.semaphore_signal(barrier, inc=1, device_id=(other, u), device_id_type=MESH)
    for o in range(1, group):
        pl.semaphore_signal(barrier, inc=1, device_id=plane_dev(o), device_id_type=MESH)
    for o in range(1, outers):
        pl.semaphore_signal(barrier, inc=1, device_id=line_dev(o), device_id_type=MESH)

    load = pltpu.make_async_copy(tokens, tok, local_sem.at[0])
    load.start()
    pl.semaphore_wait(barrier, group + outers - 1)

    def remote(src, dst, send, recv, device):
        return pltpu.make_async_remote_copy(
            src_ref=src, dst_ref=dst, send_sem=send, recv_sem=recv,
            device_id=device, device_id_type=MESH,
        )

    def swap(t, v):
        rows_at = pl.ds(pl.multiple_of((v * 2 + 1 - core) * region, region), region)
        return remote(
            (terms if t == 0 else gup).at[rows_at], pair.at[t, v],
            psend.at[t, v], precv.at[t, v], (other, u),
        )

    def scatter(t, o):
        pu, py = split(o, 1)
        return remote(
            part.at[t, pu, subs(py)], plane_in.at[t, o],
            asend.at[t, o], arecv.at[t, o], plane_dev(o),
        )

    def pass_on(t, o):
        at = pl.ds(pl.multiple_of(peer_z(o) * piece, piece), piece)
        return remote(
            line.at[t, at], line_in.at[t, o], bsend.at[t, o], brecv.at[t, o], line_dev(o)
        )

    def whole(t, v, k, p):
        return down.at[v, k, subs(p)] if t == 0 else ups.at[k, subs(p)]

    def piece_at(p, q):
        return pl.ds(pl.multiple_of(p * sub + q * piece, piece), piece)

    def small(t, q):
        return down.at[u, core, piece_at(y, q)] if t == 0 else ups.at[core, piece_at(y, q)]

    def along(t, o):
        return remote(small(t, z), small(t, z), csend.at[t, o], crecv.at[t, o], line_dev(o))

    def came(t, o):
        here = small(t, from_z(o))
        return remote(here, here, csend.at[t, o], crecv.at[t, o], line_dev(o))

    def spread(t, o):
        here = whole(t, u, core, y)
        return remote(here, here, dsend.at[t, o], drecv.at[t, o], plane_dev(o))

    def landed(t, o):
        pu, py = split(o, -1)
        here = whole(t, pu, core, py)
        return remote(here, here, dsend.at[t, o], drecv.at[t, o], (other, u))

    def share(t, o):
        pu, py = split(o, -1)
        here = whole(t, pu, core, py)
        return remote(here, here, esend.at[t, o], erecv.at[t, o], (other, u))

    def shared(t, o):
        pu, py = split(o, -1)
        here = whole(t, pu, 1 - core, py)
        return remote(here, here, esend.at[t, o], erecv.at[t, o], (other, u))

    if part.shape[2] > region:
        part[...] = jnp.zeros_like(part)
    for v in range(nu):
        swap(1, v).start()

    load.wait()
    lows = lowrank[...]

    @pl.loop(0, width // HEAD)
    def _(h):
        cols = pl.ds(pl.multiple_of(h * HEAD, HEAD), HEAD)
        here = pl.ds(pl.multiple_of(h * 2 * rank, 2 * rank), 2 * rank)
        terms[here, :] = inner(lows, tok[:, cols]).astype(BF16)

    for v in range(nu):
        swap(0, v).start()

    for t in (1, 0):
        for v in range(nu):
            rows_at = pl.ds(pl.multiple_of((v * 2 + core) * region, region), region)
            own = (terms if t == 0 else gup)[rows_at, :]
            swap(t, v).wait_recv()
            part[t, v, pl.ds(0, region), :] = (
                own.astype(F32) + pair[t, v].astype(F32)
            ).astype(BF16)
        for o in range(1, group):
            scatter(t, o).start()

    for t in (1, 0):
        total = part[t, u, subs(y), :].astype(F32)
        for o in range(1, group):
            scatter(t, o).wait_recv()
            total = total + plane_in[t, o].astype(F32)
        line[t, :, :] = total.astype(BF16)
        for o in range(1, outers):
            pass_on(t, o).start()

    for t in (1, 0):
        total = line[t, pl.ds(pl.multiple_of(z * piece, piece), piece), :].astype(F32)
        for o in range(1, outers):
            pass_on(t, o).wait_recv()
            total = total + line_in[t, o].astype(F32)
        small(t, z)[...] = total.astype(BF16)
        for o in range(1, outers):
            along(t, o).start()

    counts = (group, inners)
    for t in (1, 0):
        for o in range(1, outers):
            came(t, o).wait_recv()
        for o in range(1, counts[t]):
            spread(t, o).start()
        share(t, 0).start()

    for t in (1, 0):
        for o in range(1, counts[t]):
            landed(t, o).wait_recv()
            share(t, o).start()

    for t in (1, 0):
        for o in range(counts[t]):
            shared(t, o).wait_recv()
        places = [(v, k) for v in range(nu if t == 0 else 1) for k in range(2)]
        for n, (v, k) in enumerate(places):
            flat[pl.ds(n * region, region), :] = (
                down[v, k, pl.ds(0, region), :] if t == 0 else ups[k, pl.ds(0, region), :]
            )
        outs = (downq_out, downv_out) if t == 0 else (upq_out, upv_out)
        for h in range(len(places) * region // (2 * rank)):
            cols = pl.ds(h * HEAD, HEAD)
            outs[0][:, cols] = flat[pl.ds(h * 2 * rank, rank), :]
            outs[1][:, cols] = flat[pl.ds(h * 2 * rank + rank, rank), :]

    for t in (1, 0):
        for v in range(nu):
            swap(t, v).wait_send()
        for o in range(1, group):
            scatter(t, o).wait_send()
        for o in range(1, outers):
            pass_on(t, o).wait_send()
            along(t, o).wait_send()
        for o in range(1, counts[t]):
            spread(t, o).wait_send()
        for o in range(counts[t]):
            share(t, o).wait_send()


def reduction(nb, nu, tokens, lowrank, gup):
    rows, width = tokens.shape
    rank = lowrank.shape[1] // 2
    half = nb // 2
    inners = 2 if half % 2 == 0 else 1
    outers = half // inners
    group = nu * inners
    region = width // (2 * nu)
    piece = -(-region // (16 * half)) * 16
    sub = outers * piece
    held = half * piece
    dma = pltpu.SemaphoreType.DMA
    here = pl.BlockSpec(memory_space=pltpu.VMEM)
    lanes = lowrank.shape[1]
    return pl.pallas_call(
        functools.partial(reduction_kernel, nb, nu),
        out_shape=(
            jax.ShapeDtypeStruct((rank, width), BF16),
            jax.ShapeDtypeStruct((rank, width), BF16),
            jax.ShapeDtypeStruct((rank, width // nu), BF16),
            jax.ShapeDtypeStruct((rank, width // nu), BF16),
        ),
        in_specs=[pl.BlockSpec(memory_space=pl.ANY), here, here],
        out_specs=(here, here, here, here),
        scratch_shapes=[
            pltpu.VMEM((rows, width), BF16),
            pltpu.VMEM((width, lanes), BF16),
            pltpu.VMEM((2, nu, region, lanes), BF16),
            pltpu.VMEM((2, nu, held, lanes), BF16),
            pltpu.VMEM((2, group, sub, lanes), BF16),
            pltpu.VMEM((2, sub, lanes), BF16),
            pltpu.VMEM((2, outers, piece, lanes), BF16),
            pltpu.VMEM((nu, 2, held, lanes), BF16),
            pltpu.VMEM((2, held, lanes), BF16),
            pltpu.VMEM((2 * nu * region, lanes), BF16),
            dma((1,)),
            dma((2, nu)), dma((2, nu)),
            dma((2, group)), dma((2, group)),
            dma((2, outers)), dma((2, outers)),
            dma((2, outers)), dma((2, outers)),
            dma((2, group)), dma((2, group)),
            dma((2, group)), dma((2, group)),
        ],
        compiler_params=pltpu.CompilerParams(collective_id=1, has_side_effects=True),
    )(tokens, lowrank, gup)


def fused_kernel(
    nb, nu,
    tokens, query_base, key_base, value_base, out_grad, down_q, up_q, down_v, up_v,
    att_out, downq_out, downv_out, upq_out, upv_out,
    kbuf, vbuf, lbuf, tok, qs, gs, downs, ups, lrq, lrv, lrin, att_ref,
    acc, pair, part, plane_in, line, line_in, res,
    local_sem, att_sem, xsend, xrecv, fsend, frecv, lsend, lrecv, msend, mrecv, rsend, rrecv,
    psend, precv, asend, arecv, bsend, brecv, csend, crecv, dsend, drecv, esend, erecv,
):
    blk = lax.axis_index("blk")
    u = lax.axis_index("uly")
    rows, width = tokens.shape
    rank = up_q.shape[0]
    span = nu * rows
    chunks = width // CHUNK
    has_prev = blk > 0
    has_next = blk < nb - 1
    mine = pl.ds(pl.multiple_of(span + u * rows, rows), rows)

    def peer(j):
        return lax.rem(u + j, nu)

    def source(j):
        return lax.rem(u - j + nu, nu)

    cells = 2 * nu
    parts = chunks // cells
    core = lax.rem(blk, 2)
    chip = blk // 2
    other = chip * 2 + 1 - core
    inners, outers = grid_of(nb)
    group = nu * inners
    y = lax.rem(chip, inners)
    z = chip // inners
    sub = CHUNK // inners
    piece = sub // outers

    def place(c):
        return lax.rem(c, cells) * parts + c // cells

    def cols(c):
        return pl.ds(pl.multiple_of(place(c) * CHUNK, CHUNK), CHUNK)

    def remote(src, dst, send, recv, device):
        return pltpu.make_async_remote_copy(
            src_ref=src, dst_ref=dst, send_sem=send, recv_sem=recv,
            device_id=device, device_id_type=MESH,
        )

    def split(o, sign):
        pu = lax.rem(u + sign * (o // inners) + nu, nu)
        py = lax.rem(y + sign * lax.rem(o, inners) + inners, inners)
        return pu, py

    def plane_dev(o):
        pu, py = split(o, 1)
        return ((z * inners + py) * 2 + core, pu)

    def peer_z(o):
        return lax.rem(z + o, outers)

    def from_z(o):
        return lax.rem(z - o + outers, outers)

    def line_dev(o):
        return ((peer_z(o) * inners + y) * 2 + core, u)

    def subs(p):
        return pl.ds(pl.multiple_of(p * sub, sub), sub)

    def piece_at(p, q):
        return pl.ds(pl.multiple_of(p * sub + q * piece, piece), piece)

    def swap(n, v):
        return remote(
            acc.at[n, v * 2 + 1 - core], pair.at[n, v],
            psend.at[n, v], precv.at[n, v], (other, u),
        )

    def scatter(n, o):
        pu, py = split(o, 1)
        return remote(
            part.at[n, pu, subs(py)], plane_in.at[n, o],
            asend.at[n, o], arecv.at[n, o], plane_dev(o),
        )

    def pass_on(n, o):
        at = pl.ds(pl.multiple_of(peer_z(o) * piece, piece), piece)
        return remote(
            line.at[n, at], line_in.at[n, o], bsend.at[n, o], brecv.at[n, o], line_dev(o)
        )

    def along(n, o):
        here = res.at[n, u * 2 + core, piece_at(y, z)]
        return remote(here, here, csend.at[n, o], crecv.at[n, o], line_dev(o))

    def came(n, o):
        here = res.at[n, u * 2 + core, piece_at(y, from_z(o))]
        return remote(here, here, csend.at[n, o], crecv.at[n, o], line_dev(o))

    def spread(n, o):
        here = res.at[n, u * 2 + core, subs(y)]
        return remote(here, here, dsend.at[n, o], drecv.at[n, o], plane_dev(o))

    def landed(n, o):
        pu, py = split(o, -1)
        here = res.at[n, pu * 2 + core, subs(py)]
        return remote(here, here, dsend.at[n, o], drecv.at[n, o], (other, u))

    def share(n, o):
        pu, py = split(o, -1)
        here = res.at[n, pu * 2 + core, subs(py)]
        return remote(here, here, esend.at[n, o], erecv.at[n, o], (other, u))

    def shared(n, o):
        pu, py = split(o, -1)
        here = res.at[n, pu * 2 + 1 - core, subs(py)]
        return remote(here, here, esend.at[n, o], erecv.at[n, o], (other, u))

    def pair_up(n):
        for v in range(nu):
            own = acc[n, v * 2 + core]
            swap(n, v).wait_recv()
            part[n, v] = (own.astype(F32) + pair[n, v].astype(F32)).astype(BF16)
        for o in range(1, group):
            scatter(n, o).start()

    def plane_sum(n):
        total = part[n, u, subs(y), :].astype(F32)
        for o in range(1, group):
            scatter(n, o).wait_recv()
            total = total + plane_in[n, o].astype(F32)
        line[n] = total.astype(BF16)
        for o in range(1, outers):
            pass_on(n, o).start()

    def line_sum(n):
        total = line[n, pl.ds(pl.multiple_of(z * piece, piece), piece), :].astype(F32)
        for o in range(1, outers):
            pass_on(n, o).wait_recv()
            total = total + line_in[n, o].astype(F32)
        res[n, u * 2 + core, piece_at(y, z), :] = total.astype(BF16)
        for o in range(1, outers):
            along(n, o).start()

    def widen(n, count):
        for o in range(1, outers):
            came(n, o).wait_recv()
        for o in range(1, count):
            spread(n, o).start()
        share(n, 0).start()

    def hand_over(n, count):
        for o in range(1, count):
            landed(n, o).wait_recv()
            share(n, o).start()

    def each(first, stop, work):
        @pl.loop(first, stop)
        def _(n):
            work(n)

    barrier = pltpu.get_barrier_semaphore()
    for j in range(1, nu):
        pl.semaphore_signal(barrier, inc=1, device_id=(blk, peer(j)), device_id_type=MESH)

    @pl.when(has_prev)
    def _():
        for j in range(nu):
            pl.semaphore_signal(barrier, inc=1, device_id=(blk - 1, peer(j)), device_id_type=MESH)

    @pl.when(has_next)
    def _():
        for j in range(nu):
            pl.semaphore_signal(barrier, inc=1, device_id=(blk + 1, peer(j)), device_id_type=MESH)

    for o in range(1, group):
        pl.semaphore_signal(barrier, inc=1, device_id=plane_dev(o), device_id_type=MESH)
    for o in range(1, outers):
        pl.semaphore_signal(barrier, inc=1, device_id=line_dev(o), device_id_type=MESH)

    local = [
        pltpu.make_async_copy(src, dst, local_sem.at[i])
        for i, (src, dst) in enumerate(
            (
                (tokens, tok), (down_q, downs.at[pl.ds(0, rank)]), (down_v, downs.at[pl.ds(rank, rank)]),
                (up_q, ups.at[pl.ds(0, rank)]), (up_v, ups.at[pl.ds(rank, rank)]),
                (value_base, vbuf.at[mine]), (key_base, kbuf.at[mine]),
                (query_base, qs), (out_grad, gs),
            )
        )
    ]
    for copy in local:
        copy.start()

    edge = jnp.logical_or(blk == 0, blk == nb - 1)

    @pl.when(edge)
    def _():
        pl.semaphore_wait(barrier, 2 * nu - 1 + group + outers - 2)

    @pl.when(jnp.logical_not(edge))
    def _():
        pl.semaphore_wait(barrier, 3 * nu - 1 + group + outers - 2)

    bufs = (kbuf, vbuf)

    def across(a, j, c):
        src = key_base.at[:, cols(c)] if a == 0 else vbuf.at[mine, cols(c)]
        return pltpu.make_async_remote_copy(
            src_ref=src, dst_ref=bufs[a].at[mine, cols(c)],
            send_sem=xsend.at[a, j, c], recv_sem=xrecv.at[a, j, c],
            device_id=(blk, peer(j)), device_id_type=MESH,
        )

    def crossed(a, j, c):
        here = bufs[a].at[pl.ds(pl.multiple_of(span + source(j) * rows, rows), rows), cols(c)]
        return pltpu.make_async_remote_copy(
            src_ref=here, dst_ref=here,
            send_sem=xsend.at[a, j, c], recv_sem=xrecv.at[a, j, c],
            device_id=(blk, peer(j)), device_id_type=MESH,
        )

    def onward(a, j, c):
        s = source(j)
        if a == 0 and j == 0:
            src = key_base.at[:, cols(c)]
        else:
            src = bufs[a].at[pl.ds(pl.multiple_of(span + s * rows, rows), rows), cols(c)]
        return pltpu.make_async_remote_copy(
            src_ref=src, dst_ref=bufs[a].at[pl.ds(pl.multiple_of(s * rows, rows), rows), cols(c)],
            send_sem=fsend.at[a, j, c], recv_sem=frecv.at[a, j, c],
            device_id=(blk + 1, u), device_id_type=MESH,
        )

    def arrived(a, j, c):
        here = bufs[a].at[pl.ds(pl.multiple_of(source(j) * rows, rows), rows), cols(c)]
        return pltpu.make_async_remote_copy(
            src_ref=here, dst_ref=here,
            send_sem=fsend.at[a, j, c], recv_sem=frecv.at[a, j, c],
            device_id=(blk, peer(1)), device_id_type=MESH,
        )

    def low_across(j):
        return pltpu.make_async_remote_copy(
            src_ref=lbuf.at[mine], dst_ref=lbuf.at[mine],
            send_sem=lsend.at[j], recv_sem=lrecv.at[j],
            device_id=(blk, peer(j)), device_id_type=MESH,
        )

    def low_crossed(j):
        here = lbuf.at[pl.ds(pl.multiple_of(span + source(j) * rows, rows), rows)]
        return pltpu.make_async_remote_copy(
            src_ref=here, dst_ref=here, send_sem=lsend.at[j], recv_sem=lrecv.at[j],
            device_id=(blk, peer(j)), device_id_type=MESH,
        )

    def low_onward(j):
        s = source(j)
        return pltpu.make_async_remote_copy(
            src_ref=lbuf.at[pl.ds(pl.multiple_of(span + s * rows, rows), rows)],
            dst_ref=lbuf.at[pl.ds(pl.multiple_of(s * rows, rows), rows)],
            send_sem=msend.at[j], recv_sem=mrecv.at[j],
            device_id=(blk + 1, u), device_id_type=MESH,
        )

    def low_arrived(j):
        here = lbuf.at[pl.ds(pl.multiple_of(source(j) * rows, rows), rows)]
        return pltpu.make_async_remote_copy(
            src_ref=here, dst_ref=here, send_sem=msend.at[j], recv_sem=mrecv.at[j],
            device_id=(blk, peer(1)), device_id_type=MESH,
        )

    early = min(3 * 512 // CHUNK, chunks)
    ahead = min(2048 // CHUNK, chunks)
    for c in range(early):
        for j in range(1, nu):
            across(0, j, c).start()

    @pl.when(has_next)
    def _():
        for c in range(ahead):
            onward(0, 0, c).start()

    lane = lax.broadcasted_iota(jnp.int32, (rows, 2 * rank), 1)
    for i in range(3):
        local[i].wait()
    low = outer(tok[...], downs[...])
    low_qm = jnp.where(lane < rank, low, 0.0).astype(BF16)
    low_vm = jnp.where(lane >= rank, low, 0.0).astype(BF16)
    lbuf[mine, :] = low_vm
    for i in range(3, 6):
        local[i].wait()

    @pl.loop(0, chunks)
    def _(c):
        part = dot(low_vm, ups[:, cols(c)])
        vbuf[mine, cols(c)] = (vbuf[mine, cols(c)].astype(F32) + part).astype(BF16)

    for j in range(1, nu):
        low_across(j).start()

    @pl.when(has_next)
    def _():
        low_onward(0).start()

    @pl.loop(0, chunks)
    def _(c):
        @pl.when(c >= early)
        def _():
            for j in range(1, nu):
                across(0, j, c).start()

        for j in range(1, nu):
            across(1, j, c).start()

    @pl.when(has_next)
    def _():
        for c in range(ahead):
            onward(1, 0, c).start()

    lrq[...] = jnp.zeros_like(lrq)
    lrv[...] = jnp.zeros_like(lrv)

    @pl.when(jnp.logical_not(has_prev))
    def _():
        kbuf[pl.ds(0, span), :] = jnp.zeros((span, width), BF16)
        vbuf[pl.ds(0, span), :] = jnp.zeros((span, width), BF16)
        lbuf[pl.ds(0, span), :] = jnp.zeros((span, 2 * rank), BF16)

    for i in range(6, 9):
        local[i].wait()

    scale = HEAD ** (-0.5)
    key_at = lax.broadcasted_iota(jnp.int32, (rows, 2 * span), 1)
    usable = jnp.logical_or(key_at >= span, has_prev)

    def head(h):
        at = pl.ds(pl.multiple_of(h * HEAD, HEAD), HEAD)
        up = ups[:, at]
        keys = kbuf[:, at]
        values = vbuf[:, at]
        grad = gs[:, at]
        query = (qs[:, at].astype(F32) + dot(low_qm, up)).astype(BF16)
        scores = jnp.where(usable, outer(query, keys) * scale, -jnp.inf)
        weights = jnp.exp(scores - jnp.max(scores, axis=1, keepdims=True))
        total = jnp.sum(weights, axis=1, keepdims=True)
        probs = (weights * (1.0 / total)).astype(BF16)
        attended = dot(probs, values).astype(BF16)
        delta = jnp.sum(grad.astype(F32) * attended.astype(F32), axis=1, keepdims=True)
        score_grad = (probs.astype(F32) * (outer(grad, values) - delta)).astype(BF16)
        query_grad = (dot(score_grad, keys) * scale).astype(BF16)
        seen = dot(probs, lbuf[...]).astype(BF16)
        gup = (inner(low_qm, query_grad) + inner(seen, grad)).astype(BF16)
        lifted = jnp.where(lane >= rank, outer(grad, up), 0.0).astype(BF16)
        return attended, gup, outer(query_grad, up), inner(probs, lifted)

    together = 2 if span <= 2 * HEAD else 1

    def head_group(c, offset):
        first = place(c) * heads + offset
        results = [head(first + i) for i in range(together)]
        for i, (attended, gup, _, _) in enumerate(results):
            h = first + i
            att_ref[:, pl.ds(pl.multiple_of(h * HEAD, HEAD), HEAD)] = attended
            row = pl.multiple_of((offset + i) * 2 * rank, 2 * rank)
            acc[c // cells, lax.rem(c, cells), pl.ds(row, 2 * rank), :] = gup
        lrq[...] += jnp.where(lane < rank, sum(r[2] for r in results), 0.0)
        lrv[...] += sum(r[3] for r in results)

    heads = CHUNK // HEAD
    soon = max(parts - 2, 0)

    def att_copy(c):
        return pltpu.make_async_copy(
            att_ref.at[:, cols(c)], att_out.at[:, cols(c)], att_sem.at[c]
        )

    @pl.loop(0, chunks + 1)
    def _(c):
        @pl.when(c == 0)
        def _():
            for j in range(1, nu):
                low_crossed(j).wait_recv()

                @pl.when(has_next)
                def _():
                    low_onward(j).start()

            @pl.when(has_prev)
            def _():
                for j in range(nu):
                    low_arrived(j).wait_recv()

        @pl.when(c < chunks)
        def _():
            for a in range(2):
                for j in range(1, nu):
                    crossed(a, j, c).wait_recv()

                    @pl.when(has_next)
                    def _():
                        onward(a, j, c).start()

            @pl.when(jnp.logical_and(has_next, c + ahead < chunks))
            def _():
                for a in range(2):
                    onward(a, 0, c + ahead).start()

        @pl.when(c == chunks - 1)
        def _():
            each(0, soon, pair_up)

        @pl.when(c > 0)
        def _():
            @pl.when(has_prev)
            def _():
                for a in range(2):
                    for j in range(nu):
                        arrived(a, j, c - 1).wait_recv()

            @pl.loop(0, heads // together)
            def _(i):
                head_group(c - 1, i * together)

            att_copy(c - 1).start()
            cell = lax.rem(c - 1, cells)

            @pl.when(lax.rem(cell, 2) != core)
            def _():
                swap((c - 1) // cells, cell // 2).start()

    def terms(k, j, base):
        s = peer(j)
        return pltpu.make_async_remote_copy(
            src_ref=lrv.at[pl.ds(pl.multiple_of(base + s * rows, rows), rows)],
            dst_ref=lrin.at[k, j],
            send_sem=rsend.at[k, j], recv_sem=rrecv.at[k, j],
            device_id=(blk - k, s), device_id_type=MESH,
        )

    for j in range(1, nu):
        terms(0, j, span).start()

    @pl.when(has_prev)
    def _():
        for j in range(nu):
            terms(1, j, 0).start()

    each(soon, parts, pair_up)
    each(0, soon, plane_sum)

    lrq[...] += lrv[mine, :]
    for j in range(1, nu):
        terms(0, j, span).wait_recv()
        lrq[...] += lrin[0, j]

    @pl.when(has_next)
    def _():
        for j in range(nu):
            terms(1, j, 0).wait_recv()
            lrq[...] += lrin[1, j]

    lows = lrq[...].T.astype(BF16)

    def terms_of(p, r):
        at = pl.ds(pl.multiple_of((r * parts + p) * CHUNK, CHUNK), CHUNK)
        block = dot(lows, tok[:, at]).astype(BF16)
        for i in range(heads):
            acc[parts + p, r, pl.ds(i * 2 * rank, 2 * rank), :] = block[:, i * HEAD:(i + 1) * HEAD]

    def project(p):
        for v in range(nu):
            terms_of(p, v * 2 + 1 - core)
            swap(parts + p, v).start()
        for v in range(nu):
            terms_of(p, v * 2 + core)

    def lay_out(n, count, outs, base):
        for o in range(count):
            shared(n, o).wait_recv()
        for r in range(cells if count == group else 2):
            for i in range(heads):
                h = (r * parts + n - base) * heads + i
                at = pl.ds(pl.multiple_of(h * HEAD, HEAD), HEAD)
                cell = r if count == group else u * 2 + r
                outs[0][:, at] = res[n, cell, pl.ds(i * 2 * rank, rank), :]
                outs[1][:, at] = res[n, cell, pl.ds(i * 2 * rank + rank, rank), :]

    each(0, parts, project)
    each(parts, 2 * parts, pair_up)
    each(soon, parts, plane_sum)
    each(0, parts, line_sum)
    each(parts, 2 * parts, plane_sum)
    each(0, parts, lambda n: widen(n, inners))
    each(parts, 2 * parts, line_sum)
    each(0, parts, lambda n: hand_over(n, inners))
    each(parts, 2 * parts, lambda n: widen(n, group))
    each(0, parts, lambda n: lay_out(n, inners, (upq_out, upv_out), 0))
    each(parts, 2 * parts, lambda n: hand_over(n, group))
    each(parts, 2 * parts, lambda n: lay_out(n, group, (downq_out, downv_out), parts))

    def drain(n, count):
        for v in range(nu):
            swap(n, v).wait_send()
        for o in range(1, group):
            scatter(n, o).wait_send()
        for o in range(1, outers):
            pass_on(n, o).wait_send()
            along(n, o).wait_send()
        for o in range(1, count):
            spread(n, o).wait_send()
        for o in range(count):
            share(n, o).wait_send()

    each(0, parts, lambda n: drain(n, inners))
    each(parts, 2 * parts, lambda n: drain(n, group))
    each(0, chunks, lambda c: att_copy(c).wait())

    @pl.loop(0, chunks)
    def _(c):
        for a in range(2):
            for j in range(1, nu):
                across(a, j, c).wait_send()

            @pl.when(has_next)
            def _():
                for j in range(nu):
                    onward(a, j, c).wait_send()

    for j in range(1, nu):
        low_across(j).wait_send()

    @pl.when(has_next)
    def _():
        for j in range(nu):
            low_onward(j).wait_send()

    for j in range(1, nu):
        terms(0, j, span).wait_send()

    @pl.when(has_prev)
    def _():
        for j in range(nu):
            terms(1, j, 0).wait_send()


def grid_of(nb):
    half = nb // 2
    inners = 2 if half % 2 == 0 else 1
    return inners, half // inners


def fused(nb, nu, *operands):
    rows, width = operands[0].shape
    rank = operands[6].shape[0]
    span = nu * rows
    chunks = width // CHUNK
    cells = 2 * nu
    parts = chunks // cells
    inners, outers = grid_of(nb)
    group = nu * inners
    sub = CHUNK // inners
    lanes = 2 * rank
    dma = pltpu.SemaphoreType.DMA
    anywhere = pl.BlockSpec(memory_space=pl.ANY)
    here = pl.BlockSpec(memory_space=pltpu.VMEM)
    return pl.pallas_call(
        functools.partial(fused_kernel, nb, nu),
        out_shape=(
            jax.ShapeDtypeStruct((rows, width), BF16),
            jax.ShapeDtypeStruct((rank, width), BF16),
            jax.ShapeDtypeStruct((rank, width), BF16),
            jax.ShapeDtypeStruct((rank, width // nu), BF16),
            jax.ShapeDtypeStruct((rank, width // nu), BF16),
        ),
        in_specs=[anywhere] * 9,
        out_specs=(anywhere, here, here, here, here),
        scratch_shapes=[
            pltpu.VMEM((2 * span, width), BF16),
            pltpu.VMEM((2 * span, width), BF16),
            pltpu.VMEM((2 * span, lanes), BF16),
            pltpu.VMEM((rows, width), BF16),
            pltpu.VMEM((rows, width), BF16),
            pltpu.VMEM((rows, width), BF16),
            pltpu.VMEM((lanes, width), BF16),
            pltpu.VMEM((lanes, width), BF16),
            pltpu.VMEM((rows, lanes), F32),
            pltpu.VMEM((2 * span, lanes), F32),
            pltpu.VMEM((2, nu, rows, lanes), F32),
            pltpu.VMEM((rows, width), BF16),
            pltpu.VMEM((2 * parts, cells, CHUNK, lanes), BF16),
            pltpu.VMEM((2 * parts, nu, CHUNK, lanes), BF16),
            pltpu.VMEM((2 * parts, nu, CHUNK, lanes), BF16),
            pltpu.VMEM((2 * parts, group, sub, lanes), BF16),
            pltpu.VMEM((2 * parts, sub, lanes), BF16),
            pltpu.VMEM((2 * parts, outers, sub // outers, lanes), BF16),
            pltpu.VMEM((2 * parts, cells, CHUNK, lanes), BF16),
            dma((9,)), dma((chunks,)),
            dma((2, nu, chunks)), dma((2, nu, chunks)),
            dma((2, nu, chunks)), dma((2, nu, chunks)),
            dma((nu,)), dma((nu,)), dma((nu,)), dma((nu,)),
            dma((2, nu)), dma((2, nu)),
            dma((2 * parts, nu)), dma((2 * parts, nu)),
            dma((2 * parts, group)), dma((2 * parts, group)),
            dma((2 * parts, outers)), dma((2 * parts, outers)),
            dma((2 * parts, outers)), dma((2 * parts, outers)),
            dma((2 * parts, group)), dma((2 * parts, group)),
            dma((2 * parts, group)), dma((2 * parts, group)),
        ],
        compiler_params=pltpu.CompilerParams(
            collective_id=2, has_side_effects=True, vmem_limit_bytes=65_000_000
        ),
    )(*operands)


def fits(nb, nu, rows, width, rank):
    inners, outers = grid_of(nb)
    return (
        2 * rank == HEAD
        and width % (2 * nu * CHUNK) == 0
        and CHUNK % (16 * inners * outers) == 0
        and nu * rows <= CHUNK
    )


def per_device(nb, nu, tokens, query_base, key_base, value_base, out_grad, down_q, up_q, down_v, up_v):
    operands = (tokens, query_base, key_base, value_base, out_grad, down_q.T, up_q, down_v.T, up_v)
    if fits(nb, nu, *tokens.shape, up_q.shape[0]):
        attended, grad_down_q, grad_down_v, grad_up_q, grad_up_v = fused(nb, nu, *operands)
        return attended, grad_down_q.T, grad_up_q, grad_down_v.T, grad_up_v
    attended, gup, lowrank = attention(nb, nu, *operands)
    grad_down_q, grad_down_v, grad_up_q, grad_up_v = reduction(nb, nu, tokens, lowrank, gup)
    return attended, grad_down_q.T, grad_up_q, grad_down_v.T, grad_up_v


def solution(mesh):
    split = P(("blk", "uly"), None)
    return jax.shard_map(
        functools.partial(per_device, mesh.shape["blk"], mesh.shape["uly"]),
        mesh=mesh,
        in_specs=(split,) * 5 + (P(),) * 4,
        out_specs=(split, P(), P(None, "uly"), P(), P(None, "uly")),
        check_vma=False,
    )
```

```python
import functools

import jax
import jax.numpy as jnp
from jax import lax
from jax.experimental import pallas as pl
from jax.experimental.pallas import tpu as pltpu
from jax.sharding import PartitionSpec as P

HEAD = 128
CHUNK = 256
MESH = pl.DeviceIdType.MESH
F32 = jnp.float32
BF16 = jnp.bfloat16


def inner(left, right):
    return lax.dot_general(left, right, (((0,), (0,)), ((), ())), preferred_element_type=F32)


def outer(left, right):
    return lax.dot_general(left, right, (((1,), (1,)), ((), ())), preferred_element_type=F32)


def dot(left, right):
    return jnp.dot(left, right, preferred_element_type=F32)


def attention_kernel(
    nb, nu,
    tokens, query_base, key_base, value_base, out_grad, down_q, up_q, down_v, up_v,
    att_ref, gup_ref, low_out,
    kbuf, vbuf, lbuf, tok, qs, gs, downs, ups, lrq, lrv, lrin,
    local_sem, xsend, xrecv, fsend, frecv, lsend, lrecv, msend, mrecv, rsend, rrecv,
):
    blk = lax.axis_index("blk")
    u = lax.axis_index("uly")
    rows, width = tokens.shape
    rank = up_q.shape[0]
    span = nu * rows
    chunks = width // CHUNK
    has_prev = blk > 0
    has_next = blk < nb - 1
    mine = pl.ds(pl.multiple_of(span + u * rows, rows), rows)

    def peer(j):
        return lax.rem(u + j, nu)

    def source(j):
        return lax.rem(u - j + nu, nu)

    def cols(c):
        return pl.ds(pl.multiple_of(c * CHUNK, CHUNK), CHUNK)

    barrier = pltpu.get_barrier_semaphore()
    for j in range(1, nu):
        pl.semaphore_signal(barrier, inc=1, device_id=(blk, peer(j)), device_id_type=MESH)

    @pl.when(has_prev)
    def _():
        for j in range(nu):
            pl.semaphore_signal(barrier, inc=1, device_id=(blk - 1, peer(j)), device_id_type=MESH)

    @pl.when(has_next)
    def _():
        for j in range(nu):
            pl.semaphore_signal(barrier, inc=1, device_id=(blk + 1, peer(j)), device_id_type=MESH)

    local = [
        pltpu.make_async_copy(src, dst, local_sem.at[i])
        for i, (src, dst) in enumerate(
            (
                (tokens, tok), (down_q, downs.at[pl.ds(0, rank)]), (down_v, downs.at[pl.ds(rank, rank)]),
                (up_q, ups.at[pl.ds(0, rank)]), (up_v, ups.at[pl.ds(rank, rank)]),
                (value_base, vbuf.at[mine]), (key_base, kbuf.at[mine]),
                (query_base, qs), (out_grad, gs),
            )
        )
    ]
    for copy in local:
        copy.start()

    edge = jnp.logical_or(blk == 0, blk == nb - 1)

    @pl.when(edge)
    def _():
        pl.semaphore_wait(barrier, 2 * nu - 1)

    @pl.when(jnp.logical_not(edge))
    def _():
        pl.semaphore_wait(barrier, 3 * nu - 1)

    bufs = (kbuf, vbuf)

    def across(a, j, c):
        src = key_base.at[:, cols(c)] if a == 0 else vbuf.at[mine, cols(c)]
        return pltpu.make_async_remote_copy(
            src_ref=src, dst_ref=bufs[a].at[mine, cols(c)],
            send_sem=xsend.at[a, j, c], recv_sem=xrecv.at[a, j, c],
            device_id=(blk, peer(j)), device_id_type=MESH,
        )

    def crossed(a, j, c):
        here = bufs[a].at[pl.ds(pl.multiple_of(span + source(j) * rows, rows), rows), cols(c)]
        return pltpu.make_async_remote_copy(
            src_ref=here, dst_ref=here,
            send_sem=xsend.at[a, j, c], recv_sem=xrecv.at[a, j, c],
            device_id=(blk, peer(j)), device_id_type=MESH,
        )

    def onward(a, j, c):
        s = source(j)
        if a == 0 and j == 0:
            src = key_base.at[:, cols(c)]
        else:
            src = bufs[a].at[pl.ds(pl.multiple_of(span + s * rows, rows), rows), cols(c)]
        return pltpu.make_async_remote_copy(
            src_ref=src, dst_ref=bufs[a].at[pl.ds(pl.multiple_of(s * rows, rows), rows), cols(c)],
            send_sem=fsend.at[a, j, c], recv_sem=frecv.at[a, j, c],
            device_id=(blk + 1, u), device_id_type=MESH,
        )

    def arrived(a, j, c):
        here = bufs[a].at[pl.ds(pl.multiple_of(source(j) * rows, rows), rows), cols(c)]
        return pltpu.make_async_remote_copy(
            src_ref=here, dst_ref=here,
            send_sem=fsend.at[a, j, c], recv_sem=frecv.at[a, j, c],
            device_id=(blk, peer(1)), device_id_type=MESH,
        )

    def low_across(j):
        return pltpu.make_async_remote_copy(
            src_ref=lbuf.at[mine], dst_ref=lbuf.at[mine],
            send_sem=lsend.at[j], recv_sem=lrecv.at[j],
            device_id=(blk, peer(j)), device_id_type=MESH,
        )

    def low_crossed(j):
        here = lbuf.at[pl.ds(pl.multiple_of(span + source(j) * rows, rows), rows)]
        return pltpu.make_async_remote_copy(
            src_ref=here, dst_ref=here, send_sem=lsend.at[j], recv_sem=lrecv.at[j],
            device_id=(blk, peer(j)), device_id_type=MESH,
        )

    def low_onward(j):
        s = source(j)
        return pltpu.make_async_remote_copy(
            src_ref=lbuf.at[pl.ds(pl.multiple_of(span + s * rows, rows), rows)],
            dst_ref=lbuf.at[pl.ds(pl.multiple_of(s * rows, rows), rows)],
            send_sem=msend.at[j], recv_sem=mrecv.at[j],
            device_id=(blk + 1, u), device_id_type=MESH,
        )

    def low_arrived(j):
        here = lbuf.at[pl.ds(pl.multiple_of(source(j) * rows, rows), rows)]
        return pltpu.make_async_remote_copy(
            src_ref=here, dst_ref=here, send_sem=msend.at[j], recv_sem=mrecv.at[j],
            device_id=(blk, peer(1)), device_id_type=MESH,
        )

    early = min(3 * 512 // CHUNK, chunks)
    ahead = min(2048 // CHUNK, chunks)
    for c in range(early):
        for j in range(1, nu):
            across(0, j, c).start()

    @pl.when(has_next)
    def _():
        for c in range(ahead):
            onward(0, 0, c).start()

    lane = lax.broadcasted_iota(jnp.int32, (rows, 2 * rank), 1)
    for i in range(3):
        local[i].wait()
    low = outer(tok[...], downs[...])
    low_qm = jnp.where(lane < rank, low, 0.0).astype(BF16)
    low_vm = jnp.where(lane >= rank, low, 0.0).astype(BF16)
    lbuf[mine, :] = low_vm
    for i in range(3, 6):
        local[i].wait()

    @pl.loop(0, chunks)
    def _(c):
        part = dot(low_vm, ups[:, cols(c)])
        vbuf[mine, cols(c)] = (vbuf[mine, cols(c)].astype(F32) + part).astype(BF16)

    for j in range(1, nu):
        low_across(j).start()

    @pl.when(has_next)
    def _():
        low_onward(0).start()

    @pl.loop(0, chunks)
    def _(c):
        @pl.when(c >= early)
        def _():
            for j in range(1, nu):
                across(0, j, c).start()

        for j in range(1, nu):
            across(1, j, c).start()

    @pl.when(has_next)
    def _():
        for c in range(ahead):
            onward(1, 0, c).start()

    lrq[...] = jnp.zeros_like(lrq)
    lrv[...] = jnp.zeros_like(lrv)

    @pl.when(jnp.logical_not(has_prev))
    def _():
        kbuf[pl.ds(0, span), :] = jnp.zeros((span, width), BF16)
        vbuf[pl.ds(0, span), :] = jnp.zeros((span, width), BF16)
        lbuf[pl.ds(0, span), :] = jnp.zeros((span, 2 * rank), BF16)

    for i in range(6, 9):
        local[i].wait()

    scale = HEAD ** (-0.5)
    key_at = lax.broadcasted_iota(jnp.int32, (rows, 2 * span), 1)
    usable = jnp.logical_or(key_at >= span, has_prev)

    def head(h):
        at = pl.ds(pl.multiple_of(h * HEAD, HEAD), HEAD)
        up = ups[:, at]
        keys = kbuf[:, at]
        values = vbuf[:, at]
        grad = gs[:, at]
        query = (qs[:, at].astype(F32) + dot(low_qm, up)).astype(BF16)
        scores = jnp.where(usable, outer(query, keys) * scale, -jnp.inf)
        weights = jnp.exp(scores - jnp.max(scores, axis=1, keepdims=True))
        total = jnp.sum(weights, axis=1, keepdims=True)
        probs = (weights * (1.0 / total)).astype(BF16)
        attended = dot(probs, values).astype(BF16)
        delta = jnp.sum(grad.astype(F32) * attended.astype(F32), axis=1, keepdims=True)
        score_grad = (probs.astype(F32) * (outer(grad, values) - delta)).astype(BF16)
        query_grad = (dot(score_grad, keys) * scale).astype(BF16)
        seen = dot(probs, lbuf[...]).astype(BF16)
        gup = (inner(low_qm, query_grad) + inner(seen, grad)).astype(BF16)
        lifted = jnp.where(lane >= rank, outer(grad, up), 0.0).astype(BF16)
        return attended, gup, outer(query_grad, up), inner(probs, lifted)

    together = 2 if span <= 2 * HEAD else 1

    def head_group(first):
        results = [head(first + i) for i in range(together)]
        for i, (attended, gup, _, _) in enumerate(results):
            h = first + i
            att_ref[:, pl.ds(pl.multiple_of(h * HEAD, HEAD), HEAD)] = attended
            gup_ref[pl.ds(pl.multiple_of(h * 2 * rank, 2 * rank), 2 * rank), :] = gup
        lrq[...] += jnp.where(lane < rank, sum(r[2] for r in results), 0.0)
        lrv[...] += sum(r[3] for r in results)

    heads = CHUNK // HEAD

    @pl.loop(0, chunks + 1)
    def _(c):
        @pl.when(c == 0)
        def _():
            for j in range(1, nu):
                low_crossed(j).wait_recv()

                @pl.when(has_next)
                def _():
                    low_onward(j).start()

            @pl.when(has_prev)
            def _():
                for j in range(nu):
                    low_arrived(j).wait_recv()

        @pl.when(c < chunks)
        def _():
            for a in range(2):
                for j in range(1, nu):
                    crossed(a, j, c).wait_recv()

                    @pl.when(has_next)
                    def _():
                        onward(a, j, c).start()

            @pl.when(jnp.logical_and(has_next, c + ahead < chunks))
            def _():
                for a in range(2):
                    onward(a, 0, c + ahead).start()

        @pl.when(c > 0)
        def _():
            @pl.when(has_prev)
            def _():
                for a in range(2):
                    for j in range(nu):
                        arrived(a, j, c - 1).wait_recv()

            @pl.loop(0, heads // together)
            def _(i):
                head_group((c - 1) * heads + i * together)

    def terms(k, j, base):
        s = peer(j)
        return pltpu.make_async_remote_copy(
            src_ref=lrv.at[pl.ds(pl.multiple_of(base + s * rows, rows), rows)],
            dst_ref=lrin.at[k, j],
            send_sem=rsend.at[k, j], recv_sem=rrecv.at[k, j],
            device_id=(blk - k, s), device_id_type=MESH,
        )

    for j in range(1, nu):
        terms(0, j, span).start()

    @pl.when(has_prev)
    def _():
        for j in range(nu):
            terms(1, j, 0).start()

    @pl.loop(0, chunks)
    def _(c):
        for a in range(2):
            for j in range(1, nu):
                across(a, j, c).wait_send()

            @pl.when(has_next)
            def _():
                for j in range(nu):
                    onward(a, j, c).wait_send()

    for j in range(1, nu):
        low_across(j).wait_send()

    @pl.when(has_next)
    def _():
        for j in range(nu):
            low_onward(j).wait_send()

    lrq[...] += lrv[mine, :]
    for j in range(1, nu):
        terms(0, j, span).wait_recv()
        lrq[...] += lrin[0, j]

    @pl.when(has_next)
    def _():
        for j in range(nu):
            terms(1, j, 0).wait_recv()
            lrq[...] += lrin[1, j]

    low_out[...] = lrq[...].astype(BF16)
    for j in range(1, nu):
        terms(0, j, span).wait_send()

    @pl.when(has_prev)
    def _():
        for j in range(nu):
            terms(1, j, 0).wait_send()


def attention(nb, nu, *operands):
    rows, width = operands[0].shape
    rank = operands[6].shape[0]
    span = nu * rows
    chunks = width // CHUNK
    dma = pltpu.SemaphoreType.DMA
    anywhere = pl.BlockSpec(memory_space=pl.ANY)
    here = pl.BlockSpec(memory_space=pltpu.VMEM)
    return pl.pallas_call(
        functools.partial(attention_kernel, nb, nu),
        out_shape=(
            jax.ShapeDtypeStruct((rows, width), BF16),
            jax.ShapeDtypeStruct((width // HEAD * 2 * rank, HEAD), BF16),
            jax.ShapeDtypeStruct((rows, 2 * rank), BF16),
        ),
        in_specs=[anywhere] * 9,
        out_specs=(here, here, here),
        scratch_shapes=[
            pltpu.VMEM((2 * span, width), BF16),
            pltpu.VMEM((2 * span, width), BF16),
            pltpu.VMEM((2 * span, 2 * rank), BF16),
            pltpu.VMEM((rows, width), BF16),
            pltpu.VMEM((rows, width), BF16),
            pltpu.VMEM((rows, width), BF16),
            pltpu.VMEM((2 * rank, width), BF16),
            pltpu.VMEM((2 * rank, width), BF16),
            pltpu.VMEM((rows, 2 * rank), F32),
            pltpu.VMEM((2 * span, 2 * rank), F32),
            pltpu.VMEM((2, nu, rows, 2 * rank), F32),
            dma((9,)),
            dma((2, nu, chunks)), dma((2, nu, chunks)),
            dma((2, nu, chunks)), dma((2, nu, chunks)),
            dma((nu,)), dma((nu,)), dma((nu,)), dma((nu,)),
            dma((2, nu)), dma((2, nu)),
        ],
        compiler_params=pltpu.CompilerParams(
            collective_id=0, has_side_effects=True, vmem_limit_bytes=65_000_000
        ),
    )(*operands)


def reduction_kernel(
    nb, nu,
    tokens, lowrank, gup,
    downq_out, downv_out, upq_out, upv_out,
    tok, terms, pair, part, plane_in, line, line_in, down, ups, flat,
    local_sem, psend, precv, asend, arecv, bsend, brecv, csend, crecv, dsend, drecv, esend, erecv,
):
    blk = lax.axis_index("blk")
    u = lax.axis_index("uly")
    core = lax.rem(blk, 2)
    chip = blk // 2
    other = chip * 2 + 1 - core
    half = nb // 2
    inners = plane_in.shape[1] // nu
    outers = half // inners
    y = lax.rem(chip, inners)
    z = chip // inners
    group = nu * inners
    rows, width = tokens.shape
    rank = upq_out.shape[0]
    region = pair.shape[2]
    sub = plane_in.shape[2]
    piece = line_in.shape[2]

    def split(o, sign):
        pu = lax.rem(u + sign * (o // inners) + nu, nu)
        py = lax.rem(y + sign * lax.rem(o, inners) + inners, inners)
        return pu, py

    def plane_dev(o):
        pu, py = split(o, 1)
        return ((z * inners + py) * 2 + core, pu)

    def peer_z(o):
        return lax.rem(z + o, outers)

    def from_z(o):
        return lax.rem(z - o + outers, outers)

    def line_dev(o):
        return ((peer_z(o) * inners + y) * 2 + core, u)

    def subs(p):
        return pl.ds(pl.multiple_of(p * sub, sub), sub)

    barrier = pltpu.get_barrier_semaphore()
    pl.semaphore_signal(barrier, inc=1, device_id=(other, u), device_id_type=MESH)
    for o in range(1, group):
        pl.semaphore_signal(barrier, inc=1, device_id=plane_dev(o), device_id_type=MESH)
    for o in range(1, outers):
        pl.semaphore_signal(barrier, inc=1, device_id=line_dev(o), device_id_type=MESH)

    load = pltpu.make_async_copy(tokens, tok, local_sem.at[0])
    load.start()
    pl.semaphore_wait(barrier, group + outers - 1)

    def remote(src, dst, send, recv, device):
        return pltpu.make_async_remote_copy(
            src_ref=src, dst_ref=dst, send_sem=send, recv_sem=recv,
            device_id=device, device_id_type=MESH,
        )

    def swap(t, v):
        rows_at = pl.ds(pl.multiple_of((v * 2 + 1 - core) * region, region), region)
        return remote(
            (terms if t == 0 else gup).at[rows_at], pair.at[t, v],
            psend.at[t, v], precv.at[t, v], (other, u),
        )

    def scatter(t, o):
        pu, py = split(o, 1)
        return remote(
            part.at[t, pu, subs(py)], plane_in.at[t, o],
            asend.at[t, o], arecv.at[t, o], plane_dev(o),
        )

    def pass_on(t, o):
        at = pl.ds(pl.multiple_of(peer_z(o) * piece, piece), piece)
        return remote(
            line.at[t, at], line_in.at[t, o], bsend.at[t, o], brecv.at[t, o], line_dev(o)
        )

    def whole(t, v, k, p):
        return down.at[v, k, subs(p)] if t == 0 else ups.at[k, subs(p)]

    def piece_at(p, q):
        return pl.ds(pl.multiple_of(p * sub + q * piece, piece), piece)

    def small(t, q):
        return down.at[u, core, piece_at(y, q)] if t == 0 else ups.at[core, piece_at(y, q)]

    def along(t, o):
        return remote(small(t, z), small(t, z), csend.at[t, o], crecv.at[t, o], line_dev(o))

    def came(t, o):
        here = small(t, from_z(o))
        return remote(here, here, csend.at[t, o], crecv.at[t, o], line_dev(o))

    def spread(t, o):
        here = whole(t, u, core, y)
        return remote(here, here, dsend.at[t, o], drecv.at[t, o], plane_dev(o))

    def landed(t, o):
        pu, py = split(o, -1)
        here = whole(t, pu, core, py)
        return remote(here, here, dsend.at[t, o], drecv.at[t, o], (other, u))

    def share(t, o):
        pu, py = split(o, -1)
        here = whole(t, pu, core, py)
        return remote(here, here, esend.at[t, o], erecv.at[t, o], (other, u))

    def shared(t, o):
        pu, py = split(o, -1)
        here = whole(t, pu, 1 - core, py)
        return remote(here, here, esend.at[t, o], erecv.at[t, o], (other, u))

    if part.shape[2] > region:
        part[...] = jnp.zeros_like(part)
    for v in range(nu):
        swap(1, v).start()

    load.wait()
    lows = lowrank[...]

    @pl.loop(0, width // HEAD)
    def _(h):
        cols = pl.ds(pl.multiple_of(h * HEAD, HEAD), HEAD)
        here = pl.ds(pl.multiple_of(h * 2 * rank, 2 * rank), 2 * rank)
        terms[here, :] = inner(lows, tok[:, cols]).astype(BF16)

    for v in range(nu):
        swap(0, v).start()

    for t in (1, 0):
        for v in range(nu):
            rows_at = pl.ds(pl.multiple_of((v * 2 + core) * region, region), region)
            own = (terms if t == 0 else gup)[rows_at, :]
            swap(t, v).wait_recv()
            part[t, v, pl.ds(0, region), :] = (
                own.astype(F32) + pair[t, v].astype(F32)
            ).astype(BF16)
        for o in range(1, group):
            scatter(t, o).start()

    for t in (1, 0):
        total = part[t, u, subs(y), :].astype(F32)
        for o in range(1, group):
            scatter(t, o).wait_recv()
            total = total + plane_in[t, o].astype(F32)
        line[t, :, :] = total.astype(BF16)
        for o in range(1, outers):
            pass_on(t, o).start()

    for t in (1, 0):
        total = line[t, pl.ds(pl.multiple_of(z * piece, piece), piece), :].astype(F32)
        for o in range(1, outers):
            pass_on(t, o).wait_recv()
            total = total + line_in[t, o].astype(F32)
        small(t, z)[...] = total.astype(BF16)
        for o in range(1, outers):
            along(t, o).start()

    counts = (group, inners)
    for t in (1, 0):
        for o in range(1, outers):
            came(t, o).wait_recv()
        for o in range(1, counts[t]):
            spread(t, o).start()
        share(t, 0).start()

    for t in (1, 0):
        for o in range(1, counts[t]):
            landed(t, o).wait_recv()
            share(t, o).start()

    for t in (1, 0):
        for o in range(counts[t]):
            shared(t, o).wait_recv()
        places = [(v, k) for v in range(nu if t == 0 else 1) for k in range(2)]
        for n, (v, k) in enumerate(places):
            flat[pl.ds(n * region, region), :] = (
                down[v, k, pl.ds(0, region), :] if t == 0 else ups[k, pl.ds(0, region), :]
            )
        outs = (downq_out, downv_out) if t == 0 else (upq_out, upv_out)
        for h in range(len(places) * region // (2 * rank)):
            cols = pl.ds(h * HEAD, HEAD)
            outs[0][:, cols] = flat[pl.ds(h * 2 * rank, rank), :]
            outs[1][:, cols] = flat[pl.ds(h * 2 * rank + rank, rank), :]

    for t in (1, 0):
        for v in range(nu):
            swap(t, v).wait_send()
        for o in range(1, group):
            scatter(t, o).wait_send()
        for o in range(1, outers):
            pass_on(t, o).wait_send()
            along(t, o).wait_send()
        for o in range(1, counts[t]):
            spread(t, o).wait_send()
        for o in range(counts[t]):
            share(t, o).wait_send()


def reduction(nb, nu, tokens, lowrank, gup):
    rows, width = tokens.shape
    rank = lowrank.shape[1] // 2
    half = nb // 2
    inners = 2 if half % 2 == 0 else 1
    outers = half // inners
    group = nu * inners
    region = width // (2 * nu)
    piece = -(-region // (16 * half)) * 16
    sub = outers * piece
    held = half * piece
    dma = pltpu.SemaphoreType.DMA
    here = pl.BlockSpec(memory_space=pltpu.VMEM)
    lanes = lowrank.shape[1]
    return pl.pallas_call(
        functools.partial(reduction_kernel, nb, nu),
        out_shape=(
            jax.ShapeDtypeStruct((rank, width), BF16),
            jax.ShapeDtypeStruct((rank, width), BF16),
            jax.ShapeDtypeStruct((rank, width // nu), BF16),
            jax.ShapeDtypeStruct((rank, width // nu), BF16),
        ),
        in_specs=[pl.BlockSpec(memory_space=pl.ANY), here, here],
        out_specs=(here, here, here, here),
        scratch_shapes=[
            pltpu.VMEM((rows, width), BF16),
            pltpu.VMEM((width, lanes), BF16),
            pltpu.VMEM((2, nu, region, lanes), BF16),
            pltpu.VMEM((2, nu, held, lanes), BF16),
            pltpu.VMEM((2, group, sub, lanes), BF16),
            pltpu.VMEM((2, sub, lanes), BF16),
            pltpu.VMEM((2, outers, piece, lanes), BF16),
            pltpu.VMEM((nu, 2, held, lanes), BF16),
            pltpu.VMEM((2, held, lanes), BF16),
            pltpu.VMEM((2 * nu * region, lanes), BF16),
            dma((1,)),
            dma((2, nu)), dma((2, nu)),
            dma((2, group)), dma((2, group)),
            dma((2, outers)), dma((2, outers)),
            dma((2, outers)), dma((2, outers)),
            dma((2, group)), dma((2, group)),
            dma((2, group)), dma((2, group)),
        ],
        compiler_params=pltpu.CompilerParams(collective_id=1, has_side_effects=True),
    )(tokens, lowrank, gup)


def fused_kernel(
    nb, nu,
    tokens, query_base, key_base, value_base, out_grad, down_q, up_q, down_v, up_v,
    att_out, downq_out, downv_out, upq_out, upv_out,
    kv, lbuf, tok, qs, gs, downs, ups, lrq, lrv, lrin, att_ref,
    acc, pair, part, plane_in, line, line_in, res,
    local_sem, att_sem, xsend, xrecv, fsend, frecv, lsend, lrecv, msend, mrecv, rsend, rrecv,
    psend, precv, asend, arecv, bsend, brecv, csend, crecv, dsend, drecv, esend, erecv,
):
    kbuf, vbuf = kv.at[0], kv.at[1]
    blk = lax.axis_index("blk")
    u = lax.axis_index("uly")
    rows, width = tokens.shape
    rank = up_q.shape[0]
    span = nu * rows
    chunks = width // CHUNK
    has_prev = blk > 0
    has_next = blk < nb - 1
    mine = pl.ds(pl.multiple_of(span + u * rows, rows), rows)

    def peer(j):
        return lax.rem(u + j, nu)

    def source(j):
        return lax.rem(u - j + nu, nu)

    cells = 2 * nu
    parts = chunks // cells
    core = lax.rem(blk, 2)
    chip = blk // 2
    other = chip * 2 + 1 - core
    inners, outers = grid_of(nb)
    group = nu * inners
    y = lax.rem(chip, inners)
    z = chip // inners
    sub = CHUNK // inners
    piece = sub // outers

    def place(c):
        return lax.rem(c, cells) * parts + c // cells

    def cols(c):
        return pl.ds(pl.multiple_of(place(c) * CHUNK, CHUNK), CHUNK)

    def remote(src, dst, send, recv, device):
        return pltpu.make_async_remote_copy(
            src_ref=src, dst_ref=dst, send_sem=send, recv_sem=recv,
            device_id=device, device_id_type=MESH,
        )

    def split(o, sign):
        pu = lax.rem(u + sign * (o // inners) + nu, nu)
        py = lax.rem(y + sign * lax.rem(o, inners) + inners, inners)
        return pu, py

    def plane_dev(o):
        pu, py = split(o, 1)
        return ((z * inners + py) * 2 + core, pu)

    def peer_z(o):
        return lax.rem(z + o, outers)

    def from_z(o):
        return lax.rem(z - o + outers, outers)

    def line_dev(o):
        return ((peer_z(o) * inners + y) * 2 + core, u)

    def subs(p):
        return pl.ds(pl.multiple_of(p * sub, sub), sub)

    def piece_at(p, q):
        return pl.ds(pl.multiple_of(p * sub + q * piece, piece), piece)

    def swap(n):
        return remote(
            acc.at[n, 1 - core], pair.at[n], psend.at[0], precv.at[n], (other, u)
        )

    def scatter(n, o):
        pu, py = split(o, 1)
        return remote(
            part.at[n, pu, subs(py)], plane_in.at[n, o - 1],
            asend.at[0], arecv.at[n], plane_dev(o),
        )

    def pass_on(n, o):
        at = pl.ds(pl.multiple_of(peer_z(o) * piece, piece), piece)
        return remote(
            line.at[n, at], line_in.at[n, o - 1], bsend.at[0], brecv.at[n], line_dev(o)
        )

    def along(n, o):
        here = res.at[n, core, u, piece_at(y, z)]
        return remote(here, here, csend.at[0], crecv.at[n], line_dev(o))

    def spread(n, o, t):
        here = res.at[n, core, u, subs(y)]
        return remote(here, here, dsend.at[t], drecv.at[n], plane_dev(o))

    def share(n, t):
        here = res.at[n, core] if t == 1 else res.at[n, core, u]
        return remote(here, here, esend.at[t], erecv.at[n], (other, u))

    def whole(src, send, recv):
        return remote(src, src, send, recv, (other, u))

    def pair_up(n):
        swap(n).wait_recv()
        part[n] = (acc[n, core].astype(F32) + pair[n].astype(F32)).astype(BF16)
        for o in range(1, group):
            scatter(n, o).start()

    def plane_sum(n):
        total = part[n, u, subs(y), :].astype(F32)
        whole(plane_in.at[n], asend.at[0], arecv.at[n]).wait_recv()
        for o in range(1, group):
            total = total + plane_in[n, o - 1].astype(F32)
        line[n] = total.astype(BF16)
        for o in range(1, outers):
            pass_on(n, o).start()

    def line_sum(n):
        total = line[n, pl.ds(pl.multiple_of(z * piece, piece), piece), :].astype(F32)
        whole(line_in.at[n], bsend.at[0], brecv.at[n]).wait_recv()
        for o in range(1, outers):
            total = total + line_in[n, o - 1].astype(F32)
        res[n, core, u, piece_at(y, z), :] = total.astype(BF16)
        for o in range(1, outers):
            along(n, o).start()

    def widen(n, t):
        whole(line_in.at[n], csend.at[0], crecv.at[n]).wait_recv()
        for o in range(1, (inners, group)[t]):
            spread(n, o, t).start()

    def hand_over(n, t):
        whole(plane_in.at[n, pl.ds(0, (inners, group)[t] - 1)], dsend.at[t], drecv.at[n]).wait_recv()
        share(n, t).start()

    def each(first, stop, work):
        @pl.loop(first, stop)
        def _(n):
            work(n)

    barrier = pltpu.get_barrier_semaphore()
    for j in range(1, nu):
        pl.semaphore_signal(barrier, inc=1, device_id=(blk, peer(j)), device_id_type=MESH)

    @pl.when(has_prev)
    def _():
        for j in range(nu):
            pl.semaphore_signal(barrier, inc=1, device_id=(blk - 1, peer(j)), device_id_type=MESH)

    @pl.when(has_next)
    def _():
        for j in range(nu):
            pl.semaphore_signal(barrier, inc=1, device_id=(blk + 1, peer(j)), device_id_type=MESH)

    for o in range(1, group):
        pl.semaphore_signal(barrier, inc=1, device_id=plane_dev(o), device_id_type=MESH)
    for o in range(1, outers):
        pl.semaphore_signal(barrier, inc=1, device_id=line_dev(o), device_id_type=MESH)

    local = [
        pltpu.make_async_copy(src, dst, local_sem.at[i])
        for i, (src, dst) in enumerate(
            (
                (tokens, tok), (down_q, downs.at[pl.ds(0, rank)]), (down_v, downs.at[pl.ds(rank, rank)]),
                (up_q, ups.at[pl.ds(0, rank)]), (up_v, ups.at[pl.ds(rank, rank)]),
                (value_base, vbuf.at[mine]), (key_base, kbuf.at[mine]),
                (query_base, qs), (out_grad, gs),
            )
        )
    ]
    for copy in local:
        copy.start()

    edge = jnp.logical_or(blk == 0, blk == nb - 1)

    @pl.when(edge)
    def _():
        pl.semaphore_wait(barrier, 2 * nu - 1 + group + outers - 2)

    @pl.when(jnp.logical_not(edge))
    def _():
        pl.semaphore_wait(barrier, 3 * nu - 1 + group + outers - 2)

    def rows_of(first, j):
        return pl.ds(pl.multiple_of(first + source(j) * rows, rows), rows)

    def cross(j, c, what):
        at = cols(c)
        src, dst = {
            0: (key_base.at[:, at], kv.at[0, mine, at]),
            1: (kv.at[1, mine, at], kv.at[1, mine, at]),
            2: (kv.at[:, mine, at], kv.at[:, mine, at]),
        }[what]
        return remote(src, dst, xsend.at[j], xrecv.at[j, c], (blk, peer(j)))

    def crossed(j, c):
        here = kv.at[:, rows_of(span, j), cols(c)]
        return remote(here, here, xsend.at[j], xrecv.at[j, c], (blk, peer(j)))

    def onward(j, c, what):
        at = cols(c)
        old, new = rows_of(span, j), rows_of(0, j)
        src, dst = {
            0: (key_base.at[:, at], kv.at[0, new, at]),
            1: (kv.at[1, old, at], kv.at[1, new, at]),
            2: (kv.at[:, old, at], kv.at[:, new, at]),
        }[what]
        return remote(src, dst, fsend.at[j], frecv.at[c], (blk + 1, u))

    def arrived(c):
        here = kv.at[:, pl.ds(0, span), cols(c)]
        return remote(here, here, fsend.at[0], frecv.at[c], (blk, peer(1)))

    def low_across(j):
        return pltpu.make_async_remote_copy(
            src_ref=lbuf.at[mine], dst_ref=lbuf.at[mine],
            send_sem=lsend.at[j], recv_sem=lrecv.at[j],
            device_id=(blk, peer(j)), device_id_type=MESH,
        )

    def low_crossed(j):
        here = lbuf.at[pl.ds(pl.multiple_of(span + source(j) * rows, rows), rows)]
        return pltpu.make_async_remote_copy(
            src_ref=here, dst_ref=here, send_sem=lsend.at[j], recv_sem=lrecv.at[j],
            device_id=(blk, peer(j)), device_id_type=MESH,
        )

    def low_onward(j):
        s = source(j)
        return pltpu.make_async_remote_copy(
            src_ref=lbuf.at[pl.ds(pl.multiple_of(span + s * rows, rows), rows)],
            dst_ref=lbuf.at[pl.ds(pl.multiple_of(s * rows, rows), rows)],
            send_sem=msend.at[j], recv_sem=mrecv.at[j],
            device_id=(blk + 1, u), device_id_type=MESH,
        )

    def low_arrived(j):
        here = lbuf.at[pl.ds(pl.multiple_of(source(j) * rows, rows), rows)]
        return pltpu.make_async_remote_copy(
            src_ref=here, dst_ref=here, send_sem=msend.at[j], recv_sem=mrecv.at[j],
            device_id=(blk, peer(1)), device_id_type=MESH,
        )

    early = min(3 * 512 // CHUNK, chunks)
    ahead = min(2048 // CHUNK, chunks)
    for c in range(early):
        for j in range(1, nu):
            cross(j, c, 0).start()

    @pl.when(has_next)
    def _():
        for c in range(ahead):
            onward(0, c, 0).start()

    lane = lax.broadcasted_iota(jnp.int32, (rows, 2 * rank), 1)
    for i in range(3):
        local[i].wait()
    low = outer(tok[...], downs[...])
    low_qm = jnp.where(lane < rank, low, 0.0).astype(BF16)
    low_vm = jnp.where(lane >= rank, low, 0.0).astype(BF16)
    lbuf[mine, :] = low_vm
    for i in range(3, 7):
        local[i].wait()

    @pl.loop(0, chunks)
    def _(c):
        part = dot(low_vm, ups[:, cols(c)])
        vbuf[mine, cols(c)] = (vbuf[mine, cols(c)].astype(F32) + part).astype(BF16)

    for j in range(1, nu):
        low_across(j).start()

    @pl.when(has_next)
    def _():
        low_onward(0).start()

    @pl.loop(0, early)
    def _(c):
        for j in range(1, nu):
            cross(j, c, 1).start()

    @pl.when(has_next)
    def _():
        @pl.loop(0, ahead)
        def _(c):
            onward(0, c, 1).start()

    @pl.loop(early, chunks)
    def _(c):
        for j in range(1, nu):
            cross(j, c, 2).start()

    lrq[...] = jnp.zeros_like(lrq)
    lrv[...] = jnp.zeros_like(lrv)

    @pl.when(jnp.logical_not(has_prev))
    def _():
        kbuf[pl.ds(0, span), :] = jnp.zeros((span, width), BF16)
        vbuf[pl.ds(0, span), :] = jnp.zeros((span, width), BF16)
        lbuf[pl.ds(0, span), :] = jnp.zeros((span, 2 * rank), BF16)

    for i in range(7, 9):
        local[i].wait()

    scale = HEAD ** (-0.5)
    key_at = lax.broadcasted_iota(jnp.int32, (rows, 2 * span), 1)
    usable = jnp.logical_or(key_at >= span, has_prev)

    def head(h):
        at = pl.ds(pl.multiple_of(h * HEAD, HEAD), HEAD)
        up = ups[:, at]
        keys = kbuf[:, at]
        values = vbuf[:, at]
        grad = gs[:, at]
        query = (qs[:, at].astype(F32) + dot(low_qm, up)).astype(BF16)
        scores = jnp.where(usable, outer(query, keys) * scale, -jnp.inf)
        weights = jnp.exp(scores - jnp.max(scores, axis=1, keepdims=True))
        total = jnp.sum(weights, axis=1, keepdims=True)
        probs = (weights * (1.0 / total)).astype(BF16)
        attended = dot(probs, values).astype(BF16)
        delta = jnp.sum(grad.astype(F32) * attended.astype(F32), axis=1, keepdims=True)
        score_grad = (probs.astype(F32) * (outer(grad, values) - delta)).astype(BF16)
        query_grad = (dot(score_grad, keys) * scale).astype(BF16)
        seen = dot(probs, lbuf[...]).astype(BF16)
        gup = (inner(low_qm, query_grad) + inner(seen, grad)).astype(BF16)
        lifted = jnp.where(lane >= rank, outer(grad, up), 0.0).astype(BF16)
        return attended, gup, outer(query_grad, up), inner(probs, lifted)

    together = 2 if span <= 2 * HEAD else 1

    def head_group(c, offset):
        first = place(c) * heads + offset
        results = [head(first + i) for i in range(together)]
        for i, (attended, gup, _, _) in enumerate(results):
            h = first + i
            att_ref[:, pl.ds(pl.multiple_of(h * HEAD, HEAD), HEAD)] = attended
            row = pl.multiple_of((offset + i) * 2 * rank, 2 * rank)
            cell = lax.rem(c, cells)
            acc[c // cells, lax.rem(cell, 2), cell // 2, pl.ds(row, 2 * rank), :] = gup
        lrq[...] += jnp.where(lane < rank, sum(r[2] for r in results), 0.0)
        lrv[...] += sum(r[3] for r in results)

    heads = CHUNK // HEAD
    soon = max(parts - 2, 0)

    def att_copy(c):
        return pltpu.make_async_copy(
            att_ref.at[:, cols(c)], att_out.at[:, cols(c)], att_sem.at[0]
        )

    @pl.loop(0, chunks + 1)
    def _(c):
        @pl.when(c == 0)
        def _():
            for j in range(1, nu):
                low_crossed(j).wait_recv()

                @pl.when(has_next)
                def _():
                    low_onward(j).start()

            @pl.when(has_prev)
            def _():
                for j in range(nu):
                    low_arrived(j).wait_recv()

        @pl.when(c < chunks)
        def _():
            for j in range(1, nu):
                crossed(j, c).wait_recv()

                @pl.when(has_next)
                def _():
                    onward(j, c, 2).start()

            @pl.when(jnp.logical_and(has_next, c + ahead < chunks))
            def _():
                onward(0, c + ahead, 2).start()

        @pl.when(c == chunks - 1)
        def _():
            each(0, soon, pair_up)

        @pl.when(c > 0)
        def _():
            @pl.when(has_prev)
            def _():
                arrived(c - 1).wait_recv()

            @pl.loop(0, heads // together)
            def _(i):
                head_group(c - 1, i * together)

            att_copy(c - 1).start()

            @pl.when(lax.rem(c, cells) == 0)
            def _():
                swap(c // cells - 1).start()

    def terms(k, j, base):
        s = peer(j)
        return pltpu.make_async_remote_copy(
            src_ref=lrv.at[pl.ds(pl.multiple_of(base + s * rows, rows), rows)],
            dst_ref=lrin.at[k, j],
            send_sem=rsend.at[k, j], recv_sem=rrecv.at[k, j],
            device_id=(blk - k, s), device_id_type=MESH,
        )

    for j in range(1, nu):
        terms(0, j, span).start()

    @pl.when(has_prev)
    def _():
        for j in range(nu):
            terms(1, j, 0).start()

    each(soon, parts, pair_up)
    each(0, soon, plane_sum)

    lrq[...] += lrv[mine, :]
    for j in range(1, nu):
        terms(0, j, span).wait_recv()
        lrq[...] += lrin[0, j]

    @pl.when(has_next)
    def _():
        for j in range(nu):
            terms(1, j, 0).wait_recv()
            lrq[...] += lrin[1, j]

    lows = lrq[...].T.astype(BF16)

    def terms_of(p, v, k):
        at = pl.ds(pl.multiple_of(((v * 2 + k) * parts + p) * CHUNK, CHUNK), CHUNK)
        block = dot(lows, tok[:, at]).astype(BF16)
        for i in range(heads):
            acc[parts + p, k, v, pl.ds(i * 2 * rank, 2 * rank), :] = block[:, i * HEAD:(i + 1) * HEAD]

    def project(p):
        for v in range(nu):
            terms_of(p, v, 1 - core)
        swap(parts + p).start()
        for v in range(nu):
            terms_of(p, v, core)

    def lay_out(n, t, outs):
        shared_here = res.at[n, 1 - core] if t == 1 else res.at[n, 1 - core, u]
        whole(shared_here, esend.at[t], erecv.at[n]).wait_recv()
        for v in range(nu if t == 1 else 1):
            for k in range(2):
                for i in range(heads):
                    h = ((v * 2 + k) * parts + n - t * parts) * heads + i
                    at = pl.ds(pl.multiple_of(h * HEAD, HEAD), HEAD)
                    w = v if t == 1 else u
                    outs[0][:, at] = res[n, k, w, pl.ds(i * 2 * rank, rank), :]
                    outs[1][:, at] = res[n, k, w, pl.ds(i * 2 * rank + rank, rank), :]

    each(0, parts, project)
    each(parts, 2 * parts, pair_up)
    each(soon, parts, plane_sum)
    each(0, parts, line_sum)
    each(parts, 2 * parts, plane_sum)
    each(0, parts, lambda n: widen(n, 0))
    each(parts, 2 * parts, line_sum)
    each(0, parts, lambda n: hand_over(n, 0))
    each(parts, 2 * parts, lambda n: widen(n, 1))
    each(0, parts, lambda n: lay_out(n, 0, (upq_out, upv_out)))
    each(parts, 2 * parts, lambda n: hand_over(n, 1))
    each(parts, 2 * parts, lambda n: lay_out(n, 1, (downq_out, downv_out)))

    whole(pair, psend.at[0], precv.at[0]).wait_send()
    whole(plane_in, asend.at[0], arecv.at[0]).wait_send()
    whole(line_in, bsend.at[0], brecv.at[0]).wait_send()
    whole(line_in, csend.at[0], crecv.at[0]).wait_send()
    for i in range(2):
        some = pl.ds(i * parts, parts)
        whole(
            plane_in.at[some, pl.ds(0, (inners, group)[i] - 1)], dsend.at[i], drecv.at[0]
        ).wait_send()
    whole(res.at[pl.ds(0, parts), 0, 0], esend.at[0], erecv.at[0]).wait_send()
    whole(res.at[pl.ds(parts, parts), 0], esend.at[1], erecv.at[0]).wait_send()
    pltpu.make_async_copy(att_ref, att_out, att_sem.at[0]).wait()

    everything = kv.at[:, mine, :]
    for j in range(1, nu):
        remote(everything, everything, xsend.at[j], xrecv.at[j, 0], (blk, peer(j))).wait_send()

    @pl.when(has_next)
    def _():
        for j in range(nu):
            remote(everything, everything, fsend.at[j], frecv.at[0], (blk + 1, u)).wait_send()

    for j in range(1, nu):
        low_across(j).wait_send()

    @pl.when(has_next)
    def _():
        for j in range(nu):
            low_onward(j).wait_send()

    for j in range(1, nu):
        terms(0, j, span).wait_send()

    @pl.when(has_prev)
    def _():
        for j in range(nu):
            terms(1, j, 0).wait_send()


def grid_of(nb):
    half = nb // 2
    inners = 2 if half % 2 == 0 else 1
    return inners, half // inners


def fused(nb, nu, *operands):
    rows, width = operands[0].shape
    rank = operands[6].shape[0]
    span = nu * rows
    chunks = width // CHUNK
    cells = 2 * nu
    parts = chunks // cells
    inners, outers = grid_of(nb)
    group = nu * inners
    sub = CHUNK // inners
    lanes = 2 * rank
    dma = pltpu.SemaphoreType.DMA
    anywhere = pl.BlockSpec(memory_space=pl.ANY)
    here = pl.BlockSpec(memory_space=pltpu.VMEM)
    return pl.pallas_call(
        functools.partial(fused_kernel, nb, nu),
        out_shape=(
            jax.ShapeDtypeStruct((rows, width), BF16),
            jax.ShapeDtypeStruct((rank, width), BF16),
            jax.ShapeDtypeStruct((rank, width), BF16),
            jax.ShapeDtypeStruct((rank, width // nu), BF16),
            jax.ShapeDtypeStruct((rank, width // nu), BF16),
        ),
        in_specs=[anywhere] * 9,
        out_specs=(anywhere, here, here, here, here),
        scratch_shapes=[
            pltpu.VMEM((2, 2 * span, width), BF16),
            pltpu.VMEM((2 * span, lanes), BF16),
            pltpu.VMEM((rows, width), BF16),
            pltpu.VMEM((rows, width), BF16),
            pltpu.VMEM((rows, width), BF16),
            pltpu.VMEM((lanes, width), BF16),
            pltpu.VMEM((lanes, width), BF16),
            pltpu.VMEM((rows, lanes), F32),
            pltpu.VMEM((2 * span, lanes), F32),
            pltpu.VMEM((2, nu, rows, lanes), F32),
            pltpu.VMEM((rows, width), BF16),
            pltpu.VMEM((2 * parts, 2, nu, CHUNK, lanes), BF16),
            pltpu.VMEM((2 * parts, nu, CHUNK, lanes), BF16),
            pltpu.VMEM((2 * parts, nu, CHUNK, lanes), BF16),
            pltpu.VMEM((2 * parts, group - 1, sub, lanes), BF16),
            pltpu.VMEM((2 * parts, sub, lanes), BF16),
            pltpu.VMEM((2 * parts, outers - 1, sub // outers, lanes), BF16),
            pltpu.VMEM((2 * parts, 2, nu, CHUNK, lanes), BF16),
            dma((9,)), dma((1,)),
            dma((nu,)), dma((nu, chunks)),
            dma((nu,)), dma((chunks,)),
            dma((nu,)), dma((nu,)), dma((nu,)), dma((nu,)),
            dma((2, nu)), dma((2, nu)),
            dma((1,)), dma((2 * parts,)),
            dma((1,)), dma((2 * parts,)),
            dma((1,)), dma((2 * parts,)),
            dma((1,)), dma((2 * parts,)),
            dma((2,)), dma((2 * parts,)),
            dma((2,)), dma((2 * parts,)),
        ],
        compiler_params=pltpu.CompilerParams(
            collective_id=2, has_side_effects=True, vmem_limit_bytes=65_000_000
        ),
    )(*operands)


def fits(nb, nu, rows, width, rank):
    inners, outers = grid_of(nb)
    return (
        2 * rank == HEAD
        and width % (2 * nu * CHUNK) == 0
        and CHUNK % (16 * inners * outers) == 0
        and nu * rows <= CHUNK
    )


def per_device(nb, nu, tokens, query_base, key_base, value_base, out_grad, down_q, up_q, down_v, up_v):
    operands = (tokens, query_base, key_base, value_base, out_grad, down_q.T, up_q, down_v.T, up_v)
    if fits(nb, nu, *tokens.shape, up_q.shape[0]):
        attended, grad_down_q, grad_down_v, grad_up_q, grad_up_v = fused(nb, nu, *operands)
        return attended, grad_down_q.T, grad_up_q, grad_down_v.T, grad_up_v
    attended, gup, lowrank = attention(nb, nu, *operands)
    grad_down_q, grad_down_v, grad_up_q, grad_up_v = reduction(nb, nu, tokens, lowrank, gup)
    return attended, grad_down_q.T, grad_up_q, grad_down_v.T, grad_up_v


def solution(mesh):
    split = P(("blk", "uly"), None)
    return jax.shard_map(
        functools.partial(per_device, mesh.shape["blk"], mesh.shape["uly"]),
        mesh=mesh,
        in_specs=(split,) * 5 + (P(),) * 4,
        out_specs=(split, P(), P(None, "uly"), P(), P(None, "uly")),
        check_vma=False,
    )
```

```python
import functools

import jax
import jax.numpy as jnp
from jax import lax
from jax.experimental import pallas as pl
from jax.experimental.pallas import tpu as pltpu
from jax.sharding import PartitionSpec as P

HEAD = 128
CHUNK = 256
MESH = pl.DeviceIdType.MESH
F32 = jnp.float32
BF16 = jnp.bfloat16


def inner(left, right):
    return lax.dot_general(left, right, (((0,), (0,)), ((), ())), preferred_element_type=F32)


def outer(left, right):
    return lax.dot_general(left, right, (((1,), (1,)), ((), ())), preferred_element_type=F32)


def dot(left, right):
    return jnp.dot(left, right, preferred_element_type=F32)


def attention_kernel(
    nb, nu,
    tokens, query_base, key_base, value_base, out_grad, down_q, up_q, down_v, up_v,
    att_ref, gup_ref, low_out,
    kbuf, vbuf, lbuf, tok, qs, gs, downs, ups, lrq, lrv, lrin,
    local_sem, xsend, xrecv, fsend, frecv, lsend, lrecv, msend, mrecv, rsend, rrecv,
):
    blk = lax.axis_index("blk")
    u = lax.axis_index("uly")
    rows, width = tokens.shape
    rank = up_q.shape[0]
    span = nu * rows
    chunks = width // CHUNK
    has_prev = blk > 0
    has_next = blk < nb - 1
    mine = pl.ds(pl.multiple_of(span + u * rows, rows), rows)

    def peer(j):
        return lax.rem(u + j, nu)

    def source(j):
        return lax.rem(u - j + nu, nu)

    def cols(c):
        return pl.ds(pl.multiple_of(c * CHUNK, CHUNK), CHUNK)

    barrier = pltpu.get_barrier_semaphore()
    for j in range(1, nu):
        pl.semaphore_signal(barrier, inc=1, device_id=(blk, peer(j)), device_id_type=MESH)

    @pl.when(has_prev)
    def _():
        for j in range(nu):
            pl.semaphore_signal(barrier, inc=1, device_id=(blk - 1, peer(j)), device_id_type=MESH)

    @pl.when(has_next)
    def _():
        for j in range(nu):
            pl.semaphore_signal(barrier, inc=1, device_id=(blk + 1, peer(j)), device_id_type=MESH)

    local = [
        pltpu.make_async_copy(src, dst, local_sem.at[i])
        for i, (src, dst) in enumerate(
            (
                (tokens, tok), (down_q, downs.at[pl.ds(0, rank)]), (down_v, downs.at[pl.ds(rank, rank)]),
                (up_q, ups.at[pl.ds(0, rank)]), (up_v, ups.at[pl.ds(rank, rank)]),
                (value_base, vbuf.at[mine]), (key_base, kbuf.at[mine]),
                (query_base, qs), (out_grad, gs),
            )
        )
    ]
    for copy in local:
        copy.start()

    edge = jnp.logical_or(blk == 0, blk == nb - 1)

    @pl.when(edge)
    def _():
        pl.semaphore_wait(barrier, 2 * nu - 1)

    @pl.when(jnp.logical_not(edge))
    def _():
        pl.semaphore_wait(barrier, 3 * nu - 1)

    bufs = (kbuf, vbuf)

    def across(a, j, c):
        src = key_base.at[:, cols(c)] if a == 0 else vbuf.at[mine, cols(c)]
        return pltpu.make_async_remote_copy(
            src_ref=src, dst_ref=bufs[a].at[mine, cols(c)],
            send_sem=xsend.at[a, j, c], recv_sem=xrecv.at[a, j, c],
            device_id=(blk, peer(j)), device_id_type=MESH,
        )

    def crossed(a, j, c):
        here = bufs[a].at[pl.ds(pl.multiple_of(span + source(j) * rows, rows), rows), cols(c)]
        return pltpu.make_async_remote_copy(
            src_ref=here, dst_ref=here,
            send_sem=xsend.at[a, j, c], recv_sem=xrecv.at[a, j, c],
            device_id=(blk, peer(j)), device_id_type=MESH,
        )

    def onward(a, j, c):
        s = source(j)
        if a == 0 and j == 0:
            src = key_base.at[:, cols(c)]
        else:
            src = bufs[a].at[pl.ds(pl.multiple_of(span + s * rows, rows), rows), cols(c)]
        return pltpu.make_async_remote_copy(
            src_ref=src, dst_ref=bufs[a].at[pl.ds(pl.multiple_of(s * rows, rows), rows), cols(c)],
            send_sem=fsend.at[a, j, c], recv_sem=frecv.at[a, j, c],
            device_id=(blk + 1, u), device_id_type=MESH,
        )

    def arrived(a, j, c):
        here = bufs[a].at[pl.ds(pl.multiple_of(source(j) * rows, rows), rows), cols(c)]
        return pltpu.make_async_remote_copy(
            src_ref=here, dst_ref=here,
            send_sem=fsend.at[a, j, c], recv_sem=frecv.at[a, j, c],
            device_id=(blk, peer(1)), device_id_type=MESH,
        )

    def low_across(j):
        return pltpu.make_async_remote_copy(
            src_ref=lbuf.at[mine], dst_ref=lbuf.at[mine],
            send_sem=lsend.at[j], recv_sem=lrecv.at[j],
            device_id=(blk, peer(j)), device_id_type=MESH,
        )

    def low_crossed(j):
        here = lbuf.at[pl.ds(pl.multiple_of(span + source(j) * rows, rows), rows)]
        return pltpu.make_async_remote_copy(
            src_ref=here, dst_ref=here, send_sem=lsend.at[j], recv_sem=lrecv.at[j],
            device_id=(blk, peer(j)), device_id_type=MESH,
        )

    def low_onward(j):
        s = source(j)
        return pltpu.make_async_remote_copy(
            src_ref=lbuf.at[pl.ds(pl.multiple_of(span + s * rows, rows), rows)],
            dst_ref=lbuf.at[pl.ds(pl.multiple_of(s * rows, rows), rows)],
            send_sem=msend.at[j], recv_sem=mrecv.at[j],
            device_id=(blk + 1, u), device_id_type=MESH,
        )

    def low_arrived(j):
        here = lbuf.at[pl.ds(pl.multiple_of(source(j) * rows, rows), rows)]
        return pltpu.make_async_remote_copy(
            src_ref=here, dst_ref=here, send_sem=msend.at[j], recv_sem=mrecv.at[j],
            device_id=(blk, peer(1)), device_id_type=MESH,
        )

    early = min(3 * 512 // CHUNK, chunks)
    ahead = min(2048 // CHUNK, chunks)
    for c in range(early):
        for j in range(1, nu):
            across(0, j, c).start()

    @pl.when(has_next)
    def _():
        for c in range(ahead):
            onward(0, 0, c).start()

    lane = lax.broadcasted_iota(jnp.int32, (rows, 2 * rank), 1)
    for i in range(3):
        local[i].wait()
    low = outer(tok[...], downs[...])
    low_qm = jnp.where(lane < rank, low, 0.0).astype(BF16)
    low_vm = jnp.where(lane >= rank, low, 0.0).astype(BF16)
    lbuf[mine, :] = low_vm
    for i in range(3, 6):
        local[i].wait()

    @pl.loop(0, chunks)
    def _(c):
        part = dot(low_vm, ups[:, cols(c)])
        vbuf[mine, cols(c)] = (vbuf[mine, cols(c)].astype(F32) + part).astype(BF16)

    for j in range(1, nu):
        low_across(j).start()

    @pl.when(has_next)
    def _():
        low_onward(0).start()

    @pl.loop(0, chunks)
    def _(c):
        @pl.when(c >= early)
        def _():
            for j in range(1, nu):
                across(0, j, c).start()

        for j in range(1, nu):
            across(1, j, c).start()

    @pl.when(has_next)
    def _():
        for c in range(ahead):
            onward(1, 0, c).start()

    lrq[...] = jnp.zeros_like(lrq)
    lrv[...] = jnp.zeros_like(lrv)

    @pl.when(jnp.logical_not(has_prev))
    def _():
        kbuf[pl.ds(0, span), :] = jnp.zeros((span, width), BF16)
        vbuf[pl.ds(0, span), :] = jnp.zeros((span, width), BF16)
        lbuf[pl.ds(0, span), :] = jnp.zeros((span, 2 * rank), BF16)

    for i in range(6, 9):
        local[i].wait()

    scale = HEAD ** (-0.5)
    key_at = lax.broadcasted_iota(jnp.int32, (rows, 2 * span), 1)
    usable = jnp.logical_or(key_at >= span, has_prev)

    def head(h):
        at = pl.ds(pl.multiple_of(h * HEAD, HEAD), HEAD)
        up = ups[:, at]
        keys = kbuf[:, at]
        values = vbuf[:, at]
        grad = gs[:, at]
        query = (qs[:, at].astype(F32) + dot(low_qm, up)).astype(BF16)
        scores = jnp.where(usable, outer(query, keys) * scale, -jnp.inf)
        weights = jnp.exp(scores - jnp.max(scores, axis=1, keepdims=True))
        total = jnp.sum(weights, axis=1, keepdims=True)
        probs = (weights * (1.0 / total)).astype(BF16)
        attended = dot(probs, values).astype(BF16)
        delta = jnp.sum(grad.astype(F32) * attended.astype(F32), axis=1, keepdims=True)
        score_grad = (probs.astype(F32) * (outer(grad, values) - delta)).astype(BF16)
        query_grad = (dot(score_grad, keys) * scale).astype(BF16)
        seen = dot(probs, lbuf[...]).astype(BF16)
        gup = (inner(low_qm, query_grad) + inner(seen, grad)).astype(BF16)
        lifted = jnp.where(lane >= rank, outer(grad, up), 0.0).astype(BF16)
        return attended, gup, outer(query_grad, up), inner(probs, lifted)

    together = 2 if span <= 2 * HEAD else 1

    def head_group(first):
        results = [head(first + i) for i in range(together)]
        for i, (attended, gup, _, _) in enumerate(results):
            h = first + i
            att_ref[:, pl.ds(pl.multiple_of(h * HEAD, HEAD), HEAD)] = attended
            gup_ref[pl.ds(pl.multiple_of(h * 2 * rank, 2 * rank), 2 * rank), :] = gup
        lrq[...] += jnp.where(lane < rank, sum(r[2] for r in results), 0.0)
        lrv[...] += sum(r[3] for r in results)

    heads = CHUNK // HEAD

    @pl.loop(0, chunks + 1)
    def _(c):
        @pl.when(c == 0)
        def _():
            for j in range(1, nu):
                low_crossed(j).wait_recv()

                @pl.when(has_next)
                def _():
                    low_onward(j).start()

            @pl.when(has_prev)
            def _():
                for j in range(nu):
                    low_arrived(j).wait_recv()

        @pl.when(c < chunks)
        def _():
            for a in range(2):
                for j in range(1, nu):
                    crossed(a, j, c).wait_recv()

                    @pl.when(has_next)
                    def _():
                        onward(a, j, c).start()

            @pl.when(jnp.logical_and(has_next, c + ahead < chunks))
            def _():
                for a in range(2):
                    onward(a, 0, c + ahead).start()

        @pl.when(c > 0)
        def _():
            @pl.when(has_prev)
            def _():
                for a in range(2):
                    for j in range(nu):
                        arrived(a, j, c - 1).wait_recv()

            @pl.loop(0, heads // together)
            def _(i):
                head_group((c - 1) * heads + i * together)

    def terms(k, j, base):
        s = peer(j)
        return pltpu.make_async_remote_copy(
            src_ref=lrv.at[pl.ds(pl.multiple_of(base + s * rows, rows), rows)],
            dst_ref=lrin.at[k, j],
            send_sem=rsend.at[k, j], recv_sem=rrecv.at[k, j],
            device_id=(blk - k, s), device_id_type=MESH,
        )

    for j in range(1, nu):
        terms(0, j, span).start()

    @pl.when(has_prev)
    def _():
        for j in range(nu):
            terms(1, j, 0).start()

    @pl.loop(0, chunks)
    def _(c):
        for a in range(2):
            for j in range(1, nu):
                across(a, j, c).wait_send()

            @pl.when(has_next)
            def _():
                for j in range(nu):
                    onward(a, j, c).wait_send()

    for j in range(1, nu):
        low_across(j).wait_send()

    @pl.when(has_next)
    def _():
        for j in range(nu):
            low_onward(j).wait_send()

    lrq[...] += lrv[mine, :]
    for j in range(1, nu):
        terms(0, j, span).wait_recv()
        lrq[...] += lrin[0, j]

    @pl.when(has_next)
    def _():
        for j in range(nu):
            terms(1, j, 0).wait_recv()
            lrq[...] += lrin[1, j]

    low_out[...] = lrq[...].astype(BF16)
    for j in range(1, nu):
        terms(0, j, span).wait_send()

    @pl.when(has_prev)
    def _():
        for j in range(nu):
            terms(1, j, 0).wait_send()


def attention(nb, nu, *operands):
    rows, width = operands[0].shape
    rank = operands[6].shape[0]
    span = nu * rows
    chunks = width // CHUNK
    dma = pltpu.SemaphoreType.DMA
    anywhere = pl.BlockSpec(memory_space=pl.ANY)
    here = pl.BlockSpec(memory_space=pltpu.VMEM)
    return pl.pallas_call(
        functools.partial(attention_kernel, nb, nu),
        out_shape=(
            jax.ShapeDtypeStruct((rows, width), BF16),
            jax.ShapeDtypeStruct((width // HEAD * 2 * rank, HEAD), BF16),
            jax.ShapeDtypeStruct((rows, 2 * rank), BF16),
        ),
        in_specs=[anywhere] * 9,
        out_specs=(here, here, here),
        scratch_shapes=[
            pltpu.VMEM((2 * span, width), BF16),
            pltpu.VMEM((2 * span, width), BF16),
            pltpu.VMEM((2 * span, 2 * rank), BF16),
            pltpu.VMEM((rows, width), BF16),
            pltpu.VMEM((rows, width), BF16),
            pltpu.VMEM((rows, width), BF16),
            pltpu.VMEM((2 * rank, width), BF16),
            pltpu.VMEM((2 * rank, width), BF16),
            pltpu.VMEM((rows, 2 * rank), F32),
            pltpu.VMEM((2 * span, 2 * rank), F32),
            pltpu.VMEM((2, nu, rows, 2 * rank), F32),
            dma((9,)),
            dma((2, nu, chunks)), dma((2, nu, chunks)),
            dma((2, nu, chunks)), dma((2, nu, chunks)),
            dma((nu,)), dma((nu,)), dma((nu,)), dma((nu,)),
            dma((2, nu)), dma((2, nu)),
        ],
        compiler_params=pltpu.CompilerParams(
            collective_id=0, has_side_effects=True, vmem_limit_bytes=65_000_000
        ),
    )(*operands)


def reduction_kernel(
    nb, nu,
    tokens, lowrank, gup,
    downq_out, downv_out, upq_out, upv_out,
    tok, terms, pair, part, plane_in, line, line_in, down, ups, flat,
    local_sem, psend, precv, asend, arecv, bsend, brecv, csend, crecv, dsend, drecv, esend, erecv,
):
    blk = lax.axis_index("blk")
    u = lax.axis_index("uly")
    core = lax.rem(blk, 2)
    chip = blk // 2
    other = chip * 2 + 1 - core
    half = nb // 2
    inners = plane_in.shape[1] // nu
    outers = half // inners
    y = lax.rem(chip, inners)
    z = chip // inners
    group = nu * inners
    rows, width = tokens.shape
    rank = upq_out.shape[0]
    region = pair.shape[2]
    sub = plane_in.shape[2]
    piece = line_in.shape[2]

    def split(o, sign):
        pu = lax.rem(u + sign * (o // inners) + nu, nu)
        py = lax.rem(y + sign * lax.rem(o, inners) + inners, inners)
        return pu, py

    def plane_dev(o):
        pu, py = split(o, 1)
        return ((z * inners + py) * 2 + core, pu)

    def peer_z(o):
        return lax.rem(z + o, outers)

    def from_z(o):
        return lax.rem(z - o + outers, outers)

    def line_dev(o):
        return ((peer_z(o) * inners + y) * 2 + core, u)

    def subs(p):
        return pl.ds(pl.multiple_of(p * sub, sub), sub)

    barrier = pltpu.get_barrier_semaphore()
    pl.semaphore_signal(barrier, inc=1, device_id=(other, u), device_id_type=MESH)
    for o in range(1, group):
        pl.semaphore_signal(barrier, inc=1, device_id=plane_dev(o), device_id_type=MESH)
    for o in range(1, outers):
        pl.semaphore_signal(barrier, inc=1, device_id=line_dev(o), device_id_type=MESH)

    load = pltpu.make_async_copy(tokens, tok, local_sem.at[0])
    load.start()
    pl.semaphore_wait(barrier, group + outers - 1)

    def remote(src, dst, send, recv, device):
        return pltpu.make_async_remote_copy(
            src_ref=src, dst_ref=dst, send_sem=send, recv_sem=recv,
            device_id=device, device_id_type=MESH,
        )

    def swap(t, v):
        rows_at = pl.ds(pl.multiple_of((v * 2 + 1 - core) * region, region), region)
        return remote(
            (terms if t == 0 else gup).at[rows_at], pair.at[t, v],
            psend.at[t, v], precv.at[t, v], (other, u),
        )

    def scatter(t, o):
        pu, py = split(o, 1)
        return remote(
            part.at[t, pu, subs(py)], plane_in.at[t, o],
            asend.at[t, o], arecv.at[t, o], plane_dev(o),
        )

    def pass_on(t, o):
        at = pl.ds(pl.multiple_of(peer_z(o) * piece, piece), piece)
        return remote(
            line.at[t, at], line_in.at[t, o], bsend.at[t, o], brecv.at[t, o], line_dev(o)
        )

    def whole(t, v, k, p):
        return down.at[v, k, subs(p)] if t == 0 else ups.at[k, subs(p)]

    def piece_at(p, q):
        return pl.ds(pl.multiple_of(p * sub + q * piece, piece), piece)

    def small(t, q):
        return down.at[u, core, piece_at(y, q)] if t == 0 else ups.at[core, piece_at(y, q)]

    def along(t, o):
        return remote(small(t, z), small(t, z), csend.at[t, o], crecv.at[t, o], line_dev(o))

    def came(t, o):
        here = small(t, from_z(o))
        return remote(here, here, csend.at[t, o], crecv.at[t, o], line_dev(o))

    def spread(t, o):
        here = whole(t, u, core, y)
        return remote(here, here, dsend.at[t, o], drecv.at[t, o], plane_dev(o))

    def landed(t, o):
        pu, py = split(o, -1)
        here = whole(t, pu, core, py)
        return remote(here, here, dsend.at[t, o], drecv.at[t, o], (other, u))

    def share(t, o):
        pu, py = split(o, -1)
        here = whole(t, pu, core, py)
        return remote(here, here, esend.at[t, o], erecv.at[t, o], (other, u))

    def shared(t, o):
        pu, py = split(o, -1)
        here = whole(t, pu, 1 - core, py)
        return remote(here, here, esend.at[t, o], erecv.at[t, o], (other, u))

    if part.shape[2] > region:
        part[...] = jnp.zeros_like(part)
    for v in range(nu):
        swap(1, v).start()

    load.wait()
    lows = lowrank[...]

    @pl.loop(0, width // HEAD)
    def _(h):
        cols = pl.ds(pl.multiple_of(h * HEAD, HEAD), HEAD)
        here = pl.ds(pl.multiple_of(h * 2 * rank, 2 * rank), 2 * rank)
        terms[here, :] = inner(lows, tok[:, cols]).astype(BF16)

    for v in range(nu):
        swap(0, v).start()

    for t in (1, 0):
        for v in range(nu):
            rows_at = pl.ds(pl.multiple_of((v * 2 + core) * region, region), region)
            own = (terms if t == 0 else gup)[rows_at, :]
            swap(t, v).wait_recv()
            part[t, v, pl.ds(0, region), :] = (
                own.astype(F32) + pair[t, v].astype(F32)
            ).astype(BF16)
        for o in range(1, group):
            scatter(t, o).start()

    for t in (1, 0):
        total = part[t, u, subs(y), :].astype(F32)
        for o in range(1, group):
            scatter(t, o).wait_recv()
            total = total + plane_in[t, o].astype(F32)
        line[t, :, :] = total.astype(BF16)
        for o in range(1, outers):
            pass_on(t, o).start()

    for t in (1, 0):
        total = line[t, pl.ds(pl.multiple_of(z * piece, piece), piece), :].astype(F32)
        for o in range(1, outers):
            pass_on(t, o).wait_recv()
            total = total + line_in[t, o].astype(F32)
        small(t, z)[...] = total.astype(BF16)
        for o in range(1, outers):
            along(t, o).start()

    counts = (group, inners)
    for t in (1, 0):
        for o in range(1, outers):
            came(t, o).wait_recv()
        for o in range(1, counts[t]):
            spread(t, o).start()
        share(t, 0).start()

    for t in (1, 0):
        for o in range(1, counts[t]):
            landed(t, o).wait_recv()
            share(t, o).start()

    for t in (1, 0):
        for o in range(counts[t]):
            shared(t, o).wait_recv()
        places = [(v, k) for v in range(nu if t == 0 else 1) for k in range(2)]
        for n, (v, k) in enumerate(places):
            flat[pl.ds(n * region, region), :] = (
                down[v, k, pl.ds(0, region), :] if t == 0 else ups[k, pl.ds(0, region), :]
            )
        outs = (downq_out, downv_out) if t == 0 else (upq_out, upv_out)
        for h in range(len(places) * region // (2 * rank)):
            cols = pl.ds(h * HEAD, HEAD)
            outs[0][:, cols] = flat[pl.ds(h * 2 * rank, rank), :]
            outs[1][:, cols] = flat[pl.ds(h * 2 * rank + rank, rank), :]

    for t in (1, 0):
        for v in range(nu):
            swap(t, v).wait_send()
        for o in range(1, group):
            scatter(t, o).wait_send()
        for o in range(1, outers):
            pass_on(t, o).wait_send()
            along(t, o).wait_send()
        for o in range(1, counts[t]):
            spread(t, o).wait_send()
        for o in range(counts[t]):
            share(t, o).wait_send()


def reduction(nb, nu, tokens, lowrank, gup):
    rows, width = tokens.shape
    rank = lowrank.shape[1] // 2
    half = nb // 2
    inners = 2 if half % 2 == 0 else 1
    outers = half // inners
    group = nu * inners
    region = width // (2 * nu)
    piece = -(-region // (16 * half)) * 16
    sub = outers * piece
    held = half * piece
    dma = pltpu.SemaphoreType.DMA
    here = pl.BlockSpec(memory_space=pltpu.VMEM)
    lanes = lowrank.shape[1]
    return pl.pallas_call(
        functools.partial(reduction_kernel, nb, nu),
        out_shape=(
            jax.ShapeDtypeStruct((rank, width), BF16),
            jax.ShapeDtypeStruct((rank, width), BF16),
            jax.ShapeDtypeStruct((rank, width // nu), BF16),
            jax.ShapeDtypeStruct((rank, width // nu), BF16),
        ),
        in_specs=[pl.BlockSpec(memory_space=pl.ANY), here, here],
        out_specs=(here, here, here, here),
        scratch_shapes=[
            pltpu.VMEM((rows, width), BF16),
            pltpu.VMEM((width, lanes), BF16),
            pltpu.VMEM((2, nu, region, lanes), BF16),
            pltpu.VMEM((2, nu, held, lanes), BF16),
            pltpu.VMEM((2, group, sub, lanes), BF16),
            pltpu.VMEM((2, sub, lanes), BF16),
            pltpu.VMEM((2, outers, piece, lanes), BF16),
            pltpu.VMEM((nu, 2, held, lanes), BF16),
            pltpu.VMEM((2, held, lanes), BF16),
            pltpu.VMEM((2 * nu * region, lanes), BF16),
            dma((1,)),
            dma((2, nu)), dma((2, nu)),
            dma((2, group)), dma((2, group)),
            dma((2, outers)), dma((2, outers)),
            dma((2, outers)), dma((2, outers)),
            dma((2, group)), dma((2, group)),
            dma((2, group)), dma((2, group)),
        ],
        compiler_params=pltpu.CompilerParams(collective_id=1, has_side_effects=True),
    )(tokens, lowrank, gup)


def fused_kernel(
    nb, nu,
    tokens, query_base, key_base, value_base, out_grad, down_q, up_q, down_v, up_v,
    att_ref, downq_out, downv_out, upq_out, upv_out,
    kv, lbuf, tok, qs, gs, downs, ups, lrq, lrv, lrin,
    acc, pair, part, plane_in, line, line_in, res,
    local_sem, xsend, xrecv, fsend, frecv, lsend, lrecv, msend, mrecv, rsend, rrecv,
    psend, precv, asend, arecv, bsend, brecv, csend, crecv, dsend, drecv, esend, erecv,
):
    kbuf, vbuf = kv.at[0], kv.at[1]
    blk = lax.axis_index("blk")
    u = lax.axis_index("uly")
    rows, width = tokens.shape
    rank = up_q.shape[0]
    span = nu * rows
    chunks = width // CHUNK
    has_prev = blk > 0
    has_next = blk < nb - 1
    mine = pl.ds(pl.multiple_of(span + u * rows, rows), rows)

    def peer(j):
        return lax.rem(u + j, nu)

    def source(j):
        return lax.rem(u - j + nu, nu)

    cells = 2 * nu
    parts = chunks // cells
    core = lax.rem(blk, 2)
    chip = blk // 2
    other = chip * 2 + 1 - core
    inners, outers = grid_of(nb)
    group = nu * inners
    y = lax.rem(chip, inners)
    z = chip // inners
    sub = CHUNK // inners
    piece = sub // outers

    def place(c):
        return lax.rem(c, cells) * parts + c // cells

    def cols(c):
        return pl.ds(pl.multiple_of(place(c) * CHUNK, CHUNK), CHUNK)

    def remote(src, dst, send, recv, device):
        return pltpu.make_async_remote_copy(
            src_ref=src, dst_ref=dst, send_sem=send, recv_sem=recv,
            device_id=device, device_id_type=MESH,
        )

    def split(o, sign):
        pu = lax.rem(u + sign * (o // inners) + nu, nu)
        py = lax.rem(y + sign * lax.rem(o, inners) + inners, inners)
        return pu, py

    def plane_dev(o):
        pu, py = split(o, 1)
        return ((z * inners + py) * 2 + core, pu)

    def peer_z(o):
        return lax.rem(z + o, outers)

    def from_z(o):
        return lax.rem(z - o + outers, outers)

    def line_dev(o):
        return ((peer_z(o) * inners + y) * 2 + core, u)

    def subs(p):
        return pl.ds(pl.multiple_of(p * sub, sub), sub)

    def piece_at(p, q):
        return pl.ds(pl.multiple_of(p * sub + q * piece, piece), piece)

    def swap(n):
        return remote(
            acc.at[n, 1 - core], pair.at[n], psend.at[0], precv.at[n], (other, u)
        )

    def scatter(n, o):
        pu, py = split(o, 1)
        return remote(
            part.at[n, pu, subs(py)], plane_in.at[n, o - 1],
            asend.at[0], arecv.at[n], plane_dev(o),
        )

    def pass_on(n, o):
        at = pl.ds(pl.multiple_of(peer_z(o) * piece, piece), piece)
        return remote(
            line.at[n, at], line_in.at[n, o - 1], bsend.at[0], brecv.at[n], line_dev(o)
        )

    def along(n, o):
        here = res.at[n, core, u, piece_at(y, z)]
        return remote(here, here, csend.at[0], crecv.at[n], line_dev(o))

    def spread(n, o, t):
        here = res.at[n, core, u, subs(y)]
        return remote(here, here, dsend.at[t], drecv.at[n], plane_dev(o))

    def share(n, t):
        here = res.at[n, core] if t == 1 else res.at[n, core, u]
        return remote(here, here, esend.at[t], erecv.at[n], (other, u))

    def whole(src, send, recv):
        return remote(src, src, send, recv, (other, u))

    def pair_up(n):
        swap(n).wait_recv()
        part[n] = (acc[n, core].astype(F32) + pair[n].astype(F32)).astype(BF16)
        for o in range(1, group):
            scatter(n, o).start()

    def plane_sum(n):
        total = part[n, u, subs(y), :].astype(F32)
        whole(plane_in.at[n], asend.at[0], arecv.at[n]).wait_recv()
        for o in range(1, group):
            total = total + plane_in[n, o - 1].astype(F32)
        line[n] = total.astype(BF16)
        for o in range(1, outers):
            pass_on(n, o).start()

    def line_sum(n):
        total = line[n, pl.ds(pl.multiple_of(z * piece, piece), piece), :].astype(F32)
        whole(line_in.at[n], bsend.at[0], brecv.at[n]).wait_recv()
        for o in range(1, outers):
            total = total + line_in[n, o - 1].astype(F32)
        res[n, core, u, piece_at(y, z), :] = total.astype(BF16)
        for o in range(1, outers):
            along(n, o).start()

    def widen(n, t):
        whole(line_in.at[n], csend.at[0], crecv.at[n]).wait_recv()
        for o in range(1, (inners, group)[t]):
            spread(n, o, t).start()

    def hand_over(n, t):
        whole(plane_in.at[n, pl.ds(0, (inners, group)[t] - 1)], dsend.at[t], drecv.at[n]).wait_recv()
        share(n, t).start()

    def each(first, stop, work):
        @pl.loop(first, stop)
        def _(n):
            work(n)

    barrier = pltpu.get_barrier_semaphore()
    for j in range(1, nu):
        pl.semaphore_signal(barrier, inc=1, device_id=(blk, peer(j)), device_id_type=MESH)

    @pl.when(has_prev)
    def _():
        for j in range(nu):
            pl.semaphore_signal(barrier, inc=1, device_id=(blk - 1, peer(j)), device_id_type=MESH)

    @pl.when(has_next)
    def _():
        for j in range(nu):
            pl.semaphore_signal(barrier, inc=1, device_id=(blk + 1, peer(j)), device_id_type=MESH)

    for o in range(1, group):
        pl.semaphore_signal(barrier, inc=1, device_id=plane_dev(o), device_id_type=MESH)
    for o in range(1, outers):
        pl.semaphore_signal(barrier, inc=1, device_id=line_dev(o), device_id_type=MESH)

    local = [
        pltpu.make_async_copy(src, dst, local_sem.at[i])
        for i, (src, dst) in enumerate(
            (
                (tokens, tok), (down_q, downs.at[pl.ds(0, rank)]), (down_v, downs.at[pl.ds(rank, rank)]),
                (up_q, ups.at[pl.ds(0, rank)]), (up_v, ups.at[pl.ds(rank, rank)]),
                (value_base, vbuf.at[mine]), (key_base, kbuf.at[mine]),
                (query_base, qs), (out_grad, gs),
            )
        )
    ]
    for copy in local:
        copy.start()

    edge = jnp.logical_or(blk == 0, blk == nb - 1)

    @pl.when(edge)
    def _():
        pl.semaphore_wait(barrier, 2 * nu - 1 + group + outers - 2)

    @pl.when(jnp.logical_not(edge))
    def _():
        pl.semaphore_wait(barrier, 3 * nu - 1 + group + outers - 2)

    def rows_of(first, j):
        return pl.ds(pl.multiple_of(first + source(j) * rows, rows), rows)

    def cross(j, c, what):
        at = cols(c)
        src, dst = {
            0: (key_base.at[:, at], kv.at[0, mine, at]),
            1: (kv.at[1, mine, at], kv.at[1, mine, at]),
            2: (kv.at[:, mine, at], kv.at[:, mine, at]),
        }[what]
        return remote(src, dst, xsend.at[j], xrecv.at[j, c], (blk, peer(j)))

    def crossed(j, c):
        here = kv.at[:, rows_of(span, j), cols(c)]
        return remote(here, here, xsend.at[j], xrecv.at[j, c], (blk, peer(j)))

    def onward(j, c, what):
        at = cols(c)
        old, new = rows_of(span, j), rows_of(0, j)
        src, dst = {
            0: (key_base.at[:, at], kv.at[0, new, at]),
            1: (kv.at[1, old, at], kv.at[1, new, at]),
            2: (kv.at[:, old, at], kv.at[:, new, at]),
        }[what]
        return remote(src, dst, fsend.at[j], frecv.at[c], (blk + 1, u))

    def arrived(c):
        here = kv.at[:, pl.ds(0, span), cols(c)]
        return remote(here, here, fsend.at[0], frecv.at[c], (blk, peer(1)))

    def low_across(j):
        return pltpu.make_async_remote_copy(
            src_ref=lbuf.at[mine], dst_ref=lbuf.at[mine],
            send_sem=lsend.at[j], recv_sem=lrecv.at[j],
            device_id=(blk, peer(j)), device_id_type=MESH,
        )

    def low_crossed(j):
        here = lbuf.at[pl.ds(pl.multiple_of(span + source(j) * rows, rows), rows)]
        return pltpu.make_async_remote_copy(
            src_ref=here, dst_ref=here, send_sem=lsend.at[j], recv_sem=lrecv.at[j],
            device_id=(blk, peer(j)), device_id_type=MESH,
        )

    def low_onward(j):
        s = source(j)
        return pltpu.make_async_remote_copy(
            src_ref=lbuf.at[pl.ds(pl.multiple_of(span + s * rows, rows), rows)],
            dst_ref=lbuf.at[pl.ds(pl.multiple_of(s * rows, rows), rows)],
            send_sem=msend.at[j], recv_sem=mrecv.at[j],
            device_id=(blk + 1, u), device_id_type=MESH,
        )

    def low_arrived(j):
        here = lbuf.at[pl.ds(pl.multiple_of(source(j) * rows, rows), rows)]
        return pltpu.make_async_remote_copy(
            src_ref=here, dst_ref=here, send_sem=msend.at[j], recv_sem=mrecv.at[j],
            device_id=(blk, peer(1)), device_id_type=MESH,
        )

    early = min(3 * 512 // CHUNK, chunks)
    ahead = min(2048 // CHUNK, chunks)
    for c in range(early):
        for j in range(1, nu):
            cross(j, c, 0).start()

    @pl.when(has_next)
    def _():
        for c in range(ahead):
            onward(0, c, 0).start()

    lane = lax.broadcasted_iota(jnp.int32, (rows, 2 * rank), 1)
    for i in range(3):
        local[i].wait()
    low = outer(tok[...], downs[...])
    low_qm = jnp.where(lane < rank, low, 0.0).astype(BF16)
    low_vm = jnp.where(lane >= rank, low, 0.0).astype(BF16)
    lbuf[mine, :] = low_vm
    for i in range(3, 7):
        local[i].wait()

    @pl.loop(0, chunks)
    def _(c):
        part = dot(low_vm, ups[:, cols(c)])
        vbuf[mine, cols(c)] = (vbuf[mine, cols(c)].astype(F32) + part).astype(BF16)

    for j in range(1, nu):
        low_across(j).start()

    @pl.when(has_next)
    def _():
        low_onward(0).start()

    @pl.loop(0, early)
    def _(c):
        for j in range(1, nu):
            cross(j, c, 1).start()

    @pl.when(has_next)
    def _():
        @pl.loop(0, ahead)
        def _(c):
            onward(0, c, 1).start()

    @pl.loop(early, chunks)
    def _(c):
        for j in range(1, nu):
            cross(j, c, 2).start()

    lrq[...] = jnp.zeros_like(lrq)
    lrv[...] = jnp.zeros_like(lrv)

    @pl.when(jnp.logical_not(has_prev))
    def _():
        kbuf[pl.ds(0, span), :] = jnp.zeros((span, width), BF16)
        vbuf[pl.ds(0, span), :] = jnp.zeros((span, width), BF16)
        lbuf[pl.ds(0, span), :] = jnp.zeros((span, 2 * rank), BF16)

    for i in range(7, 9):
        local[i].wait()

    scale = HEAD ** (-0.5)
    key_at = lax.broadcasted_iota(jnp.int32, (rows, 2 * span), 1)
    usable = jnp.logical_or(key_at >= span, has_prev)

    def head(h):
        at = pl.ds(pl.multiple_of(h * HEAD, HEAD), HEAD)
        up = ups[:, at]
        keys = kbuf[:, at]
        values = vbuf[:, at]
        grad = gs[:, at]
        query = (qs[:, at].astype(F32) + dot(low_qm, up)).astype(BF16)
        scores = jnp.where(usable, outer(query, keys) * scale, -jnp.inf)
        weights = jnp.exp(scores - jnp.max(scores, axis=1, keepdims=True))
        total = jnp.sum(weights, axis=1, keepdims=True)
        probs = (weights * (1.0 / total)).astype(BF16)
        attended = dot(probs, values).astype(BF16)
        delta = jnp.sum(grad.astype(F32) * attended.astype(F32), axis=1, keepdims=True)
        score_grad = (probs.astype(F32) * (outer(grad, values) - delta)).astype(BF16)
        query_grad = (dot(score_grad, keys) * scale).astype(BF16)
        seen = dot(probs, lbuf[...]).astype(BF16)
        gup = (inner(low_qm, query_grad) + inner(seen, grad)).astype(BF16)
        lifted = jnp.where(lane >= rank, outer(grad, up), 0.0).astype(BF16)
        return attended, gup, outer(query_grad, up), inner(probs, lifted)

    together = 2 if span <= 2 * HEAD else 1

    def head_group(c, offset):
        first = place(c) * heads + offset
        results = [head(first + i) for i in range(together)]
        for i, (attended, gup, _, _) in enumerate(results):
            h = first + i
            att_ref[:, pl.ds(pl.multiple_of(h * HEAD, HEAD), HEAD)] = attended
            row = pl.multiple_of((offset + i) * 2 * rank, 2 * rank)
            cell = lax.rem(c, cells)
            acc[c // cells, lax.rem(cell, 2), cell // 2, pl.ds(row, 2 * rank), :] = gup
        lrq[...] += jnp.where(lane < rank, sum(r[2] for r in results), 0.0)
        lrv[...] += sum(r[3] for r in results)

    heads = CHUNK // HEAD
    soon = max(parts - 2, 0)

    @pl.loop(0, chunks + 1)
    def _(c):
        @pl.when(c == 0)
        def _():
            for j in range(1, nu):
                low_crossed(j).wait_recv()

                @pl.when(has_next)
                def _():
                    low_onward(j).start()

            @pl.when(has_prev)
            def _():
                for j in range(nu):
                    low_arrived(j).wait_recv()

        @pl.when(c < chunks)
        def _():
            for j in range(1, nu):
                crossed(j, c).wait_recv()

                @pl.when(has_next)
                def _():
                    onward(j, c, 2).start()

            @pl.when(jnp.logical_and(has_next, c + ahead < chunks))
            def _():
                onward(0, c + ahead, 2).start()

        @pl.when(c == chunks - 1)
        def _():
            each(0, soon, pair_up)

        @pl.when(c > 0)
        def _():
            @pl.when(has_prev)
            def _():
                arrived(c - 1).wait_recv()

            @pl.loop(0, heads // together)
            def _(i):
                head_group(c - 1, i * together)


            @pl.when(lax.rem(c, cells) == 0)
            def _():
                swap(c // cells - 1).start()

    def terms(k, j, base):
        s = peer(j)
        return pltpu.make_async_remote_copy(
            src_ref=lrv.at[pl.ds(pl.multiple_of(base + s * rows, rows), rows)],
            dst_ref=lrin.at[k, j],
            send_sem=rsend.at[k, j], recv_sem=rrecv.at[k, j],
            device_id=(blk - k, s), device_id_type=MESH,
        )

    for j in range(1, nu):
        terms(0, j, span).start()

    @pl.when(has_prev)
    def _():
        for j in range(nu):
            terms(1, j, 0).start()

    each(soon, parts, pair_up)
    each(0, soon, plane_sum)

    lrq[...] += lrv[mine, :]
    for j in range(1, nu):
        terms(0, j, span).wait_recv()
        lrq[...] += lrin[0, j]

    @pl.when(has_next)
    def _():
        for j in range(nu):
            terms(1, j, 0).wait_recv()
            lrq[...] += lrin[1, j]

    lows = lrq[...].T.astype(BF16)

    def terms_of(p, v, k):
        at = pl.ds(pl.multiple_of(((v * 2 + k) * parts + p) * CHUNK, CHUNK), CHUNK)
        block = dot(lows, tok[:, at]).astype(BF16)
        for i in range(heads):
            acc[parts + p, k, v, pl.ds(i * 2 * rank, 2 * rank), :] = block[:, i * HEAD:(i + 1) * HEAD]

    def project(p):
        for v in range(nu):
            terms_of(p, v, 1 - core)
        swap(parts + p).start()
        for v in range(nu):
            terms_of(p, v, core)

    def lay_out(n, t, outs):
        shared_here = res.at[n, 1 - core] if t == 1 else res.at[n, 1 - core, u]
        whole(shared_here, esend.at[t], erecv.at[n]).wait_recv()
        for v in range(nu if t == 1 else 1):
            for k in range(2):
                for i in range(heads):
                    h = ((v * 2 + k) * parts + n - t * parts) * heads + i
                    at = pl.ds(pl.multiple_of(h * HEAD, HEAD), HEAD)
                    w = v if t == 1 else u
                    outs[0][:, at] = res[n, k, w, pl.ds(i * 2 * rank, rank), :]
                    outs[1][:, at] = res[n, k, w, pl.ds(i * 2 * rank + rank, rank), :]

    each(0, parts, project)
    each(parts, 2 * parts, pair_up)
    each(soon, parts, plane_sum)
    each(0, parts, line_sum)
    each(parts, 2 * parts, plane_sum)
    each(0, parts, lambda n: widen(n, 0))
    each(parts, 2 * parts, line_sum)
    each(0, parts, lambda n: hand_over(n, 0))
    each(parts, 2 * parts, lambda n: widen(n, 1))
    each(0, parts, lambda n: lay_out(n, 0, (upq_out, upv_out)))
    each(parts, 2 * parts, lambda n: hand_over(n, 1))
    each(parts, 2 * parts, lambda n: lay_out(n, 1, (downq_out, downv_out)))

    whole(pair, psend.at[0], precv.at[0]).wait_send()
    whole(plane_in, asend.at[0], arecv.at[0]).wait_send()
    whole(line_in, bsend.at[0], brecv.at[0]).wait_send()
    whole(line_in, csend.at[0], crecv.at[0]).wait_send()
    for i in range(2):
        some = pl.ds(i * parts, parts)
        whole(
            plane_in.at[some, pl.ds(0, (inners, group)[i] - 1)], dsend.at[i], drecv.at[0]
        ).wait_send()
    whole(res.at[pl.ds(0, parts), 0, 0], esend.at[0], erecv.at[0]).wait_send()
    whole(res.at[pl.ds(parts, parts), 0], esend.at[1], erecv.at[0]).wait_send()

    everything = kv.at[:, mine, :]
    for j in range(1, nu):
        remote(everything, everything, xsend.at[j], xrecv.at[j, 0], (blk, peer(j))).wait_send()

    @pl.when(has_next)
    def _():
        for j in range(nu):
            remote(everything, everything, fsend.at[j], frecv.at[0], (blk + 1, u)).wait_send()

    for j in range(1, nu):
        low_across(j).wait_send()

    @pl.when(has_next)
    def _():
        for j in range(nu):
            low_onward(j).wait_send()

    for j in range(1, nu):
        terms(0, j, span).wait_send()

    @pl.when(has_prev)
    def _():
        for j in range(nu):
            terms(1, j, 0).wait_send()


def grid_of(nb):
    half = nb // 2
    inners = 2 if half % 2 == 0 else 1
    return inners, half // inners


def fused(nb, nu, *operands):
    rows, width = operands[0].shape
    rank = operands[6].shape[0]
    span = nu * rows
    chunks = width // CHUNK
    cells = 2 * nu
    parts = chunks // cells
    inners, outers = grid_of(nb)
    group = nu * inners
    sub = CHUNK // inners
    lanes = 2 * rank
    dma = pltpu.SemaphoreType.DMA
    anywhere = pl.BlockSpec(memory_space=pl.ANY)
    here = pl.BlockSpec(memory_space=pltpu.VMEM)
    return pl.pallas_call(
        functools.partial(fused_kernel, nb, nu),
        out_shape=(
            pltpu.VMEM((rows, width), BF16),
            pltpu.VMEM((rank, width), BF16),
            pltpu.VMEM((rank, width), BF16),
            pltpu.VMEM((rank, width // nu), BF16),
            pltpu.VMEM((rank, width // nu), BF16),
        ),
        in_specs=[anywhere] * 9,
        out_specs=(here,) * 5,
        scratch_shapes=[
            pltpu.VMEM((2, 2 * span, width), BF16),
            pltpu.VMEM((2 * span, lanes), BF16),
            pltpu.VMEM((rows, width), BF16),
            pltpu.VMEM((rows, width), BF16),
            pltpu.VMEM((rows, width), BF16),
            pltpu.VMEM((lanes, width), BF16),
            pltpu.VMEM((lanes, width), BF16),
            pltpu.VMEM((rows, lanes), F32),
            pltpu.VMEM((2 * span, lanes), F32),
            pltpu.VMEM((2, nu, rows, lanes), F32),
            pltpu.VMEM((2 * parts, 2, nu, CHUNK, lanes), BF16),
            pltpu.VMEM((2 * parts, nu, CHUNK, lanes), BF16),
            pltpu.VMEM((2 * parts, nu, CHUNK, lanes), BF16),
            pltpu.VMEM((2 * parts, group - 1, sub, lanes), BF16),
            pltpu.VMEM((2 * parts, sub, lanes), BF16),
            pltpu.VMEM((2 * parts, outers - 1, sub // outers, lanes), BF16),
            pltpu.VMEM((2 * parts, 2, nu, CHUNK, lanes), BF16),
            dma((9,)),
            dma((nu,)), dma((nu, chunks)),
            dma((nu,)), dma((chunks,)),
            dma((nu,)), dma((nu,)), dma((nu,)), dma((nu,)),
            dma((2, nu)), dma((2, nu)),
            dma((1,)), dma((2 * parts,)),
            dma((1,)), dma((2 * parts,)),
            dma((1,)), dma((2 * parts,)),
            dma((1,)), dma((2 * parts,)),
            dma((2,)), dma((2 * parts,)),
            dma((2,)), dma((2 * parts,)),
        ],
        compiler_params=pltpu.CompilerParams(
            collective_id=2, has_side_effects=True, vmem_limit_bytes=60_000_000
        ),
    )(*operands)


def fits(nb, nu, rows, width, rank):
    inners, outers = grid_of(nb)
    return (
        2 * rank == HEAD
        and width % (2 * nu * CHUNK) == 0
        and CHUNK % (16 * inners * outers) == 0
        and nu * rows <= CHUNK
    )


def deliver_kernel(*refs):
    count = len(refs) // 2
    sources, targets, sem = refs[:count], refs[count:2 * count], refs[-1]
    copies = [pltpu.make_async_copy(a, b, sem.at[i]) for i, (a, b) in enumerate(zip(sources, targets))]
    for copy in copies:
        copy.start()
    for copy in copies:
        copy.wait()


def deliver(*arrays):
    return pl.pallas_call(
        deliver_kernel,
        out_shape=tuple(jax.ShapeDtypeStruct(a.shape, a.dtype) for a in arrays),
        in_specs=[pl.BlockSpec(memory_space=pl.ANY)] * len(arrays),
        out_specs=tuple(pl.BlockSpec(memory_space=pl.ANY) for _ in arrays),
        scratch_shapes=[pltpu.SemaphoreType.DMA((len(arrays),))],
    )(*(pltpu.with_memory_space_constraint(a, pltpu.VMEM) for a in arrays))


def per_device(nb, nu, tokens, query_base, key_base, value_base, out_grad, down_q, up_q, down_v, up_v):
    operands = (tokens, query_base, key_base, value_base, out_grad, down_q.T, up_q, down_v.T, up_v)
    if fits(nb, nu, *tokens.shape, up_q.shape[0]):
        attended, grad_down_q, grad_down_v, grad_up_q, grad_up_v = deliver(*fused(nb, nu, *operands))
        return attended, grad_down_q.T, grad_up_q, grad_down_v.T, grad_up_v
    attended, gup, lowrank = attention(nb, nu, *operands)
    grad_down_q, grad_down_v, grad_up_q, grad_up_v = reduction(nb, nu, tokens, lowrank, gup)
    return attended, grad_down_q.T, grad_up_q, grad_down_v.T, grad_up_v


def solution(mesh):
    split = P(("blk", "uly"), None)
    return jax.shard_map(
        functools.partial(per_device, mesh.shape["blk"], mesh.shape["uly"]),
        mesh=mesh,
        in_specs=(split,) * 5 + (P(),) * 4,
        out_specs=(split, P(), P(None, "uly"), P(), P(None, "uly")),
        check_vma=False,
    )
```

```python
import functools

import jax
import jax.numpy as jnp
from jax import lax
from jax.experimental import pallas as pl
from jax.experimental.pallas import tpu as pltpu
from jax.sharding import PartitionSpec as P

HEAD = 128
CHUNK = 256
MESH = pl.DeviceIdType.MESH
F32 = jnp.float32
BF16 = jnp.bfloat16


def inner(left, right):
    return lax.dot_general(left, right, (((0,), (0,)), ((), ())), preferred_element_type=F32)


def outer(left, right):
    return lax.dot_general(left, right, (((1,), (1,)), ((), ())), preferred_element_type=F32)


def dot(left, right):
    return jnp.dot(left, right, preferred_element_type=F32)


def attention_kernel(
    nb, nu,
    tokens, query_base, key_base, value_base, out_grad, down_q, up_q, down_v, up_v,
    att_ref, gup_ref, low_out,
    kbuf, vbuf, lbuf, tok, qs, gs, downs, ups, lrq, lrv, lrin,
    local_sem, xsend, xrecv, fsend, frecv, lsend, lrecv, msend, mrecv, rsend, rrecv,
):
    blk = lax.axis_index("blk")
    u = lax.axis_index("uly")
    rows, width = tokens.shape
    rank = up_q.shape[0]
    span = nu * rows
    chunks = width // CHUNK
    has_prev = blk > 0
    has_next = blk < nb - 1
    mine = pl.ds(pl.multiple_of(span + u * rows, rows), rows)

    def peer(j):
        return lax.rem(u + j, nu)

    def source(j):
        return lax.rem(u - j + nu, nu)

    def cols(c):
        return pl.ds(pl.multiple_of(c * CHUNK, CHUNK), CHUNK)

    barrier = pltpu.get_barrier_semaphore()
    for j in range(1, nu):
        pl.semaphore_signal(barrier, inc=1, device_id=(blk, peer(j)), device_id_type=MESH)

    @pl.when(has_prev)
    def _():
        for j in range(nu):
            pl.semaphore_signal(barrier, inc=1, device_id=(blk - 1, peer(j)), device_id_type=MESH)

    @pl.when(has_next)
    def _():
        for j in range(nu):
            pl.semaphore_signal(barrier, inc=1, device_id=(blk + 1, peer(j)), device_id_type=MESH)

    local = [
        pltpu.make_async_copy(src, dst, local_sem.at[i])
        for i, (src, dst) in enumerate(
            (
                (tokens, tok), (down_q, downs.at[pl.ds(0, rank)]), (down_v, downs.at[pl.ds(rank, rank)]),
                (up_q, ups.at[pl.ds(0, rank)]), (up_v, ups.at[pl.ds(rank, rank)]),
                (value_base, vbuf.at[mine]), (key_base, kbuf.at[mine]),
                (query_base, qs), (out_grad, gs),
            )
        )
    ]
    for copy in local:
        copy.start()

    edge = jnp.logical_or(blk == 0, blk == nb - 1)

    @pl.when(edge)
    def _():
        pl.semaphore_wait(barrier, 2 * nu - 1)

    @pl.when(jnp.logical_not(edge))
    def _():
        pl.semaphore_wait(barrier, 3 * nu - 1)

    bufs = (kbuf, vbuf)

    def across(a, j, c):
        src = key_base.at[:, cols(c)] if a == 0 else vbuf.at[mine, cols(c)]
        return pltpu.make_async_remote_copy(
            src_ref=src, dst_ref=bufs[a].at[mine, cols(c)],
            send_sem=xsend.at[a, j, c], recv_sem=xrecv.at[a, j, c],
            device_id=(blk, peer(j)), device_id_type=MESH,
        )

    def crossed(a, j, c):
        here = bufs[a].at[pl.ds(pl.multiple_of(span + source(j) * rows, rows), rows), cols(c)]
        return pltpu.make_async_remote_copy(
            src_ref=here, dst_ref=here,
            send_sem=xsend.at[a, j, c], recv_sem=xrecv.at[a, j, c],
            device_id=(blk, peer(j)), device_id_type=MESH,
        )

    def onward(a, j, c):
        s = source(j)
        if a == 0 and j == 0:
            src = key_base.at[:, cols(c)]
        else:
            src = bufs[a].at[pl.ds(pl.multiple_of(span + s * rows, rows), rows), cols(c)]
        return pltpu.make_async_remote_copy(
            src_ref=src, dst_ref=bufs[a].at[pl.ds(pl.multiple_of(s * rows, rows), rows), cols(c)],
            send_sem=fsend.at[a, j, c], recv_sem=frecv.at[a, j, c],
            device_id=(blk + 1, u), device_id_type=MESH,
        )

    def arrived(a, j, c):
        here = bufs[a].at[pl.ds(pl.multiple_of(source(j) * rows, rows), rows), cols(c)]
        return pltpu.make_async_remote_copy(
            src_ref=here, dst_ref=here,
            send_sem=fsend.at[a, j, c], recv_sem=frecv.at[a, j, c],
            device_id=(blk, peer(1)), device_id_type=MESH,
        )

    def low_across(j):
        return pltpu.make_async_remote_copy(
            src_ref=lbuf.at[mine], dst_ref=lbuf.at[mine],
            send_sem=lsend.at[j], recv_sem=lrecv.at[j],
            device_id=(blk, peer(j)), device_id_type=MESH,
        )

    def low_crossed(j):
        here = lbuf.at[pl.ds(pl.multiple_of(span + source(j) * rows, rows), rows)]
        return pltpu.make_async_remote_copy(
            src_ref=here, dst_ref=here, send_sem=lsend.at[j], recv_sem=lrecv.at[j],
            device_id=(blk, peer(j)), device_id_type=MESH,
        )

    def low_onward(j):
        s = source(j)
        return pltpu.make_async_remote_copy(
            src_ref=lbuf.at[pl.ds(pl.multiple_of(span + s * rows, rows), rows)],
            dst_ref=lbuf.at[pl.ds(pl.multiple_of(s * rows, rows), rows)],
            send_sem=msend.at[j], recv_sem=mrecv.at[j],
            device_id=(blk + 1, u), device_id_type=MESH,
        )

    def low_arrived(j):
        here = lbuf.at[pl.ds(pl.multiple_of(source(j) * rows, rows), rows)]
        return pltpu.make_async_remote_copy(
            src_ref=here, dst_ref=here, send_sem=msend.at[j], recv_sem=mrecv.at[j],
            device_id=(blk, peer(1)), device_id_type=MESH,
        )

    early = min(3 * 512 // CHUNK, chunks)
    ahead = min(2048 // CHUNK, chunks)
    for c in range(early):
        for j in range(1, nu):
            across(0, j, c).start()

    @pl.when(has_next)
    def _():
        for c in range(ahead):
            onward(0, 0, c).start()

    lane = lax.broadcasted_iota(jnp.int32, (rows, 2 * rank), 1)
    for i in range(3):
        local[i].wait()
    low = outer(tok[...], downs[...])
    low_qm = jnp.where(lane < rank, low, 0.0).astype(BF16)
    low_vm = jnp.where(lane >= rank, low, 0.0).astype(BF16)
    lbuf[mine, :] = low_vm
    for i in range(3, 6):
        local[i].wait()

    @pl.loop(0, chunks)
    def _(c):
        part = dot(low_vm, ups[:, cols(c)])
        vbuf[mine, cols(c)] = (vbuf[mine, cols(c)].astype(F32) + part).astype(BF16)

    for j in range(1, nu):
        low_across(j).start()

    @pl.when(has_next)
    def _():
        low_onward(0).start()

    @pl.loop(0, chunks)
    def _(c):
        @pl.when(c >= early)
        def _():
            for j in range(1, nu):
                across(0, j, c).start()

        for j in range(1, nu):
            across(1, j, c).start()

    @pl.when(has_next)
    def _():
        for c in range(ahead):
            onward(1, 0, c).start()

    lrq[...] = jnp.zeros_like(lrq)
    lrv[...] = jnp.zeros_like(lrv)

    @pl.when(jnp.logical_not(has_prev))
    def _():
        kbuf[pl.ds(0, span), :] = jnp.zeros((span, width), BF16)
        vbuf[pl.ds(0, span), :] = jnp.zeros((span, width), BF16)
        lbuf[pl.ds(0, span), :] = jnp.zeros((span, 2 * rank), BF16)

    for i in range(6, 9):
        local[i].wait()

    scale = HEAD ** (-0.5)
    key_at = lax.broadcasted_iota(jnp.int32, (rows, 2 * span), 1)
    usable = jnp.logical_or(key_at >= span, has_prev)

    def head(h):
        at = pl.ds(pl.multiple_of(h * HEAD, HEAD), HEAD)
        up = ups[:, at]
        keys = kbuf[:, at]
        values = vbuf[:, at]
        grad = gs[:, at]
        query = (qs[:, at].astype(F32) + dot(low_qm, up)).astype(BF16)
        scores = jnp.where(usable, outer(query, keys) * scale, -jnp.inf)
        weights = jnp.exp(scores - jnp.max(scores, axis=1, keepdims=True))
        total = jnp.sum(weights, axis=1, keepdims=True)
        probs = (weights * (1.0 / total)).astype(BF16)
        attended = dot(probs, values).astype(BF16)
        delta = jnp.sum(grad.astype(F32) * attended.astype(F32), axis=1, keepdims=True)
        score_grad = (probs.astype(F32) * (outer(grad, values) - delta)).astype(BF16)
        query_grad = (dot(score_grad, keys) * scale).astype(BF16)
        seen = dot(probs, lbuf[...]).astype(BF16)
        gup = (inner(low_qm, query_grad) + inner(seen, grad)).astype(BF16)
        lifted = jnp.where(lane >= rank, outer(grad, up), 0.0).astype(BF16)
        return attended, gup, outer(query_grad, up), inner(probs, lifted)

    together = 2 if span <= 2 * HEAD else 1

    def head_group(first):
        results = [head(first + i) for i in range(together)]
        for i, (attended, gup, _, _) in enumerate(results):
            h = first + i
            att_ref[:, pl.ds(pl.multiple_of(h * HEAD, HEAD), HEAD)] = attended
            gup_ref[pl.ds(pl.multiple_of(h * 2 * rank, 2 * rank), 2 * rank), :] = gup
        lrq[...] += jnp.where(lane < rank, sum(r[2] for r in results), 0.0)
        lrv[...] += sum(r[3] for r in results)

    heads = CHUNK // HEAD

    @pl.loop(0, chunks + 1)
    def _(c):
        @pl.when(c == 0)
        def _():
            for j in range(1, nu):
                low_crossed(j).wait_recv()

                @pl.when(has_next)
                def _():
                    low_onward(j).start()

            @pl.when(has_prev)
            def _():
                for j in range(nu):
                    low_arrived(j).wait_recv()

        @pl.when(c < chunks)
        def _():
            for a in range(2):
                for j in range(1, nu):
                    crossed(a, j, c).wait_recv()

                    @pl.when(has_next)
                    def _():
                        onward(a, j, c).start()

            @pl.when(jnp.logical_and(has_next, c + ahead < chunks))
            def _():
                for a in range(2):
                    onward(a, 0, c + ahead).start()

        @pl.when(c > 0)
        def _():
            @pl.when(has_prev)
            def _():
                for a in range(2):
                    for j in range(nu):
                        arrived(a, j, c - 1).wait_recv()

            @pl.loop(0, heads // together)
            def _(i):
                head_group((c - 1) * heads + i * together)

    def terms(k, j, base):
        s = peer(j)
        return pltpu.make_async_remote_copy(
            src_ref=lrv.at[pl.ds(pl.multiple_of(base + s * rows, rows), rows)],
            dst_ref=lrin.at[k, j],
            send_sem=rsend.at[k, j], recv_sem=rrecv.at[k, j],
            device_id=(blk - k, s), device_id_type=MESH,
        )

    for j in range(1, nu):
        terms(0, j, span).start()

    @pl.when(has_prev)
    def _():
        for j in range(nu):
            terms(1, j, 0).start()

    @pl.loop(0, chunks)
    def _(c):
        for a in range(2):
            for j in range(1, nu):
                across(a, j, c).wait_send()

            @pl.when(has_next)
            def _():
                for j in range(nu):
                    onward(a, j, c).wait_send()

    for j in range(1, nu):
        low_across(j).wait_send()

    @pl.when(has_next)
    def _():
        for j in range(nu):
            low_onward(j).wait_send()

    lrq[...] += lrv[mine, :]
    for j in range(1, nu):
        terms(0, j, span).wait_recv()
        lrq[...] += lrin[0, j]

    @pl.when(has_next)
    def _():
        for j in range(nu):
            terms(1, j, 0).wait_recv()
            lrq[...] += lrin[1, j]

    low_out[...] = lrq[...].astype(BF16)
    for j in range(1, nu):
        terms(0, j, span).wait_send()

    @pl.when(has_prev)
    def _():
        for j in range(nu):
            terms(1, j, 0).wait_send()


def attention(nb, nu, *operands):
    rows, width = operands[0].shape
    rank = operands[6].shape[0]
    span = nu * rows
    chunks = width // CHUNK
    dma = pltpu.SemaphoreType.DMA
    anywhere = pl.BlockSpec(memory_space=pl.ANY)
    here = pl.BlockSpec(memory_space=pltpu.VMEM)
    return pl.pallas_call(
        functools.partial(attention_kernel, nb, nu),
        out_shape=(
            jax.ShapeDtypeStruct((rows, width), BF16),
            jax.ShapeDtypeStruct((width // HEAD * 2 * rank, HEAD), BF16),
            jax.ShapeDtypeStruct((rows, 2 * rank), BF16),
        ),
        in_specs=[anywhere] * 9,
        out_specs=(here, here, here),
        scratch_shapes=[
            pltpu.VMEM((2 * span, width), BF16),
            pltpu.VMEM((2 * span, width), BF16),
            pltpu.VMEM((2 * span, 2 * rank), BF16),
            pltpu.VMEM((rows, width), BF16),
            pltpu.VMEM((rows, width), BF16),
            pltpu.VMEM((rows, width), BF16),
            pltpu.VMEM((2 * rank, width), BF16),
            pltpu.VMEM((2 * rank, width), BF16),
            pltpu.VMEM((rows, 2 * rank), F32),
            pltpu.VMEM((2 * span, 2 * rank), F32),
            pltpu.VMEM((2, nu, rows, 2 * rank), F32),
            dma((9,)),
            dma((2, nu, chunks)), dma((2, nu, chunks)),
            dma((2, nu, chunks)), dma((2, nu, chunks)),
            dma((nu,)), dma((nu,)), dma((nu,)), dma((nu,)),
            dma((2, nu)), dma((2, nu)),
        ],
        compiler_params=pltpu.CompilerParams(
            collective_id=0, has_side_effects=True, vmem_limit_bytes=65_000_000
        ),
    )(*operands)


def reduction_kernel(
    nb, nu,
    tokens, lowrank, gup,
    downq_out, downv_out, upq_out, upv_out,
    tok, terms, pair, part, plane_in, line, line_in, down, ups, flat,
    local_sem, psend, precv, asend, arecv, bsend, brecv, csend, crecv, dsend, drecv, esend, erecv,
):
    blk = lax.axis_index("blk")
    u = lax.axis_index("uly")
    core = lax.rem(blk, 2)
    chip = blk // 2
    other = chip * 2 + 1 - core
    half = nb // 2
    inners = plane_in.shape[1] // nu
    outers = half // inners
    y = lax.rem(chip, inners)
    z = chip // inners
    group = nu * inners
    rows, width = tokens.shape
    rank = upq_out.shape[0]
    region = pair.shape[2]
    sub = plane_in.shape[2]
    piece = line_in.shape[2]

    def split(o, sign):
        pu = lax.rem(u + sign * (o // inners) + nu, nu)
        py = lax.rem(y + sign * lax.rem(o, inners) + inners, inners)
        return pu, py

    def plane_dev(o):
        pu, py = split(o, 1)
        return ((z * inners + py) * 2 + core, pu)

    def peer_z(o):
        return lax.rem(z + o, outers)

    def from_z(o):
        return lax.rem(z - o + outers, outers)

    def line_dev(o):
        return ((peer_z(o) * inners + y) * 2 + core, u)

    def subs(p):
        return pl.ds(pl.multiple_of(p * sub, sub), sub)

    barrier = pltpu.get_barrier_semaphore()
    pl.semaphore_signal(barrier, inc=1, device_id=(other, u), device_id_type=MESH)
    for o in range(1, group):
        pl.semaphore_signal(barrier, inc=1, device_id=plane_dev(o), device_id_type=MESH)
    for o in range(1, outers):
        pl.semaphore_signal(barrier, inc=1, device_id=line_dev(o), device_id_type=MESH)

    load = pltpu.make_async_copy(tokens, tok, local_sem.at[0])
    load.start()
    pl.semaphore_wait(barrier, group + outers - 1)

    def remote(src, dst, send, recv, device):
        return pltpu.make_async_remote_copy(
            src_ref=src, dst_ref=dst, send_sem=send, recv_sem=recv,
            device_id=device, device_id_type=MESH,
        )

    def swap(t, v):
        rows_at = pl.ds(pl.multiple_of((v * 2 + 1 - core) * region, region), region)
        return remote(
            (terms if t == 0 else gup).at[rows_at], pair.at[t, v],
            psend.at[t, v], precv.at[t, v], (other, u),
        )

    def scatter(t, o):
        pu, py = split(o, 1)
        return remote(
            part.at[t, pu, subs(py)], plane_in.at[t, o],
            asend.at[t, o], arecv.at[t, o], plane_dev(o),
        )

    def pass_on(t, o):
        at = pl.ds(pl.multiple_of(peer_z(o) * piece, piece), piece)
        return remote(
            line.at[t, at], line_in.at[t, o], bsend.at[t, o], brecv.at[t, o], line_dev(o)
        )

    def whole(t, v, k, p):
        return down.at[v, k, subs(p)] if t == 0 else ups.at[k, subs(p)]

    def piece_at(p, q):
        return pl.ds(pl.multiple_of(p * sub + q * piece, piece), piece)

    def small(t, q):
        return down.at[u, core, piece_at(y, q)] if t == 0 else ups.at[core, piece_at(y, q)]

    def along(t, o):
        return remote(small(t, z), small(t, z), csend.at[t, o], crecv.at[t, o], line_dev(o))

    def came(t, o):
        here = small(t, from_z(o))
        return remote(here, here, csend.at[t, o], crecv.at[t, o], line_dev(o))

    def spread(t, o):
        here = whole(t, u, core, y)
        return remote(here, here, dsend.at[t, o], drecv.at[t, o], plane_dev(o))

    def landed(t, o):
        pu, py = split(o, -1)
        here = whole(t, pu, core, py)
        return remote(here, here, dsend.at[t, o], drecv.at[t, o], (other, u))

    def share(t, o):
        pu, py = split(o, -1)
        here = whole(t, pu, core, py)
        return remote(here, here, esend.at[t, o], erecv.at[t, o], (other, u))

    def shared(t, o):
        pu, py = split(o, -1)
        here = whole(t, pu, 1 - core, py)
        return remote(here, here, esend.at[t, o], erecv.at[t, o], (other, u))

    if part.shape[2] > region:
        part[...] = jnp.zeros_like(part)
    for v in range(nu):
        swap(1, v).start()

    load.wait()
    lows = lowrank[...]

    @pl.loop(0, width // HEAD)
    def _(h):
        cols = pl.ds(pl.multiple_of(h * HEAD, HEAD), HEAD)
        here = pl.ds(pl.multiple_of(h * 2 * rank, 2 * rank), 2 * rank)
        terms[here, :] = inner(lows, tok[:, cols]).astype(BF16)

    for v in range(nu):
        swap(0, v).start()

    for t in (1, 0):
        for v in range(nu):
            rows_at = pl.ds(pl.multiple_of((v * 2 + core) * region, region), region)
            own = (terms if t == 0 else gup)[rows_at, :]
            swap(t, v).wait_recv()
            part[t, v, pl.ds(0, region), :] = (
                own.astype(F32) + pair[t, v].astype(F32)
            ).astype(BF16)
        for o in range(1, group):
            scatter(t, o).start()

    for t in (1, 0):
        total = part[t, u, subs(y), :].astype(F32)
        for o in range(1, group):
            scatter(t, o).wait_recv()
            total = total + plane_in[t, o].astype(F32)
        line[t, :, :] = total.astype(BF16)
        for o in range(1, outers):
            pass_on(t, o).start()

    for t in (1, 0):
        total = line[t, pl.ds(pl.multiple_of(z * piece, piece), piece), :].astype(F32)
        for o in range(1, outers):
            pass_on(t, o).wait_recv()
            total = total + line_in[t, o].astype(F32)
        small(t, z)[...] = total.astype(BF16)
        for o in range(1, outers):
            along(t, o).start()

    counts = (group, inners)
    for t in (1, 0):
        for o in range(1, outers):
            came(t, o).wait_recv()
        for o in range(1, counts[t]):
            spread(t, o).start()
        share(t, 0).start()

    for t in (1, 0):
        for o in range(1, counts[t]):
            landed(t, o).wait_recv()
            share(t, o).start()

    for t in (1, 0):
        for o in range(counts[t]):
            shared(t, o).wait_recv()
        places = [(v, k) for v in range(nu if t == 0 else 1) for k in range(2)]
        for n, (v, k) in enumerate(places):
            flat[pl.ds(n * region, region), :] = (
                down[v, k, pl.ds(0, region), :] if t == 0 else ups[k, pl.ds(0, region), :]
            )
        outs = (downq_out, downv_out) if t == 0 else (upq_out, upv_out)
        for h in range(len(places) * region // (2 * rank)):
            cols = pl.ds(h * HEAD, HEAD)
            outs[0][:, cols] = flat[pl.ds(h * 2 * rank, rank), :]
            outs[1][:, cols] = flat[pl.ds(h * 2 * rank + rank, rank), :]

    for t in (1, 0):
        for v in range(nu):
            swap(t, v).wait_send()
        for o in range(1, group):
            scatter(t, o).wait_send()
        for o in range(1, outers):
            pass_on(t, o).wait_send()
            along(t, o).wait_send()
        for o in range(1, counts[t]):
            spread(t, o).wait_send()
        for o in range(counts[t]):
            share(t, o).wait_send()


def reduction(nb, nu, tokens, lowrank, gup):
    rows, width = tokens.shape
    rank = lowrank.shape[1] // 2
    half = nb // 2
    inners = 2 if half % 2 == 0 else 1
    outers = half // inners
    group = nu * inners
    region = width // (2 * nu)
    piece = -(-region // (16 * half)) * 16
    sub = outers * piece
    held = half * piece
    dma = pltpu.SemaphoreType.DMA
    here = pl.BlockSpec(memory_space=pltpu.VMEM)
    lanes = lowrank.shape[1]
    return pl.pallas_call(
        functools.partial(reduction_kernel, nb, nu),
        out_shape=(
            jax.ShapeDtypeStruct((rank, width), BF16),
            jax.ShapeDtypeStruct((rank, width), BF16),
            jax.ShapeDtypeStruct((rank, width // nu), BF16),
            jax.ShapeDtypeStruct((rank, width // nu), BF16),
        ),
        in_specs=[pl.BlockSpec(memory_space=pl.ANY), here, here],
        out_specs=(here, here, here, here),
        scratch_shapes=[
            pltpu.VMEM((rows, width), BF16),
            pltpu.VMEM((width, lanes), BF16),
            pltpu.VMEM((2, nu, region, lanes), BF16),
            pltpu.VMEM((2, nu, held, lanes), BF16),
            pltpu.VMEM((2, group, sub, lanes), BF16),
            pltpu.VMEM((2, sub, lanes), BF16),
            pltpu.VMEM((2, outers, piece, lanes), BF16),
            pltpu.VMEM((nu, 2, held, lanes), BF16),
            pltpu.VMEM((2, held, lanes), BF16),
            pltpu.VMEM((2 * nu * region, lanes), BF16),
            dma((1,)),
            dma((2, nu)), dma((2, nu)),
            dma((2, group)), dma((2, group)),
            dma((2, outers)), dma((2, outers)),
            dma((2, outers)), dma((2, outers)),
            dma((2, group)), dma((2, group)),
            dma((2, group)), dma((2, group)),
        ],
        compiler_params=pltpu.CompilerParams(collective_id=1, has_side_effects=True),
    )(tokens, lowrank, gup)


def fused_kernel(
    nb, nu,
    tokens, query_base, key_base, value_base, out_grad, down_q, up_q, down_v, up_v,
    att_ref, downq_out, downv_out, upq_out, upv_out,
    kv, lbuf, tok, qs, gs, downs, ups, lrq, lrv, lrs, lrin,
    tok2, lowb, acc, pair, part, plane_in, line, line_in, res,
    local_sem, xsend, xrecv, fsend, frecv, lsend, lrecv, msend, mrecv, rsend, rrecv,
    psend, precv, asend, arecv, bsend, brecv, csend, crecv, dsend, drecv, esend, erecv, gsend, grecv,
):
    kbuf, vbuf = kv.at[0], kv.at[1]
    blk = lax.axis_index("blk")
    u = lax.axis_index("uly")
    rows, width = tokens.shape
    rank = up_q.shape[0]
    span = nu * rows
    chunks = width // CHUNK
    has_prev = blk > 0
    has_next = blk < nb - 1
    mine = pl.ds(pl.multiple_of(span + u * rows, rows), rows)

    def peer(j):
        return lax.rem(u + j, nu)

    def source(j):
        return lax.rem(u - j + nu, nu)

    cells = 2 * nu
    parts = chunks // cells
    core = lax.rem(blk, 2)
    chip = blk // 2
    other = chip * 2 + 1 - core
    inners, outers = grid_of(nb)
    group = nu * inners
    y = lax.rem(chip, inners)
    z = chip // inners
    sub = CHUNK // inners
    piece = sub // outers

    def place(c):
        return lax.rem(c, cells) * parts + c // cells

    def cols(c):
        return pl.ds(pl.multiple_of(place(c) * CHUNK, CHUNK), CHUNK)

    def remote(src, dst, send, recv, device):
        return pltpu.make_async_remote_copy(
            src_ref=src, dst_ref=dst, send_sem=send, recv_sem=recv,
            device_id=device, device_id_type=MESH,
        )

    def split(o, sign):
        pu = lax.rem(u + sign * (o // inners) + nu, nu)
        py = lax.rem(y + sign * lax.rem(o, inners) + inners, inners)
        return pu, py

    def plane_dev(o):
        pu, py = split(o, 1)
        return ((z * inners + py) * 2 + core, pu)

    def peer_z(o):
        return lax.rem(z + o, outers)

    def from_z(o):
        return lax.rem(z - o + outers, outers)

    def line_dev(o):
        return ((peer_z(o) * inners + y) * 2 + core, u)

    def subs(p):
        return pl.ds(pl.multiple_of(p * sub, sub), sub)

    def piece_at(p, q):
        return pl.ds(pl.multiple_of(p * sub + q * piece, piece), piece)

    def swap(n):
        return remote(
            acc.at[n, 1 - core], pair.at[n], psend.at[0], precv.at[n], (other, u)
        )

    def scatter(n, o):
        pu, py = split(o, 1)
        return remote(
            part.at[n, pu, subs(py)], plane_in.at[n, o - 1],
            asend.at[0], arecv.at[n], plane_dev(o),
        )

    def pass_on(n, o):
        at = pl.ds(pl.multiple_of(peer_z(o) * piece, piece), piece)
        return remote(
            line.at[n, at], line_in.at[n, o - 1], bsend.at[0], brecv.at[n], line_dev(o)
        )

    def along(n, o):
        here = res.at[n, core, u, piece_at(y, z)]
        return remote(here, here, csend.at[0], crecv.at[n], line_dev(o))

    def spread(n, o, t):
        here = res.at[n, core, u, subs(y)]
        return remote(here, here, dsend.at[t], drecv.at[n], plane_dev(o))

    def share(n, t):
        here = res.at[n, core] if t == 1 else res.at[n, core, u]
        return remote(here, here, esend.at[t], erecv.at[n], (other, u))

    def whole(src, send, recv):
        return remote(src, src, send, recv, (other, u))

    strip = parts * CHUNK

    def lend(v):
        at = pl.ds(pl.multiple_of((v * 2 + 1 - core) * strip, strip), strip)
        return remote(
            tokens.at[:, at], tok2.at[:, pl.ds(v * strip, strip)], gsend.at[0], grecv.at[0], (other, u)
        )

    def tell():
        return remote(lowb.at[0], lowb.at[1], gsend.at[1], grecv.at[1], (other, u))

    def pair_up(n):
        swap(n).wait_recv()
        part[n] = (acc[n, core].astype(F32) + pair[n].astype(F32)).astype(BF16)
        for o in range(1, group):
            scatter(n, o).start()

    def plane_sum(n):
        total = part[n, u, subs(y), :].astype(F32)
        whole(plane_in.at[n], asend.at[0], arecv.at[n]).wait_recv()
        for o in range(1, group):
            total = total + plane_in[n, o - 1].astype(F32)
        line[n] = total.astype(BF16)
        for o in range(1, outers):
            pass_on(n, o).start()

    def line_sum(n):
        total = line[n, pl.ds(pl.multiple_of(z * piece, piece), piece), :].astype(F32)
        whole(line_in.at[n], bsend.at[0], brecv.at[n]).wait_recv()
        for o in range(1, outers):
            total = total + line_in[n, o - 1].astype(F32)
        res[n, core, u, piece_at(y, z), :] = total.astype(BF16)
        for o in range(1, outers):
            along(n, o).start()

    def widen(n, t):
        whole(line_in.at[n], csend.at[0], crecv.at[n]).wait_recv()
        for o in range(1, (inners, group)[t]):
            spread(n, o, t).start()

    def hand_over(n, t):
        whole(plane_in.at[n, pl.ds(0, (inners, group)[t] - 1)], dsend.at[t], drecv.at[n]).wait_recv()
        share(n, t).start()

    def each(first, stop, work):
        @pl.loop(first, stop)
        def _(n):
            work(n)

    barrier = pltpu.get_barrier_semaphore()
    for j in range(1, nu):
        pl.semaphore_signal(barrier, inc=1, device_id=(blk, peer(j)), device_id_type=MESH)

    @pl.when(has_prev)
    def _():
        for j in range(nu):
            pl.semaphore_signal(barrier, inc=1, device_id=(blk - 1, peer(j)), device_id_type=MESH)

    @pl.when(has_next)
    def _():
        for j in range(nu):
            pl.semaphore_signal(barrier, inc=1, device_id=(blk + 1, peer(j)), device_id_type=MESH)

    for o in range(1, group):
        pl.semaphore_signal(barrier, inc=1, device_id=plane_dev(o), device_id_type=MESH)
    for o in range(1, outers):
        pl.semaphore_signal(barrier, inc=1, device_id=line_dev(o), device_id_type=MESH)

    local = [
        pltpu.make_async_copy(src, dst, local_sem.at[i])
        for i, (src, dst) in enumerate(
            (
                (tokens, tok), (down_q, downs.at[pl.ds(0, rank)]), (down_v, downs.at[pl.ds(rank, rank)]),
                (up_q, ups.at[pl.ds(0, rank)]), (up_v, ups.at[pl.ds(rank, rank)]),
                (value_base, vbuf.at[mine]), (key_base, kbuf.at[mine]),
                (query_base, qs), (out_grad, gs),
            )
        )
    ]
    for copy in local:
        copy.start()

    edge = jnp.logical_or(blk == 0, blk == nb - 1)

    @pl.when(edge)
    def _():
        pl.semaphore_wait(barrier, 2 * nu - 1 + group + outers - 2)

    @pl.when(jnp.logical_not(edge))
    def _():
        pl.semaphore_wait(barrier, 3 * nu - 1 + group + outers - 2)

    def rows_of(first, j):
        return pl.ds(pl.multiple_of(first + source(j) * rows, rows), rows)

    def cross(j, c, what):
        at = cols(c)
        src, dst = {
            0: (key_base.at[:, at], kv.at[0, mine, at]),
            1: (kv.at[1, mine, at], kv.at[1, mine, at]),
            2: (kv.at[:, mine, at], kv.at[:, mine, at]),
        }[what]
        return remote(src, dst, xsend.at[j], xrecv.at[j, c], (blk, peer(j)))

    def crossed(j, c):
        here = kv.at[:, rows_of(span, j), cols(c)]
        return remote(here, here, xsend.at[j], xrecv.at[j, c], (blk, peer(j)))

    def onward(j, c, what):
        at = cols(c)
        old, new = rows_of(span, j), rows_of(0, j)
        src, dst = {
            0: (key_base.at[:, at], kv.at[0, new, at]),
            1: (kv.at[1, old, at], kv.at[1, new, at]),
            2: (kv.at[:, old, at], kv.at[:, new, at]),
        }[what]
        return remote(src, dst, fsend.at[j], frecv.at[c], (blk + 1, u))

    def arrived(c):
        here = kv.at[:, pl.ds(0, span), cols(c)]
        return remote(here, here, fsend.at[0], frecv.at[c], (blk, peer(1)))

    def low_across(j):
        return pltpu.make_async_remote_copy(
            src_ref=lbuf.at[mine], dst_ref=lbuf.at[mine],
            send_sem=lsend.at[j], recv_sem=lrecv.at[j],
            device_id=(blk, peer(j)), device_id_type=MESH,
        )

    def low_crossed(j):
        here = lbuf.at[pl.ds(pl.multiple_of(span + source(j) * rows, rows), rows)]
        return pltpu.make_async_remote_copy(
            src_ref=here, dst_ref=here, send_sem=lsend.at[j], recv_sem=lrecv.at[j],
            device_id=(blk, peer(j)), device_id_type=MESH,
        )

    def low_onward(j):
        s = source(j)
        return pltpu.make_async_remote_copy(
            src_ref=lbuf.at[pl.ds(pl.multiple_of(span + s * rows, rows), rows)],
            dst_ref=lbuf.at[pl.ds(pl.multiple_of(s * rows, rows), rows)],
            send_sem=msend.at[j], recv_sem=mrecv.at[j],
            device_id=(blk + 1, u), device_id_type=MESH,
        )

    def low_arrived(j):
        here = lbuf.at[pl.ds(pl.multiple_of(source(j) * rows, rows), rows)]
        return pltpu.make_async_remote_copy(
            src_ref=here, dst_ref=here, send_sem=msend.at[j], recv_sem=mrecv.at[j],
            device_id=(blk, peer(1)), device_id_type=MESH,
        )

    early = min(2, chunks)
    ahead = min(4, chunks)
    for c in range(early):
        for j in range(1, nu):
            cross(j, c, 0).start()

    @pl.when(has_next)
    def _():
        for c in range(ahead):
            onward(0, c, 0).start()

    for v in range(nu):
        lend(v).start()

    lane = lax.broadcasted_iota(jnp.int32, (rows, 2 * rank), 1)
    for i in range(3):
        local[i].wait()
    low = outer(tok[...], downs[...])
    low_qm = jnp.where(lane < rank, low, 0.0).astype(BF16)
    low_vm = jnp.where(lane >= rank, low, 0.0).astype(BF16)
    lbuf[mine, :] = low_vm
    for i in range(3, 7):
        local[i].wait()

    def lift(c):
        extra = dot(low_vm, ups[:, cols(c)])
        vbuf[mine, cols(c)] = (vbuf[mine, cols(c)].astype(F32) + extra).astype(BF16)

    for j in range(1, nu):
        low_across(j).start()

    @pl.when(has_next)
    def _():
        low_onward(0).start()

    @pl.loop(0, early)
    def _(c):
        lift(c)
        for j in range(1, nu):
            cross(j, c, 1).start()

    @pl.loop(early, ahead)
    def _(c):
        lift(c)
        for j in range(1, nu):
            cross(j, c, 2).start()

    @pl.when(has_next)
    def _():
        @pl.loop(0, ahead)
        def _(c):
            onward(0, c, 1).start()

    @pl.loop(ahead, chunks)
    def _(c):
        lift(c)
        for j in range(1, nu):
            cross(j, c, 2).start()

    lrq[...] = jnp.zeros_like(lrq)
    lrv[...] = jnp.zeros_like(lrv)

    @pl.when(jnp.logical_not(has_prev))
    def _():
        kbuf[pl.ds(0, span), :] = jnp.zeros((span, width), BF16)
        vbuf[pl.ds(0, span), :] = jnp.zeros((span, width), BF16)
        lbuf[pl.ds(0, span), :] = jnp.zeros((span, 2 * rank), BF16)

    for i in range(7, 9):
        local[i].wait()

    scale = HEAD ** (-0.5)
    key_at = lax.broadcasted_iota(jnp.int32, (rows, 2 * span), 1)
    usable = jnp.logical_or(key_at >= span, has_prev)

    def head(h):
        at = pl.ds(pl.multiple_of(h * HEAD, HEAD), HEAD)
        up = ups[:, at]
        keys = kbuf[:, at]
        values = vbuf[:, at]
        grad = gs[:, at]
        query = (qs[:, at].astype(F32) + dot(low_qm, up)).astype(BF16)
        scores = jnp.where(usable, outer(query, keys) * scale, -jnp.inf)
        weights = jnp.exp(scores - jnp.max(scores, axis=1, keepdims=True))
        total = jnp.sum(weights, axis=1, keepdims=True)
        probs = (weights * (1.0 / total)).astype(BF16)
        attended = dot(probs, values).astype(BF16)
        delta = jnp.sum(grad.astype(F32) * attended.astype(F32), axis=1, keepdims=True)
        score_grad = (probs.astype(F32) * (outer(grad, values) - delta)).astype(BF16)
        query_grad = (dot(score_grad, keys) * scale).astype(BF16)
        seen = dot(probs, lbuf[...]).astype(BF16)
        gup = (inner(low_qm, query_grad) + inner(seen, grad)).astype(BF16)
        lifted = jnp.where(lane >= rank, outer(grad, up), 0.0).astype(BF16)
        return attended, gup, outer(query_grad, up), inner(probs, lifted)

    together = 2 if span <= 2 * HEAD else 1

    def head_group(c, offset):
        first = place(c) * heads + offset
        results = [head(first + i) for i in range(together)]
        for i, (attended, gup, _, _) in enumerate(results):
            h = first + i
            att_ref[:, pl.ds(pl.multiple_of(h * HEAD, HEAD), HEAD)] = attended
            row = pl.multiple_of((offset + i) * 2 * rank, 2 * rank)
            cell = lax.rem(c, cells)
            acc[c // cells, lax.rem(cell, 2), cell // 2, pl.ds(row, 2 * rank), :] = gup
        lrq[...] += jnp.where(lane < rank, sum(r[2] for r in results), 0.0)
        lrv[...] += sum(r[3] for r in results)

    heads = CHUNK // HEAD
    soon = max(parts - 1, 0)

    @pl.loop(0, chunks + 1)
    def _(c):
        @pl.when(c < chunks)
        def _():
            for j in range(1, nu):
                crossed(j, c).wait_recv()

                @pl.when(has_next)
                def _():
                    onward(j, c, 2).start()

            @pl.when(jnp.logical_and(has_next, c + ahead < chunks))
            def _():
                onward(0, c + ahead, 2).start()

        @pl.when(c == 1)
        def _():
            for j in range(1, nu):
                low_crossed(j).wait_recv()

                @pl.when(has_next)
                def _():
                    low_onward(j).start()

            @pl.when(has_prev)
            def _():
                for j in range(nu):
                    low_arrived(j).wait_recv()

        @pl.when(c == chunks - 1)
        def _():
            each(0, soon, pair_up)

        @pl.when(c > 0)
        def _():
            @pl.when(has_prev)
            def _():
                arrived(c - 1).wait_recv()

            @pl.loop(0, heads // together)
            def _(i):
                head_group(c - 1, i * together)


            @pl.when(lax.rem(c, cells) == 0)
            def _():
                swap(c // cells - 1).start()

    lrs[...] = lrv[...].astype(BF16)

    def terms(k, j, base):
        s = peer(j)
        return pltpu.make_async_remote_copy(
            src_ref=lrs.at[pl.ds(pl.multiple_of(base + s * rows, rows), rows)],
            dst_ref=lrin.at[k, j],
            send_sem=rsend.at[k, j], recv_sem=rrecv.at[k, j],
            device_id=(blk - k, s), device_id_type=MESH,
        )

    for j in range(1, nu):
        terms(0, j, span).start()

    @pl.when(has_prev)
    def _():
        for j in range(nu):
            terms(1, j, 0).start()

    each(soon, parts, pair_up)
    each(0, soon, plane_sum)

    lrq[...] += lrv[mine, :]
    for j in range(1, nu):
        terms(0, j, span).wait_recv()
        lrq[...] += lrin[0, j].astype(F32)

    @pl.when(has_next)
    def _():
        for j in range(nu):
            terms(1, j, 0).wait_recv()
            lrq[...] += lrin[1, j].astype(F32)

    lowb[0] = lrq[...].T.astype(BF16)
    tell().start()

    def project(p):
        for v in range(nu):
            at = pl.ds(pl.multiple_of((v * 2 + core) * strip + p * CHUNK, CHUNK), CHUNK)
            there = pl.ds(pl.multiple_of(v * strip + p * CHUNK, CHUNK), CHUNK)
            block = (dot(lowb[0], tok[:, at]) + dot(lowb[1], tok2[:, there])).astype(BF16)
            for i in range(heads):
                part[parts + p, v, pl.ds(i * 2 * rank, 2 * rank), :] = block[:, i * HEAD:(i + 1) * HEAD]
        for o in range(1, group):
            scatter(parts + p, o).start()

    def lay_out(n, t, outs):
        shared_here = res.at[n, 1 - core] if t == 1 else res.at[n, 1 - core, u]
        whole(shared_here, esend.at[t], erecv.at[n]).wait_recv()
        for v in range(nu if t == 1 else 1):
            for k in range(2):
                for i in range(heads):
                    h = ((v * 2 + k) * parts + n - t * parts) * heads + i
                    at = pl.ds(pl.multiple_of(h * HEAD, HEAD), HEAD)
                    w = v if t == 1 else u
                    outs[0][:, at] = res[n, k, w, pl.ds(i * 2 * rank, rank), :]
                    outs[1][:, at] = res[n, k, w, pl.ds(i * 2 * rank + rank, rank), :]

    whole(tok2, gsend.at[0], grecv.at[0]).wait_recv()
    tell().wait_recv()
    each(0, parts, project)

    def finish_up(n):
        lay_out(n, 0, (upq_out, upv_out))

    def finish_down(n):
        lay_out(n, 1, (downq_out, downv_out))

    order = []
    for p in range(parts):
        late = 3.0 if p >= soon else 0.0
        if p >= soon:
            order.append((-0.5, plane_sum, (p,)))
        order += [
            (late, line_sum, (p,)), (3.5 + late, widen, (p, 0)),
            (11.0 + 0.7 * p, hand_over, (p, 0)), (14.0 + 0.7 * p, finish_up, (p,)),
        ]
        n, at = parts + p, 1.4 * p
        order += [
            (2.6 + at, plane_sum, (n,)), (5.9 + at, line_sum, (n,)), (9.5 + at, widen, (n, 1)),
            (13.3 + at, hand_over, (n, 1)), (14.5 + at, finish_down, (n,)),
        ]
    for _, work, what in sorted(order, key=lambda item: item[0]):
        work(*what)

    whole(tok2, gsend.at[0], grecv.at[0]).wait_send()
    tell().wait_send()
    whole(pair, psend.at[0], precv.at[0]).wait_send()
    whole(plane_in, asend.at[0], arecv.at[0]).wait_send()
    whole(line_in, bsend.at[0], brecv.at[0]).wait_send()
    whole(line_in, csend.at[0], crecv.at[0]).wait_send()
    for i in range(2):
        some = pl.ds(i * parts, parts)
        whole(
            plane_in.at[some, pl.ds(0, (inners, group)[i] - 1)], dsend.at[i], drecv.at[0]
        ).wait_send()
    whole(res.at[pl.ds(0, parts), 0, 0], esend.at[0], erecv.at[0]).wait_send()
    whole(res.at[pl.ds(parts, parts), 0], esend.at[1], erecv.at[0]).wait_send()

    everything = kv.at[:, mine, :]
    for j in range(1, nu):
        remote(everything, everything, xsend.at[j], xrecv.at[j, 0], (blk, peer(j))).wait_send()

    @pl.when(has_next)
    def _():
        for j in range(nu):
            remote(everything, everything, fsend.at[j], frecv.at[0], (blk + 1, u)).wait_send()

    for j in range(1, nu):
        low_across(j).wait_send()

    @pl.when(has_next)
    def _():
        for j in range(nu):
            low_onward(j).wait_send()

    for j in range(1, nu):
        terms(0, j, span).wait_send()

    @pl.when(has_prev)
    def _():
        for j in range(nu):
            terms(1, j, 0).wait_send()


def grid_of(nb):
    half = nb // 2
    inners = 2 if half % 2 == 0 else 1
    return inners, half // inners


def fused(nb, nu, *operands):
    rows, width = operands[0].shape
    rank = operands[6].shape[0]
    span = nu * rows
    chunks = width // CHUNK
    cells = 2 * nu
    parts = chunks // cells
    inners, outers = grid_of(nb)
    group = nu * inners
    sub = CHUNK // inners
    lanes = 2 * rank
    dma = pltpu.SemaphoreType.DMA
    anywhere = pl.BlockSpec(memory_space=pl.ANY)
    here = pl.BlockSpec(memory_space=pltpu.VMEM)
    return pl.pallas_call(
        functools.partial(fused_kernel, nb, nu),
        out_shape=(
            pltpu.VMEM((rows, width), BF16),
            pltpu.VMEM((rank, width), BF16),
            pltpu.VMEM((rank, width), BF16),
            pltpu.VMEM((rank, width // nu), BF16),
            pltpu.VMEM((rank, width // nu), BF16),
        ),
        in_specs=[anywhere] * 9,
        out_specs=(here,) * 5,
        scratch_shapes=[
            pltpu.VMEM((2, 2 * span, width), BF16),
            pltpu.VMEM((2 * span, lanes), BF16),
            pltpu.VMEM((rows, width), BF16),
            pltpu.VMEM((rows, width), BF16),
            pltpu.VMEM((rows, width), BF16),
            pltpu.VMEM((lanes, width), BF16),
            pltpu.VMEM((lanes, width), BF16),
            pltpu.VMEM((rows, lanes), F32),
            pltpu.VMEM((2 * span, lanes), F32),
            pltpu.VMEM((2 * span, lanes), BF16),
            pltpu.VMEM((2, nu, rows, lanes), BF16),
            pltpu.VMEM((rows, width // 2), BF16),
            pltpu.VMEM((2, lanes, rows), BF16),
            pltpu.VMEM((parts, 2, nu, CHUNK, lanes), BF16),
            pltpu.VMEM((parts, nu, CHUNK, lanes), BF16),
            pltpu.VMEM((2 * parts, nu, CHUNK, lanes), BF16),
            pltpu.VMEM((2 * parts, group - 1, sub, lanes), BF16),
            pltpu.VMEM((2 * parts, sub, lanes), BF16),
            pltpu.VMEM((2 * parts, outers - 1, sub // outers, lanes), BF16),
            pltpu.VMEM((2 * parts, 2, nu, CHUNK, lanes), BF16),
            dma((9,)),
            dma((nu,)), dma((nu, chunks)),
            dma((nu,)), dma((chunks,)),
            dma((nu,)), dma((nu,)), dma((nu,)), dma((nu,)),
            dma((2, nu)), dma((2, nu)),
            dma((1,)), dma((parts,)),
            dma((1,)), dma((2 * parts,)),
            dma((1,)), dma((2 * parts,)),
            dma((1,)), dma((2 * parts,)),
            dma((2,)), dma((2 * parts,)),
            dma((2,)), dma((2 * parts,)),
            dma((2,)), dma((2,)),
        ],
        compiler_params=pltpu.CompilerParams(
            collective_id=2, has_side_effects=True, vmem_limit_bytes=60_000_000
        ),
    )(*operands)


def fits(nb, nu, rows, width, rank):
    inners, outers = grid_of(nb)
    return (
        2 * rank == HEAD
        and width % (2 * nu * CHUNK) == 0
        and CHUNK % (16 * inners * outers) == 0
        and nu * rows <= CHUNK
    )


def deliver_kernel(*refs):
    count = len(refs) // 2
    sources, targets, sem = refs[:count], refs[count:2 * count], refs[-1]
    copies = [pltpu.make_async_copy(a, b, sem.at[i]) for i, (a, b) in enumerate(zip(sources, targets))]
    for copy in copies:
        copy.start()
    for copy in copies:
        copy.wait()


def deliver(*arrays):
    return pl.pallas_call(
        deliver_kernel,
        out_shape=tuple(jax.ShapeDtypeStruct(a.shape, a.dtype) for a in arrays),
        in_specs=[pl.BlockSpec(memory_space=pl.ANY)] * len(arrays),
        out_specs=tuple(pl.BlockSpec(memory_space=pl.ANY) for _ in arrays),
        scratch_shapes=[pltpu.SemaphoreType.DMA((len(arrays),))],
    )(*(pltpu.with_memory_space_constraint(a, pltpu.VMEM) for a in arrays))


def per_device(nb, nu, tokens, query_base, key_base, value_base, out_grad, down_q, up_q, down_v, up_v):
    operands = (tokens, query_base, key_base, value_base, out_grad, down_q.T, up_q, down_v.T, up_v)
    if fits(nb, nu, *tokens.shape, up_q.shape[0]):
        attended, grad_down_q, grad_down_v, grad_up_q, grad_up_v = deliver(*fused(nb, nu, *operands))
        return attended, grad_down_q.T, grad_up_q, grad_down_v.T, grad_up_v
    attended, gup, lowrank = attention(nb, nu, *operands)
    grad_down_q, grad_down_v, grad_up_q, grad_up_v = reduction(nb, nu, tokens, lowrank, gup)
    return attended, grad_down_q.T, grad_up_q, grad_down_v.T, grad_up_v


def solution(mesh):
    split = P(("blk", "uly"), None)
    return jax.shard_map(
        functools.partial(per_device, mesh.shape["blk"], mesh.shape["uly"]),
        mesh=mesh,
        in_specs=(split,) * 5 + (P(),) * 4,
        out_specs=(split, P(), P(None, "uly"), P(), P(None, "uly")),
        check_vma=False,
    )
```

```python
import functools

import jax
import jax.numpy as jnp
from jax import lax
from jax.experimental import pallas as pl
from jax.experimental.pallas import tpu as pltpu
from jax.sharding import PartitionSpec as P

HEAD = 128
CHUNK = 256
MESH = pl.DeviceIdType.MESH
F32 = jnp.float32
BF16 = jnp.bfloat16


def inner(left, right):
    return lax.dot_general(left, right, (((0,), (0,)), ((), ())), preferred_element_type=F32)


def outer(left, right):
    return lax.dot_general(left, right, (((1,), (1,)), ((), ())), preferred_element_type=F32)


def dot(left, right):
    return jnp.dot(left, right, preferred_element_type=F32)


def attention_kernel(
    nb, nu,
    tokens, query_base, key_base, value_base, out_grad, down_q, up_q, down_v, up_v,
    att_ref, gup_ref, low_out,
    kbuf, vbuf, lbuf, tok, qs, gs, downs, ups, lrq, lrv, lrin,
    local_sem, xsend, xrecv, fsend, frecv, lsend, lrecv, msend, mrecv, rsend, rrecv,
):
    blk = lax.axis_index("blk")
    u = lax.axis_index("uly")
    rows, width = tokens.shape
    rank = up_q.shape[0]
    span = nu * rows
    chunks = width // CHUNK
    has_prev = blk > 0
    has_next = blk < nb - 1
    mine = pl.ds(pl.multiple_of(span + u * rows, rows), rows)

    def peer(j):
        return lax.rem(u + j, nu)

    def source(j):
        return lax.rem(u - j + nu, nu)

    def cols(c):
        return pl.ds(pl.multiple_of(c * CHUNK, CHUNK), CHUNK)

    barrier = pltpu.get_barrier_semaphore()
    for j in range(1, nu):
        pl.semaphore_signal(barrier, inc=1, device_id=(blk, peer(j)), device_id_type=MESH)

    @pl.when(has_prev)
    def _():
        for j in range(nu):
            pl.semaphore_signal(barrier, inc=1, device_id=(blk - 1, peer(j)), device_id_type=MESH)

    @pl.when(has_next)
    def _():
        for j in range(nu):
            pl.semaphore_signal(barrier, inc=1, device_id=(blk + 1, peer(j)), device_id_type=MESH)

    local = [
        pltpu.make_async_copy(src, dst, local_sem.at[i])
        for i, (src, dst) in enumerate(
            (
                (tokens, tok), (down_q, downs.at[pl.ds(0, rank)]), (down_v, downs.at[pl.ds(rank, rank)]),
                (up_q, ups.at[pl.ds(0, rank)]), (up_v, ups.at[pl.ds(rank, rank)]),
                (value_base, vbuf.at[mine]), (key_base, kbuf.at[mine]),
                (query_base, qs), (out_grad, gs),
            )
        )
    ]
    for copy in local:
        copy.start()

    edge = jnp.logical_or(blk == 0, blk == nb - 1)

    @pl.when(edge)
    def _():
        pl.semaphore_wait(barrier, 2 * nu - 1)

    @pl.when(jnp.logical_not(edge))
    def _():
        pl.semaphore_wait(barrier, 3 * nu - 1)

    bufs = (kbuf, vbuf)

    def across(a, j, c):
        src = key_base.at[:, cols(c)] if a == 0 else vbuf.at[mine, cols(c)]
        return pltpu.make_async_remote_copy(
            src_ref=src, dst_ref=bufs[a].at[mine, cols(c)],
            send_sem=xsend.at[a, j, c], recv_sem=xrecv.at[a, j, c],
            device_id=(blk, peer(j)), device_id_type=MESH,
        )

    def crossed(a, j, c):
        here = bufs[a].at[pl.ds(pl.multiple_of(span + source(j) * rows, rows), rows), cols(c)]
        return pltpu.make_async_remote_copy(
            src_ref=here, dst_ref=here,
            send_sem=xsend.at[a, j, c], recv_sem=xrecv.at[a, j, c],
            device_id=(blk, peer(j)), device_id_type=MESH,
        )

    def onward(a, j, c):
        s = source(j)
        if a == 0 and j == 0:
            src = key_base.at[:, cols(c)]
        else:
            src = bufs[a].at[pl.ds(pl.multiple_of(span + s * rows, rows), rows), cols(c)]
        return pltpu.make_async_remote_copy(
            src_ref=src, dst_ref=bufs[a].at[pl.ds(pl.multiple_of(s * rows, rows), rows), cols(c)],
            send_sem=fsend.at[a, j, c], recv_sem=frecv.at[a, j, c],
            device_id=(blk + 1, u), device_id_type=MESH,
        )

    def arrived(a, j, c):
        here = bufs[a].at[pl.ds(pl.multiple_of(source(j) * rows, rows), rows), cols(c)]
        return pltpu.make_async_remote_copy(
            src_ref=here, dst_ref=here,
            send_sem=fsend.at[a, j, c], recv_sem=frecv.at[a, j, c],
            device_id=(blk, peer(1)), device_id_type=MESH,
        )

    def low_across(j):
        return pltpu.make_async_remote_copy(
            src_ref=lbuf.at[mine], dst_ref=lbuf.at[mine],
            send_sem=lsend.at[j], recv_sem=lrecv.at[j],
            device_id=(blk, peer(j)), device_id_type=MESH,
        )

    def low_crossed(j):
        here = lbuf.at[pl.ds(pl.multiple_of(span + source(j) * rows, rows), rows)]
        return pltpu.make_async_remote_copy(
            src_ref=here, dst_ref=here, send_sem=lsend.at[j], recv_sem=lrecv.at[j],
            device_id=(blk, peer(j)), device_id_type=MESH,
        )

    def low_onward(j):
        s = source(j)
        return pltpu.make_async_remote_copy(
            src_ref=lbuf.at[pl.ds(pl.multiple_of(span + s * rows, rows), rows)],
            dst_ref=lbuf.at[pl.ds(pl.multiple_of(s * rows, rows), rows)],
            send_sem=msend.at[j], recv_sem=mrecv.at[j],
            device_id=(blk + 1, u), device_id_type=MESH,
        )

    def low_arrived(j):
        here = lbuf.at[pl.ds(pl.multiple_of(source(j) * rows, rows), rows)]
        return pltpu.make_async_remote_copy(
            src_ref=here, dst_ref=here, send_sem=msend.at[j], recv_sem=mrecv.at[j],
            device_id=(blk, peer(1)), device_id_type=MESH,
        )

    early = min(3 * 512 // CHUNK, chunks)
    ahead = min(2048 // CHUNK, chunks)
    for c in range(early):
        for j in range(1, nu):
            across(0, j, c).start()

    @pl.when(has_next)
    def _():
        for c in range(ahead):
            onward(0, 0, c).start()

    lane = lax.broadcasted_iota(jnp.int32, (rows, 2 * rank), 1)
    for i in range(3):
        local[i].wait()
    low = outer(tok[...], downs[...])
    low_qm = jnp.where(lane < rank, low, 0.0).astype(BF16)
    low_vm = jnp.where(lane >= rank, low, 0.0).astype(BF16)
    lbuf[mine, :] = low_vm
    for i in range(3, 6):
        local[i].wait()

    @pl.loop(0, chunks)
    def _(c):
        part = dot(low_vm, ups[:, cols(c)])
        vbuf[mine, cols(c)] = (vbuf[mine, cols(c)].astype(F32) + part).astype(BF16)

    for j in range(1, nu):
        low_across(j).start()

    @pl.when(has_next)
    def _():
        low_onward(0).start()

    @pl.loop(0, chunks)
    def _(c):
        @pl.when(c >= early)
        def _():
            for j in range(1, nu):
                across(0, j, c).start()

        for j in range(1, nu):
            across(1, j, c).start()

    @pl.when(has_next)
    def _():
        for c in range(ahead):
            onward(1, 0, c).start()

    lrq[...] = jnp.zeros_like(lrq)
    lrv[...] = jnp.zeros_like(lrv)

    @pl.when(jnp.logical_not(has_prev))
    def _():
        kbuf[pl.ds(0, span), :] = jnp.zeros((span, width), BF16)
        vbuf[pl.ds(0, span), :] = jnp.zeros((span, width), BF16)
        lbuf[pl.ds(0, span), :] = jnp.zeros((span, 2 * rank), BF16)

    for i in range(6, 9):
        local[i].wait()

    scale = HEAD ** (-0.5)
    key_at = lax.broadcasted_iota(jnp.int32, (rows, 2 * span), 1)
    usable = jnp.logical_or(key_at >= span, has_prev)

    def head(h):
        at = pl.ds(pl.multiple_of(h * HEAD, HEAD), HEAD)
        up = ups[:, at]
        keys = kbuf[:, at]
        values = vbuf[:, at]
        grad = gs[:, at]
        query = (qs[:, at].astype(F32) + dot(low_qm, up)).astype(BF16)
        scores = jnp.where(usable, outer(query, keys) * scale, -jnp.inf)
        weights = jnp.exp(scores - jnp.max(scores, axis=1, keepdims=True))
        total = jnp.sum(weights, axis=1, keepdims=True)
        probs = (weights * (1.0 / total)).astype(BF16)
        attended = dot(probs, values).astype(BF16)
        delta = jnp.sum(grad.astype(F32) * attended.astype(F32), axis=1, keepdims=True)
        score_grad = (probs.astype(F32) * (outer(grad, values) - delta)).astype(BF16)
        query_grad = (dot(score_grad, keys) * scale).astype(BF16)
        seen = dot(probs, lbuf[...]).astype(BF16)
        gup = (inner(low_qm, query_grad) + inner(seen, grad)).astype(BF16)
        lifted = jnp.where(lane >= rank, outer(grad, up), 0.0).astype(BF16)
        return attended, gup, outer(query_grad, up), inner(probs, lifted)

    together = 2 if span <= 2 * HEAD else 1

    def head_group(first):
        results = [head(first + i) for i in range(together)]
        for i, (attended, gup, _, _) in enumerate(results):
            h = first + i
            att_ref[:, pl.ds(pl.multiple_of(h * HEAD, HEAD), HEAD)] = attended
            gup_ref[pl.ds(pl.multiple_of(h * 2 * rank, 2 * rank), 2 * rank), :] = gup
        lrq[...] += jnp.where(lane < rank, sum(r[2] for r in results), 0.0)
        lrv[...] += sum(r[3] for r in results)

    heads = CHUNK // HEAD

    @pl.loop(0, chunks + 1)
    def _(c):
        @pl.when(c == 0)
        def _():
            for j in range(1, nu):
                low_crossed(j).wait_recv()

                @pl.when(has_next)
                def _():
                    low_onward(j).start()

            @pl.when(has_prev)
            def _():
                for j in range(nu):
                    low_arrived(j).wait_recv()

        @pl.when(c < chunks)
        def _():
            for a in range(2):
                for j in range(1, nu):
                    crossed(a, j, c).wait_recv()

                    @pl.when(has_next)
                    def _():
                        onward(a, j, c).start()

            @pl.when(jnp.logical_and(has_next, c + ahead < chunks))
            def _():
                for a in range(2):
                    onward(a, 0, c + ahead).start()

        @pl.when(c > 0)
        def _():
            @pl.when(has_prev)
            def _():
                for a in range(2):
                    for j in range(nu):
                        arrived(a, j, c - 1).wait_recv()

            @pl.loop(0, heads // together)
            def _(i):
                head_group((c - 1) * heads + i * together)

    def terms(k, j, base):
        s = peer(j)
        return pltpu.make_async_remote_copy(
            src_ref=lrv.at[pl.ds(pl.multiple_of(base + s * rows, rows), rows)],
            dst_ref=lrin.at[k, j],
            send_sem=rsend.at[k, j], recv_sem=rrecv.at[k, j],
            device_id=(blk - k, s), device_id_type=MESH,
        )

    for j in range(1, nu):
        terms(0, j, span).start()

    @pl.when(has_prev)
    def _():
        for j in range(nu):
            terms(1, j, 0).start()

    @pl.loop(0, chunks)
    def _(c):
        for a in range(2):
            for j in range(1, nu):
                across(a, j, c).wait_send()

            @pl.when(has_next)
            def _():
                for j in range(nu):
                    onward(a, j, c).wait_send()

    for j in range(1, nu):
        low_across(j).wait_send()

    @pl.when(has_next)
    def _():
        for j in range(nu):
            low_onward(j).wait_send()

    lrq[...] += lrv[mine, :]
    for j in range(1, nu):
        terms(0, j, span).wait_recv()
        lrq[...] += lrin[0, j]

    @pl.when(has_next)
    def _():
        for j in range(nu):
            terms(1, j, 0).wait_recv()
            lrq[...] += lrin[1, j]

    low_out[...] = lrq[...].astype(BF16)
    for j in range(1, nu):
        terms(0, j, span).wait_send()

    @pl.when(has_prev)
    def _():
        for j in range(nu):
            terms(1, j, 0).wait_send()


def attention(nb, nu, *operands):
    rows, width = operands[0].shape
    rank = operands[6].shape[0]
    span = nu * rows
    chunks = width // CHUNK
    dma = pltpu.SemaphoreType.DMA
    anywhere = pl.BlockSpec(memory_space=pl.ANY)
    here = pl.BlockSpec(memory_space=pltpu.VMEM)
    return pl.pallas_call(
        functools.partial(attention_kernel, nb, nu),
        out_shape=(
            jax.ShapeDtypeStruct((rows, width), BF16),
            jax.ShapeDtypeStruct((width // HEAD * 2 * rank, HEAD), BF16),
            jax.ShapeDtypeStruct((rows, 2 * rank), BF16),
        ),
        in_specs=[anywhere] * 9,
        out_specs=(here, here, here),
        scratch_shapes=[
            pltpu.VMEM((2 * span, width), BF16),
            pltpu.VMEM((2 * span, width), BF16),
            pltpu.VMEM((2 * span, 2 * rank), BF16),
            pltpu.VMEM((rows, width), BF16),
            pltpu.VMEM((rows, width), BF16),
            pltpu.VMEM((rows, width), BF16),
            pltpu.VMEM((2 * rank, width), BF16),
            pltpu.VMEM((2 * rank, width), BF16),
            pltpu.VMEM((rows, 2 * rank), F32),
            pltpu.VMEM((2 * span, 2 * rank), F32),
            pltpu.VMEM((2, nu, rows, 2 * rank), F32),
            dma((9,)),
            dma((2, nu, chunks)), dma((2, nu, chunks)),
            dma((2, nu, chunks)), dma((2, nu, chunks)),
            dma((nu,)), dma((nu,)), dma((nu,)), dma((nu,)),
            dma((2, nu)), dma((2, nu)),
        ],
        compiler_params=pltpu.CompilerParams(
            collective_id=0, has_side_effects=True, vmem_limit_bytes=65_000_000
        ),
    )(*operands)


def reduction_kernel(
    nb, nu,
    tokens, lowrank, gup,
    downq_out, downv_out, upq_out, upv_out,
    tok, terms, pair, part, plane_in, line, line_in, down, ups, flat,
    local_sem, psend, precv, asend, arecv, bsend, brecv, csend, crecv, dsend, drecv, esend, erecv,
):
    blk = lax.axis_index("blk")
    u = lax.axis_index("uly")
    core = lax.rem(blk, 2)
    chip = blk // 2
    other = chip * 2 + 1 - core
    half = nb // 2
    inners = plane_in.shape[1] // nu
    outers = half // inners
    y = lax.rem(chip, inners)
    z = chip // inners
    group = nu * inners
    rows, width = tokens.shape
    rank = upq_out.shape[0]
    region = pair.shape[2]
    sub = plane_in.shape[2]
    piece = line_in.shape[2]

    def split(o, sign):
        pu = lax.rem(u + sign * (o // inners) + nu, nu)
        py = lax.rem(y + sign * lax.rem(o, inners) + inners, inners)
        return pu, py

    def plane_dev(o):
        pu, py = split(o, 1)
        return ((z * inners + py) * 2 + core, pu)

    def peer_z(o):
        return lax.rem(z + o, outers)

    def from_z(o):
        return lax.rem(z - o + outers, outers)

    def line_dev(o):
        return ((peer_z(o) * inners + y) * 2 + core, u)

    def subs(p):
        return pl.ds(pl.multiple_of(p * sub, sub), sub)

    barrier = pltpu.get_barrier_semaphore()
    pl.semaphore_signal(barrier, inc=1, device_id=(other, u), device_id_type=MESH)
    for o in range(1, group):
        pl.semaphore_signal(barrier, inc=1, device_id=plane_dev(o), device_id_type=MESH)
    for o in range(1, outers):
        pl.semaphore_signal(barrier, inc=1, device_id=line_dev(o), device_id_type=MESH)

    load = pltpu.make_async_copy(tokens, tok, local_sem.at[0])
    load.start()
    pl.semaphore_wait(barrier, group + outers - 1)

    def remote(src, dst, send, recv, device):
        return pltpu.make_async_remote_copy(
            src_ref=src, dst_ref=dst, send_sem=send, recv_sem=recv,
            device_id=device, device_id_type=MESH,
        )

    def swap(t, v):
        rows_at = pl.ds(pl.multiple_of((v * 2 + 1 - core) * region, region), region)
        return remote(
            (terms if t == 0 else gup).at[rows_at], pair.at[t, v],
            psend.at[t, v], precv.at[t, v], (other, u),
        )

    def scatter(t, o):
        pu, py = split(o, 1)
        return remote(
            part.at[t, pu, subs(py)], plane_in.at[t, o],
            asend.at[t, o], arecv.at[t, o], plane_dev(o),
        )

    def pass_on(t, o):
        at = pl.ds(pl.multiple_of(peer_z(o) * piece, piece), piece)
        return remote(
            line.at[t, at], line_in.at[t, o], bsend.at[t, o], brecv.at[t, o], line_dev(o)
        )

    def whole(t, v, k, p):
        return down.at[v, k, subs(p)] if t == 0 else ups.at[k, subs(p)]

    def piece_at(p, q):
        return pl.ds(pl.multiple_of(p * sub + q * piece, piece), piece)

    def small(t, q):
        return down.at[u, core, piece_at(y, q)] if t == 0 else ups.at[core, piece_at(y, q)]

    def along(t, o):
        return remote(small(t, z), small(t, z), csend.at[t, o], crecv.at[t, o], line_dev(o))

    def came(t, o):
        here = small(t, from_z(o))
        return remote(here, here, csend.at[t, o], crecv.at[t, o], line_dev(o))

    def spread(t, o):
        here = whole(t, u, core, y)
        return remote(here, here, dsend.at[t, o], drecv.at[t, o], plane_dev(o))

    def landed(t, o):
        pu, py = split(o, -1)
        here = whole(t, pu, core, py)
        return remote(here, here, dsend.at[t, o], drecv.at[t, o], (other, u))

    def share(t, o):
        pu, py = split(o, -1)
        here = whole(t, pu, core, py)
        return remote(here, here, esend.at[t, o], erecv.at[t, o], (other, u))

    def shared(t, o):
        pu, py = split(o, -1)
        here = whole(t, pu, 1 - core, py)
        return remote(here, here, esend.at[t, o], erecv.at[t, o], (other, u))

    if part.shape[2] > region:
        part[...] = jnp.zeros_like(part)
    for v in range(nu):
        swap(1, v).start()

    load.wait()
    lows = lowrank[...]

    @pl.loop(0, width // HEAD)
    def _(h):
        cols = pl.ds(pl.multiple_of(h * HEAD, HEAD), HEAD)
        here = pl.ds(pl.multiple_of(h * 2 * rank, 2 * rank), 2 * rank)
        terms[here, :] = inner(lows, tok[:, cols]).astype(BF16)

    for v in range(nu):
        swap(0, v).start()

    for t in (1, 0):
        for v in range(nu):
            rows_at = pl.ds(pl.multiple_of((v * 2 + core) * region, region), region)
            own = (terms if t == 0 else gup)[rows_at, :]
            swap(t, v).wait_recv()
            part[t, v, pl.ds(0, region), :] = (
                own.astype(F32) + pair[t, v].astype(F32)
            ).astype(BF16)
        for o in range(1, group):
            scatter(t, o).start()

    for t in (1, 0):
        total = part[t, u, subs(y), :].astype(F32)
        for o in range(1, group):
            scatter(t, o).wait_recv()
            total = total + plane_in[t, o].astype(F32)
        line[t, :, :] = total.astype(BF16)
        for o in range(1, outers):
            pass_on(t, o).start()

    for t in (1, 0):
        total = line[t, pl.ds(pl.multiple_of(z * piece, piece), piece), :].astype(F32)
        for o in range(1, outers):
            pass_on(t, o).wait_recv()
            total = total + line_in[t, o].astype(F32)
        small(t, z)[...] = total.astype(BF16)
        for o in range(1, outers):
            along(t, o).start()

    counts = (group, inners)
    for t in (1, 0):
        for o in range(1, outers):
            came(t, o).wait_recv()
        for o in range(1, counts[t]):
            spread(t, o).start()
        share(t, 0).start()

    for t in (1, 0):
        for o in range(1, counts[t]):
            landed(t, o).wait_recv()
            share(t, o).start()

    for t in (1, 0):
        for o in range(counts[t]):
            shared(t, o).wait_recv()
        places = [(v, k) for v in range(nu if t == 0 else 1) for k in range(2)]
        for n, (v, k) in enumerate(places):
            flat[pl.ds(n * region, region), :] = (
                down[v, k, pl.ds(0, region), :] if t == 0 else ups[k, pl.ds(0, region), :]
            )
        outs = (downq_out, downv_out) if t == 0 else (upq_out, upv_out)
        for h in range(len(places) * region // (2 * rank)):
            cols = pl.ds(h * HEAD, HEAD)
            outs[0][:, cols] = flat[pl.ds(h * 2 * rank, rank), :]
            outs[1][:, cols] = flat[pl.ds(h * 2 * rank + rank, rank), :]

    for t in (1, 0):
        for v in range(nu):
            swap(t, v).wait_send()
        for o in range(1, group):
            scatter(t, o).wait_send()
        for o in range(1, outers):
            pass_on(t, o).wait_send()
            along(t, o).wait_send()
        for o in range(1, counts[t]):
            spread(t, o).wait_send()
        for o in range(counts[t]):
            share(t, o).wait_send()


def reduction(nb, nu, tokens, lowrank, gup):
    rows, width = tokens.shape
    rank = lowrank.shape[1] // 2
    half = nb // 2
    inners = 2 if half % 2 == 0 else 1
    outers = half // inners
    group = nu * inners
    region = width // (2 * nu)
    piece = -(-region // (16 * half)) * 16
    sub = outers * piece
    held = half * piece
    dma = pltpu.SemaphoreType.DMA
    here = pl.BlockSpec(memory_space=pltpu.VMEM)
    lanes = lowrank.shape[1]
    return pl.pallas_call(
        functools.partial(reduction_kernel, nb, nu),
        out_shape=(
            jax.ShapeDtypeStruct((rank, width), BF16),
            jax.ShapeDtypeStruct((rank, width), BF16),
            jax.ShapeDtypeStruct((rank, width // nu), BF16),
            jax.ShapeDtypeStruct((rank, width // nu), BF16),
        ),
        in_specs=[pl.BlockSpec(memory_space=pl.ANY), here, here],
        out_specs=(here, here, here, here),
        scratch_shapes=[
            pltpu.VMEM((rows, width), BF16),
            pltpu.VMEM((width, lanes), BF16),
            pltpu.VMEM((2, nu, region, lanes), BF16),
            pltpu.VMEM((2, nu, held, lanes), BF16),
            pltpu.VMEM((2, group, sub, lanes), BF16),
            pltpu.VMEM((2, sub, lanes), BF16),
            pltpu.VMEM((2, outers, piece, lanes), BF16),
            pltpu.VMEM((nu, 2, held, lanes), BF16),
            pltpu.VMEM((2, held, lanes), BF16),
            pltpu.VMEM((2 * nu * region, lanes), BF16),
            dma((1,)),
            dma((2, nu)), dma((2, nu)),
            dma((2, group)), dma((2, group)),
            dma((2, outers)), dma((2, outers)),
            dma((2, outers)), dma((2, outers)),
            dma((2, group)), dma((2, group)),
            dma((2, group)), dma((2, group)),
        ],
        compiler_params=pltpu.CompilerParams(collective_id=1, has_side_effects=True),
    )(tokens, lowrank, gup)


def fused_kernel(
    nb, nu,
    tokens, query_base, key_base, value_base, out_grad, down_q, up_q, down_v, up_v,
    att_ref, downq_out, downv_out, upq_out, upv_out,
    kv, lbuf, tok, qs, gs, downs, ups, lrq, lrv, lrs, lrin,
    tok2, lowb, acc, pair, part, plane_in, line, line_in, res,
    local_sem, xsend, xrecv, fsend, frecv, lsend, lrecv, msend, mrecv, rsend, rrecv,
    psend, precv, asend, arecv, bsend, brecv, csend, crecv, dsend, drecv, esend, erecv, gsend, grecv,
):
    kbuf, vbuf = kv.at[0], kv.at[1]
    blk = lax.axis_index("blk")
    u = lax.axis_index("uly")
    rows, width = tokens.shape
    rank = up_q.shape[0]
    span = nu * rows
    chunks = width // CHUNK
    has_prev = blk > 0
    has_next = blk < nb - 1
    mine = pl.ds(pl.multiple_of(span + u * rows, rows), rows)

    def peer(j):
        return lax.rem(u + j, nu)

    def source(j):
        return lax.rem(u - j + nu, nu)

    cells = 2 * nu
    parts = chunks // cells
    core = lax.rem(blk, 2)
    chip = blk // 2
    other = chip * 2 + 1 - core
    inners, outers = grid_of(nb)
    group = nu * inners
    y = lax.rem(chip, inners)
    z = chip // inners
    sub = CHUNK // inners
    piece = sub // outers

    def place(c):
        return lax.rem(c, cells) * parts + c // cells

    def cols(c):
        return pl.ds(pl.multiple_of(place(c) * CHUNK, CHUNK), CHUNK)

    def remote(src, dst, send, recv, device):
        return pltpu.make_async_remote_copy(
            src_ref=src, dst_ref=dst, send_sem=send, recv_sem=recv,
            device_id=device, device_id_type=MESH,
        )

    def split(o, sign):
        pu = lax.rem(u + sign * (o // inners) + nu, nu)
        py = lax.rem(y + sign * lax.rem(o, inners) + inners, inners)
        return pu, py

    def plane_dev(o):
        pu, py = split(o, 1)
        return ((z * inners + py) * 2 + core, pu)

    def peer_z(o):
        return lax.rem(z + o, outers)

    def from_z(o):
        return lax.rem(z - o + outers, outers)

    def line_dev(o):
        return ((peer_z(o) * inners + y) * 2 + core, u)

    def subs(p):
        return pl.ds(pl.multiple_of(p * sub, sub), sub)

    def piece_at(p, q):
        return pl.ds(pl.multiple_of(p * sub + q * piece, piece), piece)

    def swap(n):
        return remote(
            acc.at[n, 1 - core], pair.at[n], psend.at[0], precv.at[n], (other, u)
        )

    def scatter(n, o):
        pu, py = split(o, 1)
        return remote(
            part.at[n, pu, subs(py)], plane_in.at[n, o - 1],
            asend.at[0], arecv.at[n], plane_dev(o),
        )

    def pass_on(n, o):
        at = pl.ds(pl.multiple_of(peer_z(o) * piece, piece), piece)
        return remote(
            line.at[n, at], line_in.at[n, o - 1], bsend.at[0], brecv.at[n], line_dev(o)
        )

    def along(n, o):
        here = res.at[n, core, u, piece_at(y, z)]
        return remote(here, here, csend.at[0], crecv.at[n], line_dev(o))

    def spread(n, o, t):
        here = res.at[n, core, u, subs(y)]
        return remote(here, here, dsend.at[t], drecv.at[n], plane_dev(o))

    def share(n, t):
        here = res.at[n, core] if t == 1 else res.at[n, core, u]
        return remote(here, here, esend.at[t], erecv.at[n], (other, u))

    def whole(src, send, recv):
        return remote(src, src, send, recv, (other, u))

    strip = parts * CHUNK

    def lend(v):
        at = pl.ds(pl.multiple_of((v * 2 + 1 - core) * strip, strip), strip)
        return remote(
            tokens.at[:, at], tok2.at[:, pl.ds(v * strip, strip)], gsend.at[0], grecv.at[0], (other, u)
        )

    def tell():
        return remote(lowb.at[0], lowb.at[1], gsend.at[1], grecv.at[1], (other, u))

    def pair_up(n):
        swap(n).wait_recv()
        part[n] = (acc[n, core].astype(F32) + pair[n].astype(F32)).astype(BF16)
        for o in range(1, group):
            scatter(n, o).start()

    def plane_sum(n):
        total = part[n, u, subs(y), :].astype(F32)
        whole(plane_in.at[n], asend.at[0], arecv.at[n]).wait_recv()
        for o in range(1, group):
            total = total + plane_in[n, o - 1].astype(F32)
        line[n] = total.astype(BF16)
        for o in range(1, outers):
            pass_on(n, o).start()

    def line_sum(n):
        total = line[n, pl.ds(pl.multiple_of(z * piece, piece), piece), :].astype(F32)
        whole(line_in.at[n], bsend.at[0], brecv.at[n]).wait_recv()
        for o in range(1, outers):
            total = total + line_in[n, o - 1].astype(F32)
        res[n, core, u, piece_at(y, z), :] = total.astype(BF16)
        for o in range(1, outers):
            along(n, o).start()

    def widen(n, t):
        whole(line_in.at[n], csend.at[0], crecv.at[n]).wait_recv()
        for o in range(1, (inners, group)[t]):
            spread(n, o, t).start()

    def hand_over(n, t):
        whole(plane_in.at[n, pl.ds(0, (inners, group)[t] - 1)], dsend.at[t], drecv.at[n]).wait_recv()
        share(n, t).start()

    def each(first, stop, work):
        @pl.loop(first, stop)
        def _(n):
            work(n)

    barrier = pltpu.get_barrier_semaphore()
    for j in range(1, nu):
        pl.semaphore_signal(barrier, inc=1, device_id=(blk, peer(j)), device_id_type=MESH)

    @pl.when(has_prev)
    def _():
        for j in range(nu):
            pl.semaphore_signal(barrier, inc=1, device_id=(blk - 1, peer(j)), device_id_type=MESH)

    @pl.when(has_next)
    def _():
        for j in range(nu):
            pl.semaphore_signal(barrier, inc=1, device_id=(blk + 1, peer(j)), device_id_type=MESH)

    for o in range(1, group):
        pl.semaphore_signal(barrier, inc=1, device_id=plane_dev(o), device_id_type=MESH)
    for o in range(1, outers):
        pl.semaphore_signal(barrier, inc=1, device_id=line_dev(o), device_id_type=MESH)

    local = [
        pltpu.make_async_copy(src, dst, local_sem.at[i])
        for i, (src, dst) in enumerate(
            (
                (tokens, tok), (down_q, downs.at[pl.ds(0, rank)]), (down_v, downs.at[pl.ds(rank, rank)]),
                (up_q, ups.at[pl.ds(0, rank)]), (up_v, ups.at[pl.ds(rank, rank)]),
                (value_base, vbuf.at[mine]), (key_base, kbuf.at[mine]),
                (query_base, qs), (out_grad, gs),
            )
        )
    ]
    for copy in local:
        copy.start()

    edge = jnp.logical_or(blk == 0, blk == nb - 1)

    @pl.when(edge)
    def _():
        pl.semaphore_wait(barrier, 2 * nu - 1 + group + outers - 2)

    @pl.when(jnp.logical_not(edge))
    def _():
        pl.semaphore_wait(barrier, 3 * nu - 1 + group + outers - 2)

    def rows_of(first, j):
        return pl.ds(pl.multiple_of(first + source(j) * rows, rows), rows)

    def cross(j, c, what):
        at = cols(c)
        src, dst = {
            0: (key_base.at[:, at], kv.at[0, mine, at]),
            1: (kv.at[1, mine, at], kv.at[1, mine, at]),
            2: (kv.at[:, mine, at], kv.at[:, mine, at]),
        }[what]
        return remote(src, dst, xsend.at[j], xrecv.at[j - 1, c], (blk, peer(j)))

    def crossed(j, c):
        here = kv.at[:, rows_of(span, j), cols(c)]
        return remote(here, here, xsend.at[j], xrecv.at[j - 1, c], (blk, peer(j)))

    def onward(j, c, what):
        at = cols(c)
        old, new = rows_of(span, j), rows_of(0, j)
        src, dst = {
            0: (key_base.at[:, at], kv.at[0, new, at]),
            1: (kv.at[1, old, at], kv.at[1, new, at]),
            2: (kv.at[:, old, at], kv.at[:, new, at]),
        }[what]
        return remote(src, dst, fsend.at[j], frecv.at[c], (blk + 1, u))

    def arrived(c):
        here = kv.at[:, pl.ds(0, span), cols(c)]
        return remote(here, here, fsend.at[0], frecv.at[c], (blk, peer(1)))

    def low_across(j):
        return pltpu.make_async_remote_copy(
            src_ref=lbuf.at[mine], dst_ref=lbuf.at[mine],
            send_sem=lsend.at[j], recv_sem=lrecv.at[j],
            device_id=(blk, peer(j)), device_id_type=MESH,
        )

    def low_crossed(j):
        here = lbuf.at[pl.ds(pl.multiple_of(span + source(j) * rows, rows), rows)]
        return pltpu.make_async_remote_copy(
            src_ref=here, dst_ref=here, send_sem=lsend.at[j], recv_sem=lrecv.at[j],
            device_id=(blk, peer(j)), device_id_type=MESH,
        )

    def low_onward(j):
        s = source(j)
        return pltpu.make_async_remote_copy(
            src_ref=lbuf.at[pl.ds(pl.multiple_of(span + s * rows, rows), rows)],
            dst_ref=lbuf.at[pl.ds(pl.multiple_of(s * rows, rows), rows)],
            send_sem=msend.at[j], recv_sem=mrecv.at[j],
            device_id=(blk + 1, u), device_id_type=MESH,
        )

    def low_arrived(j):
        here = lbuf.at[pl.ds(pl.multiple_of(source(j) * rows, rows), rows)]
        return pltpu.make_async_remote_copy(
            src_ref=here, dst_ref=here, send_sem=msend.at[j], recv_sem=mrecv.at[j],
            device_id=(blk, peer(1)), device_id_type=MESH,
        )

    early = min(2, chunks)
    ahead = min(4, chunks)
    for c in range(early):
        for j in range(1, nu):
            cross(j, c, 0).start()

    @pl.when(has_next)
    def _():
        for c in range(ahead):
            onward(0, c, 0).start()

    for v in range(nu):
        lend(v).start()

    lane = lax.broadcasted_iota(jnp.int32, (rows, 2 * rank), 1)
    for i in range(3):
        local[i].wait()
    low = outer(tok[...], downs[...])
    low_qm = jnp.where(lane < rank, low, 0.0).astype(BF16)
    low_vm = jnp.where(lane >= rank, low, 0.0).astype(BF16)
    lbuf[mine, :] = low_vm
    for i in range(3, 7):
        local[i].wait()

    def lift(c):
        extra = dot(low_vm, ups[:, cols(c)])
        vbuf[mine, cols(c)] = (vbuf[mine, cols(c)].astype(F32) + extra).astype(BF16)

    for j in range(1, nu):
        low_across(j).start()

    @pl.when(has_next)
    def _():
        low_onward(0).start()

    @pl.loop(0, early)
    def _(c):
        lift(c)
        for j in range(1, nu):
            cross(j, c, 1).start()

    @pl.loop(early, ahead)
    def _(c):
        lift(c)
        for j in range(1, nu):
            cross(j, c, 2).start()

    @pl.when(has_next)
    def _():
        @pl.loop(0, ahead)
        def _(c):
            onward(0, c, 1).start()

    @pl.loop(ahead, chunks)
    def _(c):
        lift(c)
        for j in range(1, nu):
            cross(j, c, 2).start()

    lrq[...] = jnp.zeros_like(lrq)
    lrv[...] = jnp.zeros_like(lrv)

    @pl.when(jnp.logical_not(has_prev))
    def _():
        kbuf[pl.ds(0, span), :] = jnp.zeros((span, width), BF16)
        vbuf[pl.ds(0, span), :] = jnp.zeros((span, width), BF16)
        lbuf[pl.ds(0, span), :] = jnp.zeros((span, 2 * rank), BF16)

    for i in range(7, 9):
        local[i].wait()

    scale = HEAD ** (-0.5)
    key_at = lax.broadcasted_iota(jnp.int32, (rows, 2 * span), 1)
    usable = jnp.logical_or(key_at >= span, has_prev)

    def head(h):
        at = pl.ds(pl.multiple_of(h * HEAD, HEAD), HEAD)
        up = ups[:, at]
        keys = kbuf[:, at]
        values = vbuf[:, at]
        grad = gs[:, at]
        query = (qs[:, at].astype(F32) + dot(low_qm, up)).astype(BF16)
        scores = jnp.where(usable, outer(query, keys) * scale, -jnp.inf)
        weights = jnp.exp(scores - jnp.max(scores, axis=1, keepdims=True))
        total = jnp.sum(weights, axis=1, keepdims=True)
        probs = (weights * (1.0 / total)).astype(BF16)
        attended = dot(probs, values).astype(BF16)
        delta = jnp.sum(grad.astype(F32) * attended.astype(F32), axis=1, keepdims=True)
        score_grad = (probs.astype(F32) * (outer(grad, values) - delta)).astype(BF16)
        query_grad = (dot(score_grad, keys) * scale).astype(BF16)
        seen = dot(probs, lbuf[...]).astype(BF16)
        gup = (inner(low_qm, query_grad) + inner(seen, grad)).astype(BF16)
        lifted = jnp.where(lane >= rank, outer(grad, up), 0.0).astype(BF16)
        return attended, gup, outer(query_grad, up), inner(probs, lifted)

    together = 2 if span <= 2 * HEAD else 1

    def head_group(c, offset):
        first = place(c) * heads + offset
        results = [head(first + i) for i in range(together)]
        for i, (attended, gup, _, _) in enumerate(results):
            h = first + i
            att_ref[:, pl.ds(pl.multiple_of(h * HEAD, HEAD), HEAD)] = attended
            row = pl.multiple_of((offset + i) * 2 * rank, 2 * rank)
            cell = lax.rem(c, cells)
            acc[c // cells, lax.rem(cell, 2), cell // 2, pl.ds(row, 2 * rank), :] = gup
        lrq[...] += jnp.where(lane < rank, sum(r[2] for r in results), 0.0)
        lrv[...] += sum(r[3] for r in results)

    heads = CHUNK // HEAD
    soon = max(parts - 1, 0)

    @pl.loop(0, chunks + 1)
    def _(c):
        @pl.when(c < chunks)
        def _():
            for j in range(1, nu):
                crossed(j, c).wait_recv()

                @pl.when(has_next)
                def _():
                    onward(j, c, 2).start()

            @pl.when(jnp.logical_and(has_next, c + ahead < chunks))
            def _():
                onward(0, c + ahead, 2).start()

        @pl.when(c == 1)
        def _():
            for j in range(1, nu):
                low_crossed(j).wait_recv()

                @pl.when(has_next)
                def _():
                    low_onward(j).start()

            @pl.when(has_prev)
            def _():
                for j in range(nu):
                    low_arrived(j).wait_recv()

        @pl.when(c == chunks - 1)
        def _():
            each(0, soon, pair_up)

        @pl.when(c > 0)
        def _():
            @pl.when(has_prev)
            def _():
                arrived(c - 1).wait_recv()

            @pl.loop(0, heads // together)
            def _(i):
                head_group(c - 1, i * together)


            @pl.when(lax.rem(c, cells) == 0)
            def _():
                swap(c // cells - 1).start()

    lrs[...] = lrv[...].astype(BF16)

    def terms(k, j, base):
        s = peer(j)
        return pltpu.make_async_remote_copy(
            src_ref=lrs.at[pl.ds(pl.multiple_of(base + s * rows, rows), rows)],
            dst_ref=lrin.at[k, j],
            send_sem=rsend.at[k, j], recv_sem=rrecv.at[k, j],
            device_id=(blk - k, s), device_id_type=MESH,
        )

    for j in range(1, nu):
        terms(0, j, span).start()

    @pl.when(has_prev)
    def _():
        for j in range(nu):
            terms(1, j, 0).start()

    each(soon, parts, pair_up)
    each(0, soon, plane_sum)

    lrq[...] += lrv[mine, :]
    for j in range(1, nu):
        terms(0, j, span).wait_recv()
        lrq[...] += lrin[0, j].astype(F32)

    @pl.when(has_next)
    def _():
        for j in range(nu):
            terms(1, j, 0).wait_recv()
            lrq[...] += lrin[1, j].astype(F32)

    lowb[0] = lrq[...].T.astype(BF16)
    tell().start()

    def project(p):
        for v in range(nu):
            at = pl.ds(pl.multiple_of((v * 2 + core) * strip + p * CHUNK, CHUNK), CHUNK)
            there = pl.ds(pl.multiple_of(v * strip + p * CHUNK, CHUNK), CHUNK)
            block = (dot(lowb[0], tok[:, at]) + dot(lowb[1], tok2[:, there])).astype(BF16)
            for i in range(heads):
                part[parts + p, v, pl.ds(i * 2 * rank, 2 * rank), :] = block[:, i * HEAD:(i + 1) * HEAD]
        for o in range(1, group):
            scatter(parts + p, o).start()

    def lay_out(n, t, outs):
        shared_here = res.at[n, 1 - core] if t == 1 else res.at[n, 1 - core, u]
        whole(shared_here, esend.at[t], erecv.at[n]).wait_recv()
        for v in range(nu if t == 1 else 1):
            for k in range(2):
                for i in range(heads):
                    h = ((v * 2 + k) * parts + n - t * parts) * heads + i
                    at = pl.ds(pl.multiple_of(h * HEAD, HEAD), HEAD)
                    w = v if t == 1 else u
                    outs[0][:, at] = res[n, k, w, pl.ds(i * 2 * rank, rank), :]
                    outs[1][:, at] = res[n, k, w, pl.ds(i * 2 * rank + rank, rank), :]

    whole(tok2, gsend.at[0], grecv.at[0]).wait_recv()
    tell().wait_recv()
    each(0, parts, project)

    def finish_up(n):
        lay_out(n, 0, (upq_out, upv_out))

    def finish_down(n):
        lay_out(n, 1, (downq_out, downv_out))

    order = []
    for p in range(parts):
        late = 3.0 if p >= soon else 0.0
        if p >= soon:
            order.append((-0.5, plane_sum, (p,)))
        order += [
            (0.0 + late, line_sum, (p,)), (3.5 + late, widen, (p, 0)),
            (14.0 + 0.7 * p, hand_over, (p, 0)), (17.0 + 0.7 * p, finish_up, (p,)),
        ]
        n, at = parts + p, 1.4 * p
        order += [
            (2.6 + at, plane_sum, (n,)), (7.0 + at, line_sum, (n,)), (12.0 + at, widen, (n, 1)),
            (17.5 + at, hand_over, (n, 1)), (19.5 + at, finish_down, (n,)),
        ]
    for _, work, what in sorted(order, key=lambda item: item[0]):
        work(*what)

    whole(tok2, gsend.at[0], grecv.at[0]).wait_send()
    tell().wait_send()
    whole(pair, psend.at[0], precv.at[0]).wait_send()
    whole(plane_in, asend.at[0], arecv.at[0]).wait_send()
    whole(line_in, bsend.at[0], brecv.at[0]).wait_send()
    whole(line_in, csend.at[0], crecv.at[0]).wait_send()
    for i in range(2):
        some = pl.ds(i * parts, parts)
        whole(
            plane_in.at[some, pl.ds(0, (inners, group)[i] - 1)], dsend.at[i], drecv.at[0]
        ).wait_send()
    whole(res.at[pl.ds(0, parts), 0, 0], esend.at[0], erecv.at[0]).wait_send()
    whole(res.at[pl.ds(parts, parts), 0], esend.at[1], erecv.at[0]).wait_send()

    everything = kv.at[:, mine, :]
    for j in range(1, nu):
        remote(everything, everything, xsend.at[j], xrecv.at[j - 1, 0], (blk, peer(j))).wait_send()

    @pl.when(has_next)
    def _():
        for j in range(nu):
            remote(everything, everything, fsend.at[j], frecv.at[0], (blk + 1, u)).wait_send()

    for j in range(1, nu):
        low_across(j).wait_send()

    @pl.when(has_next)
    def _():
        for j in range(nu):
            low_onward(j).wait_send()

    for j in range(1, nu):
        terms(0, j, span).wait_send()

    @pl.when(has_prev)
    def _():
        for j in range(nu):
            terms(1, j, 0).wait_send()


def grid_of(nb):
    half = nb // 2
    inners = 2 if half % 2 == 0 else 1
    return inners, half // inners


def fused(nb, nu, *operands):
    rows, width = operands[0].shape
    rank = operands[6].shape[0]
    span = nu * rows
    chunks = width // CHUNK
    cells = 2 * nu
    parts = chunks // cells
    inners, outers = grid_of(nb)
    group = nu * inners
    sub = CHUNK // inners
    lanes = 2 * rank
    dma = pltpu.SemaphoreType.DMA
    anywhere = pl.BlockSpec(memory_space=pl.ANY)
    here = pl.BlockSpec(memory_space=pltpu.VMEM)
    return pl.pallas_call(
        functools.partial(fused_kernel, nb, nu),
        out_shape=(
            pltpu.VMEM((rows, width), BF16),
            pltpu.VMEM((rank, width), BF16),
            pltpu.VMEM((rank, width), BF16),
            pltpu.VMEM((rank, width // nu), BF16),
            pltpu.VMEM((rank, width // nu), BF16),
        ),
        in_specs=[anywhere] * 9,
        out_specs=(here,) * 5,
        scratch_shapes=[
            pltpu.VMEM((2, 2 * span, width), BF16),
            pltpu.VMEM((2 * span, lanes), BF16),
            pltpu.VMEM((rows, width), BF16),
            pltpu.VMEM((rows, width), BF16),
            pltpu.VMEM((rows, width), BF16),
            pltpu.VMEM((lanes, width), BF16),
            pltpu.VMEM((lanes, width), BF16),
            pltpu.VMEM((rows, lanes), F32),
            pltpu.VMEM((2 * span, lanes), F32),
            pltpu.VMEM((2 * span, lanes), BF16),
            pltpu.VMEM((2, nu, rows, lanes), BF16),
            pltpu.VMEM((rows, width // 2), BF16),
            pltpu.VMEM((2, lanes, rows), BF16),
            pltpu.VMEM((parts, 2, nu, CHUNK, lanes), BF16),
            pltpu.VMEM((parts, nu, CHUNK, lanes), BF16),
            pltpu.VMEM((2 * parts, nu, CHUNK, lanes), BF16),
            pltpu.VMEM((2 * parts, group - 1, sub, lanes), BF16),
            pltpu.VMEM((2 * parts, sub, lanes), BF16),
            pltpu.VMEM((2 * parts, outers - 1, sub // outers, lanes), BF16),
            pltpu.VMEM((2 * parts, 2, nu, CHUNK, lanes), BF16),
            dma((9,)),
            dma((nu,)), dma((nu - 1, chunks)),
            dma((nu,)), dma((chunks,)),
            dma((nu,)), dma((nu,)), dma((nu,)), dma((nu,)),
            dma((2, nu)), dma((2, nu)),
            dma((1,)), dma((parts,)),
            dma((1,)), dma((2 * parts,)),
            dma((1,)), dma((2 * parts,)),
            dma((1,)), dma((2 * parts,)),
            dma((2,)), dma((2 * parts,)),
            dma((2,)), dma((2 * parts,)),
            dma((2,)), dma((2,)),
        ],
        compiler_params=pltpu.CompilerParams(
            collective_id=2, has_side_effects=True, vmem_limit_bytes=60_000_000
        ),
    )(*operands)


def fits(nb, nu, rows, width, rank):
    inners, outers = grid_of(nb)
    return (
        2 * rank == HEAD
        and width % (2 * nu * CHUNK) == 0
        and CHUNK % (16 * inners * outers) == 0
        and nu * rows <= CHUNK
    )


def deliver_kernel(*refs):
    count = len(refs) // 2
    sources, targets, sem = refs[:count], refs[count:2 * count], refs[-1]
    copies = [pltpu.make_async_copy(a, b, sem.at[i]) for i, (a, b) in enumerate(zip(sources, targets))]
    for copy in copies:
        copy.start()
    for copy in copies:
        copy.wait()


def deliver(*arrays):
    return pl.pallas_call(
        deliver_kernel,
        out_shape=tuple(jax.ShapeDtypeStruct(a.shape, a.dtype) for a in arrays),
        in_specs=[pl.BlockSpec(memory_space=pl.ANY)] * len(arrays),
        out_specs=tuple(pl.BlockSpec(memory_space=pl.ANY) for _ in arrays),
        scratch_shapes=[pltpu.SemaphoreType.DMA((len(arrays),))],
    )(*(pltpu.with_memory_space_constraint(a, pltpu.VMEM) for a in arrays))


def per_device(nb, nu, tokens, query_base, key_base, value_base, out_grad, down_q, up_q, down_v, up_v):
    operands = (tokens, query_base, key_base, value_base, out_grad, down_q.T, up_q, down_v.T, up_v)
    if fits(nb, nu, *tokens.shape, up_q.shape[0]):
        attended, grad_down_q, grad_down_v, grad_up_q, grad_up_v = deliver(*fused(nb, nu, *operands))
        return attended, grad_down_q.T, grad_up_q, grad_down_v.T, grad_up_v
    attended, gup, lowrank = attention(nb, nu, *operands)
    grad_down_q, grad_down_v, grad_up_q, grad_up_v = reduction(nb, nu, tokens, lowrank, gup)
    return attended, grad_down_q.T, grad_up_q, grad_down_v.T, grad_up_v


def solution(mesh):
    split = P(("blk", "uly"), None)
    return jax.shard_map(
        functools.partial(per_device, mesh.shape["blk"], mesh.shape["uly"]),
        mesh=mesh,
        in_specs=(split,) * 5 + (P(),) * 4,
        out_specs=(split, P(), P(None, "uly"), P(), P(None, "uly")),
        check_vma=False,
    )
```

```python
import functools

import jax
import jax.numpy as jnp
from jax import lax
from jax.experimental import pallas as pl
from jax.experimental.pallas import tpu as pltpu
from jax.sharding import PartitionSpec as P

HEAD = 128
CHUNK = 256
MESH = pl.DeviceIdType.MESH
F32 = jnp.float32
BF16 = jnp.bfloat16


def inner(left, right):
    return lax.dot_general(left, right, (((0,), (0,)), ((), ())), preferred_element_type=F32)


def outer(left, right):
    return lax.dot_general(left, right, (((1,), (1,)), ((), ())), preferred_element_type=F32)


def dot(left, right):
    return jnp.dot(left, right, preferred_element_type=F32)


def attention_kernel(
    nb, nu,
    tokens, query_base, key_base, value_base, out_grad, down_q, up_q, down_v, up_v,
    att_ref, gup_ref, low_out,
    kbuf, vbuf, lbuf, tok, qs, gs, downs, ups, lrq, lrv, lrin,
    local_sem, xsend, xrecv, fsend, frecv, lsend, lrecv, msend, mrecv, rsend, rrecv,
):
    blk = lax.axis_index("blk")
    u = lax.axis_index("uly")
    rows, width = tokens.shape
    rank = up_q.shape[0]
    span = nu * rows
    chunks = width // CHUNK
    has_prev = blk > 0
    has_next = blk < nb - 1
    mine = pl.ds(pl.multiple_of(span + u * rows, rows), rows)

    def peer(j):
        return lax.rem(u + j, nu)

    def source(j):
        return lax.rem(u - j + nu, nu)

    def cols(c):
        return pl.ds(pl.multiple_of(c * CHUNK, CHUNK), CHUNK)

    barrier = pltpu.get_barrier_semaphore()
    for j in range(1, nu):
        pl.semaphore_signal(barrier, inc=1, device_id=(blk, peer(j)), device_id_type=MESH)

    @pl.when(has_prev)
    def _():
        for j in range(nu):
            pl.semaphore_signal(barrier, inc=1, device_id=(blk - 1, peer(j)), device_id_type=MESH)

    @pl.when(has_next)
    def _():
        for j in range(nu):
            pl.semaphore_signal(barrier, inc=1, device_id=(blk + 1, peer(j)), device_id_type=MESH)

    local = [
        pltpu.make_async_copy(src, dst, local_sem.at[i])
        for i, (src, dst) in enumerate(
            (
                (tokens, tok), (down_q, downs.at[pl.ds(0, rank)]), (down_v, downs.at[pl.ds(rank, rank)]),
                (up_q, ups.at[pl.ds(0, rank)]), (up_v, ups.at[pl.ds(rank, rank)]),
                (value_base, vbuf.at[mine]), (key_base, kbuf.at[mine]),
                (query_base, qs), (out_grad, gs),
            )
        )
    ]
    for copy in local:
        copy.start()

    edge = jnp.logical_or(blk == 0, blk == nb - 1)

    @pl.when(edge)
    def _():
        pl.semaphore_wait(barrier, 2 * nu - 1)

    @pl.when(jnp.logical_not(edge))
    def _():
        pl.semaphore_wait(barrier, 3 * nu - 1)

    bufs = (kbuf, vbuf)

    def across(a, j, c):
        src = key_base.at[:, cols(c)] if a == 0 else vbuf.at[mine, cols(c)]
        return pltpu.make_async_remote_copy(
            src_ref=src, dst_ref=bufs[a].at[mine, cols(c)],
            send_sem=xsend.at[a, j, c], recv_sem=xrecv.at[a, j, c],
            device_id=(blk, peer(j)), device_id_type=MESH,
        )

    def crossed(a, j, c):
        here = bufs[a].at[pl.ds(pl.multiple_of(span + source(j) * rows, rows), rows), cols(c)]
        return pltpu.make_async_remote_copy(
            src_ref=here, dst_ref=here,
            send_sem=xsend.at[a, j, c], recv_sem=xrecv.at[a, j, c],
            device_id=(blk, peer(j)), device_id_type=MESH,
        )

    def onward(a, j, c):
        s = source(j)
        if a == 0 and j == 0:
            src = key_base.at[:, cols(c)]
        else:
            src = bufs[a].at[pl.ds(pl.multiple_of(span + s * rows, rows), rows), cols(c)]
        return pltpu.make_async_remote_copy(
            src_ref=src, dst_ref=bufs[a].at[pl.ds(pl.multiple_of(s * rows, rows), rows), cols(c)],
            send_sem=fsend.at[a, j, c], recv_sem=frecv.at[a, j, c],
            device_id=(blk + 1, u), device_id_type=MESH,
        )

    def arrived(a, j, c):
        here = bufs[a].at[pl.ds(pl.multiple_of(source(j) * rows, rows), rows), cols(c)]
        return pltpu.make_async_remote_copy(
            src_ref=here, dst_ref=here,
            send_sem=fsend.at[a, j, c], recv_sem=frecv.at[a, j, c],
            device_id=(blk, peer(1)), device_id_type=MESH,
        )

    def low_across(j):
        return pltpu.make_async_remote_copy(
            src_ref=lbuf.at[mine], dst_ref=lbuf.at[mine],
            send_sem=lsend.at[j], recv_sem=lrecv.at[j],
            device_id=(blk, peer(j)), device_id_type=MESH,
        )

    def low_crossed(j):
        here = lbuf.at[pl.ds(pl.multiple_of(span + source(j) * rows, rows), rows)]
        return pltpu.make_async_remote_copy(
            src_ref=here, dst_ref=here, send_sem=lsend.at[j], recv_sem=lrecv.at[j],
            device_id=(blk, peer(j)), device_id_type=MESH,
        )

    def low_onward(j):
        s = source(j)
        return pltpu.make_async_remote_copy(
            src_ref=lbuf.at[pl.ds(pl.multiple_of(span + s * rows, rows), rows)],
            dst_ref=lbuf.at[pl.ds(pl.multiple_of(s * rows, rows), rows)],
            send_sem=msend.at[j], recv_sem=mrecv.at[j],
            device_id=(blk + 1, u), device_id_type=MESH,
        )

    def low_arrived(j):
        here = lbuf.at[pl.ds(pl.multiple_of(source(j) * rows, rows), rows)]
        return pltpu.make_async_remote_copy(
            src_ref=here, dst_ref=here, send_sem=msend.at[j], recv_sem=mrecv.at[j],
            device_id=(blk, peer(1)), device_id_type=MESH,
        )

    early = min(3 * 512 // CHUNK, chunks)
    ahead = min(2048 // CHUNK, chunks)
    for c in range(early):
        for j in range(1, nu):
            across(0, j, c).start()

    @pl.when(has_next)
    def _():
        for c in range(ahead):
            onward(0, 0, c).start()

    lane = lax.broadcasted_iota(jnp.int32, (rows, 2 * rank), 1)
    for i in range(3):
        local[i].wait()
    low = outer(tok[...], downs[...])
    low_qm = jnp.where(lane < rank, low, 0.0).astype(BF16)
    low_vm = jnp.where(lane >= rank, low, 0.0).astype(BF16)
    lbuf[mine, :] = low_vm
    for i in range(3, 6):
        local[i].wait()

    @pl.loop(0, chunks)
    def _(c):
        part = dot(low_vm, ups[:, cols(c)])
        vbuf[mine, cols(c)] = (vbuf[mine, cols(c)].astype(F32) + part).astype(BF16)

    for j in range(1, nu):
        low_across(j).start()

    @pl.when(has_next)
    def _():
        low_onward(0).start()

    @pl.loop(0, chunks)
    def _(c):
        @pl.when(c >= early)
        def _():
            for j in range(1, nu):
                across(0, j, c).start()

        for j in range(1, nu):
            across(1, j, c).start()

    @pl.when(has_next)
    def _():
        for c in range(ahead):
            onward(1, 0, c).start()

    lrq[...] = jnp.zeros_like(lrq)
    lrv[...] = jnp.zeros_like(lrv)

    @pl.when(jnp.logical_not(has_prev))
    def _():
        kbuf[pl.ds(0, span), :] = jnp.zeros((span, width), BF16)
        vbuf[pl.ds(0, span), :] = jnp.zeros((span, width), BF16)
        lbuf[pl.ds(0, span), :] = jnp.zeros((span, 2 * rank), BF16)

    for i in range(6, 9):
        local[i].wait()

    scale = HEAD ** (-0.5)
    key_at = lax.broadcasted_iota(jnp.int32, (rows, 2 * span), 1)
    usable = jnp.logical_or(key_at >= span, has_prev)

    def head(h):
        at = pl.ds(pl.multiple_of(h * HEAD, HEAD), HEAD)
        up = ups[:, at]
        keys = kbuf[:, at]
        values = vbuf[:, at]
        grad = gs[:, at]
        query = (qs[:, at].astype(F32) + dot(low_qm, up)).astype(BF16)
        scores = jnp.where(usable, outer(query, keys) * scale, -jnp.inf)
        weights = jnp.exp(scores - jnp.max(scores, axis=1, keepdims=True))
        total = jnp.sum(weights, axis=1, keepdims=True)
        probs = (weights * (1.0 / total)).astype(BF16)
        attended = dot(probs, values).astype(BF16)
        delta = jnp.sum(grad.astype(F32) * attended.astype(F32), axis=1, keepdims=True)
        score_grad = (probs.astype(F32) * (outer(grad, values) - delta)).astype(BF16)
        query_grad = (dot(score_grad, keys) * scale).astype(BF16)
        seen = dot(probs, lbuf[...]).astype(BF16)
        gup = (inner(low_qm, query_grad) + inner(seen, grad)).astype(BF16)
        lifted = jnp.where(lane >= rank, outer(grad, up), 0.0).astype(BF16)
        return attended, gup, outer(query_grad, up), inner(probs, lifted)

    together = 2 if span <= 2 * HEAD else 1

    def head_group(first):
        results = [head(first + i) for i in range(together)]
        for i, (attended, gup, _, _) in enumerate(results):
            h = first + i
            att_ref[:, pl.ds(pl.multiple_of(h * HEAD, HEAD), HEAD)] = attended
            gup_ref[pl.ds(pl.multiple_of(h * 2 * rank, 2 * rank), 2 * rank), :] = gup
        lrq[...] += jnp.where(lane < rank, sum(r[2] for r in results), 0.0)
        lrv[...] += sum(r[3] for r in results)

    heads = CHUNK // HEAD

    @pl.loop(0, chunks + 1)
    def _(c):
        @pl.when(c == 0)
        def _():
            for j in range(1, nu):
                low_crossed(j).wait_recv()

                @pl.when(has_next)
                def _():
                    low_onward(j).start()

            @pl.when(has_prev)
            def _():
                for j in range(nu):
                    low_arrived(j).wait_recv()

        @pl.when(c < chunks)
        def _():
            for a in range(2):
                for j in range(1, nu):
                    crossed(a, j, c).wait_recv()

                    @pl.when(has_next)
                    def _():
                        onward(a, j, c).start()

            @pl.when(jnp.logical_and(has_next, c + ahead < chunks))
            def _():
                for a in range(2):
                    onward(a, 0, c + ahead).start()

        @pl.when(c > 0)
        def _():
            @pl.when(has_prev)
            def _():
                for a in range(2):
                    for j in range(nu):
                        arrived(a, j, c - 1).wait_recv()

            @pl.loop(0, heads // together)
            def _(i):
                head_group((c - 1) * heads + i * together)

    def terms(k, j, base):
        s = peer(j)
        return pltpu.make_async_remote_copy(
            src_ref=lrv.at[pl.ds(pl.multiple_of(base + s * rows, rows), rows)],
            dst_ref=lrin.at[k, j],
            send_sem=rsend.at[k, j], recv_sem=rrecv.at[k, j],
            device_id=(blk - k, s), device_id_type=MESH,
        )

    for j in range(1, nu):
        terms(0, j, span).start()

    @pl.when(has_prev)
    def _():
        for j in range(nu):
            terms(1, j, 0).start()

    @pl.loop(0, chunks)
    def _(c):
        for a in range(2):
            for j in range(1, nu):
                across(a, j, c).wait_send()

            @pl.when(has_next)
            def _():
                for j in range(nu):
                    onward(a, j, c).wait_send()

    for j in range(1, nu):
        low_across(j).wait_send()

    @pl.when(has_next)
    def _():
        for j in range(nu):
            low_onward(j).wait_send()

    lrq[...] += lrv[mine, :]
    for j in range(1, nu):
        terms(0, j, span).wait_recv()
        lrq[...] += lrin[0, j]

    @pl.when(has_next)
    def _():
        for j in range(nu):
            terms(1, j, 0).wait_recv()
            lrq[...] += lrin[1, j]

    low_out[...] = lrq[...].astype(BF16)
    for j in range(1, nu):
        terms(0, j, span).wait_send()

    @pl.when(has_prev)
    def _():
        for j in range(nu):
            terms(1, j, 0).wait_send()


def attention(nb, nu, *operands):
    rows, width = operands[0].shape
    rank = operands[6].shape[0]
    span = nu * rows
    chunks = width // CHUNK
    dma = pltpu.SemaphoreType.DMA
    anywhere = pl.BlockSpec(memory_space=pl.ANY)
    here = pl.BlockSpec(memory_space=pltpu.VMEM)
    return pl.pallas_call(
        functools.partial(attention_kernel, nb, nu),
        out_shape=(
            jax.ShapeDtypeStruct((rows, width), BF16),
            jax.ShapeDtypeStruct((width // HEAD * 2 * rank, HEAD), BF16),
            jax.ShapeDtypeStruct((rows, 2 * rank), BF16),
        ),
        in_specs=[anywhere] * 9,
        out_specs=(here, here, here),
        scratch_shapes=[
            pltpu.VMEM((2 * span, width), BF16),
            pltpu.VMEM((2 * span, width), BF16),
            pltpu.VMEM((2 * span, 2 * rank), BF16),
            pltpu.VMEM((rows, width), BF16),
            pltpu.VMEM((rows, width), BF16),
            pltpu.VMEM((rows, width), BF16),
            pltpu.VMEM((2 * rank, width), BF16),
            pltpu.VMEM((2 * rank, width), BF16),
            pltpu.VMEM((rows, 2 * rank), F32),
            pltpu.VMEM((2 * span, 2 * rank), F32),
            pltpu.VMEM((2, nu, rows, 2 * rank), F32),
            dma((9,)),
            dma((2, nu, chunks)), dma((2, nu, chunks)),
            dma((2, nu, chunks)), dma((2, nu, chunks)),
            dma((nu,)), dma((nu,)), dma((nu,)), dma((nu,)),
            dma((2, nu)), dma((2, nu)),
        ],
        compiler_params=pltpu.CompilerParams(
            collective_id=0, has_side_effects=True, vmem_limit_bytes=65_000_000
        ),
    )(*operands)


def reduction_kernel(
    nb, nu,
    tokens, lowrank, gup,
    downq_out, downv_out, upq_out, upv_out,
    tok, terms, pair, part, plane_in, line, line_in, down, ups, flat,
    local_sem, psend, precv, asend, arecv, bsend, brecv, csend, crecv, dsend, drecv, esend, erecv,
):
    blk = lax.axis_index("blk")
    u = lax.axis_index("uly")
    core = lax.rem(blk, 2)
    chip = blk // 2
    other = chip * 2 + 1 - core
    half = nb // 2
    inners = plane_in.shape[1] // nu
    outers = half // inners
    y = lax.rem(chip, inners)
    z = chip // inners
    group = nu * inners
    rows, width = tokens.shape
    rank = upq_out.shape[0]
    region = pair.shape[2]
    sub = plane_in.shape[2]
    piece = line_in.shape[2]

    def split(o, sign):
        pu = lax.rem(u + sign * (o // inners) + nu, nu)
        py = lax.rem(y + sign * lax.rem(o, inners) + inners, inners)
        return pu, py

    def plane_dev(o):
        pu, py = split(o, 1)
        return ((z * inners + py) * 2 + core, pu)

    def peer_z(o):
        return lax.rem(z + o, outers)

    def from_z(o):
        return lax.rem(z - o + outers, outers)

    def line_dev(o):
        return ((peer_z(o) * inners + y) * 2 + core, u)

    def subs(p):
        return pl.ds(pl.multiple_of(p * sub, sub), sub)

    barrier = pltpu.get_barrier_semaphore()
    pl.semaphore_signal(barrier, inc=1, device_id=(other, u), device_id_type=MESH)
    for o in range(1, group):
        pl.semaphore_signal(barrier, inc=1, device_id=plane_dev(o), device_id_type=MESH)
    for o in range(1, outers):
        pl.semaphore_signal(barrier, inc=1, device_id=line_dev(o), device_id_type=MESH)

    load = pltpu.make_async_copy(tokens, tok, local_sem.at[0])
    load.start()
    pl.semaphore_wait(barrier, group + outers - 1)

    def remote(src, dst, send, recv, device):
        return pltpu.make_async_remote_copy(
            src_ref=src, dst_ref=dst, send_sem=send, recv_sem=recv,
            device_id=device, device_id_type=MESH,
        )

    def swap(t, v):
        rows_at = pl.ds(pl.multiple_of((v * 2 + 1 - core) * region, region), region)
        return remote(
            (terms if t == 0 else gup).at[rows_at], pair.at[t, v],
            psend.at[t, v], precv.at[t, v], (other, u),
        )

    def scatter(t, o):
        pu, py = split(o, 1)
        return remote(
            part.at[t, pu, subs(py)], plane_in.at[t, o],
            asend.at[t, o], arecv.at[t, o], plane_dev(o),
        )

    def pass_on(t, o):
        at = pl.ds(pl.multiple_of(peer_z(o) * piece, piece), piece)
        return remote(
            line.at[t, at], line_in.at[t, o], bsend.at[t, o], brecv.at[t, o], line_dev(o)
        )

    def whole(t, v, k, p):
        return down.at[v, k, subs(p)] if t == 0 else ups.at[k, subs(p)]

    def piece_at(p, q):
        return pl.ds(pl.multiple_of(p * sub + q * piece, piece), piece)

    def small(t, q):
        return down.at[u, core, piece_at(y, q)] if t == 0 else ups.at[core, piece_at(y, q)]

    def along(t, o):
        return remote(small(t, z), small(t, z), csend.at[t, o], crecv.at[t, o], line_dev(o))

    def came(t, o):
        here = small(t, from_z(o))
        return remote(here, here, csend.at[t, o], crecv.at[t, o], line_dev(o))

    def spread(t, o):
        here = whole(t, u, core, y)
        return remote(here, here, dsend.at[t, o], drecv.at[t, o], plane_dev(o))

    def landed(t, o):
        pu, py = split(o, -1)
        here = whole(t, pu, core, py)
        return remote(here, here, dsend.at[t, o], drecv.at[t, o], (other, u))

    def share(t, o):
        pu, py = split(o, -1)
        here = whole(t, pu, core, py)
        return remote(here, here, esend.at[t, o], erecv.at[t, o], (other, u))

    def shared(t, o):
        pu, py = split(o, -1)
        here = whole(t, pu, 1 - core, py)
        return remote(here, here, esend.at[t, o], erecv.at[t, o], (other, u))

    if part.shape[2] > region:
        part[...] = jnp.zeros_like(part)
    for v in range(nu):
        swap(1, v).start()

    load.wait()
    lows = lowrank[...]

    @pl.loop(0, width // HEAD)
    def _(h):
        cols = pl.ds(pl.multiple_of(h * HEAD, HEAD), HEAD)
        here = pl.ds(pl.multiple_of(h * 2 * rank, 2 * rank), 2 * rank)
        terms[here, :] = inner(lows, tok[:, cols]).astype(BF16)

    for v in range(nu):
        swap(0, v).start()

    for t in (1, 0):
        for v in range(nu):
            rows_at = pl.ds(pl.multiple_of((v * 2 + core) * region, region), region)
            own = (terms if t == 0 else gup)[rows_at, :]
            swap(t, v).wait_recv()
            part[t, v, pl.ds(0, region), :] = (
                own.astype(F32) + pair[t, v].astype(F32)
            ).astype(BF16)
        for o in range(1, group):
            scatter(t, o).start()

    for t in (1, 0):
        total = part[t, u, subs(y), :].astype(F32)
        for o in range(1, group):
            scatter(t, o).wait_recv()
            total = total + plane_in[t, o].astype(F32)
        line[t, :, :] = total.astype(BF16)
        for o in range(1, outers):
            pass_on(t, o).start()

    for t in (1, 0):
        total = line[t, pl.ds(pl.multiple_of(z * piece, piece), piece), :].astype(F32)
        for o in range(1, outers):
            pass_on(t, o).wait_recv()
            total = total + line_in[t, o].astype(F32)
        small(t, z)[...] = total.astype(BF16)
        for o in range(1, outers):
            along(t, o).start()

    counts = (group, inners)
    for t in (1, 0):
        for o in range(1, outers):
            came(t, o).wait_recv()
        for o in range(1, counts[t]):
            spread(t, o).start()
        share(t, 0).start()

    for t in (1, 0):
        for o in range(1, counts[t]):
            landed(t, o).wait_recv()
            share(t, o).start()

    for t in (1, 0):
        for o in range(counts[t]):
            shared(t, o).wait_recv()
        places = [(v, k) for v in range(nu if t == 0 else 1) for k in range(2)]
        for n, (v, k) in enumerate(places):
            flat[pl.ds(n * region, region), :] = (
                down[v, k, pl.ds(0, region), :] if t == 0 else ups[k, pl.ds(0, region), :]
            )
        outs = (downq_out, downv_out) if t == 0 else (upq_out, upv_out)
        for h in range(len(places) * region // (2 * rank)):
            cols = pl.ds(h * HEAD, HEAD)
            outs[0][:, cols] = flat[pl.ds(h * 2 * rank, rank), :]
            outs[1][:, cols] = flat[pl.ds(h * 2 * rank + rank, rank), :]

    for t in (1, 0):
        for v in range(nu):
            swap(t, v).wait_send()
        for o in range(1, group):
            scatter(t, o).wait_send()
        for o in range(1, outers):
            pass_on(t, o).wait_send()
            along(t, o).wait_send()
        for o in range(1, counts[t]):
            spread(t, o).wait_send()
        for o in range(counts[t]):
            share(t, o).wait_send()


def reduction(nb, nu, tokens, lowrank, gup):
    rows, width = tokens.shape
    rank = lowrank.shape[1] // 2
    half = nb // 2
    inners = 2 if half % 2 == 0 else 1
    outers = half // inners
    group = nu * inners
    region = width // (2 * nu)
    piece = -(-region // (16 * half)) * 16
    sub = outers * piece
    held = half * piece
    dma = pltpu.SemaphoreType.DMA
    here = pl.BlockSpec(memory_space=pltpu.VMEM)
    lanes = lowrank.shape[1]
    return pl.pallas_call(
        functools.partial(reduction_kernel, nb, nu),
        out_shape=(
            jax.ShapeDtypeStruct((rank, width), BF16),
            jax.ShapeDtypeStruct((rank, width), BF16),
            jax.ShapeDtypeStruct((rank, width // nu), BF16),
            jax.ShapeDtypeStruct((rank, width // nu), BF16),
        ),
        in_specs=[pl.BlockSpec(memory_space=pl.ANY), here, here],
        out_specs=(here, here, here, here),
        scratch_shapes=[
            pltpu.VMEM((rows, width), BF16),
            pltpu.VMEM((width, lanes), BF16),
            pltpu.VMEM((2, nu, region, lanes), BF16),
            pltpu.VMEM((2, nu, held, lanes), BF16),
            pltpu.VMEM((2, group, sub, lanes), BF16),
            pltpu.VMEM((2, sub, lanes), BF16),
            pltpu.VMEM((2, outers, piece, lanes), BF16),
            pltpu.VMEM((nu, 2, held, lanes), BF16),
            pltpu.VMEM((2, held, lanes), BF16),
            pltpu.VMEM((2 * nu * region, lanes), BF16),
            dma((1,)),
            dma((2, nu)), dma((2, nu)),
            dma((2, group)), dma((2, group)),
            dma((2, outers)), dma((2, outers)),
            dma((2, outers)), dma((2, outers)),
            dma((2, group)), dma((2, group)),
            dma((2, group)), dma((2, group)),
        ],
        compiler_params=pltpu.CompilerParams(collective_id=1, has_side_effects=True),
    )(tokens, lowrank, gup)


def fused_kernel(
    nb, nu,
    tokens, query_base, key_base, value_base, out_grad, down_q, up_q, down_v, up_v,
    att_ref, downq_out, downv_out, upq_out, upv_out,
    kv, lbuf, tok, qs, gs, downs, ups, lrq, lrv, lrs, lrin,
    tok2, lowb, acc, pair, part, plane_in, line, line_in, res,
    local_sem, xsend, xrecv, fsend, frecv, lsend, lrecv, msend, mrecv, rsend, rrecv,
    psend, precv, asend, arecv, bsend, brecv, csend, crecv, dsend, drecv, esend, erecv, gsend, grecv,
):
    kbuf, vbuf = kv.at[0], kv.at[1]
    blk = lax.axis_index("blk")
    u = lax.axis_index("uly")
    rows, width = tokens.shape
    rank = up_q.shape[0]
    span = nu * rows
    chunks = width // CHUNK
    has_prev = blk > 0
    has_next = blk < nb - 1
    mine = pl.ds(pl.multiple_of(span + u * rows, rows), rows)

    def peer(j):
        return lax.rem(u + j, nu)

    def source(j):
        return lax.rem(u - j + nu, nu)

    cells = 2 * nu
    parts = chunks // cells
    core = lax.rem(blk, 2)
    chip = blk // 2
    other = chip * 2 + 1 - core
    inners, outers = grid_of(nb)
    group = nu * inners
    y = lax.rem(chip, inners)
    z = chip // inners
    sub = CHUNK // inners
    piece = sub // outers

    def place(c):
        return lax.rem(c, cells) * parts + c // cells

    def cols(c):
        return pl.ds(pl.multiple_of(place(c) * CHUNK, CHUNK), CHUNK)

    def remote(src, dst, send, recv, device):
        return pltpu.make_async_remote_copy(
            src_ref=src, dst_ref=dst, send_sem=send, recv_sem=recv,
            device_id=device, device_id_type=MESH,
        )

    def split(o, sign):
        pu = lax.rem(u + sign * (o // inners) + nu, nu)
        py = lax.rem(y + sign * lax.rem(o, inners) + inners, inners)
        return pu, py

    def plane_dev(o):
        pu, py = split(o, 1)
        return ((z * inners + py) * 2 + core, pu)

    def peer_z(o):
        return lax.rem(z + o, outers)

    def from_z(o):
        return lax.rem(z - o + outers, outers)

    def line_dev(o):
        return ((peer_z(o) * inners + y) * 2 + core, u)

    def subs(p):
        return pl.ds(pl.multiple_of(p * sub, sub), sub)

    def piece_at(p, q):
        return pl.ds(pl.multiple_of(p * sub + q * piece, piece), piece)

    def swap(n):
        return remote(
            acc.at[n, 1 - core], pair.at[n], psend.at[0], precv.at[n], (other, u)
        )

    def scatter(n, o):
        pu, py = split(o, 1)
        return remote(
            part.at[n, pu, subs(py)], plane_in.at[n, o - 1],
            asend.at[0], arecv.at[n], plane_dev(o),
        )

    def pass_on(n, o):
        at = pl.ds(pl.multiple_of(peer_z(o) * piece, piece), piece)
        return remote(
            line.at[n, at], line_in.at[n, o - 1], bsend.at[0], brecv.at[n], line_dev(o)
        )

    def along(n, o):
        here = res.at[n, core, u, piece_at(y, z)]
        return remote(here, here, csend.at[0], crecv.at[n], line_dev(o))

    def spread(n, o, t):
        here = res.at[n, core, u, subs(y)]
        return remote(here, here, dsend.at[t], drecv.at[n], plane_dev(o))

    def share(n, t):
        here = res.at[n, core] if t == 1 else res.at[n, core, u]
        return remote(here, here, esend.at[t], erecv.at[n], (other, u))

    def whole(src, send, recv):
        return remote(src, src, send, recv, (other, u))

    strip = parts * CHUNK

    def lend(v):
        at = pl.ds(pl.multiple_of((v * 2 + 1 - core) * strip, strip), strip)
        return remote(
            tokens.at[:, at], tok2.at[:, pl.ds(v * strip, strip)], gsend.at[0], grecv.at[0], (other, u)
        )

    def tell():
        return remote(lowb.at[0], lowb.at[1], gsend.at[1], grecv.at[1], (other, u))

    def pair_sum(n):
        swap(n).wait_recv()
        part[n] = (acc[n, core].astype(F32) + pair[n].astype(F32)).astype(BF16)

    def send_out(n):
        for o in range(1, group):
            scatter(n, o).start()

    def pair_up(n):
        pair_sum(n)
        send_out(n)

    def plane_sum(n):
        total = part[n, u, subs(y), :].astype(F32)
        whole(plane_in.at[n], asend.at[0], arecv.at[n]).wait_recv()
        for o in range(1, group):
            total = total + plane_in[n, o - 1].astype(F32)
        line[n] = total.astype(BF16)
        for o in range(1, outers):
            pass_on(n, o).start()

    def line_sum(n):
        total = line[n, pl.ds(pl.multiple_of(z * piece, piece), piece), :].astype(F32)
        whole(line_in.at[n], bsend.at[0], brecv.at[n]).wait_recv()
        for o in range(1, outers):
            total = total + line_in[n, o - 1].astype(F32)
        res[n, core, u, piece_at(y, z), :] = total.astype(BF16)
        for o in range(1, outers):
            along(n, o).start()

    def widen(n, t):
        whole(line_in.at[n], csend.at[0], crecv.at[n]).wait_recv()
        for o in range(1, (inners, group)[t]):
            spread(n, o, t).start()

    def hand_over(n, t):
        whole(plane_in.at[n, pl.ds(0, (inners, group)[t] - 1)], dsend.at[t], drecv.at[n]).wait_recv()
        share(n, t).start()

    def each(first, stop, work):
        @pl.loop(first, stop)
        def _(n):
            work(n)

    barrier = pltpu.get_barrier_semaphore()
    for j in range(1, nu):
        pl.semaphore_signal(barrier, inc=1, device_id=(blk, peer(j)), device_id_type=MESH)

    @pl.when(has_prev)
    def _():
        for j in range(nu):
            pl.semaphore_signal(barrier, inc=1, device_id=(blk - 1, peer(j)), device_id_type=MESH)

    @pl.when(has_next)
    def _():
        for j in range(nu):
            pl.semaphore_signal(barrier, inc=1, device_id=(blk + 1, peer(j)), device_id_type=MESH)

    for o in range(1, group):
        pl.semaphore_signal(barrier, inc=1, device_id=plane_dev(o), device_id_type=MESH)
    for o in range(1, outers):
        pl.semaphore_signal(barrier, inc=1, device_id=line_dev(o), device_id_type=MESH)

    local = [
        pltpu.make_async_copy(src, dst, local_sem.at[i])
        for i, (src, dst) in enumerate(
            (
                (tokens, tok), (down_q, downs.at[pl.ds(0, rank)]), (down_v, downs.at[pl.ds(rank, rank)]),
                (up_q, ups.at[pl.ds(0, rank)]), (up_v, ups.at[pl.ds(rank, rank)]),
                (value_base, vbuf.at[mine]), (key_base, kbuf.at[mine]),
                (query_base, qs), (out_grad, gs),
            )
        )
    ]
    for copy in local:
        copy.start()

    edge = jnp.logical_or(blk == 0, blk == nb - 1)

    @pl.when(edge)
    def _():
        pl.semaphore_wait(barrier, 2 * nu - 1 + group + outers - 2)

    @pl.when(jnp.logical_not(edge))
    def _():
        pl.semaphore_wait(barrier, 3 * nu - 1 + group + outers - 2)

    def rows_of(first, j):
        return pl.ds(pl.multiple_of(first + source(j) * rows, rows), rows)

    def cross(j, c, what):
        at = cols(c)
        src, dst = {
            0: (key_base.at[:, at], kv.at[0, mine, at]),
            1: (kv.at[1, mine, at], kv.at[1, mine, at]),
            2: (kv.at[:, mine, at], kv.at[:, mine, at]),
        }[what]
        return remote(src, dst, xsend.at[j], xrecv.at[j - 1, c], (blk, peer(j)))

    def crossed(j, c):
        here = kv.at[:, rows_of(span, j), cols(c)]
        return remote(here, here, xsend.at[j], xrecv.at[j - 1, c], (blk, peer(j)))

    def onward(j, c, what):
        at = cols(c)
        old, new = rows_of(span, j), rows_of(0, j)
        src, dst = {
            0: (key_base.at[:, at], kv.at[0, new, at]),
            1: (kv.at[1, old, at], kv.at[1, new, at]),
            2: (kv.at[:, old, at], kv.at[:, new, at]),
        }[what]
        return remote(src, dst, fsend.at[j], frecv.at[c], (blk + 1, u))

    def arrived(c):
        here = kv.at[:, pl.ds(0, span), cols(c)]
        return remote(here, here, fsend.at[0], frecv.at[c], (blk, peer(1)))

    def low_across(j):
        return pltpu.make_async_remote_copy(
            src_ref=lbuf.at[mine], dst_ref=lbuf.at[mine],
            send_sem=lsend.at[j], recv_sem=lrecv.at[j],
            device_id=(blk, peer(j)), device_id_type=MESH,
        )

    def low_crossed(j):
        here = lbuf.at[pl.ds(pl.multiple_of(span + source(j) * rows, rows), rows)]
        return pltpu.make_async_remote_copy(
            src_ref=here, dst_ref=here, send_sem=lsend.at[j], recv_sem=lrecv.at[j],
            device_id=(blk, peer(j)), device_id_type=MESH,
        )

    def low_onward(j):
        s = source(j)
        return pltpu.make_async_remote_copy(
            src_ref=lbuf.at[pl.ds(pl.multiple_of(span + s * rows, rows), rows)],
            dst_ref=lbuf.at[pl.ds(pl.multiple_of(s * rows, rows), rows)],
            send_sem=msend.at[j], recv_sem=mrecv.at[j],
            device_id=(blk + 1, u), device_id_type=MESH,
        )

    def low_arrived(j):
        here = lbuf.at[pl.ds(pl.multiple_of(source(j) * rows, rows), rows)]
        return pltpu.make_async_remote_copy(
            src_ref=here, dst_ref=here, send_sem=msend.at[j], recv_sem=mrecv.at[j],
            device_id=(blk, peer(1)), device_id_type=MESH,
        )

    early = min(1, chunks)
    ahead = min(3, chunks)
    for c in range(early):
        for j in range(1, nu):
            cross(j, c, 0).start()

    @pl.when(has_next)
    def _():
        for c in range(ahead):
            onward(0, c, 0).start()

    for v in range(nu):
        lend(v).start()

    lane = lax.broadcasted_iota(jnp.int32, (rows, 2 * rank), 1)
    for i in range(3):
        local[i].wait()
    low = outer(tok[...], downs[...])
    low_qm = jnp.where(lane < rank, low, 0.0).astype(BF16)
    low_vm = jnp.where(lane >= rank, low, 0.0).astype(BF16)
    lbuf[mine, :] = low_vm
    for i in range(3, 7):
        local[i].wait()

    def lift(c):
        extra = dot(low_vm, ups[:, cols(c)])
        vbuf[mine, cols(c)] = (vbuf[mine, cols(c)].astype(F32) + extra).astype(BF16)

    for j in range(1, nu):
        low_across(j).start()

    @pl.when(has_next)
    def _():
        low_onward(0).start()

    @pl.loop(0, early)
    def _(c):
        lift(c)
        for j in range(1, nu):
            cross(j, c, 1).start()

    @pl.loop(early, ahead)
    def _(c):
        lift(c)
        for j in range(1, nu):
            cross(j, c, 2).start()

    @pl.when(has_next)
    def _():
        @pl.loop(0, ahead)
        def _(c):
            onward(0, c, 1).start()

    @pl.loop(ahead, chunks)
    def _(c):
        lift(c)
        for j in range(1, nu):
            cross(j, c, 2).start()

    lrq[...] = jnp.zeros_like(lrq)
    lrv[...] = jnp.zeros_like(lrv)

    @pl.when(jnp.logical_not(has_prev))
    def _():
        kbuf[pl.ds(0, span), :] = jnp.zeros((span, width), BF16)
        vbuf[pl.ds(0, span), :] = jnp.zeros((span, width), BF16)
        lbuf[pl.ds(0, span), :] = jnp.zeros((span, 2 * rank), BF16)

    for i in range(7, 9):
        local[i].wait()

    scale = HEAD ** (-0.5)
    key_at = lax.broadcasted_iota(jnp.int32, (rows, 2 * span), 1)
    usable = jnp.logical_or(key_at >= span, has_prev)

    def head(h):
        at = pl.ds(pl.multiple_of(h * HEAD, HEAD), HEAD)
        up = ups[:, at]
        keys = kbuf[:, at]
        values = vbuf[:, at]
        grad = gs[:, at]
        query = (qs[:, at].astype(F32) + dot(low_qm, up)).astype(BF16)
        scores = jnp.where(usable, outer(query, keys) * scale, -jnp.inf)
        weights = jnp.exp(scores - jnp.max(scores, axis=1, keepdims=True))
        total = jnp.sum(weights, axis=1, keepdims=True)
        probs = (weights * (1.0 / total)).astype(BF16)
        attended = dot(probs, values).astype(BF16)
        delta = jnp.sum(grad.astype(F32) * attended.astype(F32), axis=1, keepdims=True)
        score_grad = (probs.astype(F32) * (outer(grad, values) - delta)).astype(BF16)
        query_grad = (dot(score_grad, keys) * scale).astype(BF16)
        seen = dot(probs, lbuf[...]).astype(BF16)
        gup = (inner(low_qm, query_grad) + inner(seen, grad)).astype(BF16)
        lifted = jnp.where(lane >= rank, outer(grad, up), 0.0).astype(BF16)
        return attended, gup, outer(query_grad, up), inner(probs, lifted)

    together = 2 if span <= 2 * HEAD else 1

    def head_group(c, offset):
        first = place(c) * heads + offset
        results = [head(first + i) for i in range(together)]
        for i, (attended, gup, _, _) in enumerate(results):
            h = first + i
            att_ref[:, pl.ds(pl.multiple_of(h * HEAD, HEAD), HEAD)] = attended
            row = pl.multiple_of((offset + i) * 2 * rank, 2 * rank)
            cell = lax.rem(c, cells)
            acc[c // cells, lax.rem(cell, 2), cell // 2, pl.ds(row, 2 * rank), :] = gup
        lrq[...] += jnp.where(lane < rank, sum(r[2] for r in results), 0.0)
        lrv[...] += sum(r[3] for r in results)

    heads = CHUNK // HEAD
    soon = max(parts - 1, 0)

    @pl.loop(0, chunks + 1)
    def _(c):
        @pl.when(c < chunks)
        def _():
            for j in range(1, nu):
                crossed(j, c).wait_recv()

                @pl.when(has_next)
                def _():
                    onward(j, c, 2).start()

            @pl.when(jnp.logical_and(has_next, c + ahead < chunks))
            def _():
                onward(0, c + ahead, 2).start()

        @pl.when(c == 1)
        def _():
            for j in range(1, nu):
                low_crossed(j).wait_recv()

                @pl.when(has_next)
                def _():
                    low_onward(j).start()

            @pl.when(has_prev)
            def _():
                for j in range(nu):
                    low_arrived(j).wait_recv()

        @pl.when(c == chunks - 1)
        def _():
            each(0, soon, send_out)

        @pl.when(c > 0)
        def _():
            @pl.when(has_prev)
            def _():
                arrived(c - 1).wait_recv()

            @pl.loop(0, heads // together)
            def _(i):
                head_group(c - 1, i * together)


            @pl.when(lax.rem(c, cells) == 0)
            def _():
                swap(c // cells - 1).start()

            @pl.when(jnp.logical_and(lax.rem(c, cells) == 2 % cells, jnp.logical_and(c >= cells + 2, c < chunks)))
            def _():
                pair_sum((c - 2) // cells - 1)

    lrs[...] = lrv[...].astype(BF16)

    def terms(k, j, base):
        s = peer(j)
        return pltpu.make_async_remote_copy(
            src_ref=lrs.at[pl.ds(pl.multiple_of(base + s * rows, rows), rows)],
            dst_ref=lrin.at[k, j],
            send_sem=rsend.at[k, j], recv_sem=rrecv.at[k, j],
            device_id=(blk - k, s), device_id_type=MESH,
        )

    for j in range(1, nu):
        terms(0, j, span).start()

    @pl.when(has_prev)
    def _():
        for j in range(nu):
            terms(1, j, 0).start()

    each(soon, parts, pair_up)
    each(0, soon, plane_sum)

    lrq[...] += lrv[mine, :]
    for j in range(1, nu):
        terms(0, j, span).wait_recv()
        lrq[...] += lrin[0, j].astype(F32)

    @pl.when(has_next)
    def _():
        for j in range(nu):
            terms(1, j, 0).wait_recv()
            lrq[...] += lrin[1, j].astype(F32)

    lowb[0] = lrq[...].T.astype(BF16)
    tell().start()

    def project(p):
        for v in range(nu):
            at = pl.ds(pl.multiple_of((v * 2 + core) * strip + p * CHUNK, CHUNK), CHUNK)
            there = pl.ds(pl.multiple_of(v * strip + p * CHUNK, CHUNK), CHUNK)
            block = (dot(lowb[0], tok[:, at]) + dot(lowb[1], tok2[:, there])).astype(BF16)
            for i in range(heads):
                part[parts + p, v, pl.ds(i * 2 * rank, 2 * rank), :] = block[:, i * HEAD:(i + 1) * HEAD]
        for o in range(1, group):
            scatter(parts + p, o).start()

    def lay_out(n, t, outs):
        shared_here = res.at[n, 1 - core] if t == 1 else res.at[n, 1 - core, u]
        whole(shared_here, esend.at[t], erecv.at[n]).wait_recv()
        for v in range(nu if t == 1 else 1):
            for k in range(2):
                for i in range(heads):
                    h = ((v * 2 + k) * parts + n - t * parts) * heads + i
                    at = pl.ds(pl.multiple_of(h * HEAD, HEAD), HEAD)
                    w = v if t == 1 else u
                    outs[0][:, at] = res[n, k, w, pl.ds(i * 2 * rank, rank), :]
                    outs[1][:, at] = res[n, k, w, pl.ds(i * 2 * rank + rank, rank), :]

    whole(tok2, gsend.at[0], grecv.at[0]).wait_recv()
    tell().wait_recv()
    each(0, parts, project)

    def finish_up(n):
        lay_out(n, 0, (upq_out, upv_out))

    def finish_down(n):
        lay_out(n, 1, (downq_out, downv_out))

    order = []
    for p in range(parts):
        late = 3.0 if p >= soon else 0.0
        if p >= soon:
            order.append((-0.5, plane_sum, (p,)))
        order += [
            (0.0 + late, line_sum, (p,)), (3.5 + late, widen, (p, 0)),
            (14.0 + 0.7 * p, hand_over, (p, 0)), (17.0 + 0.7 * p, finish_up, (p,)),
        ]
        n, at = parts + p, 1.4 * p
        order += [
            (2.6 + at, plane_sum, (n,)), (7.0 + at, line_sum, (n,)), (12.0 + at, widen, (n, 1)),
            (17.5 + at, hand_over, (n, 1)), (19.5 + at, finish_down, (n,)),
        ]
    for _, work, what in sorted(order, key=lambda item: item[0]):
        work(*what)

    whole(tok2, gsend.at[0], grecv.at[0]).wait_send()
    tell().wait_send()
    whole(pair, psend.at[0], precv.at[0]).wait_send()
    whole(plane_in, asend.at[0], arecv.at[0]).wait_send()
    whole(line_in, bsend.at[0], brecv.at[0]).wait_send()
    whole(line_in, csend.at[0], crecv.at[0]).wait_send()
    for i in range(2):
        some = pl.ds(i * parts, parts)
        whole(
            plane_in.at[some, pl.ds(0, (inners, group)[i] - 1)], dsend.at[i], drecv.at[0]
        ).wait_send()
    whole(res.at[pl.ds(0, parts), 0, 0], esend.at[0], erecv.at[0]).wait_send()
    whole(res.at[pl.ds(parts, parts), 0], esend.at[1], erecv.at[0]).wait_send()

    everything = kv.at[:, mine, :]
    for j in range(1, nu):
        remote(everything, everything, xsend.at[j], xrecv.at[j - 1, 0], (blk, peer(j))).wait_send()

    @pl.when(has_next)
    def _():
        for j in range(nu):
            remote(everything, everything, fsend.at[j], frecv.at[0], (blk + 1, u)).wait_send()

    for j in range(1, nu):
        low_across(j).wait_send()

    @pl.when(has_next)
    def _():
        for j in range(nu):
            low_onward(j).wait_send()

    for j in range(1, nu):
        terms(0, j, span).wait_send()

    @pl.when(has_prev)
    def _():
        for j in range(nu):
            terms(1, j, 0).wait_send()


def grid_of(nb):
    half = nb // 2
    inners = 2 if half % 2 == 0 else 1
    return inners, half // inners


def fused(nb, nu, *operands):
    rows, width = operands[0].shape
    rank = operands[6].shape[0]
    span = nu * rows
    chunks = width // CHUNK
    cells = 2 * nu
    parts = chunks // cells
    inners, outers = grid_of(nb)
    group = nu * inners
    sub = CHUNK // inners
    lanes = 2 * rank
    dma = pltpu.SemaphoreType.DMA
    anywhere = pl.BlockSpec(memory_space=pl.ANY)
    here = pl.BlockSpec(memory_space=pltpu.VMEM)
    return pl.pallas_call(
        functools.partial(fused_kernel, nb, nu),
        out_shape=(
            pltpu.VMEM((rows, width), BF16),
            pltpu.VMEM((rank, width), BF16),
            pltpu.VMEM((rank, width), BF16),
            pltpu.VMEM((rank, width // nu), BF16),
            pltpu.VMEM((rank, width // nu), BF16),
        ),
        in_specs=[anywhere] * 9,
        out_specs=(here,) * 5,
        scratch_shapes=[
            pltpu.VMEM((2, 2 * span, width), BF16),
            pltpu.VMEM((2 * span, lanes), BF16),
            pltpu.VMEM((rows, width), BF16),
            pltpu.VMEM((rows, width), BF16),
            pltpu.VMEM((rows, width), BF16),
            pltpu.VMEM((lanes, width), BF16),
            pltpu.VMEM((lanes, width), BF16),
            pltpu.VMEM((rows, lanes), F32),
            pltpu.VMEM((2 * span, lanes), F32),
            pltpu.VMEM((2 * span, lanes), BF16),
            pltpu.VMEM((2, nu, rows, lanes), BF16),
            pltpu.VMEM((rows, width // 2), BF16),
            pltpu.VMEM((2, lanes, rows), BF16),
            pltpu.VMEM((parts, 2, nu, CHUNK, lanes), BF16),
            pltpu.VMEM((parts, nu, CHUNK, lanes), BF16),
            pltpu.VMEM((2 * parts, nu, CHUNK, lanes), BF16),
            pltpu.VMEM((2 * parts, group - 1, sub, lanes), BF16),
            pltpu.VMEM((2 * parts, sub, lanes), BF16),
            pltpu.VMEM((2 * parts, outers - 1, sub // outers, lanes), BF16),
            pltpu.VMEM((2 * parts, 2, nu, CHUNK, lanes), BF16),
            dma((9,)),
            dma((nu,)), dma((nu - 1, chunks)),
            dma((nu,)), dma((chunks,)),
            dma((nu,)), dma((nu,)), dma((nu,)), dma((nu,)),
            dma((2, nu)), dma((2, nu)),
            dma((1,)), dma((parts,)),
            dma((1,)), dma((2 * parts,)),
            dma((1,)), dma((2 * parts,)),
            dma((1,)), dma((2 * parts,)),
            dma((2,)), dma((2 * parts,)),
            dma((2,)), dma((2 * parts,)),
            dma((2,)), dma((2,)),
        ],
        compiler_params=pltpu.CompilerParams(
            collective_id=2, has_side_effects=True, vmem_limit_bytes=60_000_000
        ),
    )(*operands)


def fits(nb, nu, rows, width, rank):
    inners, outers = grid_of(nb)
    return (
        2 * rank == HEAD
        and width % (2 * nu * CHUNK) == 0
        and CHUNK % (16 * inners * outers) == 0
        and nu * rows <= CHUNK
    )


def deliver_kernel(*refs):
    count = len(refs) // 2
    sources, targets, sem = refs[:count], refs[count:2 * count], refs[-1]
    copies = [pltpu.make_async_copy(a, b, sem.at[i]) for i, (a, b) in enumerate(zip(sources, targets))]
    for copy in copies:
        copy.start()
    for copy in copies:
        copy.wait()


def deliver(*arrays):
    return pl.pallas_call(
        deliver_kernel,
        out_shape=tuple(jax.ShapeDtypeStruct(a.shape, a.dtype) for a in arrays),
        in_specs=[pl.BlockSpec(memory_space=pl.ANY)] * len(arrays),
        out_specs=tuple(pl.BlockSpec(memory_space=pl.ANY) for _ in arrays),
        scratch_shapes=[pltpu.SemaphoreType.DMA((len(arrays),))],
    )(*(pltpu.with_memory_space_constraint(a, pltpu.VMEM) for a in arrays))


def per_device(nb, nu, tokens, query_base, key_base, value_base, out_grad, down_q, up_q, down_v, up_v):
    operands = (tokens, query_base, key_base, value_base, out_grad, down_q.T, up_q, down_v.T, up_v)
    if fits(nb, nu, *tokens.shape, up_q.shape[0]):
        attended, grad_down_q, grad_down_v, grad_up_q, grad_up_v = deliver(*fused(nb, nu, *operands))
        return attended, grad_down_q.T, grad_up_q, grad_down_v.T, grad_up_v
    attended, gup, lowrank = attention(nb, nu, *operands)
    grad_down_q, grad_down_v, grad_up_q, grad_up_v = reduction(nb, nu, tokens, lowrank, gup)
    return attended, grad_down_q.T, grad_up_q, grad_down_v.T, grad_up_v


def solution(mesh):
    split = P(("blk", "uly"), None)
    return jax.shard_map(
        functools.partial(per_device, mesh.shape["blk"], mesh.shape["uly"]),
        mesh=mesh,
        in_specs=(split,) * 5 + (P(),) * 4,
        out_specs=(split, P(), P(None, "uly"), P(), P(None, "uly")),
        check_vma=False,
    )
```

```python
import functools

import jax
import jax.numpy as jnp
from jax import lax
from jax.experimental import pallas as pl
from jax.experimental.pallas import tpu as pltpu
from jax.sharding import PartitionSpec as P

HEAD = 128
CHUNK = 256
MESH = pl.DeviceIdType.MESH
F32 = jnp.float32
BF16 = jnp.bfloat16


def inner(left, right):
    return lax.dot_general(left, right, (((0,), (0,)), ((), ())), preferred_element_type=F32)


def outer(left, right):
    return lax.dot_general(left, right, (((1,), (1,)), ((), ())), preferred_element_type=F32)


def dot(left, right):
    return jnp.dot(left, right, preferred_element_type=F32)


def attention_kernel(
    nb, nu,
    tokens, query_base, key_base, value_base, out_grad, down_q, up_q, down_v, up_v,
    att_ref, gup_ref, low_out,
    kbuf, vbuf, lbuf, tok, qs, gs, downs, ups, lrq, lrv, lrin,
    local_sem, xsend, xrecv, fsend, frecv, lsend, lrecv, msend, mrecv, rsend, rrecv,
):
    blk = lax.axis_index("blk")
    u = lax.axis_index("uly")
    rows, width = tokens.shape
    rank = up_q.shape[0]
    span = nu * rows
    chunks = width // CHUNK
    has_prev = blk > 0
    has_next = blk < nb - 1
    mine = pl.ds(pl.multiple_of(span + u * rows, rows), rows)

    def peer(j):
        return lax.rem(u + j, nu)

    def source(j):
        return lax.rem(u - j + nu, nu)

    def cols(c):
        return pl.ds(pl.multiple_of(c * CHUNK, CHUNK), CHUNK)

    barrier = pltpu.get_barrier_semaphore()
    for j in range(1, nu):
        pl.semaphore_signal(barrier, inc=1, device_id=(blk, peer(j)), device_id_type=MESH)

    @pl.when(has_prev)
    def _():
        for j in range(nu):
            pl.semaphore_signal(barrier, inc=1, device_id=(blk - 1, peer(j)), device_id_type=MESH)

    @pl.when(has_next)
    def _():
        for j in range(nu):
            pl.semaphore_signal(barrier, inc=1, device_id=(blk + 1, peer(j)), device_id_type=MESH)

    local = [
        pltpu.make_async_copy(src, dst, local_sem.at[i])
        for i, (src, dst) in enumerate(
            (
                (tokens, tok), (down_q, downs.at[pl.ds(0, rank)]), (down_v, downs.at[pl.ds(rank, rank)]),
                (up_q, ups.at[pl.ds(0, rank)]), (up_v, ups.at[pl.ds(rank, rank)]),
                (value_base, vbuf.at[mine]), (key_base, kbuf.at[mine]),
                (query_base, qs), (out_grad, gs),
            )
        )
    ]
    for copy in local:
        copy.start()

    edge = jnp.logical_or(blk == 0, blk == nb - 1)

    @pl.when(edge)
    def _():
        pl.semaphore_wait(barrier, 2 * nu - 1)

    @pl.when(jnp.logical_not(edge))
    def _():
        pl.semaphore_wait(barrier, 3 * nu - 1)

    bufs = (kbuf, vbuf)

    def across(a, j, c):
        src = key_base.at[:, cols(c)] if a == 0 else vbuf.at[mine, cols(c)]
        return pltpu.make_async_remote_copy(
            src_ref=src, dst_ref=bufs[a].at[mine, cols(c)],
            send_sem=xsend.at[a, j, c], recv_sem=xrecv.at[a, j, c],
            device_id=(blk, peer(j)), device_id_type=MESH,
        )

    def crossed(a, j, c):
        here = bufs[a].at[pl.ds(pl.multiple_of(span + source(j) * rows, rows), rows), cols(c)]
        return pltpu.make_async_remote_copy(
            src_ref=here, dst_ref=here,
            send_sem=xsend.at[a, j, c], recv_sem=xrecv.at[a, j, c],
            device_id=(blk, peer(j)), device_id_type=MESH,
        )

    def onward(a, j, c):
        s = source(j)
        if a == 0 and j == 0:
            src = key_base.at[:, cols(c)]
        else:
            src = bufs[a].at[pl.ds(pl.multiple_of(span + s * rows, rows), rows), cols(c)]
        return pltpu.make_async_remote_copy(
            src_ref=src, dst_ref=bufs[a].at[pl.ds(pl.multiple_of(s * rows, rows), rows), cols(c)],
            send_sem=fsend.at[a, j, c], recv_sem=frecv.at[a, j, c],
            device_id=(blk + 1, u), device_id_type=MESH,
        )

    def arrived(a, j, c):
        here = bufs[a].at[pl.ds(pl.multiple_of(source(j) * rows, rows), rows), cols(c)]
        return pltpu.make_async_remote_copy(
            src_ref=here, dst_ref=here,
            send_sem=fsend.at[a, j, c], recv_sem=frecv.at[a, j, c],
            device_id=(blk, peer(1)), device_id_type=MESH,
        )

    def low_across(j):
        return pltpu.make_async_remote_copy(
            src_ref=lbuf.at[mine], dst_ref=lbuf.at[mine],
            send_sem=lsend.at[j], recv_sem=lrecv.at[j],
            device_id=(blk, peer(j)), device_id_type=MESH,
        )

    def low_crossed(j):
        here = lbuf.at[pl.ds(pl.multiple_of(span + source(j) * rows, rows), rows)]
        return pltpu.make_async_remote_copy(
            src_ref=here, dst_ref=here, send_sem=lsend.at[j], recv_sem=lrecv.at[j],
            device_id=(blk, peer(j)), device_id_type=MESH,
        )

    def low_onward(j):
        s = source(j)
        return pltpu.make_async_remote_copy(
            src_ref=lbuf.at[pl.ds(pl.multiple_of(span + s * rows, rows), rows)],
            dst_ref=lbuf.at[pl.ds(pl.multiple_of(s * rows, rows), rows)],
            send_sem=msend.at[j], recv_sem=mrecv.at[j],
            device_id=(blk + 1, u), device_id_type=MESH,
        )

    def low_arrived(j):
        here = lbuf.at[pl.ds(pl.multiple_of(source(j) * rows, rows), rows)]
        return pltpu.make_async_remote_copy(
            src_ref=here, dst_ref=here, send_sem=msend.at[j], recv_sem=mrecv.at[j],
            device_id=(blk, peer(1)), device_id_type=MESH,
        )

    early = min(3 * 512 // CHUNK, chunks)
    ahead = min(2048 // CHUNK, chunks)
    for c in range(early):
        for j in range(1, nu):
            across(0, j, c).start()

    @pl.when(has_next)
    def _():
        for c in range(ahead):
            onward(0, 0, c).start()

    lane = lax.broadcasted_iota(jnp.int32, (rows, 2 * rank), 1)
    for i in range(3):
        local[i].wait()
    low = outer(tok[...], downs[...])
    low_qm = jnp.where(lane < rank, low, 0.0).astype(BF16)
    low_vm = jnp.where(lane >= rank, low, 0.0).astype(BF16)
    lbuf[mine, :] = low_vm
    for i in range(3, 6):
        local[i].wait()

    @pl.loop(0, chunks)
    def _(c):
        part = dot(low_vm, ups[:, cols(c)])
        vbuf[mine, cols(c)] = (vbuf[mine, cols(c)].astype(F32) + part).astype(BF16)

    for j in range(1, nu):
        low_across(j).start()

    @pl.when(has_next)
    def _():
        low_onward(0).start()

    @pl.loop(0, chunks)
    def _(c):
        @pl.when(c >= early)
        def _():
            for j in range(1, nu):
                across(0, j, c).start()

        for j in range(1, nu):
            across(1, j, c).start()

    @pl.when(has_next)
    def _():
        for c in range(ahead):
            onward(1, 0, c).start()

    lrq[...] = jnp.zeros_like(lrq)
    lrv[...] = jnp.zeros_like(lrv)

    @pl.when(jnp.logical_not(has_prev))
    def _():
        kbuf[pl.ds(0, span), :] = jnp.zeros((span, width), BF16)
        vbuf[pl.ds(0, span), :] = jnp.zeros((span, width), BF16)
        lbuf[pl.ds(0, span), :] = jnp.zeros((span, 2 * rank), BF16)

    for i in range(6, 9):
        local[i].wait()

    scale = HEAD ** (-0.5)
    key_at = lax.broadcasted_iota(jnp.int32, (rows, 2 * span), 1)
    usable = jnp.logical_or(key_at >= span, has_prev)

    def head(h):
        at = pl.ds(pl.multiple_of(h * HEAD, HEAD), HEAD)
        up = ups[:, at]
        keys = kbuf[:, at]
        values = vbuf[:, at]
        grad = gs[:, at]
        query = (qs[:, at].astype(F32) + dot(low_qm, up)).astype(BF16)
        scores = jnp.where(usable, outer(query, keys) * scale, -jnp.inf)
        weights = jnp.exp(scores - jnp.max(scores, axis=1, keepdims=True))
        total = jnp.sum(weights, axis=1, keepdims=True)
        probs = (weights * (1.0 / total)).astype(BF16)
        attended = dot(probs, values).astype(BF16)
        delta = jnp.sum(grad.astype(F32) * attended.astype(F32), axis=1, keepdims=True)
        score_grad = (probs.astype(F32) * (outer(grad, values) - delta)).astype(BF16)
        query_grad = (dot(score_grad, keys) * scale).astype(BF16)
        seen = dot(probs, lbuf[...]).astype(BF16)
        gup = (inner(low_qm, query_grad) + inner(seen, grad)).astype(BF16)
        lifted = jnp.where(lane >= rank, outer(grad, up), 0.0).astype(BF16)
        return attended, gup, outer(query_grad, up), inner(probs, lifted)

    together = 2 if span <= 2 * HEAD else 1

    def head_group(first):
        results = [head(first + i) for i in range(together)]
        for i, (attended, gup, _, _) in enumerate(results):
            h = first + i
            att_ref[:, pl.ds(pl.multiple_of(h * HEAD, HEAD), HEAD)] = attended
            gup_ref[pl.ds(pl.multiple_of(h * 2 * rank, 2 * rank), 2 * rank), :] = gup
        lrq[...] += jnp.where(lane < rank, sum(r[2] for r in results), 0.0)
        lrv[...] += sum(r[3] for r in results)

    heads = CHUNK // HEAD

    @pl.loop(0, chunks + 1)
    def _(c):
        @pl.when(c == 0)
        def _():
            for j in range(1, nu):
                low_crossed(j).wait_recv()

                @pl.when(has_next)
                def _():
                    low_onward(j).start()

            @pl.when(has_prev)
            def _():
                for j in range(nu):
                    low_arrived(j).wait_recv()

        @pl.when(c < chunks)
        def _():
            for a in range(2):
                for j in range(1, nu):
                    crossed(a, j, c).wait_recv()

                    @pl.when(has_next)
                    def _():
                        onward(a, j, c).start()

            @pl.when(jnp.logical_and(has_next, c + ahead < chunks))
            def _():
                for a in range(2):
                    onward(a, 0, c + ahead).start()

        @pl.when(c > 0)
        def _():
            @pl.when(has_prev)
            def _():
                for a in range(2):
                    for j in range(nu):
                        arrived(a, j, c - 1).wait_recv()

            @pl.loop(0, heads // together)
            def _(i):
                head_group((c - 1) * heads + i * together)

    def terms(k, j, base):
        s = peer(j)
        return pltpu.make_async_remote_copy(
            src_ref=lrv.at[pl.ds(pl.multiple_of(base + s * rows, rows), rows)],
            dst_ref=lrin.at[k, j],
            send_sem=rsend.at[k, j], recv_sem=rrecv.at[k, j],
            device_id=(blk - k, s), device_id_type=MESH,
        )

    for j in range(1, nu):
        terms(0, j, span).start()

    @pl.when(has_prev)
    def _():
        for j in range(nu):
            terms(1, j, 0).start()

    @pl.loop(0, chunks)
    def _(c):
        for a in range(2):
            for j in range(1, nu):
                across(a, j, c).wait_send()

            @pl.when(has_next)
            def _():
                for j in range(nu):
                    onward(a, j, c).wait_send()

    for j in range(1, nu):
        low_across(j).wait_send()

    @pl.when(has_next)
    def _():
        for j in range(nu):
            low_onward(j).wait_send()

    lrq[...] += lrv[mine, :]
    for j in range(1, nu):
        terms(0, j, span).wait_recv()
        lrq[...] += lrin[0, j]

    @pl.when(has_next)
    def _():
        for j in range(nu):
            terms(1, j, 0).wait_recv()
            lrq[...] += lrin[1, j]

    low_out[...] = lrq[...].astype(BF16)
    for j in range(1, nu):
        terms(0, j, span).wait_send()

    @pl.when(has_prev)
    def _():
        for j in range(nu):
            terms(1, j, 0).wait_send()


def attention(nb, nu, *operands):
    rows, width = operands[0].shape
    rank = operands[6].shape[0]
    span = nu * rows
    chunks = width // CHUNK
    dma = pltpu.SemaphoreType.DMA
    anywhere = pl.BlockSpec(memory_space=pl.ANY)
    here = pl.BlockSpec(memory_space=pltpu.VMEM)
    return pl.pallas_call(
        functools.partial(attention_kernel, nb, nu),
        out_shape=(
            jax.ShapeDtypeStruct((rows, width), BF16),
            jax.ShapeDtypeStruct((width // HEAD * 2 * rank, HEAD), BF16),
            jax.ShapeDtypeStruct((rows, 2 * rank), BF16),
        ),
        in_specs=[anywhere] * 9,
        out_specs=(here, here, here),
        scratch_shapes=[
            pltpu.VMEM((2 * span, width), BF16),
            pltpu.VMEM((2 * span, width), BF16),
            pltpu.VMEM((2 * span, 2 * rank), BF16),
            pltpu.VMEM((rows, width), BF16),
            pltpu.VMEM((rows, width), BF16),
            pltpu.VMEM((rows, width), BF16),
            pltpu.VMEM((2 * rank, width), BF16),
            pltpu.VMEM((2 * rank, width), BF16),
            pltpu.VMEM((rows, 2 * rank), F32),
            pltpu.VMEM((2 * span, 2 * rank), F32),
            pltpu.VMEM((2, nu, rows, 2 * rank), F32),
            dma((9,)),
            dma((2, nu, chunks)), dma((2, nu, chunks)),
            dma((2, nu, chunks)), dma((2, nu, chunks)),
            dma((nu,)), dma((nu,)), dma((nu,)), dma((nu,)),
            dma((2, nu)), dma((2, nu)),
        ],
        compiler_params=pltpu.CompilerParams(
            collective_id=0, has_side_effects=True, vmem_limit_bytes=65_000_000
        ),
    )(*operands)


def reduction_kernel(
    nb, nu,
    tokens, lowrank, gup,
    downq_out, downv_out, upq_out, upv_out,
    tok, terms, pair, part, plane_in, line, line_in, down, ups, flat,
    local_sem, psend, precv, asend, arecv, bsend, brecv, csend, crecv, dsend, drecv, esend, erecv,
):
    blk = lax.axis_index("blk")
    u = lax.axis_index("uly")
    core = lax.rem(blk, 2)
    chip = blk // 2
    other = chip * 2 + 1 - core
    half = nb // 2
    inners = plane_in.shape[1] // nu
    outers = half // inners
    y = lax.rem(chip, inners)
    z = chip // inners
    group = nu * inners
    rows, width = tokens.shape
    rank = upq_out.shape[0]
    region = pair.shape[2]
    sub = plane_in.shape[2]
    piece = line_in.shape[2]

    def split(o, sign):
        pu = lax.rem(u + sign * (o // inners) + nu, nu)
        py = lax.rem(y + sign * lax.rem(o, inners) + inners, inners)
        return pu, py

    def plane_dev(o):
        pu, py = split(o, 1)
        return ((z * inners + py) * 2 + core, pu)

    def peer_z(o):
        return lax.rem(z + o, outers)

    def from_z(o):
        return lax.rem(z - o + outers, outers)

    def line_dev(o):
        return ((peer_z(o) * inners + y) * 2 + core, u)

    def subs(p):
        return pl.ds(pl.multiple_of(p * sub, sub), sub)

    barrier = pltpu.get_barrier_semaphore()
    pl.semaphore_signal(barrier, inc=1, device_id=(other, u), device_id_type=MESH)
    for o in range(1, group):
        pl.semaphore_signal(barrier, inc=1, device_id=plane_dev(o), device_id_type=MESH)
    for o in range(1, outers):
        pl.semaphore_signal(barrier, inc=1, device_id=line_dev(o), device_id_type=MESH)

    load = pltpu.make_async_copy(tokens, tok, local_sem.at[0])
    load.start()
    pl.semaphore_wait(barrier, group + outers - 1)

    def remote(src, dst, send, recv, device):
        return pltpu.make_async_remote_copy(
            src_ref=src, dst_ref=dst, send_sem=send, recv_sem=recv,
            device_id=device, device_id_type=MESH,
        )

    def swap(t, v):
        rows_at = pl.ds(pl.multiple_of((v * 2 + 1 - core) * region, region), region)
        return remote(
            (terms if t == 0 else gup).at[rows_at], pair.at[t, v],
            psend.at[t, v], precv.at[t, v], (other, u),
        )

    def scatter(t, o):
        pu, py = split(o, 1)
        return remote(
            part.at[t, pu, subs(py)], plane_in.at[t, o],
            asend.at[t, o], arecv.at[t, o], plane_dev(o),
        )

    def pass_on(t, o):
        at = pl.ds(pl.multiple_of(peer_z(o) * piece, piece), piece)
        return remote(
            line.at[t, at], line_in.at[t, o], bsend.at[t, o], brecv.at[t, o], line_dev(o)
        )

    def whole(t, v, k, p):
        return down.at[v, k, subs(p)] if t == 0 else ups.at[k, subs(p)]

    def piece_at(p, q):
        return pl.ds(pl.multiple_of(p * sub + q * piece, piece), piece)

    def small(t, q):
        return down.at[u, core, piece_at(y, q)] if t == 0 else ups.at[core, piece_at(y, q)]

    def along(t, o):
        return remote(small(t, z), small(t, z), csend.at[t, o], crecv.at[t, o], line_dev(o))

    def came(t, o):
        here = small(t, from_z(o))
        return remote(here, here, csend.at[t, o], crecv.at[t, o], line_dev(o))

    def spread(t, o):
        here = whole(t, u, core, y)
        return remote(here, here, dsend.at[t, o], drecv.at[t, o], plane_dev(o))

    def landed(t, o):
        pu, py = split(o, -1)
        here = whole(t, pu, core, py)
        return remote(here, here, dsend.at[t, o], drecv.at[t, o], (other, u))

    def share(t, o):
        pu, py = split(o, -1)
        here = whole(t, pu, core, py)
        return remote(here, here, esend.at[t, o], erecv.at[t, o], (other, u))

    def shared(t, o):
        pu, py = split(o, -1)
        here = whole(t, pu, 1 - core, py)
        return remote(here, here, esend.at[t, o], erecv.at[t, o], (other, u))

    if part.shape[2] > region:
        part[...] = jnp.zeros_like(part)
    for v in range(nu):
        swap(1, v).start()

    load.wait()
    lows = lowrank[...]

    @pl.loop(0, width // HEAD)
    def _(h):
        cols = pl.ds(pl.multiple_of(h * HEAD, HEAD), HEAD)
        here = pl.ds(pl.multiple_of(h * 2 * rank, 2 * rank), 2 * rank)
        terms[here, :] = inner(lows, tok[:, cols]).astype(BF16)

    for v in range(nu):
        swap(0, v).start()

    for t in (1, 0):
        for v in range(nu):
            rows_at = pl.ds(pl.multiple_of((v * 2 + core) * region, region), region)
            own = (terms if t == 0 else gup)[rows_at, :]
            swap(t, v).wait_recv()
            part[t, v, pl.ds(0, region), :] = (
                own.astype(F32) + pair[t, v].astype(F32)
            ).astype(BF16)
        for o in range(1, group):
            scatter(t, o).start()

    for t in (1, 0):
        total = part[t, u, subs(y), :].astype(F32)
        for o in range(1, group):
            scatter(t, o).wait_recv()
            total = total + plane_in[t, o].astype(F32)
        line[t, :, :] = total.astype(BF16)
        for o in range(1, outers):
            pass_on(t, o).start()

    for t in (1, 0):
        total = line[t, pl.ds(pl.multiple_of(z * piece, piece), piece), :].astype(F32)
        for o in range(1, outers):
            pass_on(t, o).wait_recv()
            total = total + line_in[t, o].astype(F32)
        small(t, z)[...] = total.astype(BF16)
        for o in range(1, outers):
            along(t, o).start()

    counts = (group, inners)
    for t in (1, 0):
        for o in range(1, outers):
            came(t, o).wait_recv()
        for o in range(1, counts[t]):
            spread(t, o).start()
        share(t, 0).start()

    for t in (1, 0):
        for o in range(1, counts[t]):
            landed(t, o).wait_recv()
            share(t, o).start()

    for t in (1, 0):
        for o in range(counts[t]):
            shared(t, o).wait_recv()
        places = [(v, k) for v in range(nu if t == 0 else 1) for k in range(2)]
        for n, (v, k) in enumerate(places):
            flat[pl.ds(n * region, region), :] = (
                down[v, k, pl.ds(0, region), :] if t == 0 else ups[k, pl.ds(0, region), :]
            )
        outs = (downq_out, downv_out) if t == 0 else (upq_out, upv_out)
        for h in range(len(places) * region // (2 * rank)):
            cols = pl.ds(h * HEAD, HEAD)
            outs[0][:, cols] = flat[pl.ds(h * 2 * rank, rank), :]
            outs[1][:, cols] = flat[pl.ds(h * 2 * rank + rank, rank), :]

    for t in (1, 0):
        for v in range(nu):
            swap(t, v).wait_send()
        for o in range(1, group):
            scatter(t, o).wait_send()
        for o in range(1, outers):
            pass_on(t, o).wait_send()
            along(t, o).wait_send()
        for o in range(1, counts[t]):
            spread(t, o).wait_send()
        for o in range(counts[t]):
            share(t, o).wait_send()


def reduction(nb, nu, tokens, lowrank, gup):
    rows, width = tokens.shape
    rank = lowrank.shape[1] // 2
    half = nb // 2
    inners = 2 if half % 2 == 0 else 1
    outers = half // inners
    group = nu * inners
    region = width // (2 * nu)
    piece = -(-region // (16 * half)) * 16
    sub = outers * piece
    held = half * piece
    dma = pltpu.SemaphoreType.DMA
    here = pl.BlockSpec(memory_space=pltpu.VMEM)
    lanes = lowrank.shape[1]
    return pl.pallas_call(
        functools.partial(reduction_kernel, nb, nu),
        out_shape=(
            jax.ShapeDtypeStruct((rank, width), BF16),
            jax.ShapeDtypeStruct((rank, width), BF16),
            jax.ShapeDtypeStruct((rank, width // nu), BF16),
            jax.ShapeDtypeStruct((rank, width // nu), BF16),
        ),
        in_specs=[pl.BlockSpec(memory_space=pl.ANY), here, here],
        out_specs=(here, here, here, here),
        scratch_shapes=[
            pltpu.VMEM((rows, width), BF16),
            pltpu.VMEM((width, lanes), BF16),
            pltpu.VMEM((2, nu, region, lanes), BF16),
            pltpu.VMEM((2, nu, held, lanes), BF16),
            pltpu.VMEM((2, group, sub, lanes), BF16),
            pltpu.VMEM((2, sub, lanes), BF16),
            pltpu.VMEM((2, outers, piece, lanes), BF16),
            pltpu.VMEM((nu, 2, held, lanes), BF16),
            pltpu.VMEM((2, held, lanes), BF16),
            pltpu.VMEM((2 * nu * region, lanes), BF16),
            dma((1,)),
            dma((2, nu)), dma((2, nu)),
            dma((2, group)), dma((2, group)),
            dma((2, outers)), dma((2, outers)),
            dma((2, outers)), dma((2, outers)),
            dma((2, group)), dma((2, group)),
            dma((2, group)), dma((2, group)),
        ],
        compiler_params=pltpu.CompilerParams(collective_id=1, has_side_effects=True),
    )(tokens, lowrank, gup)


def fused_kernel(
    nb, nu,
    tokens, query_base, key_base, value_base, out_grad, down_q, up_q, down_v, up_v,
    att_ref, downq_out, downv_out, upq_out, upv_out,
    kv, lbuf, tok, qs, gs, downs, ups, lrq, lrv, lrs, lrin,
    tok2, lowb, acc, pair, part, plane_in, line, line_in, res,
    local_sem, xsend, xrecv, fsend, frecv, lsend, lrecv, msend, mrecv, rsend, rrecv,
    psend, precv, asend, arecv, bsend, brecv, csend, crecv, dsend, drecv, esend, erecv, gsend, grecv,
):
    kbuf, vbuf = kv.at[0], kv.at[1]
    blk = lax.axis_index("blk")
    u = lax.axis_index("uly")
    rows, width = tokens.shape
    rank = up_q.shape[0]
    span = nu * rows
    chunks = width // CHUNK
    has_prev = blk > 0
    has_next = blk < nb - 1
    mine = pl.ds(pl.multiple_of(span + u * rows, rows), rows)

    def peer(j):
        return lax.rem(u + j, nu)

    def source(j):
        return lax.rem(u - j + nu, nu)

    cells = 2 * nu
    parts = chunks // cells
    core = lax.rem(blk, 2)
    chip = blk // 2
    other = chip * 2 + 1 - core
    inners, outers = grid_of(nb)
    group = nu * inners
    y = lax.rem(chip, inners)
    z = chip // inners
    sub = CHUNK // inners
    piece = sub // outers

    def place(c):
        return lax.rem(c, cells) * parts + c // cells

    def cols(c):
        return pl.ds(pl.multiple_of(place(c) * CHUNK, CHUNK), CHUNK)

    def remote(src, dst, send, recv, device):
        return pltpu.make_async_remote_copy(
            src_ref=src, dst_ref=dst, send_sem=send, recv_sem=recv,
            device_id=device, device_id_type=MESH,
        )

    def split(o, sign):
        pu = lax.rem(u + sign * (o // inners) + nu, nu)
        py = lax.rem(y + sign * lax.rem(o, inners) + inners, inners)
        return pu, py

    def plane_dev(o):
        pu, py = split(o, 1)
        return ((z * inners + py) * 2 + core, pu)

    def peer_z(o):
        return lax.rem(z + o, outers)

    def from_z(o):
        return lax.rem(z - o + outers, outers)

    def line_dev(o):
        return ((peer_z(o) * inners + y) * 2 + core, u)

    def subs(p):
        return pl.ds(pl.multiple_of(p * sub, sub), sub)

    def piece_at(p, q):
        return pl.ds(pl.multiple_of(p * sub + q * piece, piece), piece)

    def swap(n):
        return remote(
            acc.at[n, 1 - core], pair.at[n], psend.at[0], precv.at[n], (other, u)
        )

    def scatter(n, o):
        pu, py = split(o, 1)
        return remote(
            part.at[n, pu, subs(py)], plane_in.at[n, o - 1],
            asend.at[0], arecv.at[n], plane_dev(o),
        )

    def pass_on(n, o):
        at = pl.ds(pl.multiple_of(peer_z(o) * piece, piece), piece)
        return remote(
            line.at[n, at], line_in.at[n, o - 1], bsend.at[0], brecv.at[n], line_dev(o)
        )

    def along(n, o):
        here = res.at[n, core, u, piece_at(y, z)]
        return remote(here, here, csend.at[0], crecv.at[n], line_dev(o))

    def spread(n, o, t):
        here = res.at[n, core, u, subs(y)]
        return remote(here, here, dsend.at[t], drecv.at[n], plane_dev(o))

    def share(n, t):
        here = res.at[n, core] if t == 1 else res.at[n, core, u]
        return remote(here, here, esend.at[t], erecv.at[n], (other, u))

    def whole(src, send, recv):
        return remote(src, src, send, recv, (other, u))

    strip = parts * CHUNK

    def lend(v):
        at = pl.ds(pl.multiple_of((v * 2 + 1 - core) * strip, strip), strip)
        return remote(
            tokens.at[:, at], tok2.at[:, pl.ds(v * strip, strip)], gsend.at[0], grecv.at[0], (other, u)
        )

    def tell():
        return remote(lowb.at[0], lowb.at[1], gsend.at[1], grecv.at[1], (other, u))

    def pair_sum(n):
        swap(n).wait_recv()
        part[n] = (acc[n, core].astype(F32) + pair[n].astype(F32)).astype(BF16)

    def send_out(n):
        for o in range(1, group):
            scatter(n, o).start()

    def pair_up(n):
        pair_sum(n)
        send_out(n)

    def plane_sum(n):
        total = part[n, u, subs(y), :].astype(F32)
        whole(plane_in.at[n], asend.at[0], arecv.at[n]).wait_recv()
        for o in range(1, group):
            total = total + plane_in[n, o - 1].astype(F32)
        line[n] = total.astype(BF16)
        for o in range(1, outers):
            pass_on(n, o).start()

    def line_sum(n):
        total = line[n, pl.ds(pl.multiple_of(z * piece, piece), piece), :].astype(F32)
        whole(line_in.at[n], bsend.at[0], brecv.at[n]).wait_recv()
        for o in range(1, outers):
            total = total + line_in[n, o - 1].astype(F32)
        res[n, core, u, piece_at(y, z), :] = total.astype(BF16)
        for o in range(1, outers):
            along(n, o).start()

    def widen(n, t):
        whole(line_in.at[n], csend.at[0], crecv.at[n]).wait_recv()
        for o in range(1, (inners, group)[t]):
            spread(n, o, t).start()

    def hand_over(n, t):
        whole(plane_in.at[n, pl.ds(0, (inners, group)[t] - 1)], dsend.at[t], drecv.at[n]).wait_recv()
        share(n, t).start()

    def each(first, stop, work):
        @pl.loop(first, stop)
        def _(n):
            work(n)

    barrier = pltpu.get_barrier_semaphore()
    for j in range(1, nu):
        pl.semaphore_signal(barrier, inc=1, device_id=(blk, peer(j)), device_id_type=MESH)

    @pl.when(has_prev)
    def _():
        for j in range(nu):
            pl.semaphore_signal(barrier, inc=1, device_id=(blk - 1, peer(j)), device_id_type=MESH)

    @pl.when(has_next)
    def _():
        for j in range(nu):
            pl.semaphore_signal(barrier, inc=1, device_id=(blk + 1, peer(j)), device_id_type=MESH)

    for o in range(1, group):
        pl.semaphore_signal(barrier, inc=1, device_id=plane_dev(o), device_id_type=MESH)
    for o in range(1, outers):
        pl.semaphore_signal(barrier, inc=1, device_id=line_dev(o), device_id_type=MESH)

    local = [
        pltpu.make_async_copy(src, dst, local_sem.at[i])
        for i, (src, dst) in enumerate(
            (
                (tokens, tok), (down_q, downs.at[pl.ds(0, rank)]), (down_v, downs.at[pl.ds(rank, rank)]),
                (up_q, ups.at[pl.ds(0, rank)]), (up_v, ups.at[pl.ds(rank, rank)]),
                (value_base, vbuf.at[mine]), (key_base, kbuf.at[mine]),
                (query_base, qs), (out_grad, gs),
            )
        )
    ]
    for copy in local:
        copy.start()

    lane = lax.broadcasted_iota(jnp.int32, (rows, 2 * rank), 1)
    for i in range(3):
        local[i].wait()
    low = outer(tok[...], downs[...])
    low_qm = jnp.where(lane < rank, low, 0.0).astype(BF16)
    low_vm = jnp.where(lane >= rank, low, 0.0).astype(BF16)
    lbuf[mine, :] = low_vm
    edge = jnp.logical_or(blk == 0, blk == nb - 1)

    @pl.when(edge)
    def _():
        pl.semaphore_wait(barrier, 2 * nu - 1 + group + outers - 2)

    @pl.when(jnp.logical_not(edge))
    def _():
        pl.semaphore_wait(barrier, 3 * nu - 1 + group + outers - 2)

    def rows_of(first, j):
        return pl.ds(pl.multiple_of(first + source(j) * rows, rows), rows)

    def cross(j, c, what):
        at = cols(c)
        src, dst = {
            0: (key_base.at[:, at], kv.at[0, mine, at]),
            1: (kv.at[1, mine, at], kv.at[1, mine, at]),
            2: (kv.at[:, mine, at], kv.at[:, mine, at]),
        }[what]
        return remote(src, dst, xsend.at[j], xrecv.at[j - 1, c], (blk, peer(j)))

    def crossed(j, c):
        here = kv.at[:, rows_of(span, j), cols(c)]
        return remote(here, here, xsend.at[j], xrecv.at[j - 1, c], (blk, peer(j)))

    def onward(j, c, what):
        at = cols(c)
        old, new = rows_of(span, j), rows_of(0, j)
        src, dst = {
            0: (key_base.at[:, at], kv.at[0, new, at]),
            1: (kv.at[1, old, at], kv.at[1, new, at]),
            2: (kv.at[:, old, at], kv.at[:, new, at]),
        }[what]
        return remote(src, dst, fsend.at[j], frecv.at[c], (blk + 1, u))

    def arrived(c):
        here = kv.at[:, pl.ds(0, span), cols(c)]
        return remote(here, here, fsend.at[0], frecv.at[c], (blk, peer(1)))

    def low_across(j):
        return pltpu.make_async_remote_copy(
            src_ref=lbuf.at[mine], dst_ref=lbuf.at[mine],
            send_sem=lsend.at[j], recv_sem=lrecv.at[j],
            device_id=(blk, peer(j)), device_id_type=MESH,
        )

    def low_crossed(j):
        here = lbuf.at[pl.ds(pl.multiple_of(span + source(j) * rows, rows), rows)]
        return pltpu.make_async_remote_copy(
            src_ref=here, dst_ref=here, send_sem=lsend.at[j], recv_sem=lrecv.at[j],
            device_id=(blk, peer(j)), device_id_type=MESH,
        )

    def low_onward(j):
        s = source(j)
        return pltpu.make_async_remote_copy(
            src_ref=lbuf.at[pl.ds(pl.multiple_of(span + s * rows, rows), rows)],
            dst_ref=lbuf.at[pl.ds(pl.multiple_of(s * rows, rows), rows)],
            send_sem=msend.at[j], recv_sem=mrecv.at[j],
            device_id=(blk + 1, u), device_id_type=MESH,
        )

    def low_arrived(j):
        here = lbuf.at[pl.ds(pl.multiple_of(source(j) * rows, rows), rows)]
        return pltpu.make_async_remote_copy(
            src_ref=here, dst_ref=here, send_sem=msend.at[j], recv_sem=mrecv.at[j],
            device_id=(blk, peer(1)), device_id_type=MESH,
        )

    early = min(1, chunks)
    ahead = min(3, chunks)
    for c in range(early):
        for j in range(1, nu):
            cross(j, c, 0).start()

    @pl.when(has_next)
    def _():
        for c in range(ahead):
            onward(0, c, 0).start()

    for v in range(nu):
        lend(v).start()

    for i in range(3, 7):
        local[i].wait()

    def lift(c):
        extra = dot(low_vm, ups[:, cols(c)])
        vbuf[mine, cols(c)] = (vbuf[mine, cols(c)].astype(F32) + extra).astype(BF16)

    for j in range(1, nu):
        low_across(j).start()

    @pl.when(has_next)
    def _():
        low_onward(0).start()

    @pl.loop(0, early)
    def _(c):
        lift(c)
        for j in range(1, nu):
            cross(j, c, 1).start()

    @pl.loop(early, ahead)
    def _(c):
        lift(c)
        for j in range(1, nu):
            cross(j, c, 2).start()

    @pl.when(has_next)
    def _():
        @pl.loop(0, ahead)
        def _(c):
            onward(0, c, 1).start()

    @pl.loop(ahead, chunks)
    def _(c):
        lift(c)
        for j in range(1, nu):
            cross(j, c, 2).start()

    lrq[...] = jnp.zeros_like(lrq)
    lrv[...] = jnp.zeros_like(lrv)

    @pl.when(jnp.logical_not(has_prev))
    def _():
        kbuf[pl.ds(0, span), :] = jnp.zeros((span, width), BF16)
        vbuf[pl.ds(0, span), :] = jnp.zeros((span, width), BF16)
        lbuf[pl.ds(0, span), :] = jnp.zeros((span, 2 * rank), BF16)

    for i in range(7, 9):
        local[i].wait()

    scale = HEAD ** (-0.5)
    key_at = lax.broadcasted_iota(jnp.int32, (rows, 2 * span), 1)
    usable = jnp.logical_or(key_at >= span, has_prev)

    def head(h):
        at = pl.ds(pl.multiple_of(h * HEAD, HEAD), HEAD)
        up = ups[:, at]
        keys = kbuf[:, at]
        values = vbuf[:, at]
        grad = gs[:, at]
        query = (qs[:, at].astype(F32) + dot(low_qm, up)).astype(BF16)
        scores = jnp.where(usable, outer(query, keys) * scale, -jnp.inf)
        weights = jnp.exp(scores - jnp.max(scores, axis=1, keepdims=True))
        total = jnp.sum(weights, axis=1, keepdims=True)
        probs = (weights * (1.0 / total)).astype(BF16)
        attended = dot(probs, values).astype(BF16)
        delta = jnp.sum(grad.astype(F32) * attended.astype(F32), axis=1, keepdims=True)
        score_grad = (probs.astype(F32) * (outer(grad, values) - delta)).astype(BF16)
        query_grad = (dot(score_grad, keys) * scale).astype(BF16)
        seen = dot(probs, lbuf[...]).astype(BF16)
        gup = (inner(low_qm, query_grad) + inner(seen, grad)).astype(BF16)
        lifted = jnp.where(lane >= rank, outer(grad, up), 0.0).astype(BF16)
        return attended, gup, outer(query_grad, up), inner(probs, lifted)

    together = 2 if span <= 2 * HEAD else 1

    def head_group(c, offset):
        first = place(c) * heads + offset
        results = [head(first + i) for i in range(together)]
        for i, (attended, gup, _, _) in enumerate(results):
            h = first + i
            att_ref[:, pl.ds(pl.multiple_of(h * HEAD, HEAD), HEAD)] = attended
            row = pl.multiple_of((offset + i) * 2 * rank, 2 * rank)
            cell = lax.rem(c, cells)
            acc[c // cells, lax.rem(cell, 2), cell // 2, pl.ds(row, 2 * rank), :] = gup
        lrq[...] += jnp.where(lane < rank, sum(r[2] for r in results), 0.0)
        lrv[...] += sum(r[3] for r in results)

    heads = CHUNK // HEAD
    soon = max(parts - 1, 0)

    @pl.loop(0, chunks + 1)
    def _(c):
        @pl.when(c < chunks)
        def _():
            for j in range(1, nu):
                crossed(j, c).wait_recv()

                @pl.when(has_next)
                def _():
                    onward(j, c, 2).start()

            @pl.when(jnp.logical_and(has_next, c + ahead < chunks))
            def _():
                onward(0, c + ahead, 2).start()

        @pl.when(c == 1)
        def _():
            for j in range(1, nu):
                low_crossed(j).wait_recv()

                @pl.when(has_next)
                def _():
                    low_onward(j).start()

            @pl.when(has_prev)
            def _():
                for j in range(nu):
                    low_arrived(j).wait_recv()

        @pl.when(c == chunks - 1)
        def _():
            each(0, soon, send_out)

        @pl.when(c > 0)
        def _():
            @pl.when(has_prev)
            def _():
                arrived(c - 1).wait_recv()

            @pl.loop(0, heads // together)
            def _(i):
                head_group(c - 1, i * together)


            @pl.when(lax.rem(c, cells) == 0)
            def _():
                swap(c // cells - 1).start()

            @pl.when(jnp.logical_and(lax.rem(c, cells) == 2 % cells, jnp.logical_and(c >= cells + 2, c < chunks)))
            def _():
                pair_sum((c - 2) // cells - 1)

    lrs[...] = lrv[...].astype(BF16)

    def terms(k, j, base):
        s = peer(j)
        return pltpu.make_async_remote_copy(
            src_ref=lrs.at[pl.ds(pl.multiple_of(base + s * rows, rows), rows)],
            dst_ref=lrin.at[k, j],
            send_sem=rsend.at[k, j], recv_sem=rrecv.at[k, j],
            device_id=(blk - k, s), device_id_type=MESH,
        )

    for j in range(1, nu):
        terms(0, j, span).start()

    @pl.when(has_prev)
    def _():
        for j in range(nu):
            terms(1, j, 0).start()

    each(soon, parts, pair_up)
    each(0, soon, plane_sum)

    lrq[...] += lrv[mine, :]
    for j in range(1, nu):
        terms(0, j, span).wait_recv()
        lrq[...] += lrin[0, j].astype(F32)

    @pl.when(has_next)
    def _():
        for j in range(nu):
            terms(1, j, 0).wait_recv()
            lrq[...] += lrin[1, j].astype(F32)

    lowb[0] = lrq[...].T.astype(BF16)
    tell().start()

    def project(p):
        for v in range(nu):
            at = pl.ds(pl.multiple_of((v * 2 + core) * strip + p * CHUNK, CHUNK), CHUNK)
            there = pl.ds(pl.multiple_of(v * strip + p * CHUNK, CHUNK), CHUNK)
            block = (dot(lowb[0], tok[:, at]) + dot(lowb[1], tok2[:, there])).astype(BF16)
            for i in range(heads):
                part[parts + p, v, pl.ds(i * 2 * rank, 2 * rank), :] = block[:, i * HEAD:(i + 1) * HEAD]
        for o in range(1, group):
            scatter(parts + p, o).start()

    def lay_out(n, t, outs):
        shared_here = res.at[n, 1 - core] if t == 1 else res.at[n, 1 - core, u]
        whole(shared_here, esend.at[t], erecv.at[n]).wait_recv()
        for v in range(nu if t == 1 else 1):
            for k in range(2):
                for i in range(heads):
                    h = ((v * 2 + k) * parts + n - t * parts) * heads + i
                    at = pl.ds(pl.multiple_of(h * HEAD, HEAD), HEAD)
                    w = v if t == 1 else u
                    outs[0][:, at] = res[n, k, w, pl.ds(i * 2 * rank, rank), :]
                    outs[1][:, at] = res[n, k, w, pl.ds(i * 2 * rank + rank, rank), :]

    whole(tok2, gsend.at[0], grecv.at[0]).wait_recv()
    tell().wait_recv()
    each(0, parts, project)

    def finish_up(n):
        lay_out(n, 0, (upq_out, upv_out))

    def finish_down(n):
        lay_out(n, 1, (downq_out, downv_out))

    order = []
    for p in range(parts):
        late = 3.0 if p >= soon else 0.0
        if p >= soon:
            order.append((-0.5, plane_sum, (p,)))
        order += [
            (0.0 + late, line_sum, (p,)), (3.5 + late, widen, (p, 0)),
            (14.0 + 0.7 * p, hand_over, (p, 0)), (17.0 + 0.7 * p, finish_up, (p,)),
        ]
        n, at = parts + p, 1.4 * p
        order += [
            (2.6 + at, plane_sum, (n,)), (7.0 + at, line_sum, (n,)), (12.0 + at, widen, (n, 1)),
            (17.5 + at, hand_over, (n, 1)), (19.5 + at, finish_down, (n,)),
        ]
    for _, work, what in sorted(order, key=lambda item: item[0]):
        work(*what)

    whole(tok2, gsend.at[0], grecv.at[0]).wait_send()
    tell().wait_send()
    whole(pair, psend.at[0], precv.at[0]).wait_send()
    whole(plane_in, asend.at[0], arecv.at[0]).wait_send()
    whole(line_in, bsend.at[0], brecv.at[0]).wait_send()
    whole(line_in, csend.at[0], crecv.at[0]).wait_send()
    for i in range(2):
        some = pl.ds(i * parts, parts)
        whole(
            plane_in.at[some, pl.ds(0, (inners, group)[i] - 1)], dsend.at[i], drecv.at[0]
        ).wait_send()
    whole(res.at[pl.ds(0, parts), 0, 0], esend.at[0], erecv.at[0]).wait_send()
    whole(res.at[pl.ds(parts, parts), 0], esend.at[1], erecv.at[0]).wait_send()

    everything = kv.at[:, mine, :]
    for j in range(1, nu):
        remote(everything, everything, xsend.at[j], xrecv.at[j - 1, 0], (blk, peer(j))).wait_send()

    @pl.when(has_next)
    def _():
        for j in range(nu):
            remote(everything, everything, fsend.at[j], frecv.at[0], (blk + 1, u)).wait_send()

    for j in range(1, nu):
        low_across(j).wait_send()

    @pl.when(has_next)
    def _():
        for j in range(nu):
            low_onward(j).wait_send()

    for j in range(1, nu):
        terms(0, j, span).wait_send()

    @pl.when(has_prev)
    def _():
        for j in range(nu):
            terms(1, j, 0).wait_send()


def grid_of(nb):
    half = nb // 2
    inners = 2 if half % 2 == 0 else 1
    return inners, half // inners


def fused(nb, nu, *operands):
    rows, width = operands[0].shape
    rank = operands[6].shape[0]
    span = nu * rows
    chunks = width // CHUNK
    cells = 2 * nu
    parts = chunks // cells
    inners, outers = grid_of(nb)
    group = nu * inners
    sub = CHUNK // inners
    lanes = 2 * rank
    dma = pltpu.SemaphoreType.DMA
    anywhere = pl.BlockSpec(memory_space=pl.ANY)
    here = pl.BlockSpec(memory_space=pltpu.VMEM)
    return pl.pallas_call(
        functools.partial(fused_kernel, nb, nu),
        out_shape=(
            pltpu.VMEM((rows, width), BF16),
            pltpu.VMEM((rank, width), BF16),
            pltpu.VMEM((rank, width), BF16),
            pltpu.VMEM((rank, width // nu), BF16),
            pltpu.VMEM((rank, width // nu), BF16),
        ),
        in_specs=[anywhere] * 9,
        out_specs=(here,) * 5,
        scratch_shapes=[
            pltpu.VMEM((2, 2 * span, width), BF16),
            pltpu.VMEM((2 * span, lanes), BF16),
            pltpu.VMEM((rows, width), BF16),
            pltpu.VMEM((rows, width), BF16),
            pltpu.VMEM((rows, width), BF16),
            pltpu.VMEM((lanes, width), BF16),
            pltpu.VMEM((lanes, width), BF16),
            pltpu.VMEM((rows, lanes), F32),
            pltpu.VMEM((2 * span, lanes), F32),
            pltpu.VMEM((2 * span, lanes), BF16),
            pltpu.VMEM((2, nu, rows, lanes), BF16),
            pltpu.VMEM((rows, width // 2), BF16),
            pltpu.VMEM((2, lanes, rows), BF16),
            pltpu.VMEM((parts, 2, nu, CHUNK, lanes), BF16),
            pltpu.VMEM((parts, nu, CHUNK, lanes), BF16),
            pltpu.VMEM((2 * parts, nu, CHUNK, lanes), BF16),
            pltpu.VMEM((2 * parts, group - 1, sub, lanes), BF16),
            pltpu.VMEM((2 * parts, sub, lanes), BF16),
            pltpu.VMEM((2 * parts, outers - 1, sub // outers, lanes), BF16),
            pltpu.VMEM((2 * parts, 2, nu, CHUNK, lanes), BF16),
            dma((9,)),
            dma((nu,)), dma((nu - 1, chunks)),
            dma((nu,)), dma((chunks,)),
            dma((nu,)), dma((nu,)), dma((nu,)), dma((nu,)),
            dma((2, nu)), dma((2, nu)),
            dma((1,)), dma((parts,)),
            dma((1,)), dma((2 * parts,)),
            dma((1,)), dma((2 * parts,)),
            dma((1,)), dma((2 * parts,)),
            dma((2,)), dma((2 * parts,)),
            dma((2,)), dma((2 * parts,)),
            dma((2,)), dma((2,)),
        ],
        compiler_params=pltpu.CompilerParams(
            collective_id=2, has_side_effects=True, vmem_limit_bytes=60_000_000
        ),
    )(*operands)


def fits(nb, nu, rows, width, rank):
    inners, outers = grid_of(nb)
    return (
        2 * rank == HEAD
        and width % (2 * nu * CHUNK) == 0
        and CHUNK % (16 * inners * outers) == 0
        and nu * rows <= CHUNK
    )


def deliver_kernel(*refs):
    count = len(refs) // 2
    sources, targets, sem = refs[:count], refs[count:2 * count], refs[-1]
    copies = [pltpu.make_async_copy(a, b, sem.at[i]) for i, (a, b) in enumerate(zip(sources, targets))]
    for copy in copies:
        copy.start()
    for copy in copies:
        copy.wait()


def deliver(*arrays):
    return pl.pallas_call(
        deliver_kernel,
        out_shape=tuple(jax.ShapeDtypeStruct(a.shape, a.dtype) for a in arrays),
        in_specs=[pl.BlockSpec(memory_space=pl.ANY)] * len(arrays),
        out_specs=tuple(pl.BlockSpec(memory_space=pl.ANY) for _ in arrays),
        scratch_shapes=[pltpu.SemaphoreType.DMA((len(arrays),))],
    )(*(pltpu.with_memory_space_constraint(a, pltpu.VMEM) for a in arrays))


def per_device(nb, nu, tokens, query_base, key_base, value_base, out_grad, down_q, up_q, down_v, up_v):
    operands = (tokens, query_base, key_base, value_base, out_grad, down_q.T, up_q, down_v.T, up_v)
    if fits(nb, nu, *tokens.shape, up_q.shape[0]):
        attended, grad_down_q, grad_down_v, grad_up_q, grad_up_v = deliver(*fused(nb, nu, *operands))
        return attended, grad_down_q.T, grad_up_q, grad_down_v.T, grad_up_v
    attended, gup, lowrank = attention(nb, nu, *operands)
    grad_down_q, grad_down_v, grad_up_q, grad_up_v = reduction(nb, nu, tokens, lowrank, gup)
    return attended, grad_down_q.T, grad_up_q, grad_down_v.T, grad_up_v


def solution(mesh):
    split = P(("blk", "uly"), None)
    return jax.shard_map(
        functools.partial(per_device, mesh.shape["blk"], mesh.shape["uly"]),
        mesh=mesh,
        in_specs=(split,) * 5 + (P(),) * 4,
        out_specs=(split, P(), P(None, "uly"), P(), P(None, "uly")),
        check_vma=False,
    )
```

```python
import functools

import jax
import jax.numpy as jnp
from jax import lax
from jax.experimental import pallas as pl
from jax.experimental.pallas import tpu as pltpu
from jax.sharding import PartitionSpec as P

HEAD = 128
CHUNK = 256
MESH = pl.DeviceIdType.MESH
F32 = jnp.float32
BF16 = jnp.bfloat16


def inner(left, right):
    return lax.dot_general(left, right, (((0,), (0,)), ((), ())), preferred_element_type=F32)


def outer(left, right):
    return lax.dot_general(left, right, (((1,), (1,)), ((), ())), preferred_element_type=F32)


def dot(left, right):
    return jnp.dot(left, right, preferred_element_type=F32)


def attention_kernel(
    nb, nu,
    tokens, query_base, key_base, value_base, out_grad, down_q, up_q, down_v, up_v,
    att_ref, gup_ref, low_out,
    kbuf, vbuf, lbuf, tok, qs, gs, downs, ups, lrq, lrv, lrin,
    local_sem, xsend, xrecv, fsend, frecv, lsend, lrecv, msend, mrecv, rsend, rrecv,
):
    blk = lax.axis_index("blk")
    u = lax.axis_index("uly")
    rows, width = tokens.shape
    rank = up_q.shape[0]
    span = nu * rows
    chunks = width // CHUNK
    has_prev = blk > 0
    has_next = blk < nb - 1
    mine = pl.ds(pl.multiple_of(span + u * rows, rows), rows)

    def peer(j):
        return lax.rem(u + j, nu)

    def source(j):
        return lax.rem(u - j + nu, nu)

    def cols(c):
        return pl.ds(pl.multiple_of(c * CHUNK, CHUNK), CHUNK)

    barrier = pltpu.get_barrier_semaphore()
    for j in range(1, nu):
        pl.semaphore_signal(barrier, inc=1, device_id=(blk, peer(j)), device_id_type=MESH)

    @pl.when(has_prev)
    def _():
        for j in range(nu):
            pl.semaphore_signal(barrier, inc=1, device_id=(blk - 1, peer(j)), device_id_type=MESH)

    @pl.when(has_next)
    def _():
        for j in range(nu):
            pl.semaphore_signal(barrier, inc=1, device_id=(blk + 1, peer(j)), device_id_type=MESH)

    local = [
        pltpu.make_async_copy(src, dst, local_sem.at[i])
        for i, (src, dst) in enumerate(
            (
                (tokens, tok), (down_q, downs.at[pl.ds(0, rank)]), (down_v, downs.at[pl.ds(rank, rank)]),
                (up_q, ups.at[pl.ds(0, rank)]), (up_v, ups.at[pl.ds(rank, rank)]),
                (value_base, vbuf.at[mine]), (key_base, kbuf.at[mine]),
                (query_base, qs), (out_grad, gs),
            )
        )
    ]
    for copy in local:
        copy.start()

    edge = jnp.logical_or(blk == 0, blk == nb - 1)

    @pl.when(edge)
    def _():
        pl.semaphore_wait(barrier, 2 * nu - 1)

    @pl.when(jnp.logical_not(edge))
    def _():
        pl.semaphore_wait(barrier, 3 * nu - 1)

    bufs = (kbuf, vbuf)

    def across(a, j, c):
        src = key_base.at[:, cols(c)] if a == 0 else vbuf.at[mine, cols(c)]
        return pltpu.make_async_remote_copy(
            src_ref=src, dst_ref=bufs[a].at[mine, cols(c)],
            send_sem=xsend.at[a, j, c], recv_sem=xrecv.at[a, j, c],
            device_id=(blk, peer(j)), device_id_type=MESH,
        )

    def crossed(a, j, c):
        here = bufs[a].at[pl.ds(pl.multiple_of(span + source(j) * rows, rows), rows), cols(c)]
        return pltpu.make_async_remote_copy(
            src_ref=here, dst_ref=here,
            send_sem=xsend.at[a, j, c], recv_sem=xrecv.at[a, j, c],
            device_id=(blk, peer(j)), device_id_type=MESH,
        )

    def onward(a, j, c):
        s = source(j)
        if a == 0 and j == 0:
            src = key_base.at[:, cols(c)]
        else:
            src = bufs[a].at[pl.ds(pl.multiple_of(span + s * rows, rows), rows), cols(c)]
        return pltpu.make_async_remote_copy(
            src_ref=src, dst_ref=bufs[a].at[pl.ds(pl.multiple_of(s * rows, rows), rows), cols(c)],
            send_sem=fsend.at[a, j, c], recv_sem=frecv.at[a, j, c],
            device_id=(blk + 1, u), device_id_type=MESH,
        )

    def arrived(a, j, c):
        here = bufs[a].at[pl.ds(pl.multiple_of(source(j) * rows, rows), rows), cols(c)]
        return pltpu.make_async_remote_copy(
            src_ref=here, dst_ref=here,
            send_sem=fsend.at[a, j, c], recv_sem=frecv.at[a, j, c],
            device_id=(blk, peer(1)), device_id_type=MESH,
        )

    def low_across(j):
        return pltpu.make_async_remote_copy(
            src_ref=lbuf.at[mine], dst_ref=lbuf.at[mine],
            send_sem=lsend.at[j], recv_sem=lrecv.at[j],
            device_id=(blk, peer(j)), device_id_type=MESH,
        )

    def low_crossed(j):
        here = lbuf.at[pl.ds(pl.multiple_of(span + source(j) * rows, rows), rows)]
        return pltpu.make_async_remote_copy(
            src_ref=here, dst_ref=here, send_sem=lsend.at[j], recv_sem=lrecv.at[j],
            device_id=(blk, peer(j)), device_id_type=MESH,
        )

    def low_onward(j):
        s = source(j)
        return pltpu.make_async_remote_copy(
            src_ref=lbuf.at[pl.ds(pl.multiple_of(span + s * rows, rows), rows)],
            dst_ref=lbuf.at[pl.ds(pl.multiple_of(s * rows, rows), rows)],
            send_sem=msend.at[j], recv_sem=mrecv.at[j],
            device_id=(blk + 1, u), device_id_type=MESH,
        )

    def low_arrived(j):
        here = lbuf.at[pl.ds(pl.multiple_of(source(j) * rows, rows), rows)]
        return pltpu.make_async_remote_copy(
            src_ref=here, dst_ref=here, send_sem=msend.at[j], recv_sem=mrecv.at[j],
            device_id=(blk, peer(1)), device_id_type=MESH,
        )

    early = min(3 * 512 // CHUNK, chunks)
    ahead = min(2048 // CHUNK, chunks)
    for c in range(early):
        for j in range(1, nu):
            across(0, j, c).start()

    @pl.when(has_next)
    def _():
        for c in range(ahead):
            onward(0, 0, c).start()

    lane = lax.broadcasted_iota(jnp.int32, (rows, 2 * rank), 1)
    for i in range(3):
        local[i].wait()
    low = outer(tok[...], downs[...])
    low_qm = jnp.where(lane < rank, low, 0.0).astype(BF16)
    low_vm = jnp.where(lane >= rank, low, 0.0).astype(BF16)
    lbuf[mine, :] = low_vm
    for i in range(3, 6):
        local[i].wait()

    @pl.loop(0, chunks)
    def _(c):
        part = dot(low_vm, ups[:, cols(c)])
        vbuf[mine, cols(c)] = (vbuf[mine, cols(c)].astype(F32) + part).astype(BF16)

    for j in range(1, nu):
        low_across(j).start()

    @pl.when(has_next)
    def _():
        low_onward(0).start()

    @pl.loop(0, chunks)
    def _(c):
        @pl.when(c >= early)
        def _():
            for j in range(1, nu):
                across(0, j, c).start()

        for j in range(1, nu):
            across(1, j, c).start()

    @pl.when(has_next)
    def _():
        for c in range(ahead):
            onward(1, 0, c).start()

    lrq[...] = jnp.zeros_like(lrq)
    lrv[...] = jnp.zeros_like(lrv)

    @pl.when(jnp.logical_not(has_prev))
    def _():
        kbuf[pl.ds(0, span), :] = jnp.zeros((span, width), BF16)
        vbuf[pl.ds(0, span), :] = jnp.zeros((span, width), BF16)
        lbuf[pl.ds(0, span), :] = jnp.zeros((span, 2 * rank), BF16)

    for i in range(6, 9):
        local[i].wait()

    scale = HEAD ** (-0.5)
    key_at = lax.broadcasted_iota(jnp.int32, (rows, 2 * span), 1)
    usable = jnp.logical_or(key_at >= span, has_prev)

    def head(h):
        at = pl.ds(pl.multiple_of(h * HEAD, HEAD), HEAD)
        up = ups[:, at]
        keys = kbuf[:, at]
        values = vbuf[:, at]
        grad = gs[:, at]
        query = (qs[:, at].astype(F32) + dot(low_qm, up)).astype(BF16)
        scores = jnp.where(usable, outer(query, keys) * scale, -jnp.inf)
        weights = jnp.exp(scores - jnp.max(scores, axis=1, keepdims=True))
        total = jnp.sum(weights, axis=1, keepdims=True)
        probs = (weights * (1.0 / total)).astype(BF16)
        attended = dot(probs, values).astype(BF16)
        delta = jnp.sum(grad.astype(F32) * attended.astype(F32), axis=1, keepdims=True)
        score_grad = (probs.astype(F32) * (outer(grad, values) - delta)).astype(BF16)
        query_grad = (dot(score_grad, keys) * scale).astype(BF16)
        seen = dot(probs, lbuf[...]).astype(BF16)
        gup = (inner(low_qm, query_grad) + inner(seen, grad)).astype(BF16)
        lifted = jnp.where(lane >= rank, outer(grad, up), 0.0).astype(BF16)
        return attended, gup, outer(query_grad, up), inner(probs, lifted)

    together = 2 if span <= 2 * HEAD else 1

    def head_group(first):
        results = [head(first + i) for i in range(together)]
        for i, (attended, gup, _, _) in enumerate(results):
            h = first + i
            att_ref[:, pl.ds(pl.multiple_of(h * HEAD, HEAD), HEAD)] = attended
            gup_ref[pl.ds(pl.multiple_of(h * 2 * rank, 2 * rank), 2 * rank), :] = gup
        lrq[...] += jnp.where(lane < rank, sum(r[2] for r in results), 0.0)
        lrv[...] += sum(r[3] for r in results)

    heads = CHUNK // HEAD

    @pl.loop(0, chunks + 1)
    def _(c):
        @pl.when(c == 0)
        def _():
            for j in range(1, nu):
                low_crossed(j).wait_recv()

                @pl.when(has_next)
                def _():
                    low_onward(j).start()

            @pl.when(has_prev)
            def _():
                for j in range(nu):
                    low_arrived(j).wait_recv()

        @pl.when(c < chunks)
        def _():
            for a in range(2):
                for j in range(1, nu):
                    crossed(a, j, c).wait_recv()

                    @pl.when(has_next)
                    def _():
                        onward(a, j, c).start()

            @pl.when(jnp.logical_and(has_next, c + ahead < chunks))
            def _():
                for a in range(2):
                    onward(a, 0, c + ahead).start()

        @pl.when(c > 0)
        def _():
            @pl.when(has_prev)
            def _():
                for a in range(2):
                    for j in range(nu):
                        arrived(a, j, c - 1).wait_recv()

            @pl.loop(0, heads // together)
            def _(i):
                head_group((c - 1) * heads + i * together)

    def terms(k, j, base):
        s = peer(j)
        return pltpu.make_async_remote_copy(
            src_ref=lrv.at[pl.ds(pl.multiple_of(base + s * rows, rows), rows)],
            dst_ref=lrin.at[k, j],
            send_sem=rsend.at[k, j], recv_sem=rrecv.at[k, j],
            device_id=(blk - k, s), device_id_type=MESH,
        )

    for j in range(1, nu):
        terms(0, j, span).start()

    @pl.when(has_prev)
    def _():
        for j in range(nu):
            terms(1, j, 0).start()

    @pl.loop(0, chunks)
    def _(c):
        for a in range(2):
            for j in range(1, nu):
                across(a, j, c).wait_send()

            @pl.when(has_next)
            def _():
                for j in range(nu):
                    onward(a, j, c).wait_send()

    for j in range(1, nu):
        low_across(j).wait_send()

    @pl.when(has_next)
    def _():
        for j in range(nu):
            low_onward(j).wait_send()

    lrq[...] += lrv[mine, :]
    for j in range(1, nu):
        terms(0, j, span).wait_recv()
        lrq[...] += lrin[0, j]

    @pl.when(has_next)
    def _():
        for j in range(nu):
            terms(1, j, 0).wait_recv()
            lrq[...] += lrin[1, j]

    low_out[...] = lrq[...].astype(BF16)
    for j in range(1, nu):
        terms(0, j, span).wait_send()

    @pl.when(has_prev)
    def _():
        for j in range(nu):
            terms(1, j, 0).wait_send()


def attention(nb, nu, *operands):
    rows, width = operands[0].shape
    rank = operands[6].shape[0]
    span = nu * rows
    chunks = width // CHUNK
    dma = pltpu.SemaphoreType.DMA
    anywhere = pl.BlockSpec(memory_space=pl.ANY)
    here = pl.BlockSpec(memory_space=pltpu.VMEM)
    return pl.pallas_call(
        functools.partial(attention_kernel, nb, nu),
        out_shape=(
            jax.ShapeDtypeStruct((rows, width), BF16),
            jax.ShapeDtypeStruct((width // HEAD * 2 * rank, HEAD), BF16),
            jax.ShapeDtypeStruct((rows, 2 * rank), BF16),
        ),
        in_specs=[anywhere] * 9,
        out_specs=(here, here, here),
        scratch_shapes=[
            pltpu.VMEM((2 * span, width), BF16),
            pltpu.VMEM((2 * span, width), BF16),
            pltpu.VMEM((2 * span, 2 * rank), BF16),
            pltpu.VMEM((rows, width), BF16),
            pltpu.VMEM((rows, width), BF16),
            pltpu.VMEM((rows, width), BF16),
            pltpu.VMEM((2 * rank, width), BF16),
            pltpu.VMEM((2 * rank, width), BF16),
            pltpu.VMEM((rows, 2 * rank), F32),
            pltpu.VMEM((2 * span, 2 * rank), F32),
            pltpu.VMEM((2, nu, rows, 2 * rank), F32),
            dma((9,)),
            dma((2, nu, chunks)), dma((2, nu, chunks)),
            dma((2, nu, chunks)), dma((2, nu, chunks)),
            dma((nu,)), dma((nu,)), dma((nu,)), dma((nu,)),
            dma((2, nu)), dma((2, nu)),
        ],
        compiler_params=pltpu.CompilerParams(
            collective_id=0, has_side_effects=True, vmem_limit_bytes=65_000_000
        ),
    )(*operands)


def reduction_kernel(
    nb, nu,
    tokens, lowrank, gup,
    downq_out, downv_out, upq_out, upv_out,
    tok, terms, pair, part, plane_in, line, line_in, down, ups, flat,
    local_sem, psend, precv, asend, arecv, bsend, brecv, csend, crecv, dsend, drecv, esend, erecv,
):
    blk = lax.axis_index("blk")
    u = lax.axis_index("uly")
    core = lax.rem(blk, 2)
    chip = blk // 2
    other = chip * 2 + 1 - core
    half = nb // 2
    inners = plane_in.shape[1] // nu
    outers = half // inners
    y = lax.rem(chip, inners)
    z = chip // inners
    group = nu * inners
    rows, width = tokens.shape
    rank = upq_out.shape[0]
    region = pair.shape[2]
    sub = plane_in.shape[2]
    piece = line_in.shape[2]

    def split(o, sign):
        pu = lax.rem(u + sign * (o // inners) + nu, nu)
        py = lax.rem(y + sign * lax.rem(o, inners) + inners, inners)
        return pu, py

    def plane_dev(o):
        pu, py = split(o, 1)
        return ((z * inners + py) * 2 + core, pu)

    def peer_z(o):
        return lax.rem(z + o, outers)

    def from_z(o):
        return lax.rem(z - o + outers, outers)

    def line_dev(o):
        return ((peer_z(o) * inners + y) * 2 + core, u)

    def subs(p):
        return pl.ds(pl.multiple_of(p * sub, sub), sub)

    barrier = pltpu.get_barrier_semaphore()
    pl.semaphore_signal(barrier, inc=1, device_id=(other, u), device_id_type=MESH)
    for o in range(1, group):
        pl.semaphore_signal(barrier, inc=1, device_id=plane_dev(o), device_id_type=MESH)
    for o in range(1, outers):
        pl.semaphore_signal(barrier, inc=1, device_id=line_dev(o), device_id_type=MESH)

    load = pltpu.make_async_copy(tokens, tok, local_sem.at[0])
    load.start()
    pl.semaphore_wait(barrier, group + outers - 1)

    def remote(src, dst, send, recv, device):
        return pltpu.make_async_remote_copy(
            src_ref=src, dst_ref=dst, send_sem=send, recv_sem=recv,
            device_id=device, device_id_type=MESH,
        )

    def swap(t, v):
        rows_at = pl.ds(pl.multiple_of((v * 2 + 1 - core) * region, region), region)
        return remote(
            (terms if t == 0 else gup).at[rows_at], pair.at[t, v],
            psend.at[t, v], precv.at[t, v], (other, u),
        )

    def scatter(t, o):
        pu, py = split(o, 1)
        return remote(
            part.at[t, pu, subs(py)], plane_in.at[t, o],
            asend.at[t, o], arecv.at[t, o], plane_dev(o),
        )

    def pass_on(t, o):
        at = pl.ds(pl.multiple_of(peer_z(o) * piece, piece), piece)
        return remote(
            line.at[t, at], line_in.at[t, o], bsend.at[t, o], brecv.at[t, o], line_dev(o)
        )

    def whole(t, v, k, p):
        return down.at[v, k, subs(p)] if t == 0 else ups.at[k, subs(p)]

    def piece_at(p, q):
        return pl.ds(pl.multiple_of(p * sub + q * piece, piece), piece)

    def small(t, q):
        return down.at[u, core, piece_at(y, q)] if t == 0 else ups.at[core, piece_at(y, q)]

    def along(t, o):
        return remote(small(t, z), small(t, z), csend.at[t, o], crecv.at[t, o], line_dev(o))

    def came(t, o):
        here = small(t, from_z(o))
        return remote(here, here, csend.at[t, o], crecv.at[t, o], line_dev(o))

    def spread(t, o):
        here = whole(t, u, core, y)
        return remote(here, here, dsend.at[t, o], drecv.at[t, o], plane_dev(o))

    def landed(t, o):
        pu, py = split(o, -1)
        here = whole(t, pu, core, py)
        return remote(here, here, dsend.at[t, o], drecv.at[t, o], (other, u))

    def share(t, o):
        pu, py = split(o, -1)
        here = whole(t, pu, core, py)
        return remote(here, here, esend.at[t, o], erecv.at[t, o], (other, u))

    def shared(t, o):
        pu, py = split(o, -1)
        here = whole(t, pu, 1 - core, py)
        return remote(here, here, esend.at[t, o], erecv.at[t, o], (other, u))

    if part.shape[2] > region:
        part[...] = jnp.zeros_like(part)
    for v in range(nu):
        swap(1, v).start()

    load.wait()
    lows = lowrank[...]

    @pl.loop(0, width // HEAD)
    def _(h):
        cols = pl.ds(pl.multiple_of(h * HEAD, HEAD), HEAD)
        here = pl.ds(pl.multiple_of(h * 2 * rank, 2 * rank), 2 * rank)
        terms[here, :] = inner(lows, tok[:, cols]).astype(BF16)

    for v in range(nu):
        swap(0, v).start()

    for t in (1, 0):
        for v in range(nu):
            rows_at = pl.ds(pl.multiple_of((v * 2 + core) * region, region), region)
            own = (terms if t == 0 else gup)[rows_at, :]
            swap(t, v).wait_recv()
            part[t, v, pl.ds(0, region), :] = (
                own.astype(F32) + pair[t, v].astype(F32)
            ).astype(BF16)
        for o in range(1, group):
            scatter(t, o).start()

    for t in (1, 0):
        total = part[t, u, subs(y), :].astype(F32)
        for o in range(1, group):
            scatter(t, o).wait_recv()
            total = total + plane_in[t, o].astype(F32)
        line[t, :, :] = total.astype(BF16)
        for o in range(1, outers):
            pass_on(t, o).start()

    for t in (1, 0):
        total = line[t, pl.ds(pl.multiple_of(z * piece, piece), piece), :].astype(F32)
        for o in range(1, outers):
            pass_on(t, o).wait_recv()
            total = total + line_in[t, o].astype(F32)
        small(t, z)[...] = total.astype(BF16)
        for o in range(1, outers):
            along(t, o).start()

    counts = (group, inners)
    for t in (1, 0):
        for o in range(1, outers):
            came(t, o).wait_recv()
        for o in range(1, counts[t]):
            spread(t, o).start()
        share(t, 0).start()

    for t in (1, 0):
        for o in range(1, counts[t]):
            landed(t, o).wait_recv()
            share(t, o).start()

    for t in (1, 0):
        for o in range(counts[t]):
            shared(t, o).wait_recv()
        places = [(v, k) for v in range(nu if t == 0 else 1) for k in range(2)]
        for n, (v, k) in enumerate(places):
            flat[pl.ds(n * region, region), :] = (
                down[v, k, pl.ds(0, region), :] if t == 0 else ups[k, pl.ds(0, region), :]
            )
        outs = (downq_out, downv_out) if t == 0 else (upq_out, upv_out)
        for h in range(len(places) * region // (2 * rank)):
            cols = pl.ds(h * HEAD, HEAD)
            outs[0][:, cols] = flat[pl.ds(h * 2 * rank, rank), :]
            outs[1][:, cols] = flat[pl.ds(h * 2 * rank + rank, rank), :]

    for t in (1, 0):
        for v in range(nu):
            swap(t, v).wait_send()
        for o in range(1, group):
            scatter(t, o).wait_send()
        for o in range(1, outers):
            pass_on(t, o).wait_send()
            along(t, o).wait_send()
        for o in range(1, counts[t]):
            spread(t, o).wait_send()
        for o in range(counts[t]):
            share(t, o).wait_send()


def reduction(nb, nu, tokens, lowrank, gup):
    rows, width = tokens.shape
    rank = lowrank.shape[1] // 2
    half = nb // 2
    inners = 2 if half % 2 == 0 else 1
    outers = half // inners
    group = nu * inners
    region = width // (2 * nu)
    piece = -(-region // (16 * half)) * 16
    sub = outers * piece
    held = half * piece
    dma = pltpu.SemaphoreType.DMA
    here = pl.BlockSpec(memory_space=pltpu.VMEM)
    lanes = lowrank.shape[1]
    return pl.pallas_call(
        functools.partial(reduction_kernel, nb, nu),
        out_shape=(
            jax.ShapeDtypeStruct((rank, width), BF16),
            jax.ShapeDtypeStruct((rank, width), BF16),
            jax.ShapeDtypeStruct((rank, width // nu), BF16),
            jax.ShapeDtypeStruct((rank, width // nu), BF16),
        ),
        in_specs=[pl.BlockSpec(memory_space=pl.ANY), here, here],
        out_specs=(here, here, here, here),
        scratch_shapes=[
            pltpu.VMEM((rows, width), BF16),
            pltpu.VMEM((width, lanes), BF16),
            pltpu.VMEM((2, nu, region, lanes), BF16),
            pltpu.VMEM((2, nu, held, lanes), BF16),
            pltpu.VMEM((2, group, sub, lanes), BF16),
            pltpu.VMEM((2, sub, lanes), BF16),
            pltpu.VMEM((2, outers, piece, lanes), BF16),
            pltpu.VMEM((nu, 2, held, lanes), BF16),
            pltpu.VMEM((2, held, lanes), BF16),
            pltpu.VMEM((2 * nu * region, lanes), BF16),
            dma((1,)),
            dma((2, nu)), dma((2, nu)),
            dma((2, group)), dma((2, group)),
            dma((2, outers)), dma((2, outers)),
            dma((2, outers)), dma((2, outers)),
            dma((2, group)), dma((2, group)),
            dma((2, group)), dma((2, group)),
        ],
        compiler_params=pltpu.CompilerParams(collective_id=1, has_side_effects=True),
    )(tokens, lowrank, gup)


def fused_kernel(
    nb, nu,
    tokens, query_base, key_base, value_base, out_grad, down_q, up_q, down_v, up_v,
    att_ref, downq_out, downv_out, upq_out, upv_out,
    kv, lbuf, tok, qs, gs, downs, ups, lrq, lrv, lrs, lrin,
    tok2, lowb, acc, pair, part, plane_in, line, line_in, res,
    local_sem, xsend, xrecv, fsend, frecv, lsend, lrecv, msend, mrecv, rsend, rrecv,
    psend, precv, asend, arecv, bsend, brecv, csend, crecv, dsend, drecv, esend, erecv, gsend, grecv,
):
    kbuf, vbuf = kv.at[0], kv.at[1]
    blk = lax.axis_index("blk")
    u = lax.axis_index("uly")
    rows, width = tokens.shape
    rank = up_q.shape[0]
    span = nu * rows
    chunks = width // CHUNK
    has_prev = blk > 0
    has_next = blk < nb - 1
    mine = pl.ds(pl.multiple_of(span + u * rows, rows), rows)

    def peer(j):
        return lax.rem(u + j, nu)

    def source(j):
        return lax.rem(u - j + nu, nu)

    cells = 2 * nu
    parts = chunks // cells
    core = lax.rem(blk, 2)
    chip = blk // 2
    other = chip * 2 + 1 - core
    inners, outers = grid_of(nb)
    group = nu * inners
    y = lax.rem(chip, inners)
    z = chip // inners
    sub = CHUNK // inners
    piece = sub // outers

    def place(c):
        return lax.rem(c, cells) * parts + c // cells

    def cols(c):
        return pl.ds(pl.multiple_of(place(c) * CHUNK, CHUNK), CHUNK)

    def remote(src, dst, send, recv, device):
        return pltpu.make_async_remote_copy(
            src_ref=src, dst_ref=dst, send_sem=send, recv_sem=recv,
            device_id=device, device_id_type=MESH,
        )

    def split(o, sign):
        pu = lax.rem(u + sign * (o // inners) + nu, nu)
        py = lax.rem(y + sign * lax.rem(o, inners) + inners, inners)
        return pu, py

    def plane_dev(o):
        pu, py = split(o, 1)
        return ((z * inners + py) * 2 + core, pu)

    def peer_z(o):
        return lax.rem(z + o, outers)

    def from_z(o):
        return lax.rem(z - o + outers, outers)

    def line_dev(o):
        return ((peer_z(o) * inners + y) * 2 + core, u)

    def subs(p):
        return pl.ds(pl.multiple_of(p * sub, sub), sub)

    def piece_at(p, q):
        return pl.ds(pl.multiple_of(p * sub + q * piece, piece), piece)

    def swap(n):
        return remote(
            acc.at[n, 1 - core], pair.at[n], psend.at[0], precv.at[n], (other, u)
        )

    def scatter(n, o):
        pu, py = split(o, 1)
        return remote(
            part.at[n, pu, subs(py)], plane_in.at[n, o - 1],
            asend.at[0], arecv.at[n], plane_dev(o),
        )

    def pass_on(n, o):
        at = pl.ds(pl.multiple_of(peer_z(o) * piece, piece), piece)
        return remote(
            line.at[n, at], line_in.at[n, o - 1], bsend.at[0], brecv.at[n], line_dev(o)
        )

    def along(n, o):
        here = res.at[n, core, u, piece_at(y, z)]
        return remote(here, here, csend.at[0], crecv.at[n], line_dev(o))

    def spread(n, o, t):
        here = res.at[n, core, u, subs(y)]
        return remote(here, here, dsend.at[t], drecv.at[n], plane_dev(o))

    def share(n, t):
        here = res.at[n, core] if t == 1 else res.at[n, core, u]
        return remote(here, here, esend.at[t], erecv.at[n], (other, u))

    def whole(src, send, recv):
        return remote(src, src, send, recv, (other, u))

    strip = parts * CHUNK

    def lend(v):
        at = pl.ds(pl.multiple_of((v * 2 + 1 - core) * strip, strip), strip)
        return remote(
            tokens.at[:, at], tok2.at[:, pl.ds(v * strip, strip)], gsend.at[0], grecv.at[0], (other, u)
        )

    def tell():
        return remote(lowb.at[0], lowb.at[1], gsend.at[1], grecv.at[1], (other, u))

    def pair_sum(n):
        swap(n).wait_recv()
        part[n] = (acc[n, core].astype(F32) + pair[n].astype(F32)).astype(BF16)

    def send_out(n):
        for o in range(1, group):
            scatter(n, o).start()

    def pair_up(n):
        pair_sum(n)
        send_out(n)

    def plane_sum(n):
        total = part[n, u, subs(y), :].astype(F32)
        whole(plane_in.at[n], asend.at[0], arecv.at[n]).wait_recv()
        for o in range(1, group):
            total = total + plane_in[n, o - 1].astype(F32)
        line[n] = total.astype(BF16)
        for o in range(1, outers):
            pass_on(n, o).start()

    def line_sum(n):
        total = line[n, pl.ds(pl.multiple_of(z * piece, piece), piece), :].astype(F32)
        whole(line_in.at[n], bsend.at[0], brecv.at[n]).wait_recv()
        for o in range(1, outers):
            total = total + line_in[n, o - 1].astype(F32)
        res[n, core, u, piece_at(y, z), :] = total.astype(BF16)
        for o in range(1, outers):
            along(n, o).start()

    def widen(n, t):
        whole(line_in.at[n], csend.at[0], crecv.at[n]).wait_recv()
        for o in range(1, (inners, group)[t]):
            spread(n, o, t).start()

    def hand_over(n, t):
        whole(plane_in.at[n, pl.ds(0, (inners, group)[t] - 1)], dsend.at[t], drecv.at[n]).wait_recv()
        share(n, t).start()

    def each(first, stop, work):
        @pl.loop(first, stop)
        def _(n):
            work(n)

    barrier = pltpu.get_barrier_semaphore()
    for j in range(1, nu):
        pl.semaphore_signal(barrier, inc=1, device_id=(blk, peer(j)), device_id_type=MESH)

    @pl.when(has_prev)
    def _():
        for j in range(nu):
            pl.semaphore_signal(barrier, inc=1, device_id=(blk - 1, peer(j)), device_id_type=MESH)

    @pl.when(has_next)
    def _():
        for j in range(nu):
            pl.semaphore_signal(barrier, inc=1, device_id=(blk + 1, peer(j)), device_id_type=MESH)

    for o in range(1, group):
        pl.semaphore_signal(barrier, inc=1, device_id=plane_dev(o), device_id_type=MESH)
    for o in range(1, outers):
        pl.semaphore_signal(barrier, inc=1, device_id=line_dev(o), device_id_type=MESH)

    local = [
        pltpu.make_async_copy(src, dst, local_sem.at[i])
        for i, (src, dst) in enumerate(
            (
                (tokens, tok), (down_q, downs.at[pl.ds(0, rank)]), (down_v, downs.at[pl.ds(rank, rank)]),
                (up_q, ups.at[pl.ds(0, rank)]), (up_v, ups.at[pl.ds(rank, rank)]),
                (value_base, vbuf.at[mine]), (key_base, kbuf.at[mine]),
                (query_base, qs), (out_grad, gs),
            )
        )
    ]
    for copy in local:
        copy.start()

    lane = lax.broadcasted_iota(jnp.int32, (rows, 2 * rank), 1)
    for i in range(3):
        local[i].wait()
    low = outer(tok[...], downs[...])
    low_qm = jnp.where(lane < rank, low, 0.0).astype(BF16)
    low_vm = jnp.where(lane >= rank, low, 0.0).astype(BF16)
    lbuf[mine, :] = low_vm
    edge = jnp.logical_or(blk == 0, blk == nb - 1)

    @pl.when(edge)
    def _():
        pl.semaphore_wait(barrier, 2 * nu - 1 + group + outers - 2)

    @pl.when(jnp.logical_not(edge))
    def _():
        pl.semaphore_wait(barrier, 3 * nu - 1 + group + outers - 2)

    def rows_of(first, j):
        return pl.ds(pl.multiple_of(first + source(j) * rows, rows), rows)

    def cross(j, c, what):
        at = cols(c)
        src, dst = {
            0: (key_base.at[:, at], kv.at[0, mine, at]),
            1: (kv.at[1, mine, at], kv.at[1, mine, at]),
            2: (kv.at[:, mine, at], kv.at[:, mine, at]),
        }[what]
        return remote(src, dst, xsend.at[j], xrecv.at[j - 1, c], (blk, peer(j)))

    def crossed(j, c):
        here = kv.at[:, rows_of(span, j), cols(c)]
        return remote(here, here, xsend.at[j], xrecv.at[j - 1, c], (blk, peer(j)))

    def onward(j, c, what):
        at = cols(c)
        old, new = rows_of(span, j), rows_of(0, j)
        src, dst = {
            0: (key_base.at[:, at], kv.at[0, new, at]),
            1: (kv.at[1, old, at], kv.at[1, new, at]),
            2: (kv.at[:, old, at], kv.at[:, new, at]),
        }[what]
        return remote(src, dst, fsend.at[j], frecv.at[c], (blk + 1, u))

    def arrived(c):
        here = kv.at[:, pl.ds(0, span), cols(c)]
        return remote(here, here, fsend.at[0], frecv.at[c], (blk, peer(1)))

    def low_across(j):
        return pltpu.make_async_remote_copy(
            src_ref=lbuf.at[mine], dst_ref=lbuf.at[mine],
            send_sem=lsend.at[j], recv_sem=lrecv.at[j],
            device_id=(blk, peer(j)), device_id_type=MESH,
        )

    def low_crossed(j):
        here = lbuf.at[pl.ds(pl.multiple_of(span + source(j) * rows, rows), rows)]
        return pltpu.make_async_remote_copy(
            src_ref=here, dst_ref=here, send_sem=lsend.at[j], recv_sem=lrecv.at[j],
            device_id=(blk, peer(j)), device_id_type=MESH,
        )

    def low_onward(j):
        s = source(j)
        return pltpu.make_async_remote_copy(
            src_ref=lbuf.at[pl.ds(pl.multiple_of(span + s * rows, rows), rows)],
            dst_ref=lbuf.at[pl.ds(pl.multiple_of(s * rows, rows), rows)],
            send_sem=msend.at[j], recv_sem=mrecv.at[j],
            device_id=(blk + 1, u), device_id_type=MESH,
        )

    def low_arrived(j):
        here = lbuf.at[pl.ds(pl.multiple_of(source(j) * rows, rows), rows)]
        return pltpu.make_async_remote_copy(
            src_ref=here, dst_ref=here, send_sem=msend.at[j], recv_sem=mrecv.at[j],
            device_id=(blk, peer(1)), device_id_type=MESH,
        )

    early = min(1, chunks)
    ahead = min(3, chunks)
    for c in range(early):
        for j in range(1, nu):
            cross(j, c, 0).start()

    @pl.when(has_next)
    def _():
        for c in range(ahead):
            onward(0, c, 0).start()

    for i in range(3, 7):
        local[i].wait()

    def lift(c):
        extra = dot(low_vm, ups[:, cols(c)])
        vbuf[mine, cols(c)] = (vbuf[mine, cols(c)].astype(F32) + extra).astype(BF16)

    for j in range(1, nu):
        low_across(j).start()

    @pl.when(has_next)
    def _():
        low_onward(0).start()

    @pl.loop(0, early)
    def _(c):
        lift(c)
        for j in range(1, nu):
            cross(j, c, 1).start()

    @pl.loop(early, ahead)
    def _(c):
        lift(c)
        for j in range(1, nu):
            cross(j, c, 2).start()

    @pl.when(has_next)
    def _():
        @pl.loop(0, ahead)
        def _(c):
            onward(0, c, 1).start()

    @pl.loop(ahead, chunks)
    def _(c):
        lift(c)
        for j in range(1, nu):
            cross(j, c, 2).start()

    for v in range(nu):
        lend(v).start()

    lrq[...] = jnp.zeros_like(lrq)
    lrv[...] = jnp.zeros_like(lrv)

    @pl.when(jnp.logical_not(has_prev))
    def _():
        kbuf[pl.ds(0, span), :] = jnp.zeros((span, width), BF16)
        vbuf[pl.ds(0, span), :] = jnp.zeros((span, width), BF16)
        lbuf[pl.ds(0, span), :] = jnp.zeros((span, 2 * rank), BF16)

    for i in range(7, 9):
        local[i].wait()

    scale = HEAD ** (-0.5)
    key_at = lax.broadcasted_iota(jnp.int32, (rows, 2 * span), 1)
    usable = jnp.logical_or(key_at >= span, has_prev)

    def head(h):
        at = pl.ds(pl.multiple_of(h * HEAD, HEAD), HEAD)
        up = ups[:, at]
        keys = kbuf[:, at]
        values = vbuf[:, at]
        grad = gs[:, at]
        query = (qs[:, at].astype(F32) + dot(low_qm, up)).astype(BF16)
        scores = jnp.where(usable, outer(query, keys) * scale, -jnp.inf)
        weights = jnp.exp(scores - jnp.max(scores, axis=1, keepdims=True))
        total = jnp.sum(weights, axis=1, keepdims=True)
        probs = (weights * (1.0 / total)).astype(BF16)
        attended = dot(probs, values).astype(BF16)
        delta = jnp.sum(grad.astype(F32) * attended.astype(F32), axis=1, keepdims=True)
        score_grad = (probs.astype(F32) * (outer(grad, values) - delta)).astype(BF16)
        query_grad = (dot(score_grad, keys) * scale).astype(BF16)
        seen = dot(probs, lbuf[...]).astype(BF16)
        gup = (inner(low_qm, query_grad) + inner(seen, grad)).astype(BF16)
        lifted = jnp.where(lane >= rank, outer(grad, up), 0.0).astype(BF16)
        return attended, gup, outer(query_grad, up), inner(probs, lifted)

    together = 2 if span <= 2 * HEAD else 1

    def head_group(c, offset):
        first = place(c) * heads + offset
        results = [head(first + i) for i in range(together)]
        for i, (attended, gup, _, _) in enumerate(results):
            h = first + i
            att_ref[:, pl.ds(pl.multiple_of(h * HEAD, HEAD), HEAD)] = attended
            row = pl.multiple_of((offset + i) * 2 * rank, 2 * rank)
            cell = lax.rem(c, cells)
            acc[c // cells, lax.rem(cell, 2), cell // 2, pl.ds(row, 2 * rank), :] = gup
        lrq[...] += jnp.where(lane < rank, sum(r[2] for r in results), 0.0)
        lrv[...] += sum(r[3] for r in results)

    heads = CHUNK // HEAD
    soon = max(parts - 1, 0)

    @pl.loop(0, chunks + 1)
    def _(c):
        @pl.when(c < chunks)
        def _():
            for j in range(1, nu):
                crossed(j, c).wait_recv()

                @pl.when(has_next)
                def _():
                    onward(j, c, 2).start()

            @pl.when(jnp.logical_and(has_next, c + ahead < chunks))
            def _():
                onward(0, c + ahead, 2).start()

        @pl.when(c == 1)
        def _():
            for j in range(1, nu):
                low_crossed(j).wait_recv()

                @pl.when(has_next)
                def _():
                    low_onward(j).start()

            @pl.when(has_prev)
            def _():
                for j in range(nu):
                    low_arrived(j).wait_recv()

        @pl.when(c == chunks - 1)
        def _():
            each(0, soon, send_out)

        @pl.when(c > 0)
        def _():
            @pl.when(has_prev)
            def _():
                arrived(c - 1).wait_recv()

            @pl.loop(0, heads // together)
            def _(i):
                head_group(c - 1, i * together)


            @pl.when(lax.rem(c, cells) == 0)
            def _():
                swap(c // cells - 1).start()

            @pl.when(jnp.logical_and(lax.rem(c, cells) == 2 % cells, jnp.logical_and(c >= cells + 2, c < chunks)))
            def _():
                pair_sum((c - 2) // cells - 1)

    lrs[...] = lrv[...].astype(BF16)

    def terms(k, j, base):
        s = peer(j)
        return pltpu.make_async_remote_copy(
            src_ref=lrs.at[pl.ds(pl.multiple_of(base + s * rows, rows), rows)],
            dst_ref=lrin.at[k, j],
            send_sem=rsend.at[k, j], recv_sem=rrecv.at[k, j],
            device_id=(blk - k, s), device_id_type=MESH,
        )

    for j in range(1, nu):
        terms(0, j, span).start()

    @pl.when(has_prev)
    def _():
        for j in range(nu):
            terms(1, j, 0).start()

    each(soon, parts, pair_up)
    each(0, soon, plane_sum)

    lrq[...] += lrv[mine, :]
    for j in range(1, nu):
        terms(0, j, span).wait_recv()
        lrq[...] += lrin[0, j].astype(F32)

    @pl.when(has_next)
    def _():
        for j in range(nu):
            terms(1, j, 0).wait_recv()
            lrq[...] += lrin[1, j].astype(F32)

    lowb[0] = lrq[...].T.astype(BF16)
    tell().start()

    def project(p):
        for v in range(nu):
            at = pl.ds(pl.multiple_of((v * 2 + core) * strip + p * CHUNK, CHUNK), CHUNK)
            there = pl.ds(pl.multiple_of(v * strip + p * CHUNK, CHUNK), CHUNK)
            block = (dot(lowb[0], tok[:, at]) + dot(lowb[1], tok2[:, there])).astype(BF16)
            for i in range(heads):
                part[parts + p, v, pl.ds(i * 2 * rank, 2 * rank), :] = block[:, i * HEAD:(i + 1) * HEAD]
        for o in range(1, group):
            scatter(parts + p, o).start()

    def lay_out(n, t, outs):
        shared_here = res.at[n, 1 - core] if t == 1 else res.at[n, 1 - core, u]
        whole(shared_here, esend.at[t], erecv.at[n]).wait_recv()
        for v in range(nu if t == 1 else 1):
            for k in range(2):
                for i in range(heads):
                    h = ((v * 2 + k) * parts + n - t * parts) * heads + i
                    at = pl.ds(pl.multiple_of(h * HEAD, HEAD), HEAD)
                    w = v if t == 1 else u
                    outs[0][:, at] = res[n, k, w, pl.ds(i * 2 * rank, rank), :]
                    outs[1][:, at] = res[n, k, w, pl.ds(i * 2 * rank + rank, rank), :]

    whole(tok2, gsend.at[0], grecv.at[0]).wait_recv()
    tell().wait_recv()
    each(0, parts, project)

    def finish_up(n):
        lay_out(n, 0, (upq_out, upv_out))

    def finish_down(n):
        lay_out(n, 1, (downq_out, downv_out))

    order = []
    for p in range(parts):
        late = 3.0 if p >= soon else 0.0
        if p >= soon:
            order.append((-0.5, plane_sum, (p,)))
        order += [
            (0.0 + late, line_sum, (p,)), (3.5 + late, widen, (p, 0)),
            (14.0 + 0.7 * p, hand_over, (p, 0)), (17.0 + 0.7 * p, finish_up, (p,)),
        ]
        n, at = parts + p, 1.4 * p
        order += [
            (2.6 + at, plane_sum, (n,)), (7.0 + at, line_sum, (n,)), (12.0 + at, widen, (n, 1)),
            (17.5 + at, hand_over, (n, 1)), (19.5 + at, finish_down, (n,)),
        ]
    for _, work, what in sorted(order, key=lambda item: item[0]):
        work(*what)

    whole(tok2, gsend.at[0], grecv.at[0]).wait_send()
    tell().wait_send()
    whole(pair, psend.at[0], precv.at[0]).wait_send()
    whole(plane_in, asend.at[0], arecv.at[0]).wait_send()
    whole(line_in, bsend.at[0], brecv.at[0]).wait_send()
    whole(line_in, csend.at[0], crecv.at[0]).wait_send()
    for i in range(2):
        some = pl.ds(i * parts, parts)
        whole(
            plane_in.at[some, pl.ds(0, (inners, group)[i] - 1)], dsend.at[i], drecv.at[0]
        ).wait_send()
    whole(res.at[pl.ds(0, parts), 0, 0], esend.at[0], erecv.at[0]).wait_send()
    whole(res.at[pl.ds(parts, parts), 0], esend.at[1], erecv.at[0]).wait_send()

    everything = kv.at[:, mine, :]
    for j in range(1, nu):
        remote(everything, everything, xsend.at[j], xrecv.at[j - 1, 0], (blk, peer(j))).wait_send()

    @pl.when(has_next)
    def _():
        for j in range(nu):
            remote(everything, everything, fsend.at[j], frecv.at[0], (blk + 1, u)).wait_send()

    for j in range(1, nu):
        low_across(j).wait_send()

    @pl.when(has_next)
    def _():
        for j in range(nu):
            low_onward(j).wait_send()

    for j in range(1, nu):
        terms(0, j, span).wait_send()

    @pl.when(has_prev)
    def _():
        for j in range(nu):
            terms(1, j, 0).wait_send()


def grid_of(nb):
    half = nb // 2
    inners = 2 if half % 2 == 0 else 1
    return inners, half // inners


def fused(nb, nu, *operands):
    rows, width = operands[0].shape
    rank = operands[6].shape[0]
    span = nu * rows
    chunks = width // CHUNK
    cells = 2 * nu
    parts = chunks // cells
    inners, outers = grid_of(nb)
    group = nu * inners
    sub = CHUNK // inners
    lanes = 2 * rank
    dma = pltpu.SemaphoreType.DMA
    anywhere = pl.BlockSpec(memory_space=pl.ANY)
    here = pl.BlockSpec(memory_space=pltpu.VMEM)
    return pl.pallas_call(
        functools.partial(fused_kernel, nb, nu),
        out_shape=(
            pltpu.VMEM((rows, width), BF16),
            pltpu.VMEM((rank, width), BF16),
            pltpu.VMEM((rank, width), BF16),
            pltpu.VMEM((rank, width // nu), BF16),
            pltpu.VMEM((rank, width // nu), BF16),
        ),
        in_specs=[anywhere] * 9,
        out_specs=(here,) * 5,
        scratch_shapes=[
            pltpu.VMEM((2, 2 * span, width), BF16),
            pltpu.VMEM((2 * span, lanes), BF16),
            pltpu.VMEM((rows, width), BF16),
            pltpu.VMEM((rows, width), BF16),
            pltpu.VMEM((rows, width), BF16),
            pltpu.VMEM((lanes, width), BF16),
            pltpu.VMEM((lanes, width), BF16),
            pltpu.VMEM((rows, lanes), F32),
            pltpu.VMEM((2 * span, lanes), F32),
            pltpu.VMEM((2 * span, lanes), BF16),
            pltpu.VMEM((2, nu, rows, lanes), BF16),
            pltpu.VMEM((rows, width // 2), BF16),
            pltpu.VMEM((2, lanes, rows), BF16),
            pltpu.VMEM((parts, 2, nu, CHUNK, lanes), BF16),
            pltpu.VMEM((parts, nu, CHUNK, lanes), BF16),
            pltpu.VMEM((2 * parts, nu, CHUNK, lanes), BF16),
            pltpu.VMEM((2 * parts, group - 1, sub, lanes), BF16),
            pltpu.VMEM((2 * parts, sub, lanes), BF16),
            pltpu.VMEM((2 * parts, outers - 1, sub // outers, lanes), BF16),
            pltpu.VMEM((2 * parts, 2, nu, CHUNK, lanes), BF16),
            dma((9,)),
            dma((nu,)), dma((nu - 1, chunks)),
            dma((nu,)), dma((chunks,)),
            dma((nu,)), dma((nu,)), dma((nu,)), dma((nu,)),
            dma((2, nu)), dma((2, nu)),
            dma((1,)), dma((parts,)),
            dma((1,)), dma((2 * parts,)),
            dma((1,)), dma((2 * parts,)),
            dma((1,)), dma((2 * parts,)),
            dma((2,)), dma((2 * parts,)),
            dma((2,)), dma((2 * parts,)),
            dma((2,)), dma((2,)),
        ],
        compiler_params=pltpu.CompilerParams(
            collective_id=2, has_side_effects=True, vmem_limit_bytes=60_000_000
        ),
    )(*operands)


def fits(nb, nu, rows, width, rank):
    inners, outers = grid_of(nb)
    return (
        2 * rank == HEAD
        and width % (2 * nu * CHUNK) == 0
        and CHUNK % (16 * inners * outers) == 0
        and nu * rows <= CHUNK
    )


def deliver_kernel(*refs):
    count = len(refs) // 2
    sources, targets, sem = refs[:count], refs[count:2 * count], refs[-1]
    copies = [pltpu.make_async_copy(a, b, sem.at[i]) for i, (a, b) in enumerate(zip(sources, targets))]
    for copy in copies:
        copy.start()
    for copy in copies:
        copy.wait()


def deliver(*arrays):
    return pl.pallas_call(
        deliver_kernel,
        out_shape=tuple(jax.ShapeDtypeStruct(a.shape, a.dtype) for a in arrays),
        in_specs=[pl.BlockSpec(memory_space=pl.ANY)] * len(arrays),
        out_specs=tuple(pl.BlockSpec(memory_space=pl.ANY) for _ in arrays),
        scratch_shapes=[pltpu.SemaphoreType.DMA((len(arrays),))],
    )(*(pltpu.with_memory_space_constraint(a, pltpu.VMEM) for a in arrays))


def per_device(nb, nu, tokens, query_base, key_base, value_base, out_grad, down_q, up_q, down_v, up_v):
    operands = (tokens, query_base, key_base, value_base, out_grad, down_q.T, up_q, down_v.T, up_v)
    if fits(nb, nu, *tokens.shape, up_q.shape[0]):
        attended, grad_down_q, grad_down_v, grad_up_q, grad_up_v = deliver(*fused(nb, nu, *operands))
        return attended, grad_down_q.T, grad_up_q, grad_down_v.T, grad_up_v
    attended, gup, lowrank = attention(nb, nu, *operands)
    grad_down_q, grad_down_v, grad_up_q, grad_up_v = reduction(nb, nu, tokens, lowrank, gup)
    return attended, grad_down_q.T, grad_up_q, grad_down_v.T, grad_up_v


def solution(mesh):
    split = P(("blk", "uly"), None)
    return jax.shard_map(
        functools.partial(per_device, mesh.shape["blk"], mesh.shape["uly"]),
        mesh=mesh,
        in_specs=(split,) * 5 + (P(),) * 4,
        out_specs=(split, P(), P(None, "uly"), P(), P(None, "uly")),
        check_vma=False,
    )
```
